32 devices in a mesh: dp: 8 (over y, x, core), mp: 4 (over z).
Axes of the slice: x: 2, y: 2, z: 4, core: 2. Of those that a mesh axis runs over, the one named last changes fastest.
Arguments:
- inputs: bfloat16 [16, 512, 1024], P('dp'), may hold values from -6 to 6
- memory: bfloat16 [16, 512, 1024], P('dp'), may hold values from -6 to 6
- compressed_memory: bfloat16 [16, 512, 1024], P('dp'), may hold values from -6 to 6
- memory_fill: int32 [16], P('dp'), may hold values from 0 to 512, as said below
- compressed_fill: int32 [16], P('dp'), may hold values from 0 to 512, as said below
- first_gain: float32 [1024], replicated, may hold values from 0.5 to 1.5
- query_weight: bfloat16 [1024, 1024], P(None, 'mp'), may hold values from -0.1875 to 0.1875
- key_weight: bfloat16 [1024, 1024], P(None, 'mp'), may hold values from -0.1875 to 0.1875
- value_weight: bfloat16 [1024, 1024], P(None, 'mp'), may hold values from -0.1875 to 0.1875
- relative_bias: float32 [8, 22], P('mp'), may hold values from -1.5 to 1.5
- output_weight: bfloat16 [1024, 1024], P('mp'), may hold values from -1.5 to 1.5
- second_gain: float32 [1024], replicated, may hold values from 0.5 to 1.5
- up_weight: bfloat16 [1024, 4096], P(None, 'mp'), may hold values from -0.1875 to 0.1875
- down_weight: bfloat16 [4096, 1024], P('mp'), may hold values from -0.09375 to 0.09375
- compress_weight: bfloat16 [2048, 1024], P(None, 'mp'), may hold values from -0.125 to 0.125
- grad_output: bfloat16 [16, 512, 1024], P('dp'), may hold values from -6 to 6
- grad_compressed: bfloat16 [16, 256, 1024], P('dp', None, 'mp'), may hold values from -6 to 6
Outputs:
- outputs: bfloat16 [16, 512, 1024], P('dp')
- compressed: bfloat16 [16, 256, 1024], P('dp', None, 'mp')
- grad_inputs: bfloat16 [16, 512, 1024], P('dp')
- grad_first_gain: float32 [1024], replicated
- grad_query: float32 [1024, 1024], P(None, 'mp')
- grad_key: float32 [1024, 1024], P(None, 'mp')
- grad_value: float32 [1024, 1024], P(None, 'mp')
- grad_relative: float32 [8, 22], P('mp')
- grad_output_weight: float32 [1024, 1024], P('mp')
- grad_second_gain: float32 [1024], replicated
- grad_up: float32 [1024, 4096], P(None, 'mp')
- grad_down: float32 [4096, 1024], P('mp')
- grad_compress: float32 [2048, 1024], P(None, 'mp')
The draws below stay inside these ranges and needn't reach their ends.
Inputs may be any that keep to these rules, and one draw needn't show every extreme that they name: `memory_fill`: some stream has a full memory and some stream an empty one. `compressed_fill`: some stream has a full compressed memory and some stream an empty one.
All inputs are finite; a program needn't handle non-finite values.
Results may differ from the reference program's by a relative error of at most 0.023.
Values sent between devices are 32-bit elements; how exact they have to be, the bound alone decides.
A program may use at most 320 MiB of HBM per device.

```python
import math
import jax
import jax.numpy as jnp
from jax import lax

D = 1024
H = 8
DH = 128
FF = 4096
SEG = 512
MEM = 512
CMEM = 512
NB = 22
STREAMS = 16
CR = 256


def fill_counts(key, salt_value, most_value):
    first_key, second_key = jax.random.split(jax.random.fold_in(key, salt_value))
    counts = jax.random.randint(first_key, (STREAMS,), 0, most_value + 1)
    stream_order = jax.random.permutation(second_key, STREAMS)
    counts = counts.at[stream_order[0]].set(most_value).at[stream_order[1]].set(0)
    return counts.astype(jnp.int32)


def draw_memory_fill(key, part):
    return fill_counts(key, 11, MEM)


def draw_compressed_fill(key, part):
    return fill_counts(key, 23, CMEM)


def level_of(rng, dims, cuts, low, largest):
    def one(dim, blocks):
        draws = jax.random.uniform(jax.random.fold_in(jax.random.fold_in(rng, 6), dim), (blocks,), jnp.float32, low / len(cuts), largest / len(cuts))
        return jnp.repeat(jnp.exp(draws), dims[dim] // blocks).reshape((-1,) + (1,) * (len(dims) - dim - 1))

    factor_of = one(*cuts[0])
    for cut in cuts[1:]:
        factor_of = factor_of * one(*cut)
    return factor_of


def scatter_about(own_key, dims, width, bound, shards=(), kind=jnp.bfloat16):
    loudness = level_of(own_key, dims, shards, -0.22, 0.18) if shards else 1.0
    values = jax.random.normal(own_key, dims, jnp.float32) * width * loudness
    return jnp.minimum(jnp.maximum(values, -bound), bound).astype(kind)


def setup_inputs(seed: int = 0) -> dict:
    keys = jax.random.split(jax.random.key(seed), 18)
    inputs = scatter_about(keys[0], (STREAMS, SEG, D), 1.0, 6.0, ((0, 8),))
    memory = scatter_about(keys[1], (STREAMS, MEM, D), 1.0, 6.0, ((0, 8),))
    compressed_memory = scatter_about(keys[2], (STREAMS, CMEM, D), 1.0, 6.0, ((0, 8),))
    memory_fill = draw_memory_fill(jax.random.fold_in(keys[17], 71), 0)
    compressed_fill = draw_compressed_fill(jax.random.fold_in(keys[17], 71), 0)
    first_gain = jnp.clip(1.0 + 0.1 * jax.random.normal(keys[5], (D,), jnp.float32), 0.5, 1.5)
    query_weight = scatter_about(keys[6], (D, H * DH), D ** -0.5, 0.1875, ((1, 4),))
    key_weight = scatter_about(keys[7], (D, H * DH), D ** -0.5, 0.1875, ((1, 4),))
    value_weight = scatter_about(keys[8], (D, H * DH), D ** -0.5, 0.1875, ((1, 4),))
    relative_bias = scatter_about(keys[9], (H, NB), 0.25, 1.5, ((0, 4),), jnp.float32)
    output_weight = scatter_about(keys[10], (H * DH, D), 16 ** -0.5, 1.5, ((0, 4),))
    second_gain = jnp.clip(1.0 + 0.1 * jax.random.normal(keys[11], (D,), jnp.float32), 0.5, 1.5)
    up_weight = scatter_about(keys[12], (D, FF), D ** -0.5, 0.1875, ((1, 4),))
    down_weight = scatter_about(keys[13], (FF, D), FF ** -0.5, 0.09375, ((0, 4),))
    compress_weight = scatter_about(keys[14], (2 * D, D), (2 * D) ** -0.5, 0.125, ((1, 4),))
    grad_output = scatter_about(keys[15], (STREAMS, SEG, D), 1.0, 6.0, ((0, 8),))
    grad_compressed = scatter_about(keys[16], (STREAMS, CR, D), 1.0, 6.0, ((0, 8), (2, 4)))
    return dict(inputs=inputs, memory=memory, compressed_memory=compressed_memory, memory_fill=memory_fill, compressed_fill=compressed_fill, first_gain=first_gain, query_weight=query_weight, key_weight=key_weight, value_weight=value_weight, relative_bias=relative_bias, output_weight=output_weight, second_gain=second_gain, up_weight=up_weight, down_weight=down_weight, compress_weight=compress_weight, grad_output=grad_output, grad_compressed=grad_compressed)


reach_marks = (1, 2, 3, 4, 5, 6, 7, 8, 12, 16, 24, 32, 48, 64, 96, 128, 192, 256, 384, 512, 768, 1024)
epsilon = 1e-06
highest = lax.Precision.HIGHEST

@jax.custom_vjp
def low(v):
    return lax.optimization_barrier(v.astype(jnp.bfloat16)).astype(jnp.float32)

@jax.custom_vjp
def low_back(v):
    return v

def low_keep(v):
    return (low(v), None)

def low_pass(kept, grad):
    return (grad,)

def back_keep(v):
    return (v, None)

def back_low(kept, grad):
    return (low(grad),)
low.defvjp(low_keep, low_pass)
low_back.defvjp(back_keep, back_low)

def rms_scale(source, gain):
    return source * lax.rsqrt(lax.optimization_barrier(jnp.mean(source * source, axis=-1, keepdims=True)) + epsilon) * gain

def product(left, right):
    return jnp.dot(left, right, precision=highest)

def layer_stream(seg_rows, memory_rows, packed_rows, memory_count, packed_count, first_gain, query_weight, key_weight, value_weight, relative_bias, output_weight, second_gain, up_weight, down_weight, compress_weight):
    kept_count = CMEM + MEM
    key_count = kept_count + SEG
    stacked = jnp.concatenate([packed_rows, memory_rows, seg_rows], axis=0)
    unit_rows = low(rms_scale(stacked, first_gain))
    queries = low_back(low(product(unit_rows[kept_count:], query_weight)))
    key_rows = low_back(low(product(unit_rows, key_weight)))
    value_rows = low_back(low(product(unit_rows, value_weight)))
    distance = jnp.arange(SEG, dtype=jnp.int32)[:, None] + kept_count - jnp.arange(key_count, dtype=jnp.int32)[None, :]
    valid_keys = jnp.concatenate([jnp.arange(CMEM, dtype=jnp.int32) >= CMEM - packed_count, jnp.arange(MEM, dtype=jnp.int32) >= MEM - memory_count, jnp.ones((SEG,), jnp.bool_)])
    allowed = (distance >= 0) & valid_keys[None, :]
    bias_table = jnp.zeros((H, SEG, key_count), jnp.float32)
    for position, mark_value in enumerate(reach_marks):
        bias_table = bias_table + relative_bias[:, position][:, None, None] * (distance >= mark_value).astype(jnp.float32)[None]
    query_heads = queries.reshape(SEG, H, DH)
    key_heads = key_rows.reshape(key_count, H, DH)
    value_heads = value_rows.reshape(key_count, H, DH)
    scores = jnp.einsum('shd,khd->hsk', query_heads, key_heads, precision=highest) * (1.0 / math.sqrt(DH)) + bias_table
    scores = low_back(scores)
    masked = jnp.where(allowed[None], scores, -1e+30)
    attend_prob = low(jax.nn.softmax(masked, axis=-1))
    mixed_heads = jnp.einsum('hsk,khd->shd', attend_prob, value_heads, precision=highest).reshape(SEG, H * DH)
    mixed_heads = low_back(low(mixed_heads))
    residual = seg_rows + low_back(product(mixed_heads, output_weight))
    ffn_input = low(rms_scale(residual, second_gain))
    pre_act = low_back(product(ffn_input, up_weight))
    activated = low(jax.nn.gelu(pre_act, approximate=True))
    outputs = residual + low_back(product(activated, down_weight))
    slot_index = jnp.arange(MEM, dtype=jnp.int32)
    live_rows = jnp.where((slot_index >= MEM - memory_count)[:, None], memory_rows, jnp.zeros_like(memory_rows))
    evicted = live_rows[MEM - 2 * CR:].reshape(CR, 2 * D)
    packed_new = product(evicted, compress_weight)
    return (outputs, packed_new)

def reference(inputs, memory, compressed_memory, memory_fill, compressed_fill, first_gain, query_weight, key_weight, value_weight, relative_bias, output_weight, second_gain, up_weight, down_weight, compress_weight, grad_output, grad_compressed):
    weight_set = tuple((item.astype(jnp.float32) for item in (first_gain, query_weight, key_weight, value_weight, relative_bias, output_weight, second_gain, up_weight, down_weight, compress_weight)))

    def stream_step(totals, stream_item):
        seg_rows, memory_rows, packed_rows, memory_count, packed_count, grad_rows, grad_packed = stream_item

        def forward(rows_in, *weights):
            return layer_stream(rows_in, memory_rows, packed_rows, memory_count, packed_count, *weights)
        (outputs, packed_new), pullback = jax.vjp(forward, seg_rows, *weight_set)
        gradients = pullback((grad_rows, grad_packed))
        totals = tuple((total + grad_item for total, grad_item in zip(totals, gradients[1:])))
        return (totals, (outputs.astype(jnp.bfloat16), packed_new.astype(jnp.bfloat16), gradients[0].astype(jnp.bfloat16)))
    initial = tuple((jnp.zeros_like(item) for item in weight_set))
    stream_items = (inputs.astype(jnp.float32), memory.astype(jnp.float32), compressed_memory.astype(jnp.float32), memory_fill, compressed_fill, grad_output.astype(jnp.float32), grad_compressed.astype(jnp.float32))
    totals, (outputs, packed_all, grad_all) = lax.scan(stream_step, initial, stream_items)
    return (outputs, packed_all, grad_all, totals[0], totals[1], totals[2], totals[3], totals[4], totals[5], totals[6], totals[7], totals[8], totals[9])
```

```python
import functools
import math

import jax
import jax.numpy as jnp
from jax import lax
from jax.experimental import pallas as pl
from jax.experimental.pallas import tpu as pltpu
from jax.sharding import PartitionSpec as P

reach_marks = (1, 2, 3, 4, 5, 6, 7, 8, 12, 16, 24, 32, 48, 64, 96, 128, 192, 256, 384, 512, 768, 1024)
epsilon = 1e-06
masked_score = -1e30
block = 128
query_block = 256
f32 = jnp.float32
bf16 = jnp.bfloat16


def mm(left, right):
    return jnp.dot(left, right, preferred_element_type=f32)


def mm_t0(left, right):
    return lax.dot_general(left, right, (((0,), (0,)), ((), ())), preferred_element_type=f32)


def mm_t1(left, right):
    return lax.dot_general(left, right, (((1,), (1,)), ((), ())), preferred_element_type=f32)


def row_scale(source):
    return lax.rsqrt(jnp.mean(source * source, axis=-1, keepdims=True) + epsilon)


def diagonal_count(seg_len, kept_count):
    return (seg_len + kept_count) // block + 1


def diagonal_of(seg_len, kept_count, column):
    return (seg_len + kept_count) // block - 1 - column


def strip_start(seg_len, sub_block):
    return (seg_len // block - 1 - sub_block) * block


def bias_block(bias_ref, head, diagonal, transposed):
    rows = lax.broadcasted_iota(jnp.int32, (block, block), 0)
    cols = lax.broadcasted_iota(jnp.int32, (block, block), 1)
    distance = diagonal * block + ((cols - rows) if transposed else (rows - cols))
    lowest, highest = diagonal * block - block + 1, diagonal * block + block - 1
    base = jnp.float32(0.0)
    for position, mark_value in enumerate(reach_marks):
        if mark_value <= lowest:
            base = base + bias_ref[head, position]
    value = jnp.full((block, block), base, f32)
    for position, mark_value in enumerate(reach_marks):
        if lowest < mark_value <= highest:
            value = value + jnp.where(distance >= mark_value, bias_ref[head, position], 0.0)
    if lowest < 0:
        value = jnp.where(distance >= 0, value, masked_score)
    return value


def live_mask(shape, axis, packed_len, mem_len, packed_count, memory_count):
    slot = lax.broadcasted_iota(jnp.int32, shape, axis)
    dead_packed = (slot < packed_len) & (slot < packed_len - packed_count)
    dead_memory = (slot >= packed_len) & (slot < packed_len + mem_len - memory_count)
    return jnp.where(dead_packed | dead_memory, masked_score, 0.0).astype(f32)


def attend_kernel(
    sizes,
    memory_fill,
    packed_fill,
    bias_ref,
    seg_ref,
    memory_ref,
    packed_ref,
    gain_ref,
    wq_ref,
    wk_ref,
    wv_ref,
    unit_ref,
    q_ref,
    k_ref,
    v_ref,
    mixed_ref,
    log_ref,
    strip,
    live,
):
    seg_len, mem_len, packed_len, heads, head_dim = sizes
    kept = mem_len + packed_len
    keys = kept + seg_len
    stream = pl.program_id(0)
    scale = 1.0 / math.sqrt(head_dim)
    gain = gain_ref[...]
    start = 0
    for part_ref, size in ((packed_ref, packed_len), (memory_ref, mem_len), (seg_ref, seg_len)):
        rows = part_ref[0].astype(f32)
        unit = (rows * row_scale(rows) * gain).astype(bf16)
        unit_ref[0, start : start + size, :] = unit
        k_ref[0, start : start + size, :] = mm(unit, wk_ref[...]).astype(bf16)
        v_ref[0, start : start + size, :] = mm(unit, wv_ref[...]).astype(bf16)
        if start == kept:
            q_ref[0] = mm(unit, wq_ref[...]).astype(bf16)
        start += size
    live[...] = live_mask((8, kept), 1, packed_len, mem_len, packed_fill[stream], memory_fill[stream])
    for head in range(heads):
        lanes = slice(head * head_dim, (head + 1) * head_dim)
        for column in range(diagonal_count(seg_len, kept)):
            strip[:, column * block : (column + 1) * block] = bias_block(
                bias_ref, head, diagonal_of(seg_len, kept, column), False
            )
        for index in range(seg_len // query_block):
            reach = kept + (index + 1) * query_block
            rows = slice(index * query_block, (index + 1) * query_block)
            score = mm_t1(q_ref[0, rows, lanes], k_ref[0, :reach, lanes]) * scale
            parts = []
            for sub in range(query_block // block):
                first = strip_start(seg_len, index * (query_block // block) + sub)
                parts.append(strip[:, first : first + reach])
            score = score + jnp.concatenate(parts, axis=0)
            score = jnp.concatenate([score[:, :kept] + live[0:1, :], score[:, kept:]], axis=1)
            top = jnp.max(score, axis=-1, keepdims=True)
            weight = jnp.exp(score - top)
            total = jnp.sum(weight, axis=-1, keepdims=True)
            log_ref[0, head, rows, :] = top + jnp.log(total)
            mixed = mm(weight.astype(bf16), v_ref[0, :reach, lanes]) * (1.0 / total)
            mixed_ref[0, rows, lanes] = mixed.astype(bf16)


def attend(inputs, memory, packed, memory_fill, packed_fill, gain, wq, wk, wv, bias):
    streams, seg_len, width = inputs.shape
    mem_len, packed_len = memory.shape[1], packed.shape[1]
    heads = bias.shape[0]
    local = wq.shape[1]
    keys = seg_len + mem_len + packed_len
    sizes = (seg_len, mem_len, packed_len, heads, local // heads)
    smem = pl.BlockSpec(memory_space=pltpu.SMEM)

    def rows_of(count, columns):
        return pl.BlockSpec((1, count, columns), lambda s: (s, 0, 0))

    def whole(shape):
        return pl.BlockSpec(shape, lambda s: (0,) * len(shape))

    return pl.pallas_call(
        functools.partial(attend_kernel, sizes),
        grid=(streams,),
        in_specs=[
            smem,
            smem,
            smem,
            rows_of(seg_len, width),
            rows_of(mem_len, width),
            rows_of(packed_len, width),
            whole((1, width)),
            whole(wq.shape),
            whole(wk.shape),
            whole(wv.shape),
        ],
        out_specs=[
            rows_of(keys, width),
            rows_of(seg_len, local),
            rows_of(keys, local),
            rows_of(keys, local),
            rows_of(seg_len, local),
            pl.BlockSpec((1, heads, seg_len, 1), lambda s: (s, 0, 0, 0)),
        ],
        out_shape=[
            jax.ShapeDtypeStruct((streams, keys, width), bf16),
            jax.ShapeDtypeStruct((streams, seg_len, local), bf16),
            jax.ShapeDtypeStruct((streams, keys, local), bf16),
            jax.ShapeDtypeStruct((streams, keys, local), bf16),
            jax.ShapeDtypeStruct((streams, seg_len, local), bf16),
            jax.ShapeDtypeStruct((streams, heads, seg_len, 1), f32),
        ],
        scratch_shapes=[
            pltpu.VMEM((block, diagonal_count(seg_len, mem_len + packed_len) * block), f32),
            pltpu.VMEM((8, mem_len + packed_len), f32),
        ],
        compiler_params=pltpu.CompilerParams(vmem_limit_bytes=60 << 20),
        cost_estimate=pl.CostEstimate(
            flops=streams * (2 * keys * width * local * 3 + 4 * seg_len * keys * local),
            bytes_accessed=streams * keys * (width * 4 + local * 6),
            transcendentals=streams * heads * seg_len * keys,
        ),
        name="attend",
    )(memory_fill, packed_fill, bias, inputs, memory, packed, gain[None, :], wq, wk, wv)


def attend_back_kernel(
    sizes,
    memory_fill,
    packed_fill,
    bias_ref,
    unit_ref,
    q_ref,
    k_ref,
    v_ref,
    log_ref,
    gm_ref,
    wq_ref,
    wk_ref,
    wv_ref,
    gunit_ref,
    gq_ref,
    gk_ref,
    gv_ref,
    rel_ref,
    strip,
    live,
    dk_sum,
    dv_sum,
    dq_low,
    dk_low,
    dv_low,
    strip_sum,
):
    seg_len, mem_len, packed_len, heads, head_dim = sizes
    kept = mem_len + packed_len
    keys = kept + seg_len
    stream = pl.program_id(0)
    scale = 1.0 / math.sqrt(head_dim)

    @pl.when(stream == 0)
    def _():
        strip_sum[...] = jnp.zeros_like(strip_sum)
        gq_ref[...] = jnp.zeros_like(gq_ref)
        gk_ref[...] = jnp.zeros_like(gk_ref)
        gv_ref[...] = jnp.zeros_like(gv_ref)

    live[...] = live_mask((kept, block), 0, packed_len, mem_len, packed_fill[stream], memory_fill[stream])
    subs = query_block // block
    for head in range(heads):
        lanes = slice(head * head_dim, (head + 1) * head_dim)
        for column in range(diagonal_count(seg_len, kept)):
            strip[column * block : (column + 1) * block, :] = bias_block(
                bias_ref, head, diagonal_of(seg_len, kept, column), True
            )
        for index in range(seg_len // query_block):
            reach = kept + (index + 1) * query_block
            rows = slice(index * query_block, (index + 1) * query_block)
            queries = q_ref[0, rows, lanes]
            grads = gm_ref[0, rows, lanes]
            key_rows = k_ref[0, :reach, lanes]
            score = mm_t1(key_rows, queries) * scale
            firsts = [strip_start(seg_len, index * subs + sub) for sub in range(subs)]
            score = score + jnp.concatenate([strip[first : first + reach, :] for first in firsts], axis=1)
            live_wide = jnp.concatenate([live[...]] * subs, axis=1)
            score = jnp.concatenate([score[:kept] + live_wide, score[kept:]], axis=0)
            prob = jnp.exp(score - log_ref[0, head, :, rows])
            grad_prob = mm_t1(v_ref[0, :reach, lanes], grads)
            delta = jnp.sum(prob * grad_prob, axis=0, keepdims=True)
            grad_score = (prob * (grad_prob - delta)).astype(bf16)
            dk_part = mm(grad_score, queries)
            dv_part = mm(prob.astype(bf16), grads)
            if index == seg_len // query_block - 1:
                earlier = kept + index * query_block
                if index:
                    dk_sum[:earlier] += dk_part[:earlier]
                    dv_sum[:earlier] += dv_part[:earlier]
                    dk_sum[earlier:] = dk_part[earlier:]
                    dv_sum[earlier:] = dv_part[earlier:]
                else:
                    dk_sum[...] = dk_part
                    dv_sum[...] = dv_part
            elif index:
                earlier = kept + index * query_block
                dk_sum[:earlier] += dk_part[:earlier]
                dv_sum[:earlier] += dv_part[:earlier]
                dk_sum[earlier:reach] = dk_part[earlier:]
                dv_sum[earlier:reach] = dv_part[earlier:]
            else:
                dk_sum[:reach] = dk_part
                dv_sum[:reach] = dv_part
            dq_low[rows, lanes] = (mm_t0(grad_score, key_rows) * scale).astype(bf16)
            for sub in range(subs):
                strip_sum[head, firsts[sub] : firsts[sub] + reach, :] += grad_score[
                    :, sub * block : (sub + 1) * block
                ].astype(f32)
        dk_low[:, lanes] = (dk_sum[...] * scale).astype(bf16)
        dv_low[:, lanes] = dv_sum[...].astype(bf16)
    gq_ref[...] += mm_t0(dq_low[...], unit_ref[0, kept:, :])
    gk_ref[...] += mm_t0(dk_low[...], unit_ref[0])
    gv_ref[...] += mm_t0(dv_low[...], unit_ref[0])
    gunit_ref[0] = (
        mm_t1(dq_low[...], wq_ref[...])
        + mm_t1(dk_low[kept:, :], wk_ref[...])
        + mm_t1(dv_low[kept:, :], wv_ref[...])
    )

    @pl.when(stream == pl.num_programs(0) - 1)
    def _():
        rows = lax.broadcasted_iota(jnp.int32, (block, block), 0)
        cols = lax.broadcasted_iota(jnp.int32, (block, block), 1)
        for head in range(heads):
            blocks = []
            for column in range(diagonal_count(seg_len, kept)):
                blocks.append(strip_sum[head, column * block : (column + 1) * block, :])
            for position, mark_value in enumerate(reach_marks):
                total = jnp.zeros((1, block), f32)
                for column, value in enumerate(blocks):
                    diagonal = diagonal_of(seg_len, kept, column)
                    lowest, highest = diagonal * block - block + 1, diagonal * block + block - 1
                    if mark_value <= lowest:
                        total = total + jnp.sum(value, axis=0, keepdims=True)
                    elif mark_value <= highest:
                        distance = diagonal * block + cols - rows
                        total = total + jnp.sum(
                            jnp.where(distance >= mark_value, value, 0.0), axis=0, keepdims=True
                        )
                rel_ref[head, position : position + 1, :] = total


def attend_back(unit, q, k, v, log_total, grad_mixed, memory_fill, packed_fill, wq, wk, wv, bias, mem_len, packed_len):
    streams, keys, width = unit.shape
    seg_len, local = q.shape[1:]
    heads = bias.shape[0]
    kept = mem_len + packed_len
    sizes = (seg_len, mem_len, packed_len, heads, local // heads)
    smem = pl.BlockSpec(memory_space=pltpu.SMEM)
    strip_len = diagonal_count(seg_len, kept) * block

    def rows_of(count, columns):
        return pl.BlockSpec((1, count, columns), lambda s: (s, 0, 0))

    def whole(shape):
        return pl.BlockSpec(shape, lambda s: (0,) * len(shape))

    return pl.pallas_call(
        functools.partial(attend_back_kernel, sizes),
        grid=(streams,),
        in_specs=[
            smem,
            smem,
            smem,
            rows_of(keys, width),
            rows_of(seg_len, local),
            rows_of(keys, local),
            rows_of(keys, local),
            pl.BlockSpec((1, heads, 1, seg_len), lambda s: (s, 0, 0, 0)),
            rows_of(seg_len, local),
            whole(wq.shape),
            whole(wk.shape),
            whole(wv.shape),
        ],
        out_specs=[
            rows_of(seg_len, width),
            whole((local, width)),
            whole((local, width)),
            whole((local, width)),
            whole((heads, 24, block)),
        ],
        out_shape=[
            jax.ShapeDtypeStruct((streams, seg_len, width), f32),
            jax.ShapeDtypeStruct((local, width), f32),
            jax.ShapeDtypeStruct((local, width), f32),
            jax.ShapeDtypeStruct((local, width), f32),
            jax.ShapeDtypeStruct((heads, 24, block), f32),
        ],
        scratch_shapes=[
            pltpu.VMEM((strip_len, block), f32),
            pltpu.VMEM((kept, block), f32),
            pltpu.VMEM((keys, local // heads), f32),
            pltpu.VMEM((keys, local // heads), f32),
            pltpu.VMEM((seg_len, local), bf16),
            pltpu.VMEM((keys, local), bf16),
            pltpu.VMEM((keys, local), bf16),
            pltpu.VMEM((heads, strip_len, block), f32),
        ],
        compiler_params=pltpu.CompilerParams(vmem_limit_bytes=60 << 20),
        cost_estimate=pl.CostEstimate(
            flops=streams * (8 * keys * width * local + 10 * seg_len * keys * local),
            bytes_accessed=streams * keys * (width * 2 + local * 6),
            transcendentals=streams * heads * seg_len * keys,
        ),
        name="attend_back",
    )(
        memory_fill,
        packed_fill,
        bias,
        unit,
        q,
        k,
        v,
        log_total.reshape(streams, heads, 1, seg_len),
        grad_mixed,
        wq,
        wk,
        wv,
    )


def line_gather(shard, size):
    me = lax.axis_index("mp")
    to_right = to_left = shard
    from_left, from_right = [], []
    for step in range(1, size):
        to_right = lax.ppermute(to_right, "mp", [(i, i + 1) for i in range(step - 1, size - 1)])
        to_left = lax.ppermute(to_left, "mp", [(i, i - 1) for i in range(1, size - step + 1)])
        from_left.append(to_right)
        from_right.append(to_left)
    ordered = jnp.stack(from_left[::-1] + [shard] + from_right)
    return lax.dynamic_slice_in_dim(ordered, size - 1 - me, size, 0)


def line_scatter(parts, size):
    me = lax.axis_index("mp")

    def pick(index):
        return lax.dynamic_index_in_dim(parts, jnp.clip(index, 0, size - 1), 0, keepdims=False)

    from_left = from_right = None
    for step in range(size - 1):
        rightward = pick(size - 1 - (step - me))
        leftward = pick(step - (size - 1 - me))
        if step:
            rightward = rightward + from_left
            leftward = leftward + from_right
        pairs = [(i, i + 1) for i in range(size - 1) if step >= i and size - 1 - (step - i) > i]
        from_left = lax.ppermute(rightward, "mp", pairs)
        from_right = lax.ppermute(leftward, "mp", [(size - 1 - a, size - 1 - b) for a, b in pairs])
    return pick(me) + from_left + from_right


def body(
    inputs,
    memory,
    compressed_memory,
    memory_fill,
    compressed_fill,
    first_gain,
    query_weight,
    key_weight,
    value_weight,
    relative_bias,
    output_weight,
    second_gain,
    up_weight,
    down_weight,
    compress_weight,
    grad_output,
    grad_compressed,
    *,
    mp_size,
):
    streams, seg_len, width = inputs.shape
    mem_len = memory.shape[1]
    packed_len = compressed_memory.shape[1]
    heads_here = relative_bias.shape[0]
    local = query_weight.shape[1]
    compress_count = grad_compressed.shape[1]
    rows = streams * seg_len
    shard_rows = rows // mp_size
    me = lax.axis_index("mp")

    def own_rows(source):
        return lax.dynamic_slice_in_dim(source, me * shard_rows, shard_rows, 0)

    nothing = jnp.minimum(jnp.abs(first_gain[0]), 0.0)
    full_out = (line_gather(output_weight.astype(f32), mp_size) + nothing).reshape(width, width).astype(bf16)

    slot_index = jnp.arange(mem_len, dtype=jnp.int32)
    live_rows = jnp.where(
        (slot_index[None, :] >= mem_len - memory_fill[:, None])[:, :, None], memory, jnp.zeros_like(memory)
    )
    evicted = live_rows.reshape(streams * compress_count, 2 * width)
    packed_new = mm(evicted, compress_weight).astype(bf16).reshape(streams, compress_count, -1)
    grad_compress_w = mm_t0(evicted, grad_compressed.reshape(streams * compress_count, -1))

    unit, q, k, v, mixed, log_total = attend(
        inputs,
        memory,
        compressed_memory,
        memory_fill,
        compressed_fill,
        first_gain,
        query_weight,
        key_weight,
        value_weight,
        relative_bias,
    )
    mixed_all = line_gather(mixed.reshape(rows, local).astype(f32), mp_size)
    mixed_all = (mixed_all + nothing).transpose(1, 0, 2).reshape(rows, width).astype(bf16)
    seg_rows = inputs.reshape(rows, width)
    grad_rows = grad_output.reshape(rows, width)
    residual = seg_rows.astype(f32) + mm(mixed_all, full_out)
    second_scale = row_scale(residual)
    ffn_input = (residual * second_scale * second_gain).astype(bf16)
    pre_act = mm(ffn_input, up_weight)
    inner = math.sqrt(2.0 / math.pi)
    squared = pre_act * pre_act
    tanh = jnp.tanh(inner * (pre_act + 0.044715 * pre_act * squared))
    activated = (0.5 * pre_act * (1.0 + tanh)).astype(bf16)
    slope = 0.5 * (1.0 + tanh) + 0.5 * pre_act * (1.0 - tanh * tanh) * (
        inner * (1.0 + 3.0 * 0.044715 * squared)
    )
    grad_pre = (slope * mm_t1(grad_rows, down_weight)).astype(bf16)
    grad_ffn = mm_t1(grad_pre, up_weight)
    grad_ffn = line_scatter(grad_ffn.reshape(mp_size, shard_rows, width), mp_size)

    own_residual = own_rows(residual)
    own_scale = own_rows(second_scale)
    own_grad = own_rows(grad_rows).astype(f32)
    normed = own_residual * own_scale
    grad_second = jnp.sum(grad_ffn * normed, axis=0)
    weighted = grad_ffn * second_gain
    grad_residual = own_grad + own_scale * (
        weighted - normed * jnp.mean(weighted * normed, axis=-1, keepdims=True)
    )
    grad_attended = grad_residual.astype(bf16)
    grad_mixed_rows = mm_t1(grad_attended, full_out).astype(bf16)
    exchanged = lax.all_to_all(
        grad_mixed_rows.astype(f32).reshape(shard_rows, mp_size, local).transpose(1, 0, 2), "mp", 0, 0
    )
    grad_mixed = (exchanged + nothing).reshape(streams, seg_len, local).astype(bf16)
    grad_out_full = mm_t0(own_rows(mixed_all), grad_attended)

    branch = mm(activated, down_weight)
    branch_own = line_scatter(branch.reshape(mp_size, shard_rows, width), mp_size)
    result_own = (own_residual + branch_own).astype(bf16)
    grad_down = mm_t0(activated, grad_rows)
    grad_up = mm_t0(ffn_input, grad_pre)

    grad_unit, gq, gk, gv, rel = attend_back(
        unit,
        q,
        k,
        v,
        log_total,
        grad_mixed,
        memory_fill,
        compressed_fill,
        query_weight,
        key_weight,
        value_weight,
        relative_bias,
        mem_len,
        packed_len,
    )
    grad_relative = jnp.sum(rel, axis=-1)[:, : len(reach_marks)]
    grad_unit = line_scatter(grad_unit.reshape(mp_size, shard_rows, width), mp_size)
    own_seg = own_rows(seg_rows).astype(f32)
    seg_scale = row_scale(own_seg)
    seg_normed = own_seg * seg_scale
    seg_weighted = grad_unit * first_gain
    grad_seg_own = (
        grad_residual
        + seg_scale * (seg_weighted - seg_normed * jnp.mean(seg_weighted * seg_normed, axis=-1, keepdims=True))
    ).astype(bf16)

    result = (line_gather(result_own.astype(f32), mp_size) + nothing).reshape(inputs.shape).astype(bf16)
    grad_seg = (line_gather(grad_seg_own.astype(f32), mp_size) + nothing).reshape(inputs.shape).astype(bf16)

    grad_out_w = lax.psum_scatter(grad_out_full, "mp", scatter_dimension=0, tiled=True)
    gq, gk, gv, grad_out_w, grad_up, grad_down, grad_compress_w, grad_relative = lax.psum(
        (gq, gk, gv, grad_out_w, grad_up, grad_down, grad_compress_w, grad_relative), "dp"
    )
    grad_query_w, grad_key_w, grad_value_w = gq.T, gk.T, gv.T
    grad_first = (
        jnp.sum(
            grad_query_w * query_weight.astype(f32)
            + grad_key_w * key_weight.astype(f32)
            + grad_value_w * value_weight.astype(f32),
            axis=1,
        )
        / first_gain
    )
    grad_first = lax.psum(grad_first, "mp")
    grad_second = lax.psum(grad_second, ("dp", "mp"))
    return (
        result,
        packed_new,
        grad_seg,
        grad_first,
        grad_query_w,
        grad_key_w,
        grad_value_w,
        grad_relative,
        grad_out_w,
        grad_second,
        grad_up,
        grad_down,
        grad_compress_w,
    )


def solution(mesh):
    in_specs = (
        P("dp", None, None),
        P("dp", None, None),
        P("dp", None, None),
        P("dp"),
        P("dp"),
        P(),
        P(None, "mp"),
        P(None, "mp"),
        P(None, "mp"),
        P("mp", None),
        P("mp", None),
        P(),
        P(None, "mp"),
        P("mp", None),
        P(None, "mp"),
        P("dp", None, None),
        P("dp", None, "mp"),
    )
    out_specs = (
        P("dp", None, None),
        P("dp", None, "mp"),
        P("dp", None, None),
        P(),
        P(None, "mp"),
        P(None, "mp"),
        P(None, "mp"),
        P("mp", None),
        P("mp", None),
        P(),
        P(None, "mp"),
        P("mp", None),
        P(None, "mp"),
    )
    return jax.shard_map(
        functools.partial(body, mp_size=mesh.shape["mp"]),
        mesh=mesh,
        in_specs=in_specs,
        out_specs=out_specs,
        check_vma=False,
    )
```

```python
import functools
import math

import jax
import jax.numpy as jnp
from jax import lax
from jax.experimental import pallas as pl
from jax.experimental.pallas import tpu as pltpu
from jax.sharding import PartitionSpec as P

reach_marks = (1, 2, 3, 4, 5, 6, 7, 8, 12, 16, 24, 32, 48, 64, 96, 128, 192, 256, 384, 512, 768, 1024)
epsilon = 1e-06
masked_score = -1e30
block = 128
query_block = 256
chunk_count = 8
f32 = jnp.float32
bf16 = jnp.bfloat16


def mm(left, right):
    return jnp.dot(left, right, preferred_element_type=f32)


def mm_t0(left, right):
    return lax.dot_general(left, right, (((0,), (0,)), ((), ())), preferred_element_type=f32)


def mm_t1(left, right):
    return lax.dot_general(left, right, (((1,), (1,)), ((), ())), preferred_element_type=f32)


def row_scale(source):
    return lax.rsqrt(jnp.mean(source * source, axis=-1, keepdims=True) + epsilon)


def diagonal_count(seg_len, kept_count):
    return (seg_len + kept_count) // block + 1


def diagonal_of(seg_len, kept_count, column):
    return (seg_len + kept_count) // block - 1 - column


def strip_start(seg_len, sub_block):
    return (seg_len // block - 1 - sub_block) * block


def bias_block(bias_ref, head, diagonal, transposed):
    rows = lax.broadcasted_iota(jnp.int32, (block, block), 0)
    cols = lax.broadcasted_iota(jnp.int32, (block, block), 1)
    distance = diagonal * block + ((cols - rows) if transposed else (rows - cols))
    lowest, highest = diagonal * block - block + 1, diagonal * block + block - 1
    base = jnp.float32(0.0)
    for position, mark_value in enumerate(reach_marks):
        if mark_value <= lowest:
            base = base + bias_ref[head, position]
    value = jnp.full((block, block), base, f32)
    for position, mark_value in enumerate(reach_marks):
        if lowest < mark_value <= highest:
            value = value + jnp.where(distance >= mark_value, bias_ref[head, position], 0.0)
    if lowest < 0:
        value = jnp.where(distance >= 0, value, masked_score)
    return value


def live_mask(shape, axis, packed_len, mem_len, packed_count, memory_count):
    slot = lax.broadcasted_iota(jnp.int32, shape, axis)
    dead_packed = (slot < packed_len) & (slot < packed_len - packed_count)
    dead_memory = (slot >= packed_len) & (slot < packed_len + mem_len - memory_count)
    return jnp.where(dead_packed | dead_memory, masked_score, 0.0).astype(f32)


def attend_kernel(
    sizes,
    memory_fill,
    packed_fill,
    bias_ref,
    seg_ref,
    memory_ref,
    packed_ref,
    gain_ref,
    wq_ref,
    wk_ref,
    wv_ref,
    unit_ref,
    q_ref,
    k_ref,
    v_ref,
    mixed_ref,
    log_ref,
    strip,
    live,
):
    seg_len, mem_len, packed_len, heads, head_dim = sizes
    kept = mem_len + packed_len
    keys = kept + seg_len
    stream = pl.program_id(0)
    scale = 1.0 / math.sqrt(head_dim)
    gain = gain_ref[...]
    start = 0
    for part_ref, size in ((packed_ref, packed_len), (memory_ref, mem_len), (seg_ref, seg_len)):
        rows = part_ref[0].astype(f32)
        unit = (rows * row_scale(rows) * gain).astype(bf16)
        unit_ref[0, start : start + size, :] = unit
        k_ref[0, start : start + size, :] = mm(unit, wk_ref[...]).astype(bf16)
        v_ref[0, start : start + size, :] = mm(unit, wv_ref[...]).astype(bf16)
        if start == kept:
            q_ref[0] = mm(unit, wq_ref[...]).astype(bf16)
        start += size
    live[...] = live_mask((8, kept), 1, packed_len, mem_len, packed_fill[stream], memory_fill[stream])
    for head in range(heads):
        lanes = slice(head * head_dim, (head + 1) * head_dim)
        for column in range(diagonal_count(seg_len, kept)):
            strip[:, column * block : (column + 1) * block] = bias_block(
                bias_ref, head, diagonal_of(seg_len, kept, column), False
            )
        for index in range(seg_len // query_block):
            reach = kept + (index + 1) * query_block
            rows = slice(index * query_block, (index + 1) * query_block)
            score = mm_t1(q_ref[0, rows, lanes], k_ref[0, :reach, lanes]) * scale
            parts = []
            for sub in range(query_block // block):
                first = strip_start(seg_len, index * (query_block // block) + sub)
                parts.append(strip[:, first : first + reach])
            score = score + jnp.concatenate(parts, axis=0)
            score = jnp.concatenate([score[:, :kept] + live[0:1, :], score[:, kept:]], axis=1)
            top = jnp.max(score, axis=-1, keepdims=True)
            weight = jnp.exp(score - top)
            total = jnp.sum(weight, axis=-1, keepdims=True)
            log_ref[0, head, rows, :] = top + jnp.log(total)
            mixed = mm(weight.astype(bf16), v_ref[0, :reach, lanes]) * (1.0 / total)
            mixed_ref[0, rows, lanes] = mixed.astype(bf16)


def attend(inputs, memory, packed, memory_fill, packed_fill, gain, wq, wk, wv, bias):
    streams, seg_len, width = inputs.shape
    mem_len, packed_len = memory.shape[1], packed.shape[1]
    heads = bias.shape[0]
    local = wq.shape[1]
    keys = seg_len + mem_len + packed_len
    sizes = (seg_len, mem_len, packed_len, heads, local // heads)
    smem = pl.BlockSpec(memory_space=pltpu.SMEM)

    def rows_of(count, columns):
        return pl.BlockSpec((1, count, columns), lambda s: (s, 0, 0))

    def whole(shape):
        return pl.BlockSpec(shape, lambda s: (0,) * len(shape))

    return pl.pallas_call(
        functools.partial(attend_kernel, sizes),
        grid=(streams,),
        in_specs=[
            smem,
            smem,
            smem,
            rows_of(seg_len, width),
            rows_of(mem_len, width),
            rows_of(packed_len, width),
            whole((1, width)),
            whole(wq.shape),
            whole(wk.shape),
            whole(wv.shape),
        ],
        out_specs=[
            rows_of(keys, width),
            rows_of(seg_len, local),
            rows_of(keys, local),
            rows_of(keys, local),
            rows_of(seg_len, local),
            pl.BlockSpec((1, heads, seg_len, 1), lambda s: (s, 0, 0, 0)),
        ],
        out_shape=[
            jax.ShapeDtypeStruct((streams, keys, width), bf16),
            jax.ShapeDtypeStruct((streams, seg_len, local), bf16),
            jax.ShapeDtypeStruct((streams, keys, local), bf16),
            jax.ShapeDtypeStruct((streams, keys, local), bf16),
            jax.ShapeDtypeStruct((streams, seg_len, local), bf16),
            jax.ShapeDtypeStruct((streams, heads, seg_len, 1), f32),
        ],
        scratch_shapes=[
            pltpu.VMEM((block, diagonal_count(seg_len, mem_len + packed_len) * block), f32),
            pltpu.VMEM((8, mem_len + packed_len), f32),
        ],
        compiler_params=pltpu.CompilerParams(vmem_limit_bytes=60 << 20),
        cost_estimate=pl.CostEstimate(
            flops=streams * (2 * keys * width * local * 3 + 4 * seg_len * keys * local),
            bytes_accessed=streams * keys * (width * 4 + local * 6),
            transcendentals=streams * heads * seg_len * keys,
        ),
        name="attend",
    )(memory_fill, packed_fill, bias, inputs, memory, packed, gain[None, :], wq, wk, wv)


def attend_back_kernel(
    sizes,
    memory_fill,
    packed_fill,
    bias_ref,
    unit_ref,
    q_ref,
    k_ref,
    v_ref,
    log_ref,
    gm_ref,
    wq_ref,
    wk_ref,
    wv_ref,
    gunit_ref,
    gq_ref,
    gk_ref,
    gv_ref,
    rel_ref,
    strip,
    live,
    dk_sum,
    dv_sum,
    dq_low,
    dk_low,
    dv_low,
    strip_sum,
):
    seg_len, mem_len, packed_len, heads, head_dim = sizes
    kept = mem_len + packed_len
    keys = kept + seg_len
    stream = pl.program_id(0)
    scale = 1.0 / math.sqrt(head_dim)

    @pl.when(stream == 0)
    def _():
        strip_sum[...] = jnp.zeros_like(strip_sum)
        gq_ref[...] = jnp.zeros_like(gq_ref)
        gk_ref[...] = jnp.zeros_like(gk_ref)
        gv_ref[...] = jnp.zeros_like(gv_ref)

    live[...] = live_mask((kept, block), 0, packed_len, mem_len, packed_fill[stream], memory_fill[stream])
    subs = query_block // block
    for head in range(heads):
        lanes = slice(head * head_dim, (head + 1) * head_dim)
        for column in range(diagonal_count(seg_len, kept)):
            strip[column * block : (column + 1) * block, :] = bias_block(
                bias_ref, head, diagonal_of(seg_len, kept, column), True
            )
        for index in range(seg_len // query_block):
            reach = kept + (index + 1) * query_block
            rows = slice(index * query_block, (index + 1) * query_block)
            queries = q_ref[0, rows, lanes]
            grads = gm_ref[0, rows, lanes]
            key_rows = k_ref[0, :reach, lanes]
            score = mm_t1(key_rows, queries) * scale
            firsts = [strip_start(seg_len, index * subs + sub) for sub in range(subs)]
            score = score + jnp.concatenate([strip[first : first + reach, :] for first in firsts], axis=1)
            live_wide = jnp.concatenate([live[...]] * subs, axis=1)
            score = jnp.concatenate([score[:kept] + live_wide, score[kept:]], axis=0)
            prob = jnp.exp(score - log_ref[0, head, :, rows])
            grad_prob = mm_t1(v_ref[0, :reach, lanes], grads)
            delta = jnp.sum(prob * grad_prob, axis=0, keepdims=True)
            grad_score = (prob * (grad_prob - delta)).astype(bf16)
            dk_part = mm(grad_score, queries)
            dv_part = mm(prob.astype(bf16), grads)
            if index == seg_len // query_block - 1:
                earlier = kept + index * query_block
                if index:
                    dk_sum[:earlier] += dk_part[:earlier]
                    dv_sum[:earlier] += dv_part[:earlier]
                    dk_sum[earlier:] = dk_part[earlier:]
                    dv_sum[earlier:] = dv_part[earlier:]
                else:
                    dk_sum[...] = dk_part
                    dv_sum[...] = dv_part
            elif index:
                earlier = kept + index * query_block
                dk_sum[:earlier] += dk_part[:earlier]
                dv_sum[:earlier] += dv_part[:earlier]
                dk_sum[earlier:reach] = dk_part[earlier:]
                dv_sum[earlier:reach] = dv_part[earlier:]
            else:
                dk_sum[:reach] = dk_part
                dv_sum[:reach] = dv_part
            dq_low[rows, lanes] = (mm_t0(grad_score, key_rows) * scale).astype(bf16)
            for sub in range(subs):
                strip_sum[head, firsts[sub] : firsts[sub] + reach, :] += grad_score[
                    :, sub * block : (sub + 1) * block
                ].astype(f32)
        dk_low[:, lanes] = (dk_sum[...] * scale).astype(bf16)
        dv_low[:, lanes] = dv_sum[...].astype(bf16)
    gq_ref[...] += mm_t0(dq_low[...], unit_ref[0, kept:, :])
    gk_ref[...] += mm_t0(dk_low[...], unit_ref[0])
    gv_ref[...] += mm_t0(dv_low[...], unit_ref[0])
    gunit_ref[0] = (
        mm_t1(dq_low[...], wq_ref[...])
        + mm_t1(dk_low[kept:, :], wk_ref[...])
        + mm_t1(dv_low[kept:, :], wv_ref[...])
    )

    @pl.when(stream == pl.num_programs(0) - 1)
    def _():
        rows = lax.broadcasted_iota(jnp.int32, (block, block), 0)
        cols = lax.broadcasted_iota(jnp.int32, (block, block), 1)
        for head in range(heads):
            blocks = []
            for column in range(diagonal_count(seg_len, kept)):
                blocks.append(strip_sum[head, column * block : (column + 1) * block, :])
            for position, mark_value in enumerate(reach_marks):
                total = jnp.zeros((1, block), f32)
                for column, value in enumerate(blocks):
                    diagonal = diagonal_of(seg_len, kept, column)
                    lowest, highest = diagonal * block - block + 1, diagonal * block + block - 1
                    if mark_value <= lowest:
                        total = total + jnp.sum(value, axis=0, keepdims=True)
                    elif mark_value <= highest:
                        distance = diagonal * block + cols - rows
                        total = total + jnp.sum(
                            jnp.where(distance >= mark_value, value, 0.0), axis=0, keepdims=True
                        )
                rel_ref[head, position : position + 1, :] = total


def attend_back(unit, q, k, v, log_total, grad_mixed, memory_fill, packed_fill, wq, wk, wv, bias, mem_len, packed_len):
    streams, keys, width = unit.shape
    seg_len, local = q.shape[1:]
    heads = bias.shape[0]
    kept = mem_len + packed_len
    sizes = (seg_len, mem_len, packed_len, heads, local // heads)
    smem = pl.BlockSpec(memory_space=pltpu.SMEM)
    strip_len = diagonal_count(seg_len, kept) * block

    def rows_of(count, columns):
        return pl.BlockSpec((1, count, columns), lambda s: (s, 0, 0))

    def whole(shape):
        return pl.BlockSpec(shape, lambda s: (0,) * len(shape))

    return pl.pallas_call(
        functools.partial(attend_back_kernel, sizes),
        grid=(streams,),
        in_specs=[
            smem,
            smem,
            smem,
            rows_of(keys, width),
            rows_of(seg_len, local),
            rows_of(keys, local),
            rows_of(keys, local),
            pl.BlockSpec((1, heads, 1, seg_len), lambda s: (s, 0, 0, 0)),
            rows_of(seg_len, local),
            whole(wq.shape),
            whole(wk.shape),
            whole(wv.shape),
        ],
        out_specs=[
            rows_of(seg_len, width),
            whole((local, width)),
            whole((local, width)),
            whole((local, width)),
            whole((heads, 24, block)),
        ],
        out_shape=[
            jax.ShapeDtypeStruct((streams, seg_len, width), f32),
            jax.ShapeDtypeStruct((local, width), f32),
            jax.ShapeDtypeStruct((local, width), f32),
            jax.ShapeDtypeStruct((local, width), f32),
            jax.ShapeDtypeStruct((heads, 24, block), f32),
        ],
        scratch_shapes=[
            pltpu.VMEM((strip_len, block), f32),
            pltpu.VMEM((kept, block), f32),
            pltpu.VMEM((keys, local // heads), f32),
            pltpu.VMEM((keys, local // heads), f32),
            pltpu.VMEM((seg_len, local), bf16),
            pltpu.VMEM((keys, local), bf16),
            pltpu.VMEM((keys, local), bf16),
            pltpu.VMEM((heads, strip_len, block), f32),
        ],
        compiler_params=pltpu.CompilerParams(vmem_limit_bytes=60 << 20),
        cost_estimate=pl.CostEstimate(
            flops=streams * (8 * keys * width * local + 10 * seg_len * keys * local),
            bytes_accessed=streams * keys * (width * 2 + local * 6),
            transcendentals=streams * heads * seg_len * keys,
        ),
        name="attend_back",
    )(
        memory_fill,
        packed_fill,
        bias,
        unit,
        q,
        k,
        v,
        log_total.reshape(streams, heads, 1, seg_len),
        grad_mixed,
        wq,
        wk,
        wv,
    )


def remote(source, target, send_sems, recv_sems, source_slot, target_slot, send_slot, recv_slot, peer):
    return pltpu.make_async_remote_copy(
        src_ref=source.at[source_slot],
        dst_ref=target.at[target_slot],
        send_sem=send_sems.at[send_slot],
        recv_sem=recv_sems.at[recv_slot],
        device_id=peer,
        device_id_type=pl.DeviceIdType.MESH,
    )


class Line:
    def __init__(self, size, chunks, hop):
        self.me = lax.axis_index("mp")
        self.size, self.chunks, self.hop = size, chunks, hop
        self.reach = size - 1

    def place(self, right):
        return self.me if right else self.reach - self.me

    def peer(self, right):
        return {"mp": self.me + 1 if right else self.me - 1}

    def copy(self, source, target, sems, slot, right):
        return remote(source, target, sems[0], sems[1], slot, slot, slot, slot, self.peer(right))

    def chunk_at(self, tick):
        positive = jnp.maximum(tick, 0)
        chunk = positive // self.reach
        return chunk, (tick >= 0) & (positive == chunk * self.reach) & (chunk < self.chunks)

    def scatter_step(self, tick, part, lanes):
        for right, held, sems in lanes:
            place = self.place(right)
            late = tick - self.hop * place
            positive = jnp.maximum(late, 0)
            chunk = positive // self.reach
            goal = self.reach - (positive - self.reach * chunk)
            active = (late >= 0) & (chunk < self.chunks) & (goal > place)
            slot = chunk * self.size + (goal if right else self.reach - goal)

            @pl.when(active & (place == 0))
            def _():
                self.copy(part, held, sems, slot, right).start()

            @pl.when(active & (place > 0))
            def _():
                self.copy(held, held, sems, slot, right).wait_recv()
                held[slot] = held[slot] + part[slot]
                self.copy(held, held, sems, slot, right).start()

    def scatter_sum(self, chunk, part, lanes, total):
        slot = chunk * self.size + self.me
        total[...] = part[slot]
        for right, held, sems in lanes:

            @pl.when(self.place(right) > 0)
            def _():
                self.copy(held, held, sems, slot, right).wait_recv()
                total[...] = total[...] + held[slot]

    def gather_start(self, chunk, whole, lanes):
        slot = chunk * self.size + self.me
        for right, sems in lanes:

            @pl.when(self.place(right) < self.reach)
            def _():
                self.copy(whole, whole, sems, slot, right).start()

    def gather_step(self, tick, whole, lanes, landed=None):
        for right, sems in lanes:
            place = self.place(right)
            for distance in range(1, self.size):
                chunk, due = self.chunk_at(tick - self.hop * distance)

                @pl.when(due & (distance <= place))
                def _():
                    slot = chunk * self.size + (self.me - distance if right else self.me + distance)
                    self.copy(whole, whole, sems, slot, right).wait_recv()

                    @pl.when(place < self.reach)
                    def _():
                        self.copy(whole, whole, sems, slot, right).start()

                    if landed is not None:
                        landed(slot)

    def scatter_drain(self, chunk, part, lanes):
        for right, held, sems in lanes:
            for goal in range(1, self.size):

                @pl.when(goal > self.place(right))
                def _():
                    slot = chunk * self.size + (goal if right else self.reach - goal)
                    self.copy(part, held, sems, slot, right).wait_send()

    def gather_drain(self, chunk, whole, lanes):
        for right, sems in lanes:
            place = self.place(right)
            for distance in range(self.size):

                @pl.when((distance <= place) & (place < self.reach))
                def _():
                    slot = chunk * self.size + (self.me - distance if right else self.me + distance)
                    self.copy(whole, whole, sems, slot, right).wait_send()


def greet(peers):
    barrier = pltpu.get_barrier_semaphore()
    for peer in peers:
        pl.semaphore_signal(barrier, inc=1, device_id=peer, device_id_type=pl.DeviceIdType.MESH)
    pl.semaphore_wait(barrier, len(peers))


def feed_kernel(
    size,
    group,
    chunks,
    hop,
    delay,
    stages,
    mixed_ref,
    seg_ref,
    grad_ref,
    up_ref,
    down_ref,
    out_ref,
    gain_ref,
    gm_ref,
    gres_ref,
    res_ref,
    branch_ref,
    gdown_ref,
    gup_ref,
    gout_ref,
    gsecond_ref,
    heads_in,
    part,
    held_right,
    held_left,
    swap_out,
    swap_in,
    weights_in,
    weights,
    chunk_rows,
    total,
    own_mixed,
    own_grad,
    *sems,
):
    line = Line(size, chunks, hop)
    me = line.me
    mine = lax.axis_index("dp")
    (hr_s, hr_r, hl_s, hl_r, sr_s, sr_r, sl_s, sl_r, x_s, x_r, wz_s, wz_r, wd_s, wd_r) = sems
    gather_lanes = ((True, (hr_s, hr_r)), (False, (hl_s, hl_r)))
    scatter_lanes = ((True, held_right, (sr_s, sr_r)), (False, held_left, (sl_s, sl_r)))
    bits = group.bit_length() - 1
    piece, width = weights_in.shape[2:]
    rows = total.shape[0]
    local = mixed_ref.shape[-1]
    spot = jnp.int32(0)
    for bit in range(bits):
        spot = spot + ((mine // (1 << bit)) % 2) * (1 << (bits - 1 - bit))

    def others(offset):
        return {"mp": lax.rem(me + offset, size)}

    def partner(level):
        step = 1 << (bits - 1 - level)
        return {"dp": mine + step - 2 * step * ((mine // step) % 2)}

    greet([others(offset) for offset in range(1, size)] + [partner(level) for level in range(bits)])

    weights_in[spot, me] = out_ref[pl.ds(pl.multiple_of(mine * piece, piece), piece), :].astype(f32)

    def weight_across(offset, arriving):
        origin = lax.rem(me - offset + size, size) if arriving else me
        return pltpu.make_async_remote_copy(
            src_ref=weights_in.at[spot, origin],
            dst_ref=weights_in.at[spot, origin],
            send_sem=wz_s.at[offset],
            recv_sem=wz_r.at[offset],
            device_id=others(offset),
            device_id_type=pl.DeviceIdType.MESH,
        )

    def weight_within(level, arriving):
        count = 1 << level
        start = (spot // count) * count
        if arriving:
            start = start + count - 2 * count * ((spot // count) % 2)
        return pltpu.make_async_remote_copy(
            src_ref=weights_in.at[pl.ds(start, count)],
            dst_ref=weights_in.at[pl.ds(start, count)],
            send_sem=wd_s.at[level],
            recv_sem=wd_r.at[level],
            device_id=partner(level),
            device_id_type=pl.DeviceIdType.MESH,
        )

    for offset in range(1, size):
        weight_across(offset, False).start()

    def stage_heads(chunk, _):
        heads_in[chunk * size + me] = mixed_ref[chunk].astype(f32)
        return 0

    lax.fori_loop(0, chunks, stage_heads, 0)
    gsecond_ref[...] = jnp.zeros_like(gsecond_ref)
    gdown_ref[...] = jnp.zeros_like(gdown_ref)
    gup_ref[...] = jnp.zeros_like(gup_ref)

    def weight_step(tick):
        @pl.when(tick == stages[0])
        def _():
            for offset in range(1, size):
                weight_across(offset, True).wait_recv()
            weight_within(0, False).start()

        for level in range(1, bits):

            @pl.when(tick == stages[min(level, len(stages) - 1)] + max(0, level - len(stages) + 1))
            def _():
                weight_within(level - 1, True).wait_recv()
                weight_within(level, False).start()

    def weight_finish():
        weight_within(bits - 1, True).wait_recv()
        for index in range(size):
            pieces = []
            for member in range(group):
                place = sum(((member >> bit) & 1) << (bits - 1 - bit) for bit in range(bits))
                pieces.append(weights_in[place, index])
            weights[index * group * piece : (index + 1) * group * piece, :] = jnp.concatenate(
                pieces, axis=0
            ).astype(bf16)

    own = pl.ds(pl.multiple_of(me * rows, rows), rows)

    def feed_chunk(chunk):
        heads = [heads_in[chunk * size + index].astype(bf16) for index in range(size)]
        for index in range(size):
            own_mixed[chunk, :, index * local : (index + 1) * local] = heads_in[
                chunk * size + index, own, :
            ].astype(bf16)
        residual = seg_ref[chunk].astype(f32) + mm(jnp.concatenate(heads, axis=1), weights[...])
        chunk_rows[...] = residual
        res_ref[chunk] = chunk_rows[own, :]
        ffn_input = (residual * row_scale(residual) * gain_ref[...]).astype(bf16)
        pre_act = mm(ffn_input, up_ref[...])
        inner = math.sqrt(2.0 / math.pi)
        squared = pre_act * pre_act
        tanh = jnp.tanh(inner * (pre_act + 0.044715 * pre_act * squared))
        activated = (0.5 * pre_act * (1.0 + tanh)).astype(bf16)
        slope = 0.5 * (1.0 + tanh) + 0.5 * pre_act * (1.0 - tanh * tanh) * (
            inner * (1.0 + 3.0 * 0.044715 * squared)
        )
        grads = grad_ref[chunk]
        grad_pre = (slope * mm_t1(grads, down_ref[...])).astype(bf16)
        first = pl.ds(chunk * size, size)
        part[first] = mm_t1(grad_pre, up_ref[...]).reshape(size, rows, width)
        branch_ref[first] = mm(activated, down_ref[...]).reshape(size, rows, width)
        gdown_ref[...] += mm_t0(activated, grads)
        gup_ref[...] += mm_t0(ffn_input, grad_pre)

    def swap(chunk, offset, arriving):
        target = lax.rem(me + offset, size)
        origin = lax.rem(me - offset + size, size)
        landing = chunk * size + (origin if arriving else me)
        return remote(
            swap_out,
            swap_in,
            x_s,
            x_r,
            chunk * size + target,
            landing,
            chunk * size + target,
            landing,
            {"mp": target},
        )

    def settle(chunk):
        line.scatter_sum(chunk, part, scatter_lanes, total)
        grad_ffn = total[...]
        residual = res_ref[chunk]
        scale = row_scale(residual)
        normed = residual * scale
        gsecond_ref[...] += jnp.sum(grad_ffn * normed, axis=0, keepdims=True)
        weighted = grad_ffn * gain_ref[...]
        own_rows = grad_ref[chunk, own, :].astype(f32)
        grad_residual = own_rows + scale * (
            weighted - normed * jnp.mean(weighted * normed, axis=-1, keepdims=True)
        )
        gres_ref[chunk] = grad_residual
        low = grad_residual.astype(bf16)
        own_grad[chunk] = low
        grad_mixed = mm_t1(low, weights[...]).astype(bf16).astype(f32)
        for index in range(size):
            swap_out[chunk * size + index] = grad_mixed[:, index * local : (index + 1) * local]
        for offset in range(1, size):
            swap(chunk, offset, False).start()

    feed_at = hop * line.reach + delay

    def step(tick, _):
        weight_step(tick)

        @pl.when(tick == feed_at)
        def _():
            weight_finish()

        chunk, due = line.chunk_at(tick)

        @pl.when(due)
        def _():
            line.gather_start(chunk, heads_in, gather_lanes)

        line.gather_step(tick, heads_in, gather_lanes)
        chunk_f, due_f = line.chunk_at(tick - feed_at)

        @pl.when(due_f)
        def _():
            feed_chunk(chunk_f)

        line.scatter_step(tick - feed_at, part, scatter_lanes)
        chunk_s, due_s = line.chunk_at(tick - feed_at - hop * line.reach)

        @pl.when(due_s)
        def _():
            settle(chunk_s)

        return 0

    lax.fori_loop(0, feed_at + line.reach * (chunks - 1) + hop * line.reach + 1, step, 0)
    gout_ref[...] = mm_t0(
        own_mixed[...].reshape(chunks * rows, width), own_grad[...].reshape(chunks * rows, width)
    )

    def finish(chunk, _):
        for offset in range(1, size):
            swap(chunk, offset, True).wait_recv()
        for index in range(size):

            @pl.when(index == me)
            def _():
                gm_ref[chunk * size + index] = swap_out[chunk * size + index].astype(bf16)

            @pl.when(index != me)
            def _():
                gm_ref[chunk * size + index] = swap_in[chunk * size + index].astype(bf16)

        line.gather_drain(chunk, heads_in, gather_lanes)
        line.scatter_drain(chunk, part, scatter_lanes)
        for offset in range(1, size):
            swap(chunk, offset, False).wait_send()
        return 0

    lax.fori_loop(0, chunks, finish, 0)
    for offset in range(1, size):
        weight_across(offset, False).wait_send()
    for level in range(bits):
        weight_within(level, False).wait_send()


def feed(mixed, seg_rows, grad_rows, up, down, out, gain, size, group, chunks):
    rows, width = seg_rows.shape
    local = mixed.shape[1]
    chunk = rows // chunks
    piece = chunk // size
    hidden = up.shape[1]
    vmem = pl.BlockSpec(memory_space=pltpu.VMEM)
    slots = pltpu.SemaphoreType.DMA((chunks * size,))
    bits = group.bit_length() - 1
    return pl.pallas_call(
        functools.partial(feed_kernel, size, group, chunks, 2, 10, (3, 6, 10)),
        in_specs=[vmem] * 7,
        out_specs=[vmem] * 8,
        out_shape=[
            jax.ShapeDtypeStruct((chunks * size, piece, local), bf16),
            jax.ShapeDtypeStruct((chunks, piece, width), f32),
            jax.ShapeDtypeStruct((chunks, piece, width), f32),
            jax.ShapeDtypeStruct((chunks * size, piece, width), f32),
            jax.ShapeDtypeStruct((hidden, width), f32),
            jax.ShapeDtypeStruct((width, hidden), f32),
            jax.ShapeDtypeStruct((width, width), f32),
            jax.ShapeDtypeStruct((1, width), f32),
        ],
        scratch_shapes=[
            pltpu.VMEM((chunks * size, chunk, local), f32),
            pltpu.VMEM((chunks * size, piece, width), f32),
            pltpu.VMEM((chunks * size, piece, width), f32),
            pltpu.VMEM((chunks * size, piece, width), f32),
            pltpu.VMEM((chunks * size, piece, local), f32),
            pltpu.VMEM((chunks * size, piece, local), f32),
            pltpu.VMEM((group, size, out.shape[0] // group, width), f32),
            pltpu.VMEM((width, width), bf16),
            pltpu.VMEM((chunk, width), f32),
            pltpu.VMEM((piece, width), f32),
            pltpu.VMEM((chunks, piece, width), bf16),
            pltpu.VMEM((chunks, piece, width), bf16),
        ]
        + [slots] * 10
        + [pltpu.SemaphoreType.DMA((size,))] * 2
        + [pltpu.SemaphoreType.DMA((bits,))] * 2,
        compiler_params=pltpu.CompilerParams(
            collective_id=0, has_side_effects=True, vmem_limit_bytes=63 << 20
        ),
        name="feed",
    )(
        mixed.reshape(chunks, chunk, local),
        seg_rows.reshape(chunks, chunk, width),
        grad_rows.reshape(chunks, chunk, width),
        up,
        down,
        out,
        gain[None, :],
    )


class Pieces:
    def __init__(self, group, rows, crossing, jobs, work, landing, summed, sems):
        self.mine = lax.axis_index("dp")
        self.bits = group.bit_length() - 1
        self.rows, self.crossing, self.jobs = rows, crossing, jobs
        self.work, self.landing, self.summed = work, landing, summed
        self.slots = work.shape[0]
        (self.rs_s, self.rs_r, self.ag_s, self.ag_r, self.load_sem, self.store_sem) = sems
        self.count = crossing[0] + sum(job[2] for job in jobs)

    def step_of(self, odd, level):
        even_step = 1 << level
        odd_step = 1 << ((self.bits - level) % self.bits)
        return jnp.where(odd == 1, odd_step, even_step)

    def bit_of(self, odd, level):
        return (self.mine // self.step_of(odd, level)) % 2

    def partner(self, odd, level):
        step = self.step_of(odd, level)
        return {"dp": self.mine + step - 2 * step * self.bit_of(odd, level)}

    def start_of(self, odd, level):
        start = jnp.int32(0)
        for earlier in range(level):
            start = start + self.bit_of(odd, earlier) * (self.rows >> (earlier + 1))
        return start

    def span(self, start, level):
        length = self.rows >> level
        return pl.ds(pl.multiple_of(start, self.rows >> self.bits), length)

    def halves(self, odd, level):
        start, bit, half = self.start_of(odd, level), self.bit_of(odd, level), self.rows >> (level + 1)
        return self.span(start + bit * half, level + 1), self.span(start + (1 - bit) * half, level + 1)

    def reduce_copy(self, slot, odd, level):
        _, give = self.halves(odd, level)
        region = pl.ds(self.rows - (self.rows >> level), self.rows >> (level + 1))
        return pltpu.make_async_remote_copy(
            src_ref=self.work.at[slot, give],
            dst_ref=self.landing.at[slot, region],
            send_sem=self.rs_s.at[slot * self.bits + level],
            recv_sem=self.rs_r.at[slot * self.bits + level],
            device_id=self.partner(odd, level),
            device_id_type=pl.DeviceIdType.MESH,
        )

    def absorb(self, slot, odd, level):
        self.reduce_copy(slot, odd, level).wait_recv()
        keep, _ = self.halves(odd, level)
        region = pl.ds(self.rows - (self.rows >> level), self.rows >> (level + 1))
        self.work[slot, keep, :] = self.work[slot, keep, :] + self.landing[slot, region, :]

    def spread_copy(self, buffer, sems, slot, odd, level, arriving):
        keep, give = self.halves(odd, level)
        span = give if arriving else keep
        return pltpu.make_async_remote_copy(
            src_ref=buffer.at[slot, span],
            dst_ref=buffer.at[slot, span],
            send_sem=sems[0].at[slot * self.bits + level],
            recv_sem=sems[1].at[slot * self.bits + level],
            device_id=self.partner(odd, level),
            device_id_type=pl.DeviceIdType.MESH,
        )

    def spread(self, slot, odd, level, arriving):
        return self.spread_copy(self.summed, (self.ag_s, self.ag_r), slot, odd, level, arriving)

    def move(self, piece, slot, store, start):
        columns = self.work.shape[2]
        first = self.crossing[0]
        sources = [(self.crossing[1], None, 0, first)]
        for source, target, count in self.jobs:
            sources.append((source, target, first, first + count))
            first += count
        for source, target, low, high in sources:
            if store and target is None:
                continue

            @pl.when((piece >= low) & (piece < high))
            def _():
                across = source.shape[2] // columns
                index = (piece - low) // across
                lanes = pl.ds(pl.multiple_of((piece - low - index * across) * columns, columns), columns)
                inside = self.summed.at[slot] if store else self.work.at[slot]
                if store:
                    copy = pltpu.make_async_copy(inside, target.at[index, :, lanes], self.store_sem.at[slot])
                else:
                    copy = pltpu.make_async_copy(source.at[index, :, lanes], inside, self.load_sem.at[slot])
                copy.start() if start else copy.wait()

    def load_first(self):
        self.move(jnp.int32(0), 0, False, True)

    def step(self, tick, cross):
        bits = self.bits
        for age in reversed(range(-1, 2 * bits + 2)):
            piece = tick - age
            safe = jnp.maximum(piece, 0)
            slot, odd = safe % self.slots, safe % 2
            plain = piece >= self.crossing[0]
            inside = (piece >= 0) & (piece < self.count)
            if age == 2 * bits + 1:

                @pl.when(inside)
                def _():
                    for level in range(bits):
                        self.reduce_copy(slot, odd, level).wait_send()

                @pl.when(inside & plain)
                def _():
                    for level in range(bits):
                        self.spread(slot, odd, level, False).wait_send()
                    self.move(piece, slot, True, False)

                @pl.when(inside & jnp.logical_not(plain))
                def _():
                    cross(piece, slot, odd, False)

            elif age == 2 * bits:

                @pl.when(inside & plain)
                def _():
                    self.spread(slot, odd, 0, True).wait_recv()
                    self.move(piece, slot, True, True)

            elif age > bits:

                @pl.when(inside & plain)
                def _():
                    self.spread(slot, odd, 2 * bits - age, True).wait_recv()
                    self.spread(slot, odd, 2 * bits - 1 - age, False).start()

            elif age == bits:

                @pl.when(inside)
                def _():
                    self.absorb(slot, odd, bits - 1)

                @pl.when(inside & plain)
                def _():
                    own = self.span(self.start_of(odd, bits), bits)
                    self.summed[slot, own, :] = self.work[slot, own, :]
                    self.spread(slot, odd, bits - 1, False).start()

                @pl.when(inside & jnp.logical_not(plain))
                def _():
                    cross(piece, slot, odd, True)

            elif age > 0:

                @pl.when(inside)
                def _():
                    self.absorb(slot, odd, age - 1)
                    self.reduce_copy(slot, odd, age).start()

            elif age == 0:

                @pl.when(inside)
                def _():
                    self.move(piece, slot, False, False)
                    self.reduce_copy(slot, odd, 0).start()

            else:

                @pl.when(inside)
                def _():
                    self.move(piece, slot, False, True)


def close_kernel(
    size,
    group,
    chunks,
    hop,
    counts,
    gunit_ref,
    branch_ref,
    seg_ref,
    gres_ref,
    res_ref,
    gain_ref,
    gout_ref,
    gup_ref,
    gdown_ref,
    gq_ref,
    gk_ref,
    gv_ref,
    gpack_ref,
    small_ref,
    result_ref,
    gseg_ref,
    gout_sum,
    gup_sum,
    gdown_sum,
    gq_sum,
    gk_sum,
    gv_sum,
    gpack_sum,
    small_sum,
    whole_seg,
    whole_out,
    seg_right,
    seg_left,
    out_right,
    out_left,
    total,
    work,
    landing,
    summed,
    cross_in,
    cross_work,
    small_cross,
    small_held,
    small_in,
    *sems,
):
    line = Line(size, chunks, hop)
    me = line.me
    pairs = [sems[2 * index : 2 * index + 2] for index in range(8)]
    seg_scatter = ((True, seg_right, pairs[0]), (False, seg_left, pairs[1]))
    out_scatter = ((True, out_right, pairs[2]), (False, out_left, pairs[3]))
    seg_gather = ((True, pairs[4]), (False, pairs[5]))
    out_gather = ((True, pairs[6]), (False, pairs[7]))
    piece_sems = sems[16:22]
    cross_s, cross_r, tail_s, tail_r, tail_store = sems[22:27]
    mix_s, mix_r, small_s, small_r = sems[27:31]
    jobs = [
        (gup_ref, gup_sum, counts[1]),
        (gdown_ref, gdown_sum, counts[2]),
        (gq_ref, gq_sum, counts[3]),
        (gk_ref, gk_sum, counts[4]),
        (gv_ref, gv_sum, counts[5]),
        (gpack_ref, gpack_sum, counts[6]),
    ]
    pieces = Pieces(group, work.shape[1], (counts[0], gout_ref), jobs, work, landing, summed, piece_sems)
    bits = pieces.bits
    pieces.load_first()
    greet(
        [{"mp": lax.rem(me + offset, size)} for offset in range(1, size)]
        + [{"dp": pieces.mine + (1 << bit) - 2 * (1 << bit) * ((pieces.mine // (1 << bit)) % 2)} for bit in range(bits)]
    )

    def cross_copy(slot, odd, target, origin):
        own = pieces.span(pieces.start_of(odd, bits), bits)
        return pltpu.make_async_remote_copy(
            src_ref=work.at[slot, own],
            dst_ref=cross_in.at[odd * size + origin],
            send_sem=cross_s.at[odd * size + target],
            recv_sem=cross_r.at[odd * size + origin],
            device_id={"mp": target},
            device_id_type=pl.DeviceIdType.MESH,
        )

    def cross(piece, slot, odd, start):
        target = piece // 2

        @pl.when(target != me)
        def _():
            copy = cross_copy(slot, odd, target, me)
            copy.start() if start else copy.wait_send()

        if start:

            @pl.when(target == me)
            def _():
                own = pieces.span(pieces.start_of(odd, bits), bits)
                cross_in[odd * size + me] = work[slot, own, :]

    def tail_copy(odd):
        columns = work.shape[2]
        return pltpu.make_async_copy(
            cross_work.at[odd], gout_sum.at[0, :, odd * columns : (odd + 1) * columns], tail_store.at[odd]
        )

    def tail_step(tick):
        base = counts[0] + bits + 1
        for odd in range(2):

            @pl.when(tick == base + odd)
            def _():
                for offset in range(1, size):
                    origin = lax.rem(me + offset, size)
                    cross_copy(0, odd, me, origin).wait_recv()
                own = pieces.span(pieces.start_of(odd, bits), bits)
                cross_work[odd, own, :] = sum(
                    cross_in[odd * size + index] for index in range(1, size)
                ) + cross_in[odd * size]
                pieces.spread_copy(cross_work, (tail_s, tail_r), odd, odd, bits - 1, False).start()

            for level in reversed(range(bits)):

                @pl.when(tick == base + odd + bits - level)
                def _():
                    pieces.spread_copy(cross_work, (tail_s, tail_r), odd, odd, level, True).wait_recv()
                    if level:
                        pieces.spread_copy(cross_work, (tail_s, tail_r), odd, odd, level - 1, False).start()
                    else:
                        tail_copy(odd).start()

    def small_across(offset, arriving):
        origin = lax.rem(me - offset + size, size) if arriving else me
        return pltpu.make_async_remote_copy(
            src_ref=small_cross.at[me],
            dst_ref=small_cross.at[origin],
            send_sem=mix_s.at[offset],
            recv_sem=mix_r.at[offset],
            device_id={"mp": lax.rem(me + offset, size)},
            device_id_type=pl.DeviceIdType.MESH,
        )

    def small_within(level):
        step = 1 << level
        return pltpu.make_async_remote_copy(
            src_ref=small_held.at[level],
            dst_ref=small_in.at[level],
            send_sem=small_s.at[level],
            recv_sem=small_r.at[level],
            device_id={"dp": pieces.mine + step - 2 * step * ((pieces.mine // step) % 2)},
            device_id_type=pl.DeviceIdType.MESH,
        )

    def small_step(tick):
        @pl.when(tick == 0)
        def _():
            small_cross[me] = small_ref[...]
            for offset in range(1, size):
                small_across(offset, False).start()

        @pl.when(tick == 2)
        def _():
            value = small_ref[...]
            shared = lax.broadcasted_iota(jnp.int32, value.shape, 0) < 2
            for offset in range(1, size):
                small_across(offset, True).wait_recv()
                origin = lax.rem(me - offset + size, size)
                value = value + jnp.where(shared, small_cross[origin], 0.0)
            small_held[0] = value
            small_within(0).start()

        for level in range(bits):

            @pl.when(tick == 4 + 2 * level)
            def _():
                small_within(level).wait_recv()
                value = small_held[level] + small_in[level]
                if level + 1 < bits:
                    small_held[level + 1] = value
                    small_within(level + 1).start()
                else:
                    small_sum[...] = value

    def settle(chunk):
        slot = chunk * size + me
        line.scatter_sum(chunk, gunit_ref, seg_scatter, total)
        rows = seg_ref[slot].astype(f32)
        scale = row_scale(rows)
        normed = rows * scale
        weighted = total[...] * gain_ref[...]
        grad = gres_ref[chunk] + scale * (
            weighted - normed * jnp.mean(weighted * normed, axis=-1, keepdims=True)
        )
        low = grad.astype(bf16)
        gseg_ref[slot] = low
        whole_seg[slot] = low.astype(f32)
        line.gather_start(chunk, whole_seg, seg_gather)
        line.scatter_sum(chunk, branch_ref, out_scatter, total)
        low = (res_ref[chunk] + total[...]).astype(bf16)
        result_ref[slot] = low
        whole_out[slot] = low.astype(f32)
        line.gather_start(chunk, whole_out, out_gather)

    def seg_landed(slot):
        gseg_ref[slot] = whole_seg[slot].astype(bf16)

    def out_landed(slot):
        result_ref[slot] = whole_out[slot].astype(bf16)

    settle_at = hop * line.reach

    def step(tick, _):
        line.scatter_step(tick, gunit_ref, seg_scatter)
        line.scatter_step(tick, branch_ref, out_scatter)
        chunk, due = line.chunk_at(tick - settle_at)

        @pl.when(due)
        def _():
            settle(chunk)

        line.gather_step(tick - settle_at, whole_seg, seg_gather, seg_landed)
        line.gather_step(tick - settle_at, whole_out, out_gather, out_landed)
        small_step(tick)

        def piece_step(beat, _):
            pieces.step(beat, cross)
            tail_step(beat)
            return 0

        lax.fori_loop(beats(tick), beats(tick + 1), piece_step, 0)
        return 0

    line_ticks = line.reach * (chunks - 1) + 2 * settle_at + 1
    piece_ticks = pieces.count + 2 * bits + 1

    def beats(tick):
        return jnp.minimum((tick * piece_ticks + line_ticks - 3) // (line_ticks - 2), piece_ticks)

    lax.fori_loop(0, line_ticks, step, 0)

    def drain(chunk, _):
        line.scatter_drain(chunk, gunit_ref, seg_scatter)
        line.scatter_drain(chunk, branch_ref, out_scatter)
        line.gather_drain(chunk, whole_seg, seg_gather)
        line.gather_drain(chunk, whole_out, out_gather)
        return 0

    lax.fori_loop(0, chunks, drain, 0)
    for odd in range(2):
        for level in range(bits):
            pieces.spread_copy(cross_work, (tail_s, tail_r), odd, odd, level, False).wait_send()
        tail_copy(odd).wait()
    for offset in range(1, size):
        small_across(offset, False).wait_send()
    for level in range(bits):
        small_within(level).wait_send()


def close(grad_unit, branch, seg_rows, grad_residual, residual, gain, grads, small, size, group, chunks):
    rows, width = seg_rows.shape
    piece = rows // (chunks * size)
    vmem = pl.BlockSpec(memory_space=pltpu.VMEM)
    whole = (chunks * size, piece, width)
    piece_rows, columns = max(256, 8 * group), width // 2
    bits = group.bit_length() - 1
    slots = 2 * bits + 2
    views = [grad.reshape(-1, piece_rows, grad.shape[1]) for grad in grads]
    counts = tuple(view.shape[0] * (view.shape[2] // columns) for view in views)
    anywhere = pl.BlockSpec(memory_space=pl.ANY)
    dma = pltpu.SemaphoreType.DMA
    sums = [jax.ShapeDtypeStruct(view.shape, f32) for view in views]
    sums[0] = jax.ShapeDtypeStruct((1, piece_rows, width), f32)
    return pl.pallas_call(
        functools.partial(close_kernel, size, group, chunks, 2, counts),
        in_specs=[vmem] * 6 + [anywhere] * len(views) + [vmem],
        out_specs=[vmem] * 2 + [anywhere] * len(views) + [vmem],
        out_shape=[jax.ShapeDtypeStruct(whole, bf16)] * 2 + sums + [jax.ShapeDtypeStruct(small.shape, f32)],
        scratch_shapes=[pltpu.VMEM(whole, f32)] * 6
        + [
            pltpu.VMEM((piece, width), f32),
            pltpu.VMEM((slots, piece_rows, columns), f32),
            pltpu.VMEM((slots, piece_rows, columns), f32),
            pltpu.VMEM((slots, piece_rows, columns), f32),
            pltpu.VMEM((2 * size, piece_rows // group, columns), f32),
            pltpu.VMEM((2, piece_rows, columns), f32),
            pltpu.VMEM((size, *small.shape), f32),
            pltpu.VMEM((bits, *small.shape), f32),
            pltpu.VMEM((bits, *small.shape), f32),
        ]
        + [dma((chunks * size,))] * 16
        + [dma((slots * bits,))] * 4
        + [dma((slots,))] * 2
        + [dma((2 * size,))] * 2
        + [dma((2 * bits,))] * 2
        + [dma((2,))]
        + [dma((size,))] * 2
        + [dma((bits,))] * 2,
        compiler_params=pltpu.CompilerParams(
            collective_id=1, has_side_effects=True, vmem_limit_bytes=63 << 20
        ),
        cost_estimate=pl.CostEstimate(flops=10**11, bytes_accessed=10**9, transcendentals=0),
        name="close",
    )(
        grad_unit.reshape(whole),
        branch,
        seg_rows.reshape(whole),
        grad_residual,
        residual,
        gain[None, :],
        *views,
        small,
    )


def body(
    inputs,
    memory,
    compressed_memory,
    memory_fill,
    compressed_fill,
    first_gain,
    query_weight,
    key_weight,
    value_weight,
    relative_bias,
    output_weight,
    second_gain,
    up_weight,
    down_weight,
    compress_weight,
    grad_output,
    grad_compressed,
    *,
    mp_size,
    dp_size,
):
    streams, seg_len, width = inputs.shape
    mem_len = memory.shape[1]
    packed_len = compressed_memory.shape[1]
    heads_here = relative_bias.shape[0]
    local = query_weight.shape[1]
    compress_count = grad_compressed.shape[1]
    rows = streams * seg_len
    slot_index = jnp.arange(mem_len, dtype=jnp.int32)
    live_rows = jnp.where(
        (slot_index[None, :] >= mem_len - memory_fill[:, None])[:, :, None], memory, jnp.zeros_like(memory)
    )
    evicted = live_rows.reshape(streams * compress_count, 2 * width)
    packed_new = mm(evicted, compress_weight).astype(bf16).reshape(streams, compress_count, -1)
    grad_pack = mm_t0(grad_compressed.reshape(streams * compress_count, -1), evicted)

    unit, q, k, v, mixed, log_total = attend(
        inputs,
        memory,
        compressed_memory,
        memory_fill,
        compressed_fill,
        first_gain,
        query_weight,
        key_weight,
        value_weight,
        relative_bias,
    )
    seg_rows = inputs.reshape(rows, width)
    grad_mixed, grad_residual, residual, branch, grad_down, grad_up, grad_out_full, grad_second = feed(
        mixed.reshape(rows, local),
        seg_rows,
        grad_output.reshape(rows, width),
        up_weight,
        down_weight,
        output_weight,
        second_gain,
        mp_size,
        dp_size,
        chunk_count,
    )
    grad_mixed = grad_mixed.reshape(streams, seg_len, local)
    grad_unit, gq, gk, gv, rel = attend_back(
        unit,
        q,
        k,
        v,
        log_total,
        grad_mixed,
        memory_fill,
        compressed_fill,
        query_weight,
        key_weight,
        value_weight,
        relative_bias,
        mem_len,
        packed_len,
    )
    grad_relative = jnp.sum(rel, axis=-1)[:, : len(reach_marks)]
    local_first = sum(
        jnp.sum(grad * weight.astype(f32).T, axis=0)
        for grad, weight in ((gq, query_weight), (gk, key_weight), (gv, value_weight))
    )
    flat_relative = jnp.pad(grad_relative.reshape(-1), (0, width - grad_relative.size))
    small = jnp.pad(jnp.stack([local_first / first_gain, grad_second[0], flat_relative]), ((0, 5), (0, 0)))
    result, grad_seg, grad_out_w, grad_up, grad_down, gq, gk, gv, grad_pack, small = close(
        grad_unit,
        branch,
        seg_rows,
        grad_residual,
        residual,
        first_gain,
        (grad_out_full, grad_up, grad_down, gq, gk, gv, grad_pack),
        small,
        mp_size,
        dp_size,
        chunk_count,
    )
    grad_first, grad_second = small[0], small[1]
    grad_relative = small[2, : grad_relative.size].reshape(grad_relative.shape)
    result = result.reshape(inputs.shape)
    grad_seg = grad_seg.reshape(inputs.shape)
    grad_query_w = gq.reshape(local, width).T
    grad_key_w = gk.reshape(local, width).T
    grad_value_w = gv.reshape(local, width).T
    grad_out_w = grad_out_w.reshape(local, width)
    grad_compress_w = grad_pack.reshape(-1, 2 * width).T
    grad_up = grad_up.reshape(up_weight.shape)
    grad_down = grad_down.reshape(down_weight.shape)
    return (
        result,
        packed_new,
        grad_seg,
        grad_first,
        grad_query_w,
        grad_key_w,
        grad_value_w,
        grad_relative,
        grad_out_w,
        grad_second,
        grad_up,
        grad_down,
        grad_compress_w,
    )


def solution(mesh):
    in_specs = (
        P("dp", None, None),
        P("dp", None, None),
        P("dp", None, None),
        P("dp"),
        P("dp"),
        P(),
        P(None, "mp"),
        P(None, "mp"),
        P(None, "mp"),
        P("mp", None),
        P("mp", None),
        P(),
        P(None, "mp"),
        P("mp", None),
        P(None, "mp"),
        P("dp", None, None),
        P("dp", None, "mp"),
    )
    out_specs = (
        P("dp", None, None),
        P("dp", None, "mp"),
        P("dp", None, None),
        P(),
        P(None, "mp"),
        P(None, "mp"),
        P(None, "mp"),
        P("mp", None),
        P("mp", None),
        P(),
        P(None, "mp"),
        P("mp", None),
        P(None, "mp"),
    )
    return jax.shard_map(
        functools.partial(body, mp_size=mesh.shape["mp"], dp_size=mesh.shape["dp"]),
        mesh=mesh,
        in_specs=in_specs,
        out_specs=out_specs,
        check_vma=False,
    )
```

```python
import functools
import math

import jax
import jax.numpy as jnp
from jax import lax
from jax.experimental import pallas as pl
from jax.experimental.pallas import tpu as pltpu
from jax.sharding import PartitionSpec as P

reach_marks = (1, 2, 3, 4, 5, 6, 7, 8, 12, 16, 24, 32, 48, 64, 96, 128, 192, 256, 384, 512, 768, 1024)
epsilon = 1e-06
masked_score = -1e30
block = 128
query_block = 256
chunk_count = 8
f32 = jnp.float32
bf16 = jnp.bfloat16


def mm(left, right):
    return jnp.dot(left, right, preferred_element_type=f32)


def mm_t0(left, right):
    return lax.dot_general(left, right, (((0,), (0,)), ((), ())), preferred_element_type=f32)


def mm_t1(left, right):
    return lax.dot_general(left, right, (((1,), (1,)), ((), ())), preferred_element_type=f32)


def row_scale(source):
    return lax.rsqrt(jnp.mean(source * source, axis=-1, keepdims=True) + epsilon)


def diagonal_count(seg_len, kept_count):
    return (seg_len + kept_count) // block + 1


def diagonal_of(seg_len, kept_count, column):
    return (seg_len + kept_count) // block - 1 - column


def strip_start(seg_len, sub_block):
    return (seg_len // block - 1 - sub_block) * block


def bias_block(bias_ref, head, diagonal, transposed):
    rows = lax.broadcasted_iota(jnp.int32, (block, block), 0)
    cols = lax.broadcasted_iota(jnp.int32, (block, block), 1)
    distance = diagonal * block + ((cols - rows) if transposed else (rows - cols))
    lowest, highest = diagonal * block - block + 1, diagonal * block + block - 1
    base = jnp.float32(0.0)
    for position, mark_value in enumerate(reach_marks):
        if mark_value <= lowest:
            base = base + bias_ref[head, position]
    value = jnp.full((block, block), base, f32)
    for position, mark_value in enumerate(reach_marks):
        if lowest < mark_value <= highest:
            value = value + jnp.where(distance >= mark_value, bias_ref[head, position], 0.0)
    if lowest < 0:
        value = jnp.where(distance >= 0, value, masked_score)
    return value


def live_mask(shape, axis, packed_len, mem_len, packed_count, memory_count):
    slot = lax.broadcasted_iota(jnp.int32, shape, axis)
    dead_packed = (slot < packed_len) & (slot < packed_len - packed_count)
    dead_memory = (slot >= packed_len) & (slot < packed_len + mem_len - memory_count)
    return jnp.where(dead_packed | dead_memory, masked_score, 0.0).astype(f32)


def greet(peers):
    barrier = pltpu.get_barrier_semaphore()
    for peer in peers:
        pl.semaphore_signal(barrier, inc=1, device_id=peer, device_id_type=pl.DeviceIdType.MESH)
    pl.semaphore_wait(barrier, len(peers))


class Spread:
    def __init__(self, size, group, buffer, sems):
        self.me, self.mine = lax.axis_index("mp"), lax.axis_index("dp")
        self.size, self.group, self.buffer = size, group, buffer
        self.bits = group.bit_length() - 1
        self.across_s, self.across_r, self.within_s, self.within_r = sems
        order = list(reversed(range(self.bits)))
        self.orders = (order, order[1::-1] + order[2:])
        self.spots = []
        for order in self.orders:
            spot = jnp.int32(0)
            for level, bit in enumerate(order):
                spot = spot + ((self.mine // (1 << bit)) % 2) * (1 << level)
            self.spots.append(spot)

    def place_of(self, half, member):
        return sum(((member >> bit) & 1) << level for level, bit in enumerate(self.orders[half]))

    def others(self, offset):
        return {"mp": lax.rem(self.me + offset, self.size)}

    def partner(self, half, level):
        step = 1 << self.orders[half][level]
        return {"dp": self.mine + step - 2 * step * ((self.mine // step) % 2)}

    def across(self, half, offset, arriving):
        origin = lax.rem(self.me - offset + self.size, self.size) if arriving else self.me
        return pltpu.make_async_remote_copy(
            src_ref=self.buffer.at[half, self.spots[half], origin],
            dst_ref=self.buffer.at[half, self.spots[half], origin],
            send_sem=self.across_s.at[half * self.size + offset],
            recv_sem=self.across_r.at[half * self.size + offset],
            device_id=self.others(offset),
            device_id_type=pl.DeviceIdType.MESH,
        )

    def block(self, half, level, other):
        count = 1 << level
        start = (self.spots[half] // count) * count
        if other:
            start = start + count - 2 * count * ((self.spots[half] // count) % 2)
        return pl.ds(start, count)

    def within(self, half, level, arriving):
        span = self.block(half, level, arriving)
        return pltpu.make_async_remote_copy(
            src_ref=self.buffer.at[half, span],
            dst_ref=self.buffer.at[half, span],
            send_sem=self.within_s.at[half * self.bits + level],
            recv_sem=self.within_r.at[half * self.bits + level],
            device_id=self.partner(half, level),
            device_id_type=pl.DeviceIdType.MESH,
        )

    def start_level(self, level):
        for half in range(2):
            if level:
                self.within(half, level - 1, True).wait_recv()
            self.within(half, level, False).start()


def attend_kernel(
    sizes,
    size,
    group,
    memory_fill,
    packed_fill,
    bias_ref,
    seg_ref,
    memory_ref,
    packed_ref,
    gain_ref,
    wq_ref,
    wk_ref,
    wv_ref,
    wc_ref,
    gcomp_ref,
    wo_ref,
    unit_ref,
    q_ref,
    k_ref,
    v_ref,
    mixed_ref,
    log_ref,
    packed_new_ref,
    gpack_ref,
    begun_ref,
    strip,
    live,
    mem_rows,
    spread_in,
    *sems,
):
    seg_len, mem_len, packed_len, heads, head_dim = sizes
    kept = mem_len + packed_len
    keys = kept + seg_len
    stream = pl.program_id(0)
    scale = 1.0 / math.sqrt(head_dim)
    gain = gain_ref[...]
    spread = Spread(size, group, spread_in, sems[:4])
    piece, columns = spread_in.shape[3:]
    width = gain.shape[1]

    @pl.when(stream == 0)
    def _():
        greet(
            [spread.others(offset) for offset in range(1, size)]
            + [spread.partner(half, 0) for half in range(2)]
        )
        rows = pl.ds(pl.multiple_of(spread.mine * piece, piece), piece)
        for half in range(2):
            lanes = slice(half * columns, (half + 1) * columns)
            spread_in[half, spread.spots[half], spread.me] = wo_ref[rows, lanes].astype(f32)
            for offset in range(1, size):
                spread.across(half, offset, False).start()
        gpack_ref[...] = jnp.zeros_like(gpack_ref)

    slot = lax.broadcasted_iota(jnp.int32, mem_rows.shape[1:], 0)
    keep = slot >= mem_len - memory_fill[stream]
    count = packed_new_ref.shape[1]
    for column in range(mem_rows.shape[0]):
        lanes = slice(column * block, (column + 1) * block)
        mem_rows[column] = jnp.where(keep, memory_ref[0, :, lanes].astype(f32), 0.0)
    packed_new = jnp.zeros(packed_new_ref.shape[1:], f32)
    for parity in range(2):
        rows = jnp.concatenate(
            [mem_rows[column, pl.ds(parity, count, stride=2), :] for column in range(mem_rows.shape[0])], axis=1
        ).astype(bf16)
        lanes = slice(parity * width, (parity + 1) * width)
        packed_new = packed_new + mm(rows, wc_ref[lanes, :])
        gpack_ref[:, lanes] += mm_t0(gcomp_ref[0], rows)
    packed_new_ref[0] = packed_new.astype(bf16)
    start = 0
    for part_ref, length in ((packed_ref, packed_len), (memory_ref, mem_len), (seg_ref, seg_len)):
        rows = part_ref[0].astype(f32)
        unit = (rows * row_scale(rows) * gain).astype(bf16)
        unit_ref[0, start : start + length, :] = unit
        k_ref[0, start : start + length, :] = mm(unit, wk_ref[...]).astype(bf16)
        v_ref[0, start : start + length, :] = mm(unit, wv_ref[...]).astype(bf16)
        if start == kept:
            q_ref[0] = mm(unit, wq_ref[...]).astype(bf16)
        start += length
    live[...] = live_mask((8, kept), 1, packed_len, mem_len, packed_fill[stream], memory_fill[stream])
    for head in range(heads):
        lanes = slice(head * head_dim, (head + 1) * head_dim)
        for column in range(diagonal_count(seg_len, kept)):
            strip[:, column * block : (column + 1) * block] = bias_block(
                bias_ref, head, diagonal_of(seg_len, kept, column), False
            )
        for index in range(seg_len // query_block):
            reach = kept + (index + 1) * query_block
            rows = slice(index * query_block, (index + 1) * query_block)
            score = mm_t1(q_ref[0, rows, lanes], k_ref[0, :reach, lanes]) * scale
            parts = []
            for sub in range(query_block // block):
                first = strip_start(seg_len, index * (query_block // block) + sub)
                parts.append(strip[:, first : first + reach])
            score = score + jnp.concatenate(parts, axis=0)
            score = jnp.concatenate([score[:, :kept] + live[0:1, :], score[:, kept:]], axis=1)
            top = jnp.max(score, axis=-1, keepdims=True)
            weight = jnp.exp(score - top)
            total = jnp.sum(weight, axis=-1, keepdims=True)
            log_total = jnp.broadcast_to(top + jnp.log(total), (query_block, block))
            log_ref[0, head, :, rows] = log_total.T[0:1, :]
            mixed = mm(weight.astype(bf16), v_ref[0, :reach, lanes]) * (1.0 / total)
            mixed_ref[0, rows, lanes] = mixed.astype(bf16)

    @pl.when(stream == 0)
    def _():
        for half in range(2):
            for offset in range(1, size):
                spread.across(half, offset, True).wait_recv()
        spread.start_level(0)

    @pl.when(stream == pl.num_programs(0) - 1)
    def _():
        copies = []
        for half in range(2):
            spread.within(half, 0, True).wait_recv()
            pair = spread_in.at[half, pl.ds((spread.spots[half] // 2) * 2, 2)]
            copies.append(pltpu.make_async_copy(pair, begun_ref.at[half], sems[4].at[half]))
            copies[-1].start()
        for half in range(2):
            for offset in range(1, size):
                spread.across(half, offset, False).wait_send()
            spread.within(half, 0, False).wait_send()
            copies[half].wait()


def attend(
    inputs, memory, packed, memory_fill, packed_fill, gain, wq, wk, wv, bias, wc, gcomp, wo, size, group
):
    streams, seg_len, width = inputs.shape
    mem_len, packed_len = memory.shape[1], packed.shape[1]
    heads = bias.shape[0]
    local = wq.shape[1]
    keys = seg_len + mem_len + packed_len
    sizes = (seg_len, mem_len, packed_len, heads, local // heads)
    smem = pl.BlockSpec(memory_space=pltpu.SMEM)
    compress_count = gcomp.shape[1]
    piece = wo.shape[0] // group
    bits = group.bit_length() - 1

    def rows_of(count, columns):
        return pl.BlockSpec((1, count, columns), lambda s: (s, 0, 0))

    def whole(shape):
        return pl.BlockSpec(shape, lambda s: (0,) * len(shape))

    return pl.pallas_call(
        functools.partial(attend_kernel, sizes, size, group),
        grid=(streams,),
        in_specs=[
            smem,
            smem,
            smem,
            rows_of(seg_len, width),
            rows_of(mem_len, width),
            rows_of(packed_len, width),
            whole((1, width)),
            whole(wq.shape),
            whole(wk.shape),
            whole(wv.shape),
            whole(wc.shape),
            rows_of(compress_count, local),
            whole(wo.shape),
        ],
        out_specs=[
            rows_of(keys, width),
            rows_of(seg_len, local),
            rows_of(keys, local),
            rows_of(keys, local),
            rows_of(seg_len, local),
            pl.BlockSpec((1, heads, 1, seg_len), lambda s: (s, 0, 0, 0)),
            rows_of(compress_count, local),
            whole((local, 2 * width)),
            pl.BlockSpec(memory_space=pl.ANY),
        ],
        out_shape=[
            jax.ShapeDtypeStruct((streams, keys, width), bf16),
            jax.ShapeDtypeStruct((streams, seg_len, local), bf16),
            jax.ShapeDtypeStruct((streams, keys, local), bf16),
            jax.ShapeDtypeStruct((streams, keys, local), bf16),
            jax.ShapeDtypeStruct((streams, seg_len, local), bf16),
            jax.ShapeDtypeStruct((streams, heads, 1, seg_len), f32),
            jax.ShapeDtypeStruct((streams, compress_count, local), bf16),
            jax.ShapeDtypeStruct((local, 2 * width), f32),
            jax.ShapeDtypeStruct((2, 2, size, piece, width // 2), f32),
        ],
        scratch_shapes=[
            pltpu.VMEM((block, diagonal_count(seg_len, mem_len + packed_len) * block), f32),
            pltpu.VMEM((8, mem_len + packed_len), f32),
            pltpu.VMEM((width // block, mem_len, block), f32),
            pltpu.VMEM((2, group, size, piece, width // 2), f32),
            pltpu.SemaphoreType.DMA((2 * size,)),
            pltpu.SemaphoreType.DMA((2 * size,)),
            pltpu.SemaphoreType.DMA((2 * bits,)),
            pltpu.SemaphoreType.DMA((2 * bits,)),
            pltpu.SemaphoreType.DMA((2,)),
        ],
        compiler_params=pltpu.CompilerParams(
            collective_id=2, has_side_effects=True, vmem_limit_bytes=60 << 20
        ),
        cost_estimate=pl.CostEstimate(
            flops=streams * (2 * keys * width * local * 3 + 4 * seg_len * keys * local),
            bytes_accessed=streams * keys * (width * 4 + local * 6),
            transcendentals=streams * heads * seg_len * keys,
        ),
        name="attend",
    )(memory_fill, packed_fill, bias, inputs, memory, packed, gain[None, :], wq, wk, wv, wc, gcomp, wo)


def attend_back_kernel(
    sizes,
    memory_fill,
    packed_fill,
    bias_ref,
    unit_ref,
    q_ref,
    k_ref,
    v_ref,
    log_ref,
    gm_ref,
    wq_ref,
    wk_ref,
    wv_ref,
    gain_ref,
    gsecond_ref,
    gunit_ref,
    gq_ref,
    gk_ref,
    gv_ref,
    small_ref,
    strip,
    live,
    dk_sum,
    dv_sum,
    dq_low,
    dk_low,
    dv_low,
    strip_sum,
):
    seg_len, mem_len, packed_len, heads, head_dim = sizes
    kept = mem_len + packed_len
    keys = kept + seg_len
    stream = pl.program_id(0)
    scale = 1.0 / math.sqrt(head_dim)

    @pl.when(stream == 0)
    def _():
        strip_sum[...] = jnp.zeros_like(strip_sum)
        gq_ref[...] = jnp.zeros_like(gq_ref)
        gk_ref[...] = jnp.zeros_like(gk_ref)
        gv_ref[...] = jnp.zeros_like(gv_ref)

    live[...] = live_mask((kept, block), 0, packed_len, mem_len, packed_fill[stream], memory_fill[stream])
    subs = query_block // block
    for head in range(heads):
        lanes = slice(head * head_dim, (head + 1) * head_dim)
        for column in range(diagonal_count(seg_len, kept)):
            strip[column * block : (column + 1) * block, :] = bias_block(
                bias_ref, head, diagonal_of(seg_len, kept, column), True
            )
        for index in range(seg_len // query_block):
            reach = kept + (index + 1) * query_block
            rows = slice(index * query_block, (index + 1) * query_block)
            queries = q_ref[0, rows, lanes]
            grads = gm_ref[0, rows, lanes]
            key_rows = k_ref[0, :reach, lanes]
            score = mm_t1(key_rows, queries) * scale
            firsts = [strip_start(seg_len, index * subs + sub) for sub in range(subs)]
            score = score + jnp.concatenate([strip[first : first + reach, :] for first in firsts], axis=1)
            live_wide = jnp.concatenate([live[...]] * subs, axis=1)
            score = jnp.concatenate([score[:kept] + live_wide, score[kept:]], axis=0)
            prob = jnp.exp(score - log_ref[0, head, :, rows])
            grad_prob = mm_t1(v_ref[0, :reach, lanes], grads)
            delta = jnp.sum(prob * grad_prob, axis=0, keepdims=True)
            grad_score = (prob * (grad_prob - delta)).astype(bf16)
            dk_part = mm(grad_score, queries)
            dv_part = mm(prob.astype(bf16), grads)
            if index == seg_len // query_block - 1:
                earlier = kept + index * query_block
                if index:
                    dk_sum[:earlier] += dk_part[:earlier]
                    dv_sum[:earlier] += dv_part[:earlier]
                    dk_sum[earlier:] = dk_part[earlier:]
                    dv_sum[earlier:] = dv_part[earlier:]
                else:
                    dk_sum[...] = dk_part
                    dv_sum[...] = dv_part
            elif index:
                earlier = kept + index * query_block
                dk_sum[:earlier] += dk_part[:earlier]
                dv_sum[:earlier] += dv_part[:earlier]
                dk_sum[earlier:reach] = dk_part[earlier:]
                dv_sum[earlier:reach] = dv_part[earlier:]
            else:
                dk_sum[:reach] = dk_part
                dv_sum[:reach] = dv_part
            dq_low[rows, lanes] = (mm_t0(grad_score, key_rows) * scale).astype(bf16)
            for sub in range(subs):
                strip_sum[head, firsts[sub] : firsts[sub] + reach, :] += grad_score[
                    :, sub * block : (sub + 1) * block
                ].astype(f32)
        dk_low[:, lanes] = (dk_sum[...] * scale).astype(bf16)
        dv_low[:, lanes] = dv_sum[...].astype(bf16)
    gq_ref[...] += mm_t0(dq_low[...], unit_ref[0, kept:, :])
    gk_ref[...] += mm_t0(dk_low[...], unit_ref[0])
    gv_ref[...] += mm_t0(dv_low[...], unit_ref[0])
    gunit_ref[0] = (
        mm_t1(dq_low[...], wq_ref[...])
        + mm_t1(dk_low[kept:, :], wk_ref[...])
        + mm_t1(dv_low[kept:, :], wv_ref[...])
    )

    @pl.when(stream == pl.num_programs(0) - 1)
    def _():
        rows = lax.broadcasted_iota(jnp.int32, (block, block), 0)
        cols = lax.broadcasted_iota(jnp.int32, (block, block), 1)
        width = gain_ref.shape[1]
        lane = lax.broadcasted_iota(jnp.int32, (1, width), 1)
        relative = jnp.zeros((1, width), f32)
        for head in range(heads):
            blocks = []
            for column in range(diagonal_count(seg_len, kept)):
                blocks.append(strip_sum[head, column * block : (column + 1) * block, :])
            for position, mark_value in enumerate(reach_marks):
                total = jnp.zeros((1, block), f32)
                for column, value in enumerate(blocks):
                    diagonal = diagonal_of(seg_len, kept, column)
                    lowest, highest = diagonal * block - block + 1, diagonal * block + block - 1
                    if mark_value <= lowest:
                        total = total + jnp.sum(value, axis=0, keepdims=True)
                    elif mark_value <= highest:
                        distance = diagonal * block + cols - rows
                        total = total + jnp.sum(
                            jnp.where(distance >= mark_value, value, 0.0), axis=0, keepdims=True
                        )
                total = jnp.sum(total, axis=1, keepdims=True)
                relative = jnp.where(lane == head * len(reach_marks) + position, total, relative)
        first = jnp.zeros((1, width), f32)
        for grad_ref, weight_ref in ((gq_ref, wq_ref), (gk_ref, wk_ref), (gv_ref, wv_ref)):
            turned = weight_ref[...].astype(f32).T
            first = first + jnp.sum(grad_ref[...] * turned, axis=0, keepdims=True)
        small_ref[...] = jnp.concatenate(
            [first / gain_ref[...], gsecond_ref[...], relative, jnp.zeros((5, width), f32)], axis=0
        )


def attend_back(
    unit, q, k, v, log_total, grad_mixed, memory_fill, packed_fill, wq, wk, wv, bias, gain, grad_second, mem_len, packed_len
):
    streams, keys, width = unit.shape
    seg_len, local = q.shape[1:]
    heads = bias.shape[0]
    kept = mem_len + packed_len
    sizes = (seg_len, mem_len, packed_len, heads, local // heads)
    smem = pl.BlockSpec(memory_space=pltpu.SMEM)
    strip_len = diagonal_count(seg_len, kept) * block

    def rows_of(count, columns):
        return pl.BlockSpec((1, count, columns), lambda s: (s, 0, 0))

    def whole(shape):
        return pl.BlockSpec(shape, lambda s: (0,) * len(shape))

    return pl.pallas_call(
        functools.partial(attend_back_kernel, sizes),
        grid=(streams,),
        in_specs=[
            smem,
            smem,
            smem,
            rows_of(keys, width),
            rows_of(seg_len, local),
            rows_of(keys, local),
            rows_of(keys, local),
            pl.BlockSpec((1, heads, 1, seg_len), lambda s: (s, 0, 0, 0)),
            rows_of(seg_len, local),
            whole(wq.shape),
            whole(wk.shape),
            whole(wv.shape),
            whole((1, width)),
            whole((1, width)),
        ],
        out_specs=[
            rows_of(seg_len, width),
            whole((local, width)),
            whole((local, width)),
            whole((local, width)),
            whole((8, width)),
        ],
        out_shape=[
            jax.ShapeDtypeStruct((streams, seg_len, width), f32),
            jax.ShapeDtypeStruct((local, width), f32),
            jax.ShapeDtypeStruct((local, width), f32),
            jax.ShapeDtypeStruct((local, width), f32),
            jax.ShapeDtypeStruct((8, width), f32),
        ],
        scratch_shapes=[
            pltpu.VMEM((strip_len, block), f32),
            pltpu.VMEM((kept, block), f32),
            pltpu.VMEM((keys, local // heads), f32),
            pltpu.VMEM((keys, local // heads), f32),
            pltpu.VMEM((seg_len, local), bf16),
            pltpu.VMEM((keys, local), bf16),
            pltpu.VMEM((keys, local), bf16),
            pltpu.VMEM((heads, strip_len, block), f32),
        ],
        compiler_params=pltpu.CompilerParams(vmem_limit_bytes=60 << 20),
        cost_estimate=pl.CostEstimate(
            flops=streams * (8 * keys * width * local + 10 * seg_len * keys * local),
            bytes_accessed=streams * keys * (width * 2 + local * 6),
            transcendentals=streams * heads * seg_len * keys,
        ),
        name="attend_back",
    )(
        memory_fill,
        packed_fill,
        bias,
        unit,
        q,
        k,
        v,
        log_total,
        grad_mixed,
        wq,
        wk,
        wv,
        gain[None, :],
        grad_second,
    )


def remote(source, target, send_sems, recv_sems, source_slot, target_slot, send_slot, recv_slot, peer):
    return pltpu.make_async_remote_copy(
        src_ref=source.at[source_slot],
        dst_ref=target.at[target_slot],
        send_sem=send_sems.at[send_slot],
        recv_sem=recv_sems.at[recv_slot],
        device_id=peer,
        device_id_type=pl.DeviceIdType.MESH,
    )


class Line:
    def __init__(self, size, chunks, hop):
        self.me = lax.axis_index("mp")
        self.size, self.chunks, self.hop = size, chunks, hop
        self.reach = size - 1

    def place(self, right):
        return self.me if right else self.reach - self.me

    def peer(self, right):
        return {"mp": self.me + 1 if right else self.me - 1}

    def copy(self, source, target, sems, slot, right):
        return remote(source, target, sems[0], sems[1], slot, slot, slot, slot, self.peer(right))

    def chunk_at(self, tick):
        positive = jnp.maximum(tick, 0)
        chunk = positive // self.reach
        return chunk, (tick >= 0) & (positive == chunk * self.reach) & (chunk < self.chunks)

    def scatter_step(self, tick, part, lanes):
        for right, held, sems in lanes:
            place = self.place(right)
            late = tick - self.hop * place
            positive = jnp.maximum(late, 0)
            chunk = positive // self.reach
            goal = self.reach - (positive - self.reach * chunk)
            active = (late >= 0) & (chunk < self.chunks) & (goal > place)
            slot = chunk * self.size + (goal if right else self.reach - goal)

            @pl.when(active & (place == 0))
            def _():
                self.copy(part, held, sems, slot, right).start()

            @pl.when(active & (place > 0))
            def _():
                self.copy(held, held, sems, slot, right).wait_recv()
                held[slot] = held[slot] + part[slot]
                self.copy(held, held, sems, slot, right).start()

    def scatter_sum(self, chunk, part, lanes, total):
        slot = chunk * self.size + self.me
        total[...] = part[slot]
        for right, held, sems in lanes:

            @pl.when(self.place(right) > 0)
            def _():
                self.copy(held, held, sems, slot, right).wait_recv()
                total[...] = total[...] + held[slot]

    def gather_start(self, chunk, whole, lanes):
        slot = chunk * self.size + self.me
        for right, sems in lanes:

            @pl.when(self.place(right) < self.reach)
            def _():
                self.copy(whole, whole, sems, slot, right).start()

    def gather_step(self, tick, whole, lanes, landed=None):
        for right, sems in lanes:
            place = self.place(right)
            for distance in range(1, self.size):
                chunk, due = self.chunk_at(tick - self.hop * distance)

                @pl.when(due & (distance <= place))
                def _():
                    slot = chunk * self.size + (self.me - distance if right else self.me + distance)
                    self.copy(whole, whole, sems, slot, right).wait_recv()

                    @pl.when(place < self.reach)
                    def _():
                        self.copy(whole, whole, sems, slot, right).start()

                    if landed is not None:
                        landed(slot)

    def scatter_drain(self, chunk, part, lanes):
        for right, held, sems in lanes:
            for goal in range(1, self.size):

                @pl.when(goal > self.place(right))
                def _():
                    slot = chunk * self.size + (goal if right else self.reach - goal)
                    self.copy(part, held, sems, slot, right).wait_send()

    def gather_drain(self, chunk, whole, lanes):
        for right, sems in lanes:
            place = self.place(right)
            for distance in range(self.size):

                @pl.when((distance <= place) & (place < self.reach))
                def _():
                    slot = chunk * self.size + (self.me - distance if right else self.me + distance)
                    self.copy(whole, whole, sems, slot, right).wait_send()


def feed_kernel(
    size,
    group,
    chunks,
    hop,
    delay,
    beat,
    mixed_ref,
    seg_ref,
    grad_ref,
    up_ref,
    down_ref,
    begun_ref,
    gain_ref,
    gm_ref,
    gres_ref,
    res_ref,
    branch_ref,
    gdown_ref,
    gup_ref,
    gout_ref,
    gsecond_ref,
    heads_in,
    part,
    held_right,
    held_left,
    swap_out,
    swap_in,
    weights_in,
    weights,
    chunk_rows,
    total,
    own_mixed,
    own_grad,
    *sems,
):
    line = Line(size, chunks, hop)
    me = line.me
    (hr_s, hr_r, hl_s, hl_r, sr_s, sr_r, sl_s, sl_r, x_s, x_r, wd_s, wd_r) = sems
    gather_lanes = ((True, (hr_s, hr_r)), (False, (hl_s, hl_r)))
    scatter_lanes = ((True, held_right, (sr_s, sr_r)), (False, held_left, (sl_s, sl_r)))
    spread = Spread(size, group, weights_in, (None, None, wd_s, wd_r))
    bits = spread.bits
    piece, columns = weights_in.shape[3:]
    width = weights.shape[1]
    rows = total.shape[0]
    local = mixed_ref.shape[-1]
    greet(
        [spread.others(offset) for offset in range(1, size)]
        + [spread.partner(half, level) for half in range(2) for level in range(1, bits)]
    )
    for half in range(2):
        weights_in[half, pl.ds((spread.spots[half] // 2) * 2, 2)] = begun_ref[half]
        spread.within(half, 1, False).start()

    def stage_heads(chunk, _):
        heads_in[chunk * size + me] = mixed_ref[chunk].astype(f32)
        return 0

    lax.fori_loop(0, chunks, stage_heads, 0)
    gsecond_ref[...] = jnp.zeros_like(gsecond_ref)
    gdown_ref[...] = jnp.zeros_like(gdown_ref)
    gup_ref[...] = jnp.zeros_like(gup_ref)

    def weight_step(tick):
        for level in range(2, bits):

            @pl.when(tick == beat + level - 2)
            def _():
                spread.start_level(level)

    def weight_finish():
        for half in range(2):
            spread.within(half, bits - 1, True).wait_recv()
            for index in range(size):
                pieces = [weights_in[half, spread.place_of(half, member), index] for member in range(group)]
                weights[index * group * piece : (index + 1) * group * piece, half * columns : (half + 1) * columns] = (
                    jnp.concatenate(pieces, axis=0).astype(bf16)
                )

    own = pl.ds(pl.multiple_of(me * rows, rows), rows)

    def feed_chunk(chunk):
        heads = [heads_in[chunk * size + index].astype(bf16) for index in range(size)]
        for index in range(size):
            own_mixed[chunk, :, index * local : (index + 1) * local] = heads_in[
                chunk * size + index, own, :
            ].astype(bf16)
        residual = seg_ref[chunk].astype(f32) + mm(jnp.concatenate(heads, axis=1), weights[...])
        chunk_rows[...] = residual
        res_ref[chunk] = chunk_rows[own, :]
        ffn_input = (residual * row_scale(residual) * gain_ref[...]).astype(bf16)
        pre_act = mm(ffn_input, up_ref[...])
        inner = math.sqrt(2.0 / math.pi)
        squared = pre_act * pre_act
        tanh = jnp.tanh(inner * (pre_act + 0.044715 * pre_act * squared))
        activated = (0.5 * pre_act * (1.0 + tanh)).astype(bf16)
        slope = 0.5 * (1.0 + tanh) + 0.5 * pre_act * (1.0 - tanh * tanh) * (
            inner * (1.0 + 3.0 * 0.044715 * squared)
        )
        grads = grad_ref[chunk]
        grad_pre = (slope * mm_t1(grads, down_ref[...])).astype(bf16)
        first = pl.ds(chunk * size, size)
        part[first] = mm_t1(grad_pre, up_ref[...]).reshape(size, rows, width)
        branch_ref[first] = mm(activated, down_ref[...]).reshape(size, rows, width)
        gdown_ref[...] += mm_t0(activated, grads)
        gup_ref[...] += mm_t0(ffn_input, grad_pre)

    def swap(chunk, offset, arriving):
        target = lax.rem(me + offset, size)
        origin = lax.rem(me - offset + size, size)
        landing = chunk * size + (origin if arriving else me)
        return remote(
            swap_out,
            swap_in,
            x_s,
            x_r,
            chunk * size + target,
            landing,
            chunk * size + target,
            landing,
            {"mp": target},
        )

    def settle(chunk):
        line.scatter_sum(chunk, part, scatter_lanes, total)
        grad_ffn = total[...]
        residual = res_ref[chunk]
        scale = row_scale(residual)
        normed = residual * scale
        gsecond_ref[...] += jnp.sum(grad_ffn * normed, axis=0, keepdims=True)
        weighted = grad_ffn * gain_ref[...]
        own_rows = grad_ref[chunk, own, :].astype(f32)
        grad_residual = own_rows + scale * (
            weighted - normed * jnp.mean(weighted * normed, axis=-1, keepdims=True)
        )
        gres_ref[chunk] = grad_residual
        low = grad_residual.astype(bf16)
        own_grad[chunk] = low
        grad_mixed = mm_t1(low, weights[...]).astype(bf16).astype(f32)
        for index in range(size):
            swap_out[chunk * size + index] = grad_mixed[:, index * local : (index + 1) * local]
        for offset in range(1, size):
            swap(chunk, offset, False).start()

    feed_at = hop * line.reach + delay

    def step(tick, _):
        weight_step(tick)

        @pl.when(tick == feed_at)
        def _():
            weight_finish()

        chunk, due = line.chunk_at(tick)

        @pl.when(due)
        def _():
            line.gather_start(chunk, heads_in, gather_lanes)

        line.gather_step(tick, heads_in, gather_lanes)
        chunk_f, due_f = line.chunk_at(tick - feed_at)

        @pl.when(due_f)
        def _():
            feed_chunk(chunk_f)

        line.scatter_step(tick - feed_at, part, scatter_lanes)
        chunk_s, due_s = line.chunk_at(tick - feed_at - hop * line.reach)

        @pl.when(due_s)
        def _():
            settle(chunk_s)

        return 0

    lax.fori_loop(0, feed_at + line.reach * (chunks - 1) + hop * line.reach + 1, step, 0)
    gout_ref[...] = mm_t0(
        own_mixed[...].reshape(chunks * rows, width), own_grad[...].reshape(chunks * rows, width)
    )

    def finish(chunk, _):
        for offset in range(1, size):
            swap(chunk, offset, True).wait_recv()
        for index in range(size):

            @pl.when(index == me)
            def _():
                gm_ref[chunk * size + index] = swap_out[chunk * size + index].astype(bf16)

            @pl.when(index != me)
            def _():
                gm_ref[chunk * size + index] = swap_in[chunk * size + index].astype(bf16)

        line.gather_drain(chunk, heads_in, gather_lanes)
        line.scatter_drain(chunk, part, scatter_lanes)
        for offset in range(1, size):
            swap(chunk, offset, False).wait_send()
        return 0

    lax.fori_loop(0, chunks, finish, 0)
    for half in range(2):
        for level in range(1, bits):
            spread.within(half, level, False).wait_send()


def feed(mixed, seg_rows, grad_rows, up, down, begun, gain, size, group, chunks):
    rows, width = seg_rows.shape
    local = mixed.shape[1]
    chunk = rows // chunks
    piece = chunk // size
    hidden = up.shape[1]
    vmem = pl.BlockSpec(memory_space=pltpu.VMEM)
    slots = pltpu.SemaphoreType.DMA((chunks * size,))
    bits = group.bit_length() - 1
    return pl.pallas_call(
        functools.partial(feed_kernel, size, group, chunks, 2, 0, 4),
        in_specs=[vmem] * 7,
        out_specs=[vmem] * 8,
        out_shape=[
            jax.ShapeDtypeStruct((chunks * size, piece, local), bf16),
            jax.ShapeDtypeStruct((chunks, piece, width), f32),
            jax.ShapeDtypeStruct((chunks, piece, width), f32),
            jax.ShapeDtypeStruct((chunks * size, piece, width), f32),
            jax.ShapeDtypeStruct((hidden, width), f32),
            jax.ShapeDtypeStruct((width, hidden), f32),
            jax.ShapeDtypeStruct((width, width), f32),
            jax.ShapeDtypeStruct((1, width), f32),
        ],
        scratch_shapes=[
            pltpu.VMEM((chunks * size, chunk, local), f32),
            pltpu.VMEM((chunks * size, piece, width), f32),
            pltpu.VMEM((chunks * size, piece, width), f32),
            pltpu.VMEM((chunks * size, piece, width), f32),
            pltpu.VMEM((chunks * size, piece, local), f32),
            pltpu.VMEM((chunks * size, piece, local), f32),
            pltpu.VMEM((2, group, *begun.shape[2:]), f32),
            pltpu.VMEM((width, width), bf16),
            pltpu.VMEM((chunk, width), f32),
            pltpu.VMEM((piece, width), f32),
            pltpu.VMEM((chunks, piece, width), bf16),
            pltpu.VMEM((chunks, piece, width), bf16),
        ]
        + [slots] * 10
        + [pltpu.SemaphoreType.DMA((2 * bits,))] * 2,
        compiler_params=pltpu.CompilerParams(
            collective_id=0, has_side_effects=True, vmem_limit_bytes=63 << 20
        ),
        name="feed",
    )(
        mixed.reshape(chunks, chunk, local),
        seg_rows.reshape(chunks, chunk, width),
        grad_rows.reshape(chunks, chunk, width),
        up,
        down,
        begun,
        gain[None, :],
    )


class Pieces:
    def __init__(self, group, rows, gap, crossing, jobs, work, landing, summed, sems):
        self.mine = lax.axis_index("dp")
        self.bits = group.bit_length() - 1
        self.rows, self.gap, self.crossing, self.jobs = rows, gap, crossing, jobs
        self.work, self.landing, self.summed = work, landing, summed
        self.slots = work.shape[0]
        (self.rs_s, self.rs_r, self.ag_s, self.ag_r, self.load_sem, self.store_sem) = sems
        self.count = crossing[0] + sum(job[2] for job in jobs)
        self.beats = self.count + 2 * self.bits * gap + 2

    def step_of(self, odd, level):
        even_step = 1 << level
        odd_step = 1 << ((self.bits - level) % self.bits)
        return jnp.where(odd == 1, odd_step, even_step)

    def bit_of(self, odd, level):
        return (self.mine // self.step_of(odd, level)) % 2

    def partner(self, odd, level):
        step = self.step_of(odd, level)
        return {"dp": self.mine + step - 2 * step * self.bit_of(odd, level)}

    def start_of(self, odd, level):
        start = jnp.int32(0)
        for earlier in range(level):
            start = start + self.bit_of(odd, earlier) * (self.rows >> (earlier + 1))
        return start

    def span(self, start, level):
        length = self.rows >> level
        return pl.ds(pl.multiple_of(start, self.rows >> self.bits), length)

    def halves(self, odd, level):
        start, bit, half = self.start_of(odd, level), self.bit_of(odd, level), self.rows >> (level + 1)
        return self.span(start + bit * half, level + 1), self.span(start + (1 - bit) * half, level + 1)

    def reduce_copy(self, slot, odd, level):
        _, give = self.halves(odd, level)
        region = pl.ds(self.rows - (self.rows >> level), self.rows >> (level + 1))
        return pltpu.make_async_remote_copy(
            src_ref=self.work.at[slot, give],
            dst_ref=self.landing.at[slot, region],
            send_sem=self.rs_s.at[slot * self.bits + level],
            recv_sem=self.rs_r.at[slot * self.bits + level],
            device_id=self.partner(odd, level),
            device_id_type=pl.DeviceIdType.MESH,
        )

    def absorb(self, slot, odd, level):
        self.reduce_copy(slot, odd, level).wait_recv()
        keep, _ = self.halves(odd, level)
        region = pl.ds(self.rows - (self.rows >> level), self.rows >> (level + 1))
        self.work[slot, keep, :] = self.work[slot, keep, :] + self.landing[slot, region, :]

    def spread_copy(self, buffer, sems, slot, odd, level, arriving):
        keep, give = self.halves(odd, level)
        span = give if arriving else keep
        return pltpu.make_async_remote_copy(
            src_ref=buffer.at[slot, span],
            dst_ref=buffer.at[slot, span],
            send_sem=sems[0].at[slot * self.bits + level],
            recv_sem=sems[1].at[slot * self.bits + level],
            device_id=self.partner(odd, level),
            device_id_type=pl.DeviceIdType.MESH,
        )

    def spread(self, slot, odd, level, arriving):
        return self.spread_copy(self.summed, (self.ag_s, self.ag_r), slot, odd, level, arriving)

    def move(self, piece, slot, store, start):
        columns = self.work.shape[2]
        first = self.crossing[0]
        sources = [(self.crossing[1], None, 0, first)]
        for source, target, count in self.jobs:
            sources.append((source, target, first, first + count))
            first += count
        for source, target, low, high in sources:
            if store and target is None:
                continue

            @pl.when((piece >= low) & (piece < high))
            def _():
                across = source.shape[2] // columns
                index = (piece - low) // across
                lanes = pl.ds(pl.multiple_of((piece - low - index * across) * columns, columns), columns)
                inside = self.summed.at[slot] if store else self.work.at[slot]
                if store:
                    copy = pltpu.make_async_copy(inside, target.at[index, :, lanes], self.store_sem.at[slot])
                else:
                    copy = pltpu.make_async_copy(source.at[index, :, lanes], inside, self.load_sem.at[slot])
                copy.start() if start else copy.wait()

    def load_first(self):
        self.move(jnp.int32(0), 0, False, True)

    def step(self, tick, cross):
        bits = self.bits
        for age in reversed(range(-1, 2 * bits + 2)):
            piece = tick - (age if age < 0 else min(age * self.gap, 2 * bits * self.gap + 1))
            safe = jnp.maximum(piece, 0)
            slot, odd = safe % self.slots, safe % 2
            plain = piece >= self.crossing[0]
            inside = (piece >= 0) & (piece < self.count)
            if age == 2 * bits + 1:

                @pl.when(inside)
                def _():
                    for level in range(bits):
                        self.reduce_copy(slot, odd, level).wait_send()

                @pl.when(inside & plain)
                def _():
                    for level in range(bits):
                        self.spread(slot, odd, level, False).wait_send()
                    self.move(piece, slot, True, False)

                @pl.when(inside & jnp.logical_not(plain))
                def _():
                    cross(piece, slot, odd, False)

            elif age == 2 * bits:

                @pl.when(inside & plain)
                def _():
                    self.spread(slot, odd, 0, True).wait_recv()
                    self.move(piece, slot, True, True)

            elif age > bits:

                @pl.when(inside & plain)
                def _():
                    self.spread(slot, odd, 2 * bits - age, True).wait_recv()
                    self.spread(slot, odd, 2 * bits - 1 - age, False).start()

            elif age == bits:

                @pl.when(inside)
                def _():
                    self.absorb(slot, odd, bits - 1)

                @pl.when(inside & plain)
                def _():
                    own = self.span(self.start_of(odd, bits), bits)
                    self.summed[slot, own, :] = self.work[slot, own, :]
                    self.spread(slot, odd, bits - 1, False).start()

                @pl.when(inside & jnp.logical_not(plain))
                def _():
                    cross(piece, slot, odd, True)

            elif age > 0:

                @pl.when(inside)
                def _():
                    self.absorb(slot, odd, age - 1)
                    self.reduce_copy(slot, odd, age).start()

            elif age == 0:

                @pl.when(inside)
                def _():
                    self.move(piece, slot, False, False)
                    self.reduce_copy(slot, odd, 0).start()

            else:

                @pl.when(inside)
                def _():
                    self.move(piece, slot, False, True)


def close_kernel(
    size,
    group,
    chunks,
    hop,
    counts,
    gap,
    lag,
    gunit_ref,
    branch_ref,
    seg_ref,
    gres_ref,
    res_ref,
    gain_ref,
    gout_ref,
    gup_ref,
    gdown_ref,
    gq_ref,
    gk_ref,
    gv_ref,
    gpack_ref,
    small_ref,
    result_ref,
    gseg_ref,
    gout_sum,
    gup_sum,
    gdown_sum,
    gq_sum,
    gk_sum,
    gv_sum,
    gpack_sum,
    small_sum,
    whole_seg,
    whole_out,
    seg_right,
    seg_left,
    out_right,
    out_left,
    total,
    work,
    landing,
    summed,
    cross_in,
    cross_work,
    small_cross,
    small_held,
    small_in,
    *sems,
):
    line = Line(size, chunks, hop)
    me = line.me
    pairs = [sems[2 * index : 2 * index + 2] for index in range(8)]
    seg_scatter = ((True, seg_right, pairs[0]), (False, seg_left, pairs[1]))
    out_scatter = ((True, out_right, pairs[2]), (False, out_left, pairs[3]))
    seg_gather = ((True, pairs[4]), (False, pairs[5]))
    out_gather = ((True, pairs[6]), (False, pairs[7]))
    piece_sems = sems[16:22]
    cross_s, cross_r, tail_s, tail_r, tail_store = sems[22:27]
    mix_s, mix_r, small_s, small_r = sems[27:31]
    jobs = [
        (gup_ref, gup_sum, counts[1]),
        (gdown_ref, gdown_sum, counts[2]),
        (gq_ref, gq_sum, counts[3]),
        (gk_ref, gk_sum, counts[4]),
        (gv_ref, gv_sum, counts[5]),
        (gpack_ref, gpack_sum, counts[6]),
    ]
    pieces = Pieces(group, work.shape[1], gap, (counts[0], gout_ref), jobs, work, landing, summed, piece_sems)
    bits = pieces.bits
    pieces.load_first()
    greet(
        [{"mp": lax.rem(me + offset, size)} for offset in range(1, size)]
        + [{"dp": pieces.mine + (1 << bit) - 2 * (1 << bit) * ((pieces.mine // (1 << bit)) % 2)} for bit in range(bits)]
    )

    across, columns = cross_work.shape[0], work.shape[2]

    def cross_copy(slot, column, target, origin):
        own = pieces.span(pieces.start_of(column % 2, bits), bits)
        return pltpu.make_async_remote_copy(
            src_ref=work.at[slot, own],
            dst_ref=cross_in.at[column * size + origin],
            send_sem=cross_s.at[column * size + target],
            recv_sem=cross_r.at[column * size + origin],
            device_id={"mp": target},
            device_id_type=pl.DeviceIdType.MESH,
        )

    def cross(piece, slot, odd, start):
        target, column = piece // across, piece % across

        @pl.when(target != me)
        def _():
            copy = cross_copy(slot, column, target, me)
            copy.start() if start else copy.wait_send()

        if start:

            @pl.when(target == me)
            def _():
                own = pieces.span(pieces.start_of(odd, bits), bits)
                cross_in[column * size + me] = work[slot, own, :]

    def tail_copy(column):
        return pltpu.make_async_copy(
            cross_work.at[column],
            gout_sum.at[0, :, column * columns : (column + 1) * columns],
            tail_store.at[column],
        )

    def tail_spread(column, level, arriving):
        return pieces.spread_copy(cross_work, (tail_s, tail_r), column, column % 2, level, arriving)

    def tail_step(tick):
        base = counts[0] + bits * gap + gap
        for column in range(across):

            @pl.when(tick == base + column)
            def _():
                for offset in range(1, size):
                    cross_copy(0, column, me, lax.rem(me + offset, size)).wait_recv()
                own = pieces.span(pieces.start_of(column % 2, bits), bits)
                cross_work[column, own, :] = (
                    sum(cross_in[column * size + index] for index in range(1, size)) + cross_in[column * size]
                )
                tail_spread(column, bits - 1, False).start()

            for level in reversed(range(bits)):

                @pl.when(tick == base + column + (bits - level) * gap)
                def _():
                    tail_spread(column, level, True).wait_recv()
                    if level:
                        tail_spread(column, level - 1, False).start()
                    else:
                        tail_copy(column).start()

    def small_across(offset, arriving):
        origin = lax.rem(me - offset + size, size) if arriving else me
        return pltpu.make_async_remote_copy(
            src_ref=small_cross.at[me],
            dst_ref=small_cross.at[origin],
            send_sem=mix_s.at[offset],
            recv_sem=mix_r.at[offset],
            device_id={"mp": lax.rem(me + offset, size)},
            device_id_type=pl.DeviceIdType.MESH,
        )

    def small_within(level):
        step = 1 << level
        return pltpu.make_async_remote_copy(
            src_ref=small_held.at[level],
            dst_ref=small_in.at[level],
            send_sem=small_s.at[level],
            recv_sem=small_r.at[level],
            device_id={"dp": pieces.mine + step - 2 * step * ((pieces.mine // step) % 2)},
            device_id_type=pl.DeviceIdType.MESH,
        )

    def small_step(tick):
        @pl.when(tick == 0)
        def _():
            small_cross[me] = small_ref[...]
            for offset in range(1, size):
                small_across(offset, False).start()

        @pl.when(tick == 2)
        def _():
            value = small_ref[...]
            shared = lax.broadcasted_iota(jnp.int32, value.shape, 0) < 2
            for offset in range(1, size):
                small_across(offset, True).wait_recv()
                origin = lax.rem(me - offset + size, size)
                value = value + jnp.where(shared, small_cross[origin], 0.0)
            small_held[0] = value
            small_within(0).start()

        for level in range(bits):

            @pl.when(tick == 4 + 2 * level)
            def _():
                small_within(level).wait_recv()
                value = small_held[level] + small_in[level]
                if level + 1 < bits:
                    small_held[level + 1] = value
                    small_within(level + 1).start()
                else:
                    small_sum[...] = value

    def settle_seg(chunk):
        slot = chunk * size + me
        line.scatter_sum(chunk, gunit_ref, seg_scatter, total)
        rows = seg_ref[slot].astype(f32)
        scale = row_scale(rows)
        normed = rows * scale
        weighted = total[...] * gain_ref[...]
        grad = gres_ref[chunk] + scale * (
            weighted - normed * jnp.mean(weighted * normed, axis=-1, keepdims=True)
        )
        low = grad.astype(bf16)
        gseg_ref[slot] = low
        whole_seg[slot] = low.astype(f32)
        line.gather_start(chunk, whole_seg, seg_gather)

    def settle_out(chunk):
        slot = chunk * size + me
        line.scatter_sum(chunk, branch_ref, out_scatter, total)
        low = (res_ref[chunk] + total[...]).astype(bf16)
        result_ref[slot] = low
        whole_out[slot] = low.astype(f32)
        line.gather_start(chunk, whole_out, out_gather)

    def seg_landed(slot):
        gseg_ref[slot] = whole_seg[slot].astype(bf16)

    def out_landed(slot):
        result_ref[slot] = whole_out[slot].astype(bf16)

    settle_at = hop * line.reach
    seg_lag, out_lag = max(-lag, 0), max(lag, 0)

    def step(tick, _):
        flows = (
            (seg_lag, gunit_ref, seg_scatter, settle_seg, whole_seg, seg_gather, seg_landed),
            (out_lag, branch_ref, out_scatter, settle_out, whole_out, out_gather, out_landed),
        )
        for late, part, scatter, settle, whole, gather, landed in flows:
            line.scatter_step(tick - late, part, scatter)
            chunk, due = line.chunk_at(tick - late - settle_at)

            @pl.when(due)
            def _():
                settle(chunk)

        for late, part, scatter, settle, whole, gather, landed in flows:
            line.gather_step(tick - late - settle_at, whole, gather, landed)
        small_step(tick)

        def piece_step(beat, _):
            pieces.step(beat, cross)
            tail_step(beat)
            return 0

        lax.fori_loop(beats(tick), beats(tick + 1), piece_step, 0)
        return 0

    line_ticks = line.reach * (chunks - 1) + 2 * settle_at + 1 + abs(lag)

    def beats(tick):
        return jnp.minimum((tick * pieces.beats + line_ticks - 3) // (line_ticks - 2), pieces.beats)

    lax.fori_loop(0, line_ticks, step, 0)

    def drain(chunk, _):
        line.scatter_drain(chunk, gunit_ref, seg_scatter)
        line.scatter_drain(chunk, branch_ref, out_scatter)
        line.gather_drain(chunk, whole_seg, seg_gather)
        line.gather_drain(chunk, whole_out, out_gather)
        return 0

    lax.fori_loop(0, chunks, drain, 0)
    for column in range(across):
        for level in range(bits):
            tail_spread(column, level, False).wait_send()
        tail_copy(column).wait()
    for offset in range(1, size):
        small_across(offset, False).wait_send()
    for level in range(bits):
        small_within(level).wait_send()


def close(grad_unit, branch, seg_rows, grad_residual, residual, gain, grads, small, size, group, chunks):
    rows, width = seg_rows.shape
    piece = rows // (chunks * size)
    vmem = pl.BlockSpec(memory_space=pltpu.VMEM)
    whole = (chunks * size, piece, width)
    piece_rows, columns, gap = max(256, 8 * group), width // 4, 2
    bits = group.bit_length() - 1
    slots = 2 * bits * gap + 2
    views = [grad.reshape(-1, piece_rows, grad.shape[1]) for grad in grads]
    counts = tuple(view.shape[0] * (view.shape[2] // columns) for view in views)
    anywhere = pl.BlockSpec(memory_space=pl.ANY)
    dma = pltpu.SemaphoreType.DMA
    sums = [jax.ShapeDtypeStruct(view.shape, f32) for view in views]
    sums[0] = jax.ShapeDtypeStruct((1, piece_rows, width), f32)
    return pl.pallas_call(
        functools.partial(close_kernel, size, group, chunks, 2, counts, gap, 3),
        in_specs=[vmem] * 6 + [anywhere] * len(views) + [vmem],
        out_specs=[vmem] * 2 + [anywhere] * len(views) + [vmem],
        out_shape=[jax.ShapeDtypeStruct(whole, bf16)] * 2 + sums + [jax.ShapeDtypeStruct(small.shape, f32)],
        scratch_shapes=[pltpu.VMEM(whole, f32)] * 6
        + [
            pltpu.VMEM((piece, width), f32),
            pltpu.VMEM((slots, piece_rows, columns), f32),
            pltpu.VMEM((slots, piece_rows, columns), f32),
            pltpu.VMEM((slots, piece_rows, columns), f32),
            pltpu.VMEM((width // columns * size, piece_rows // group, columns), f32),
            pltpu.VMEM((width // columns, piece_rows, columns), f32),
            pltpu.VMEM((size, *small.shape), f32),
            pltpu.VMEM((bits, *small.shape), f32),
            pltpu.VMEM((bits, *small.shape), f32),
        ]
        + [dma((chunks * size,))] * 16
        + [dma((slots * bits,))] * 4
        + [dma((slots,))] * 2
        + [dma((width // columns * size,))] * 2
        + [dma((width // columns * bits,))] * 2
        + [dma((width // columns,))]
        + [dma((size,))] * 2
        + [dma((bits,))] * 2,
        compiler_params=pltpu.CompilerParams(
            collective_id=1, has_side_effects=True, vmem_limit_bytes=63 << 20
        ),
        cost_estimate=pl.CostEstimate(flops=10**11, bytes_accessed=10**9, transcendentals=0),
        name="close",
    )(
        grad_unit.reshape(whole),
        branch,
        seg_rows.reshape(whole),
        grad_residual,
        residual,
        gain[None, :],
        *views,
        small,
    )


def body(
    inputs,
    memory,
    compressed_memory,
    memory_fill,
    compressed_fill,
    first_gain,
    query_weight,
    key_weight,
    value_weight,
    relative_bias,
    output_weight,
    second_gain,
    up_weight,
    down_weight,
    compress_weight,
    grad_output,
    grad_compressed,
    *,
    mp_size,
    dp_size,
):
    streams, seg_len, width = inputs.shape
    mem_len = memory.shape[1]
    packed_len = compressed_memory.shape[1]
    local = query_weight.shape[1]
    rows = streams * seg_len
    unit, q, k, v, mixed, log_total, packed_new, grad_pack, begun = attend(
        inputs,
        memory,
        compressed_memory,
        memory_fill,
        compressed_fill,
        first_gain,
        query_weight,
        key_weight,
        value_weight,
        relative_bias,
        compress_weight,
        grad_compressed,
        output_weight,
        mp_size,
        dp_size,
    )
    seg_rows = inputs.reshape(rows, width)
    grad_mixed, grad_residual, residual, branch, grad_down, grad_up, grad_out_full, grad_second = feed(
        mixed.reshape(rows, local),
        seg_rows,
        grad_output.reshape(rows, width),
        up_weight,
        down_weight,
        begun,
        second_gain,
        mp_size,
        dp_size,
        chunk_count,
    )
    grad_mixed = grad_mixed.reshape(streams, seg_len, local)
    grad_unit, gq, gk, gv, small = attend_back(
        unit,
        q,
        k,
        v,
        log_total,
        grad_mixed,
        memory_fill,
        compressed_fill,
        query_weight,
        key_weight,
        value_weight,
        relative_bias,
        first_gain,
        grad_second,
        mem_len,
        packed_len,
    )
    result, grad_seg, grad_out_w, grad_up, grad_down, gq, gk, gv, grad_pack, small = close(
        grad_unit,
        branch,
        seg_rows,
        grad_residual,
        residual,
        first_gain,
        (grad_out_full, grad_up, grad_down, gq, gk, gv, grad_pack),
        small,
        mp_size,
        dp_size,
        chunk_count,
    )
    grad_first, grad_second = small[0], small[1]
    grad_relative = small[2, : relative_bias.size].reshape(relative_bias.shape)
    result = result.reshape(inputs.shape)
    grad_seg = grad_seg.reshape(inputs.shape)
    grad_query_w = gq.reshape(local, width).T
    grad_key_w = gk.reshape(local, width).T
    grad_value_w = gv.reshape(local, width).T
    grad_out_w = grad_out_w.reshape(local, width)
    grad_compress_w = grad_pack.reshape(-1, 2 * width).T
    grad_up = grad_up.reshape(up_weight.shape)
    grad_down = grad_down.reshape(down_weight.shape)
    return (
        result,
        packed_new,
        grad_seg,
        grad_first,
        grad_query_w,
        grad_key_w,
        grad_value_w,
        grad_relative,
        grad_out_w,
        grad_second,
        grad_up,
        grad_down,
        grad_compress_w,
    )


def solution(mesh):
    in_specs = (
        P("dp", None, None),
        P("dp", None, None),
        P("dp", None, None),
        P("dp"),
        P("dp"),
        P(),
        P(None, "mp"),
        P(None, "mp"),
        P(None, "mp"),
        P("mp", None),
        P("mp", None),
        P(),
        P(None, "mp"),
        P("mp", None),
        P(None, "mp"),
        P("dp", None, None),
        P("dp", None, "mp"),
    )
    out_specs = (
        P("dp", None, None),
        P("dp", None, "mp"),
        P("dp", None, None),
        P(),
        P(None, "mp"),
        P(None, "mp"),
        P(None, "mp"),
        P("mp", None),
        P("mp", None),
        P(),
        P(None, "mp"),
        P("mp", None),
        P(None, "mp"),
    )
    return jax.shard_map(
        functools.partial(body, mp_size=mesh.shape["mp"], dp_size=mesh.shape["dp"]),
        mesh=mesh,
        in_specs=in_specs,
        out_specs=out_specs,
        check_vma=False,
    )
```

```python
import functools
import math

import jax
import jax.numpy as jnp
from jax import lax
from jax.experimental import pallas as pl
from jax.experimental.pallas import tpu as pltpu
from jax.sharding import PartitionSpec as P

reach_marks = (1, 2, 3, 4, 5, 6, 7, 8, 12, 16, 24, 32, 48, 64, 96, 128, 192, 256, 384, 512, 768, 1024)
epsilon = 1e-06
masked_score = -1e30
block = 128
query_block = 256
chunk_count = 8
early_chunks = 2
f32 = jnp.float32
bf16 = jnp.bfloat16


def mm(left, right):
    return jnp.dot(left, right, preferred_element_type=f32)


def mm_t0(left, right):
    return lax.dot_general(left, right, (((0,), (0,)), ((), ())), preferred_element_type=f32)


def mm_t1(left, right):
    return lax.dot_general(left, right, (((1,), (1,)), ((), ())), preferred_element_type=f32)


def row_scale(source):
    return lax.rsqrt(jnp.mean(source * source, axis=-1, keepdims=True) + epsilon)


def diagonal_count(seg_len, kept_count):
    return (seg_len + kept_count) // block + 1


def diagonal_of(seg_len, kept_count, column):
    return (seg_len + kept_count) // block - 1 - column


def strip_start(seg_len, sub_block):
    return (seg_len // block - 1 - sub_block) * block


def bias_block(bias_ref, head, diagonal, transposed):
    rows = lax.broadcasted_iota(jnp.int32, (block, block), 0)
    cols = lax.broadcasted_iota(jnp.int32, (block, block), 1)
    distance = diagonal * block + ((cols - rows) if transposed else (rows - cols))
    lowest, highest = diagonal * block - block + 1, diagonal * block + block - 1
    base = jnp.float32(0.0)
    for position, mark_value in enumerate(reach_marks):
        if mark_value <= lowest:
            base = base + bias_ref[head, position]
    value = jnp.full((block, block), base, f32)
    for position, mark_value in enumerate(reach_marks):
        if lowest < mark_value <= highest:
            value = value + jnp.where(distance >= mark_value, bias_ref[head, position], 0.0)
    if lowest < 0:
        value = jnp.where(distance >= 0, value, masked_score)
    return value


def live_mask(shape, axis, packed_len, mem_len, packed_count, memory_count):
    slot = lax.broadcasted_iota(jnp.int32, shape, axis)
    dead_packed = (slot < packed_len) & (slot < packed_len - packed_count)
    dead_memory = (slot >= packed_len) & (slot < packed_len + mem_len - memory_count)
    return jnp.where(dead_packed | dead_memory, masked_score, 0.0).astype(f32)


def greet(peers):
    barrier = pltpu.get_barrier_semaphore()
    for peer in peers:
        pl.semaphore_signal(barrier, inc=1, device_id=peer, device_id_type=pl.DeviceIdType.MESH)
    pl.semaphore_wait(barrier, len(peers))


class Spread:
    def __init__(self, size, group, buffer, sems):
        self.me, self.mine = lax.axis_index("mp"), lax.axis_index("dp")
        self.size, self.group, self.buffer = size, group, buffer
        self.bits = group.bit_length() - 1
        self.across_s, self.across_r, self.within_s, self.within_r = sems
        order = list(reversed(range(self.bits)))
        self.orders = (order, order[1::-1] + order[2:])
        self.spots = []
        for order in self.orders:
            spot = jnp.int32(0)
            for level, bit in enumerate(order):
                spot = spot + ((self.mine // (1 << bit)) % 2) * (1 << level)
            self.spots.append(spot)

    def place_of(self, half, member):
        return sum(((member >> bit) & 1) << level for level, bit in enumerate(self.orders[half]))

    def others(self, offset):
        return {"mp": lax.rem(self.me + offset, self.size)}

    def partner(self, half, level):
        step = 1 << self.orders[half][level]
        return {"dp": self.mine + step - 2 * step * ((self.mine // step) % 2)}

    def across(self, half, offset, arriving):
        origin = lax.rem(self.me - offset + self.size, self.size) if arriving else self.me
        return pltpu.make_async_remote_copy(
            src_ref=self.buffer.at[half, self.spots[half], origin],
            dst_ref=self.buffer.at[half, self.spots[half], origin],
            send_sem=self.across_s.at[half * self.size + offset],
            recv_sem=self.across_r.at[half * self.size + offset],
            device_id=self.others(offset),
            device_id_type=pl.DeviceIdType.MESH,
        )

    def block(self, half, level, other):
        count = 1 << level
        start = (self.spots[half] // count) * count
        if other:
            start = start + count - 2 * count * ((self.spots[half] // count) % 2)
        return pl.ds(start, count)

    def within(self, half, level, arriving):
        span = self.block(half, level, arriving)
        return pltpu.make_async_remote_copy(
            src_ref=self.buffer.at[half, span],
            dst_ref=self.buffer.at[half, span],
            send_sem=self.within_s.at[half * self.bits + level],
            recv_sem=self.within_r.at[half * self.bits + level],
            device_id=self.partner(half, level),
            device_id_type=pl.DeviceIdType.MESH,
        )

    def start_level(self, level):
        for half in range(2):
            if level:
                self.within(half, level - 1, True).wait_recv()
            self.within(half, level, False).start()


def attend_kernel(
    sizes,
    size,
    group,
    memory_fill,
    packed_fill,
    bias_ref,
    seg_ref,
    memory_ref,
    packed_ref,
    gain_ref,
    wq_ref,
    wk_ref,
    wv_ref,
    wc_ref,
    gcomp_ref,
    wo_ref,
    unit_ref,
    q_ref,
    k_ref,
    v_ref,
    mixed_ref,
    log_ref,
    packed_new_ref,
    gpack_ref,
    begun_ref,
    strip,
    live,
    mem_rows,
    spread_in,
    *sems,
):
    seg_len, mem_len, packed_len, heads, head_dim = sizes
    kept = mem_len + packed_len
    keys = kept + seg_len
    stream = pl.program_id(0)
    scale = 1.0 / math.sqrt(head_dim)
    gain = gain_ref[...]
    spread = Spread(size, group, spread_in, sems[:4])
    piece, columns = spread_in.shape[3:]
    width = gain.shape[1]

    @pl.when(stream == 0)
    def _():
        greet(
            [spread.others(offset) for offset in range(1, size)]
            + [spread.partner(half, 0) for half in range(2)]
        )
        rows = pl.ds(pl.multiple_of(spread.mine * piece, piece), piece)
        for half in range(2):
            lanes = slice(half * columns, (half + 1) * columns)
            spread_in[half, spread.spots[half], spread.me] = wo_ref[rows, lanes].astype(f32)
            for offset in range(1, size):
                spread.across(half, offset, False).start()
        gpack_ref[...] = jnp.zeros_like(gpack_ref)

    slot = lax.broadcasted_iota(jnp.int32, mem_rows.shape[1:], 0)
    keep = slot >= mem_len - memory_fill[stream]
    count = packed_new_ref.shape[1]
    for column in range(mem_rows.shape[0]):
        lanes = slice(column * block, (column + 1) * block)
        mem_rows[column] = jnp.where(keep, memory_ref[0, :, lanes].astype(f32), 0.0)
    packed_new = jnp.zeros(packed_new_ref.shape[1:], f32)
    for parity in range(2):
        rows = jnp.concatenate(
            [mem_rows[column, pl.ds(parity, count, stride=2), :] for column in range(mem_rows.shape[0])], axis=1
        ).astype(bf16)
        lanes = slice(parity * width, (parity + 1) * width)
        packed_new = packed_new + mm(rows, wc_ref[lanes, :])
        gpack_ref[:, lanes] += mm_t0(gcomp_ref[0], rows)
    packed_new_ref[0] = packed_new.astype(bf16)
    start = 0
    for part_ref, length in ((packed_ref, packed_len), (memory_ref, mem_len), (seg_ref, seg_len)):
        rows = part_ref[0].astype(f32)
        unit = (rows * row_scale(rows) * gain).astype(bf16)
        unit_ref[0, start : start + length, :] = unit
        k_ref[0, start : start + length, :] = mm(unit, wk_ref[...]).astype(bf16)
        v_ref[0, start : start + length, :] = mm(unit, wv_ref[...]).astype(bf16)
        if start == kept:
            q_ref[0] = mm(unit, wq_ref[...]).astype(bf16)
        start += length
    live[...] = live_mask((8, kept), 1, packed_len, mem_len, packed_fill[stream], memory_fill[stream])
    for head in range(heads):
        lanes = slice(head * head_dim, (head + 1) * head_dim)
        for column in range(diagonal_count(seg_len, kept)):
            strip[:, column * block : (column + 1) * block] = bias_block(
                bias_ref, head, diagonal_of(seg_len, kept, column), False
            )
        for index in range(seg_len // query_block):
            reach = kept + (index + 1) * query_block
            rows = slice(index * query_block, (index + 1) * query_block)
            score = mm_t1(q_ref[0, rows, lanes], k_ref[0, :reach, lanes]) * scale
            parts = []
            for sub in range(query_block // block):
                first = strip_start(seg_len, index * (query_block // block) + sub)
                parts.append(strip[:, first : first + reach])
            score = score + jnp.concatenate(parts, axis=0)
            score = jnp.concatenate([score[:, :kept] + live[0:1, :], score[:, kept:]], axis=1)
            top = jnp.max(score, axis=-1, keepdims=True)
            weight = jnp.exp(score - top)
            total = jnp.sum(weight, axis=-1, keepdims=True)
            log_total = jnp.broadcast_to(top + jnp.log(total), (query_block, block))
            log_ref[0, head, :, rows] = log_total.T[0:1, :]
            mixed = mm(weight.astype(bf16), v_ref[0, :reach, lanes]) * (1.0 / total)
            mixed_ref[0, rows, lanes] = mixed.astype(bf16)

    @pl.when(stream == 0)
    def _():
        for half in range(2):
            for offset in range(1, size):
                spread.across(half, offset, True).wait_recv()
        spread.start_level(0)

    @pl.when(stream == pl.num_programs(0) - 1)
    def _():
        copies = []
        for half in range(2):
            spread.within(half, 0, True).wait_recv()
            pair = spread_in.at[half, pl.ds((spread.spots[half] // 2) * 2, 2)]
            copies.append(pltpu.make_async_copy(pair, begun_ref.at[half], sems[4].at[half]))
            copies[-1].start()
        for half in range(2):
            for offset in range(1, size):
                spread.across(half, offset, False).wait_send()
            spread.within(half, 0, False).wait_send()
            copies[half].wait()


def attend(
    inputs, memory, packed, memory_fill, packed_fill, gain, wq, wk, wv, bias, wc, gcomp, wo, size, group
):
    streams, seg_len, width = inputs.shape
    mem_len, packed_len = memory.shape[1], packed.shape[1]
    heads = bias.shape[0]
    local = wq.shape[1]
    keys = seg_len + mem_len + packed_len
    sizes = (seg_len, mem_len, packed_len, heads, local // heads)
    smem = pl.BlockSpec(memory_space=pltpu.SMEM)
    compress_count = gcomp.shape[1]
    piece = wo.shape[0] // group
    bits = group.bit_length() - 1

    def rows_of(count, columns):
        return pl.BlockSpec((1, count, columns), lambda s: (s, 0, 0))

    def whole(shape):
        return pl.BlockSpec(shape, lambda s: (0,) * len(shape))

    return pl.pallas_call(
        functools.partial(attend_kernel, sizes, size, group),
        grid=(streams,),
        in_specs=[
            smem,
            smem,
            smem,
            rows_of(seg_len, width),
            rows_of(mem_len, width),
            rows_of(packed_len, width),
            whole((1, width)),
            whole(wq.shape),
            whole(wk.shape),
            whole(wv.shape),
            whole(wc.shape),
            rows_of(compress_count, local),
            whole(wo.shape),
        ],
        out_specs=[
            rows_of(keys, width),
            rows_of(seg_len, local),
            rows_of(keys, local),
            rows_of(keys, local),
            rows_of(seg_len, local),
            pl.BlockSpec((1, heads, 1, seg_len), lambda s: (s, 0, 0, 0)),
            rows_of(compress_count, local),
            whole((local, 2 * width)),
            pl.BlockSpec(memory_space=pl.ANY),
        ],
        out_shape=[
            jax.ShapeDtypeStruct((streams, keys, width), bf16),
            jax.ShapeDtypeStruct((streams, seg_len, local), bf16),
            jax.ShapeDtypeStruct((streams, keys, local), bf16),
            jax.ShapeDtypeStruct((streams, keys, local), bf16),
            jax.ShapeDtypeStruct((streams, seg_len, local), bf16),
            jax.ShapeDtypeStruct((streams, heads, 1, seg_len), f32),
            jax.ShapeDtypeStruct((streams, compress_count, local), bf16),
            jax.ShapeDtypeStruct((local, 2 * width), f32),
            jax.ShapeDtypeStruct((2, 2, size, piece, width // 2), f32),
        ],
        scratch_shapes=[
            pltpu.VMEM((block, diagonal_count(seg_len, mem_len + packed_len) * block), f32),
            pltpu.VMEM((8, mem_len + packed_len), f32),
            pltpu.VMEM((width // block, mem_len, block), f32),
            pltpu.VMEM((2, group, size, piece, width // 2), f32),
            pltpu.SemaphoreType.DMA((2 * size,)),
            pltpu.SemaphoreType.DMA((2 * size,)),
            pltpu.SemaphoreType.DMA((2 * bits,)),
            pltpu.SemaphoreType.DMA((2 * bits,)),
            pltpu.SemaphoreType.DMA((2,)),
        ],
        compiler_params=pltpu.CompilerParams(
            collective_id=2, has_side_effects=True, vmem_limit_bytes=60 << 20
        ),
        cost_estimate=pl.CostEstimate(
            flops=streams * (2 * keys * width * local * 3 + 4 * seg_len * keys * local),
            bytes_accessed=streams * keys * (width * 4 + local * 6),
            transcendentals=streams * heads * seg_len * keys,
        ),
        name="attend",
    )(memory_fill, packed_fill, bias, inputs, memory, packed, gain[None, :], wq, wk, wv, wc, gcomp, wo)


class Line:
    def __init__(self, size, chunks, hop):
        self.me = lax.axis_index("mp")
        self.size, self.chunks, self.hop = size, chunks, hop
        self.reach = size - 1

    def place(self, right):
        return self.me if right else self.reach - self.me

    def peer(self, right):
        return {"mp": self.me + 1 if right else self.me - 1}

    def copy(self, source, target, sems, slot, right):
        return pltpu.make_async_remote_copy(
            src_ref=source.at[slot],
            dst_ref=target.at[slot],
            send_sem=sems[0],
            recv_sem=sems[1].at[slot],
            device_id=self.peer(right),
            device_id_type=pl.DeviceIdType.MESH,
        )

    def chunk_at(self, tick):
        positive = jnp.maximum(tick, 0)
        chunk = positive // self.reach
        return chunk, (tick >= 0) & (positive == chunk * self.reach) & (chunk < self.chunks)

    def scatter_step(self, tick, part, lanes, first=0):
        for right, held, sems in lanes:
            place = self.place(right)
            late = tick - self.hop * place
            positive = jnp.maximum(late, 0)
            chunk = positive // self.reach
            goal = self.reach - (positive - self.reach * chunk)
            active = (late >= 0) & (chunk >= first) & (chunk < self.chunks) & (goal > place)
            slot = chunk * self.size + (goal if right else self.reach - goal)

            @pl.when(active & (place == 0))
            def _():
                self.copy(part, held, sems, slot, right).start()

            @pl.when(active & (place > 0))
            def _():
                self.copy(held, held, sems, slot, right).wait_recv()
                held[slot] = held[slot] + part[slot]
                self.copy(held, held, sems, slot, right).start()

    def scatter_sum(self, chunk, part, lanes, total):
        slot = chunk * self.size + self.me
        total[...] = part[slot]
        for right, held, sems in lanes:

            @pl.when(self.place(right) > 0)
            def _():
                self.copy(held, held, sems, slot, right).wait_recv()
                total[...] = total[...] + held[slot]

    def gather_start(self, chunk, whole, lanes):
        slot = chunk * self.size + self.me
        for right, sems in lanes:

            @pl.when(self.place(right) < self.reach)
            def _():
                self.copy(whole, whole, sems, slot, right).start()

    def gather_step(self, tick, whole, lanes, landed=None):
        for right, sems in lanes:
            place = self.place(right)
            for distance in range(1, self.size):
                chunk, due = self.chunk_at(tick - self.hop * distance)

                @pl.when(due & (distance <= place))
                def _():
                    slot = chunk * self.size + (self.me - distance if right else self.me + distance)
                    self.copy(whole, whole, sems, slot, right).wait_recv()

                    @pl.when(place < self.reach)
                    def _():
                        self.copy(whole, whole, sems, slot, right).start()

                    if landed is not None:
                        landed(slot)

    def sent(self, buffer, send_sem, count, right):
        some = buffer.at[pl.ds(0, count)]
        return pltpu.make_async_remote_copy(
            src_ref=some,
            dst_ref=some,
            send_sem=send_sem,
            recv_sem=send_sem,
            device_id=self.peer(right),
            device_id_type=pl.DeviceIdType.MESH,
        )

    def scatter_drain(self, part, lanes, first=0):
        for right, held, sems in lanes:
            for place in range(self.reach):

                @pl.when(self.place(right) == place)
                def _():
                    self.sent(part, sems[0], (self.reach - place) * (self.chunks - first), right).wait_send()

    def gather_drain(self, whole, lanes):
        for right, sems in lanes:
            for place in range(self.reach):

                @pl.when(self.place(right) == place)
                def _():
                    self.sent(whole, sems[0], (place + 1) * self.chunks, right).wait_send()


def meet(line):
    barrier = pltpu.get_barrier_semaphore()
    for right in (True, False):

        @pl.when(line.place(right) < line.reach)
        def _():
            pl.semaphore_signal(
                barrier, inc=1, device_id=line.peer(right), device_id_type=pl.DeviceIdType.MESH
            )

    inner = (line.me > 0) & (line.me < line.reach)

    @pl.when(inner)
    def _():
        pl.semaphore_wait(barrier, 2)

    @pl.when(jnp.logical_not(inner))
    def _():
        pl.semaphore_wait(barrier, 1)


def attend_back_kernel(
    sizes,
    size,
    early,
    hop,
    memory_fill,
    packed_fill,
    bias_ref,
    unit_ref,
    q_ref,
    k_ref,
    v_ref,
    log_ref,
    gm_ref,
    wq_ref,
    wk_ref,
    wv_ref,
    gain_ref,
    gsecond_ref,
    branch_hbm,
    res_hbm,
    gunit_ref,
    gq_ref,
    gk_ref,
    gv_ref,
    small_ref,
    early_ref,
    strip,
    live,
    dk_sum,
    dv_sum,
    dq_low,
    dk_low,
    dv_low,
    strip_sum,
    branch_ref,
    res_ref,
    held_right,
    held_left,
    total_ref,
    load_sem,
    line_s,
    right_r,
    left_r,
):
    seg_len, mem_len, packed_len, heads, head_dim = sizes
    kept = mem_len + packed_len
    keys = kept + seg_len
    stream = pl.program_id(0)
    scale = 1.0 / math.sqrt(head_dim)

    line = Line(size, early, hop)
    lanes_out = ((True, held_right, (line_s.at[0], right_r)), (False, held_left, (line_s.at[1], left_r)))
    loads = (
        pltpu.make_async_copy(branch_hbm.at[pl.ds(0, early * size)], branch_ref, load_sem.at[0]),
        pltpu.make_async_copy(res_hbm.at[pl.ds(0, early)], res_ref, load_sem.at[1]),
    )
    ticks = line.reach * (early - 1) + hop * line.reach + 1
    spans = heads * (seg_len // query_block)

    def line_step(tick, _):
        line.scatter_step(tick, branch_ref, lanes_out)
        chunk, due = line.chunk_at(tick - hop * line.reach)

        @pl.when(due)
        def _():
            line.scatter_sum(chunk, branch_ref, lanes_out, total_ref)
            early_ref[chunk] = (res_ref[chunk] + total_ref[...]).astype(bf16).astype(f32)

        return 0

    def line_span(index):
        unit = stream * spans + index
        every = spans * pl.num_programs(0)
        lax.fori_loop((unit * ticks) // every, ((unit + 1) * ticks) // every, line_step, 0)

    @pl.when(stream == 0)
    def _():
        for load in loads:
            load.start()
        meet(line)
        for load in loads:
            load.wait()
        strip_sum[...] = jnp.zeros_like(strip_sum)
        gq_ref[...] = jnp.zeros_like(gq_ref)
        gk_ref[...] = jnp.zeros_like(gk_ref)
        gv_ref[...] = jnp.zeros_like(gv_ref)

    live[...] = live_mask((kept, block), 0, packed_len, mem_len, packed_fill[stream], memory_fill[stream])
    subs = query_block // block
    for head in range(heads):
        lanes = slice(head * head_dim, (head + 1) * head_dim)
        for column in range(diagonal_count(seg_len, kept)):
            strip[column * block : (column + 1) * block, :] = bias_block(
                bias_ref, head, diagonal_of(seg_len, kept, column), True
            )
        for index in range(seg_len // query_block):
            line_span(head * (seg_len // query_block) + index)
            reach = kept + (index + 1) * query_block
            rows = slice(index * query_block, (index + 1) * query_block)
            queries = q_ref[0, rows, lanes]
            grads = gm_ref[0, rows, lanes]
            key_rows = k_ref[0, :reach, lanes]
            score = mm_t1(key_rows, queries) * scale
            firsts = [strip_start(seg_len, index * subs + sub) for sub in range(subs)]
            score = score + jnp.concatenate([strip[first : first + reach, :] for first in firsts], axis=1)
            live_wide = jnp.concatenate([live[...]] * subs, axis=1)
            score = jnp.concatenate([score[:kept] + live_wide, score[kept:]], axis=0)
            prob = jnp.exp(score - log_ref[0, head, :, rows])
            grad_prob = mm_t1(v_ref[0, :reach, lanes], grads)
            delta = jnp.sum(prob * grad_prob, axis=0, keepdims=True)
            grad_score = (prob * (grad_prob - delta)).astype(bf16)
            dk_part = mm(grad_score, queries)
            dv_part = mm(prob.astype(bf16), grads)
            if index == seg_len // query_block - 1:
                earlier = kept + index * query_block
                if index:
                    dk_sum[:earlier] += dk_part[:earlier]
                    dv_sum[:earlier] += dv_part[:earlier]
                    dk_sum[earlier:] = dk_part[earlier:]
                    dv_sum[earlier:] = dv_part[earlier:]
                else:
                    dk_sum[...] = dk_part
                    dv_sum[...] = dv_part
            elif index:
                earlier = kept + index * query_block
                dk_sum[:earlier] += dk_part[:earlier]
                dv_sum[:earlier] += dv_part[:earlier]
                dk_sum[earlier:reach] = dk_part[earlier:]
                dv_sum[earlier:reach] = dv_part[earlier:]
            else:
                dk_sum[:reach] = dk_part
                dv_sum[:reach] = dv_part
            dq_low[rows, lanes] = (mm_t0(grad_score, key_rows) * scale).astype(bf16)
            for sub in range(subs):
                strip_sum[head, firsts[sub] : firsts[sub] + reach, :] += grad_score[
                    :, sub * block : (sub + 1) * block
                ].astype(f32)
        dk_low[:, lanes] = (dk_sum[...] * scale).astype(bf16)
        dv_low[:, lanes] = dv_sum[...].astype(bf16)
    gq_ref[...] += mm_t0(dq_low[...], unit_ref[0, kept:, :])
    gk_ref[...] += mm_t0(dk_low[...], unit_ref[0])
    gv_ref[...] += mm_t0(dv_low[...], unit_ref[0])
    gunit_ref[0] = (
        mm_t1(dq_low[...], wq_ref[...])
        + mm_t1(dk_low[kept:, :], wk_ref[...])
        + mm_t1(dv_low[kept:, :], wv_ref[...])
    )

    @pl.when(stream == pl.num_programs(0) - 1)
    def _():
        line.scatter_drain(branch_ref, lanes_out)
        rows = lax.broadcasted_iota(jnp.int32, (block, block), 0)
        cols = lax.broadcasted_iota(jnp.int32, (block, block), 1)
        width = gain_ref.shape[1]
        lane = lax.broadcasted_iota(jnp.int32, (1, width), 1)
        relative = jnp.zeros((1, width), f32)
        for head in range(heads):
            blocks = []
            for column in range(diagonal_count(seg_len, kept)):
                blocks.append(strip_sum[head, column * block : (column + 1) * block, :])
            for position, mark_value in enumerate(reach_marks):
                total = jnp.zeros((1, block), f32)
                for column, value in enumerate(blocks):
                    diagonal = diagonal_of(seg_len, kept, column)
                    lowest, highest = diagonal * block - block + 1, diagonal * block + block - 1
                    if mark_value <= lowest:
                        total = total + jnp.sum(value, axis=0, keepdims=True)
                    elif mark_value <= highest:
                        distance = diagonal * block + cols - rows
                        total = total + jnp.sum(
                            jnp.where(distance >= mark_value, value, 0.0), axis=0, keepdims=True
                        )
                total = jnp.sum(total, axis=1, keepdims=True)
                relative = jnp.where(lane == head * len(reach_marks) + position, total, relative)
        first = jnp.zeros((1, width), f32)
        for grad_ref, weight_ref in ((gq_ref, wq_ref), (gk_ref, wk_ref), (gv_ref, wv_ref)):
            turned = weight_ref[...].astype(f32).T
            first = first + jnp.sum(grad_ref[...] * turned, axis=0, keepdims=True)
        small_ref[...] = jnp.concatenate(
            [first / gain_ref[...], gsecond_ref[...], relative, jnp.zeros((5, width), f32)], axis=0
        )


def attend_back(
    unit, q, k, v, log_total, grad_mixed, memory_fill, packed_fill, wq, wk, wv, bias, gain, grad_second, mem_len, packed_len,
    branch, residual, size, early,
):
    streams, keys, width = unit.shape
    seg_len, local = q.shape[1:]
    heads = bias.shape[0]
    kept = mem_len + packed_len
    sizes = (seg_len, mem_len, packed_len, heads, local // heads)
    smem = pl.BlockSpec(memory_space=pltpu.SMEM)
    strip_len = diagonal_count(seg_len, kept) * block
    part = (early * size, *branch.shape[1:])

    def rows_of(count, columns):
        return pl.BlockSpec((1, count, columns), lambda s: (s, 0, 0))

    def whole(shape):
        return pl.BlockSpec(shape, lambda s: (0,) * len(shape))

    return pl.pallas_call(
        functools.partial(attend_back_kernel, sizes, size, early, 2),
        grid=(streams,),
        in_specs=[
            smem,
            smem,
            smem,
            rows_of(keys, width),
            rows_of(seg_len, local),
            rows_of(keys, local),
            rows_of(keys, local),
            pl.BlockSpec((1, heads, 1, seg_len), lambda s: (s, 0, 0, 0)),
            rows_of(seg_len, local),
            whole(wq.shape),
            whole(wk.shape),
            whole(wv.shape),
            whole((1, width)),
            whole((1, width)),
            pl.BlockSpec(memory_space=pl.ANY),
            pl.BlockSpec(memory_space=pl.ANY),
        ],
        out_specs=[
            rows_of(seg_len, width),
            whole((local, width)),
            whole((local, width)),
            whole((local, width)),
            whole((8, width)),
            whole((early, *residual.shape[1:])),
        ],
        out_shape=[
            jax.ShapeDtypeStruct((streams, seg_len, width), f32),
            jax.ShapeDtypeStruct((local, width), f32),
            jax.ShapeDtypeStruct((local, width), f32),
            jax.ShapeDtypeStruct((local, width), f32),
            jax.ShapeDtypeStruct((8, width), f32),
            jax.ShapeDtypeStruct((early, *residual.shape[1:]), f32),
        ],
        scratch_shapes=[
            pltpu.VMEM((strip_len, block), f32),
            pltpu.VMEM((kept, block), f32),
            pltpu.VMEM((keys, local // heads), f32),
            pltpu.VMEM((keys, local // heads), f32),
            pltpu.VMEM((seg_len, local), bf16),
            pltpu.VMEM((keys, local), bf16),
            pltpu.VMEM((keys, local), bf16),
            pltpu.VMEM((heads, strip_len, block), f32),
            pltpu.VMEM(part, f32),
            pltpu.VMEM((early, *part[1:]), f32),
            pltpu.VMEM(part, f32),
            pltpu.VMEM(part, f32),
            pltpu.VMEM(part[1:], f32),
            pltpu.SemaphoreType.DMA((2,)),
            pltpu.SemaphoreType.DMA((2,)),
            pltpu.SemaphoreType.DMA((early * size,)),
            pltpu.SemaphoreType.DMA((early * size,)),
        ],
        compiler_params=pltpu.CompilerParams(
            collective_id=3, has_side_effects=True, vmem_limit_bytes=60 << 20
        ),
        cost_estimate=pl.CostEstimate(
            flops=streams * (8 * keys * width * local + 10 * seg_len * keys * local),
            bytes_accessed=streams * keys * (width * 2 + local * 6),
            transcendentals=streams * heads * seg_len * keys,
        ),
        name="attend_back",
    )(
        memory_fill,
        packed_fill,
        bias,
        unit,
        q,
        k,
        v,
        log_total,
        grad_mixed,
        wq,
        wk,
        wv,
        gain[None, :],
        grad_second,
        branch,
        residual,
    )


def feed_kernel(
    size,
    group,
    chunks,
    hop,
    delay,
    beat,
    mixed_ref,
    seg_hbm,
    grad_hbm,
    up_hbm,
    down_hbm,
    begun_ref,
    gain_ref,
    gm_ref,
    gres_ref,
    res_ref,
    branch_hbm,
    gdown_hbm,
    gup_hbm,
    gout_hbm,
    gsecond_ref,
    seg_ref,
    grad_ref,
    up_ref,
    down_ref,
    branch_ref,
    gdown_ref,
    gup_ref,
    gout_ref,
    acted,
    graded,
    normed_low,
    heads_in,
    part,
    held_right,
    held_left,
    swap_out,
    swap_in,
    weights_in,
    weights,
    chunk_rows,
    total,
    own_mixed,
    own_grad,
    *sems,
):
    line = Line(size, chunks, hop)
    me = line.me
    (line_s, hr_r, hl_r, sr_r, sl_r, swap_sem, wd_s, wd_r, load_sem, save_sem, branch_sem) = sems
    gather_lanes = ((True, (line_s.at[0], hr_r)), (False, (line_s.at[1], hl_r)))
    scatter_lanes = ((True, held_right, (line_s.at[2], sr_r)), (False, held_left, (line_s.at[3], sl_r)))
    loads = [
        pltpu.make_async_copy(source, target, load_sem.at[index])
        for index, (source, target) in enumerate(
            ((seg_hbm, seg_ref), (grad_hbm, grad_ref), (up_hbm, up_ref), (down_hbm, down_ref))
        )
    ]
    for load in loads:
        load.start()
    spread = Spread(size, group, weights_in, (None, None, wd_s, wd_r))
    bits = spread.bits
    piece, columns = weights_in.shape[3:]
    width = weights.shape[1]
    rows = total.shape[0]
    local = mixed_ref.shape[-1]
    greet(
        [spread.others(offset) for offset in range(1, size)]
        + [spread.partner(half, level) for half in range(2) for level in range(1, bits)]
    )
    for half in range(2):
        weights_in[half, pl.ds((spread.spots[half] // 2) * 2, 2)] = begun_ref[half]
        spread.within(half, 1, False).start()

    def stage_heads(chunk, _):
        heads_in[chunk * size + me] = mixed_ref[chunk].astype(f32)
        return 0

    lax.fori_loop(0, chunks, stage_heads, 0)
    gsecond_ref[...] = jnp.zeros_like(gsecond_ref)
    gdown_ref[...] = jnp.zeros_like(gdown_ref)
    gup_ref[...] = jnp.zeros_like(gup_ref)

    def weight_step(tick):
        for level in range(2, bits):

            @pl.when(tick == beat + level - 2)
            def _():
                spread.start_level(level)

    def weight_finish():
        for half in range(2):
            spread.within(half, bits - 1, True).wait_recv()
            for index in range(size):
                pieces = [weights_in[half, spread.place_of(half, member), index] for member in range(group)]
                weights[index * group * piece : (index + 1) * group * piece, half * columns : (half + 1) * columns] = (
                    jnp.concatenate(pieces, axis=0).astype(bf16)
                )

    own = pl.ds(pl.multiple_of(me * rows, rows), rows)

    def feed_chunk(chunk):
        heads = [heads_in[chunk * size + index].astype(bf16) for index in range(size)]
        for index in range(size):
            own_mixed[chunk, :, index * local : (index + 1) * local] = heads_in[
                chunk * size + index, own, :
            ].astype(bf16)
        residual = seg_ref[chunk].astype(f32) + mm(jnp.concatenate(heads, axis=1), weights[...])
        chunk_rows[...] = residual
        res_ref[chunk] = chunk_rows[own, :]
        ffn_input = (residual * row_scale(residual) * gain_ref[...]).astype(bf16)
        pre_act = mm(ffn_input, up_ref[...])
        inner = math.sqrt(2.0 / math.pi)
        squared = pre_act * pre_act
        tanh = jnp.tanh(inner * (pre_act + 0.044715 * pre_act * squared))
        activated = (0.5 * pre_act * (1.0 + tanh)).astype(bf16)
        slope = 0.5 * (1.0 + tanh) + 0.5 * pre_act * (1.0 - tanh * tanh) * (
            inner * (1.0 + 3.0 * 0.044715 * squared)
        )
        grads = grad_ref[chunk]
        grad_pre = (slope * mm_t1(grads, down_ref[...])).astype(bf16)
        first = pl.ds(chunk * size, size)
        part[first] = mm_t1(grad_pre, up_ref[...]).reshape(size, rows, width)
        acted[...] = activated
        graded[...] = grad_pre
        normed_low[...] = ffn_input

    def save_branch(chunk):
        here = pl.ds(chunk * size, size)
        return pltpu.make_async_copy(branch_ref.at[here], branch_hbm.at[here], branch_sem.at[chunk])

    def feed_branch(chunk):
        branch_ref[pl.ds(chunk * size, size)] = mm(acted[...], down_ref[...]).reshape(size, rows, width)
        save_branch(chunk).start()
        gdown_ref[...] += mm_t0(acted[...], grad_ref[chunk])

    def feed_grads(chunk):
        gup_ref[...] += mm_t0(normed_low[...], graded[...])

    saves = [
        pltpu.make_async_copy(source, target, save_sem.at[index])
        for index, (source, target) in enumerate(
            ((gdown_ref, gdown_hbm), (gup_ref, gup_hbm), (gout_ref, gout_hbm))
        )
    ]

    def swap(chunk, offset):
        target = lax.rem(me + offset, size)
        return pltpu.make_async_remote_copy(
            src_ref=swap_out.at[chunk * size + target],
            dst_ref=swap_in.at[chunk * size + me],
            send_sem=swap_sem.at[0],
            recv_sem=swap_sem.at[1],
            device_id={"mp": target},
            device_id_type=pl.DeviceIdType.MESH,
        )

    def all_swaps():
        some = pl.ds(0, chunks * (size - 1))
        return pltpu.make_async_remote_copy(
            src_ref=swap_out.at[some],
            dst_ref=swap_in.at[some],
            send_sem=swap_sem.at[0],
            recv_sem=swap_sem.at[1],
            device_id=spread.others(1),
            device_id_type=pl.DeviceIdType.MESH,
        )

    def settle(chunk):
        line.scatter_sum(chunk, part, scatter_lanes, total)
        grad_ffn = total[...]
        residual = res_ref[chunk]
        scale = row_scale(residual)
        normed = residual * scale
        gsecond_ref[...] += jnp.sum(grad_ffn * normed, axis=0, keepdims=True)
        weighted = grad_ffn * gain_ref[...]
        own_rows = grad_ref[chunk, own, :].astype(f32)
        grad_residual = own_rows + scale * (
            weighted - normed * jnp.mean(weighted * normed, axis=-1, keepdims=True)
        )
        gres_ref[chunk] = grad_residual
        low = grad_residual.astype(bf16)
        own_grad[chunk] = low
        grad_mixed = mm_t1(low, weights[...]).astype(bf16).astype(f32)
        for index in range(size):
            swap_out[chunk * size + index] = grad_mixed[:, index * local : (index + 1) * local]
        for offset in range(1, size):
            swap(chunk, offset).start()

    feed_at = hop * line.reach + delay

    def step(tick, _):
        weight_step(tick)

        @pl.when(tick == feed_at)
        def _():
            weight_finish()
            for load in loads:
                load.wait()

        chunk, due = line.chunk_at(tick)

        @pl.when(due)
        def _():
            line.gather_start(chunk, heads_in, gather_lanes)

        line.gather_step(tick, heads_in, gather_lanes)
        chunk_f, due_f = line.chunk_at(tick - feed_at)

        @pl.when(due_f)
        def _():
            feed_chunk(chunk_f)

        line.scatter_step(tick - feed_at, part, scatter_lanes)
        for late, work in ((1, feed_branch), (2, feed_grads)):
            chunk_w, due_w = line.chunk_at(tick - feed_at - late)

            @pl.when(due_w)
            def _():
                work(chunk_w)

        @pl.when(tick == feed_at + line.reach * (chunks - 1) + 3)
        def _():
            for save in saves[:2]:
                save.start()

        chunk_s, due_s = line.chunk_at(tick - feed_at - hop * line.reach)

        @pl.when(due_s)
        def _():
            settle(chunk_s)

        return 0

    lax.fori_loop(0, feed_at + line.reach * (chunks - 1) + hop * line.reach + 1, step, 0)
    gout_ref[...] = mm_t0(
        own_mixed[...].reshape(chunks * rows, width), own_grad[...].reshape(chunks * rows, width)
    )

    saves[2].start()
    all_swaps().wait_recv()

    def finish(chunk, _):
        save_branch(chunk).wait()
        for index in range(size):

            @pl.when(index == me)
            def _():
                gm_ref[chunk * size + index] = swap_out[chunk * size + index].astype(bf16)

            @pl.when(index != me)
            def _():
                gm_ref[chunk * size + index] = swap_in[chunk * size + index].astype(bf16)

        return 0

    lax.fori_loop(0, chunks, finish, 0)
    line.gather_drain(heads_in, gather_lanes)
    line.scatter_drain(part, scatter_lanes)
    all_swaps().wait_send()
    for save in saves:
        save.wait()
    for half in range(2):
        for level in range(1, bits):
            spread.within(half, level, False).wait_send()


def feed(mixed, seg_rows, grad_rows, up, down, begun, gain, size, group, chunks):
    rows, width = seg_rows.shape
    local = mixed.shape[1]
    chunk = rows // chunks
    piece = chunk // size
    hidden = up.shape[1]
    vmem = pl.BlockSpec(memory_space=pltpu.VMEM)
    anywhere = pl.BlockSpec(memory_space=pl.ANY)
    dma = pltpu.SemaphoreType.DMA
    slots = dma((chunks * size,))
    bits = group.bit_length() - 1
    return pl.pallas_call(
        functools.partial(feed_kernel, size, group, chunks, 2, 0, 4),
        in_specs=[vmem] + [anywhere] * 4 + [vmem] * 2,
        out_specs=[vmem] * 3 + [anywhere] * 4 + [vmem],
        out_shape=[
            jax.ShapeDtypeStruct((chunks * size, piece, local), bf16),
            jax.ShapeDtypeStruct((chunks, piece, width), f32),
            jax.ShapeDtypeStruct((chunks, piece, width), f32),
            jax.ShapeDtypeStruct((chunks * size, piece, width), f32),
            jax.ShapeDtypeStruct((hidden, width), f32),
            jax.ShapeDtypeStruct((width, hidden), f32),
            jax.ShapeDtypeStruct((width, width), f32),
            jax.ShapeDtypeStruct((1, width), f32),
        ],
        scratch_shapes=[
            pltpu.VMEM((chunks, chunk, width), bf16),
            pltpu.VMEM((chunks, chunk, width), bf16),
            pltpu.VMEM(up.shape, bf16),
            pltpu.VMEM(down.shape, bf16),
            pltpu.VMEM((chunks * size, piece, width), f32),
            pltpu.VMEM((hidden, width), f32),
            pltpu.VMEM((width, hidden), f32),
            pltpu.VMEM((width, width), f32),
            pltpu.VMEM((chunk, hidden), bf16),
            pltpu.VMEM((chunk, hidden), bf16),
            pltpu.VMEM((chunk, width), bf16),
            pltpu.VMEM((chunks * size, chunk, local), f32),
            pltpu.VMEM((chunks * size, piece, width), f32),
            pltpu.VMEM((chunks * size, piece, width), f32),
            pltpu.VMEM((chunks * size, piece, width), f32),
            pltpu.VMEM((chunks * size, piece, local), f32),
            pltpu.VMEM((chunks * size, piece, local), f32),
            pltpu.VMEM((2, group, *begun.shape[2:]), f32),
            pltpu.VMEM((width, width), bf16),
            pltpu.VMEM((chunk, width), f32),
            pltpu.VMEM((piece, width), f32),
            pltpu.VMEM((chunks, piece, width), bf16),
            pltpu.VMEM((chunks, piece, width), bf16),
        ]
        + [dma((4,))]
        + [slots] * 4
        + [dma((2,)), dma((2 * bits,)), dma((2 * bits,)), dma((4,)), dma((3,)), dma((chunks,))],
        compiler_params=pltpu.CompilerParams(
            collective_id=0, has_side_effects=True, vmem_limit_bytes=63 << 20
        ),
        name="feed",
    )(
        mixed.reshape(chunks, chunk, local),
        seg_rows.reshape(chunks, chunk, width),
        grad_rows.reshape(chunks, chunk, width),
        up,
        down,
        begun,
        gain[None, :],
    )


class Pieces:
    def __init__(self, group, rows, gap, crossing, jobs, work, landing, summed, sems):
        self.mine = lax.axis_index("dp")
        self.bits = group.bit_length() - 1
        self.rows, self.gap, self.crossing, self.jobs = rows, gap, crossing, jobs
        self.work, self.landing, self.summed = work, landing, summed
        self.slots = work.shape[0]
        (self.rs_s, self.rs_r, self.ag_s, self.ag_r, self.load_sem, self.store_sem) = sems
        self.count = crossing[0] + sum(job[2] for job in jobs)
        self.beats = self.count + 2 * self.bits * gap + 2

    def step_of(self, odd, level):
        even_step = 1 << level
        odd_step = 1 << ((self.bits - level) % self.bits)
        return jnp.where(odd == 1, odd_step, even_step)

    def bit_of(self, odd, level):
        return (self.mine // self.step_of(odd, level)) % 2

    def partner(self, odd, level):
        step = self.step_of(odd, level)
        return {"dp": self.mine + step - 2 * step * self.bit_of(odd, level)}

    def start_of(self, odd, level):
        start = jnp.int32(0)
        for earlier in range(level):
            start = start + self.bit_of(odd, earlier) * (self.rows >> (earlier + 1))
        return start

    def span(self, start, level):
        length = self.rows >> level
        return pl.ds(pl.multiple_of(start, self.rows >> self.bits), length)

    def halves(self, odd, level):
        start, bit, half = self.start_of(odd, level), self.bit_of(odd, level), self.rows >> (level + 1)
        return self.span(start + bit * half, level + 1), self.span(start + (1 - bit) * half, level + 1)

    def reduce_copy(self, slot, odd, level):
        _, give = self.halves(odd, level)
        region = pl.ds(self.rows - (self.rows >> level), self.rows >> (level + 1))
        return pltpu.make_async_remote_copy(
            src_ref=self.work.at[slot, give],
            dst_ref=self.landing.at[slot, region],
            send_sem=self.rs_s.at[slot * self.bits + level],
            recv_sem=self.rs_r.at[slot * self.bits + level],
            device_id=self.partner(odd, level),
            device_id_type=pl.DeviceIdType.MESH,
        )

    def absorb(self, slot, odd, level):
        self.reduce_copy(slot, odd, level).wait_recv()
        keep, _ = self.halves(odd, level)
        region = pl.ds(self.rows - (self.rows >> level), self.rows >> (level + 1))
        self.work[slot, keep, :] = self.work[slot, keep, :] + self.landing[slot, region, :]

    def spread_copy(self, buffer, sems, slot, odd, level, arriving):
        keep, give = self.halves(odd, level)
        span = give if arriving else keep
        return pltpu.make_async_remote_copy(
            src_ref=buffer.at[slot, span],
            dst_ref=buffer.at[slot, span],
            send_sem=sems[0].at[slot * self.bits + level],
            recv_sem=sems[1].at[slot * self.bits + level],
            device_id=self.partner(odd, level),
            device_id_type=pl.DeviceIdType.MESH,
        )

    def spread(self, slot, odd, level, arriving):
        return self.spread_copy(self.summed, (self.ag_s, self.ag_r), slot, odd, level, arriving)

    def move(self, piece, slot, store, start):
        columns = self.work.shape[2]
        first = self.crossing[0]
        sources = [(self.crossing[1], None, 0, first)]
        for source, target, count in self.jobs:
            sources.append((source, target, first, first + count))
            first += count
        for source, target, low, high in sources:
            if store and target is None:
                continue

            @pl.when((piece >= low) & (piece < high))
            def _():
                across = source.shape[2] // columns
                index = (piece - low) // across
                lanes = pl.ds(pl.multiple_of((piece - low - index * across) * columns, columns), columns)
                inside = self.summed.at[slot] if store else self.work.at[slot]
                if store:
                    copy = pltpu.make_async_copy(inside, target.at[index, :, lanes], self.store_sem.at[slot])
                else:
                    copy = pltpu.make_async_copy(source.at[index, :, lanes], inside, self.load_sem.at[slot])
                copy.start() if start else copy.wait()

    def load_first(self):
        self.move(jnp.int32(0), 0, False, True)

    def step(self, tick, cross):
        bits = self.bits
        for age in reversed(range(-1, 2 * bits + 2)):
            piece = tick - (age if age < 0 else min(age * self.gap, 2 * bits * self.gap + 1))
            safe = jnp.maximum(piece, 0)
            slot, odd = safe % self.slots, safe % 2
            plain = piece >= self.crossing[0]
            inside = (piece >= 0) & (piece < self.count)
            if age == 2 * bits + 1:

                @pl.when(inside)
                def _():
                    for level in range(bits):
                        self.reduce_copy(slot, odd, level).wait_send()

                @pl.when(inside & plain)
                def _():
                    for level in range(bits):
                        self.spread(slot, odd, level, False).wait_send()
                    self.move(piece, slot, True, False)

                @pl.when(inside & jnp.logical_not(plain))
                def _():
                    cross(piece, slot, odd, False)

            elif age == 2 * bits:

                @pl.when(inside & plain)
                def _():
                    self.spread(slot, odd, 0, True).wait_recv()
                    self.move(piece, slot, True, True)

            elif age > bits:

                @pl.when(inside & plain)
                def _():
                    self.spread(slot, odd, 2 * bits - age, True).wait_recv()
                    self.spread(slot, odd, 2 * bits - 1 - age, False).start()

            elif age == bits:

                @pl.when(inside)
                def _():
                    self.absorb(slot, odd, bits - 1)

                @pl.when(inside & plain)
                def _():
                    own = self.span(self.start_of(odd, bits), bits)
                    self.summed[slot, own, :] = self.work[slot, own, :]
                    self.spread(slot, odd, bits - 1, False).start()

                @pl.when(inside & jnp.logical_not(plain))
                def _():
                    cross(piece, slot, odd, True)

            elif age > 0:

                @pl.when(inside)
                def _():
                    self.absorb(slot, odd, age - 1)
                    self.reduce_copy(slot, odd, age).start()

            elif age == 0:

                @pl.when(inside)
                def _():
                    self.move(piece, slot, False, False)
                    self.reduce_copy(slot, odd, 0).start()

            else:

                @pl.when(inside)
                def _():
                    self.move(piece, slot, False, True)


def close_kernel(
    size,
    group,
    chunks,
    hop,
    counts,
    gap,
    early,
    gunit_hbm,
    branch_hbm,
    seg_hbm,
    gres_hbm,
    res_hbm,
    gain_ref,
    early_ref,
    gout_ref,
    gup_ref,
    gdown_ref,
    gq_ref,
    gk_ref,
    gv_ref,
    gpack_ref,
    small_ref,
    result_ref,
    gseg_ref,
    gout_sum,
    gup_sum,
    gdown_sum,
    gq_sum,
    gk_sum,
    gv_sum,
    gpack_sum,
    small_sum,
    gunit_ref,
    branch_ref,
    seg_ref,
    gres_ref,
    res_ref,
    whole_seg,
    whole_out,
    seg_right,
    seg_left,
    out_right,
    out_left,
    total,
    work,
    landing,
    summed,
    cross_in,
    cross_work,
    small_cross,
    small_held,
    small_in,
    *sems,
):
    line = Line(size, chunks, hop)
    me = line.me
    line_s, recvs, sems = sems[0], sems[1:9], sems[9:]
    seg_scatter = ((True, seg_right, (line_s.at[0], recvs[0])), (False, seg_left, (line_s.at[1], recvs[1])))
    out_scatter = ((True, out_right, (line_s.at[2], recvs[2])), (False, out_left, (line_s.at[3], recvs[3])))
    seg_gather = ((True, (line_s.at[4], recvs[4])), (False, (line_s.at[5], recvs[5])))
    out_gather = ((True, (line_s.at[6], recvs[6])), (False, (line_s.at[7], recvs[7])))
    piece_sems = sems[:6]
    cross_s, cross_r, tail_s, tail_r, tail_store = sems[6:11]
    mix_s, mix_r, small_s, small_r = sems[11:15]
    seg_load, out_load, load_sem = sems[15:18]
    loads = [
        pltpu.make_async_copy(source, target, load_sem.at[index])
        for index, (source, target) in enumerate(((seg_hbm, seg_ref), (gres_hbm, gres_ref), (res_hbm, res_ref)))
    ]

    def part_load(source, target, load, chunk):
        here = pl.ds(chunk * size, size)
        return pltpu.make_async_copy(source.at[here], target.at[here], load.at[chunk])

    for chunk in range(chunks):
        part_load(gunit_hbm, gunit_ref, seg_load, chunk).start()
        if chunk >= early:
            part_load(branch_hbm, branch_ref, out_load, chunk).start()
    for load in loads:
        load.start()
    jobs = [
        (gup_ref, gup_sum, counts[1]),
        (gdown_ref, gdown_sum, counts[2]),
        (gq_ref, gq_sum, counts[3]),
        (gk_ref, gk_sum, counts[4]),
        (gv_ref, gv_sum, counts[5]),
        (gpack_ref, gpack_sum, counts[6]),
    ]
    pieces = Pieces(group, work.shape[1], gap, (counts[0], gout_ref), jobs, work, landing, summed, piece_sems)
    bits = pieces.bits
    pieces.load_first()
    greet(
        [{"mp": lax.rem(me + offset, size)} for offset in range(1, size)]
        + [{"dp": pieces.mine + (1 << bit) - 2 * (1 << bit) * ((pieces.mine // (1 << bit)) % 2)} for bit in range(bits)]
    )

    across, columns = cross_work.shape[0], work.shape[2]

    def cross_copy(slot, column, target, origin):
        own = pieces.span(pieces.start_of(column % 2, bits), bits)
        return pltpu.make_async_remote_copy(
            src_ref=work.at[slot, own],
            dst_ref=cross_in.at[column * size + origin],
            send_sem=cross_s.at[column * size + target],
            recv_sem=cross_r.at[column * size + origin],
            device_id={"mp": target},
            device_id_type=pl.DeviceIdType.MESH,
        )

    def cross(piece, slot, odd, start):
        target, column = piece // across, piece % across

        @pl.when(target != me)
        def _():
            copy = cross_copy(slot, column, target, me)
            copy.start() if start else copy.wait_send()

        if start:

            @pl.when(target == me)
            def _():
                own = pieces.span(pieces.start_of(odd, bits), bits)
                cross_in[column * size + me] = work[slot, own, :]

    def tail_copy(column):
        return pltpu.make_async_copy(
            cross_work.at[column],
            gout_sum.at[0, :, column * columns : (column + 1) * columns],
            tail_store.at[column],
        )

    def tail_spread(column, level, arriving):
        return pieces.spread_copy(cross_work, (tail_s, tail_r), column, column % 2, level, arriving)

    def tail_step(tick):
        base = counts[0] + bits * gap + gap
        for column in range(across):

            @pl.when(tick == base + column)
            def _():
                for offset in range(1, size):
                    cross_copy(0, column, me, lax.rem(me + offset, size)).wait_recv()
                own = pieces.span(pieces.start_of(column % 2, bits), bits)
                cross_work[column, own, :] = (
                    sum(cross_in[column * size + index] for index in range(1, size)) + cross_in[column * size]
                )
                tail_spread(column, bits - 1, False).start()

            for level in reversed(range(bits)):

                @pl.when(tick == base + column + (bits - level) * gap)
                def _():
                    tail_spread(column, level, True).wait_recv()
                    if level:
                        tail_spread(column, level - 1, False).start()
                    else:
                        tail_copy(column).start()

    def small_across(offset, arriving):
        origin = lax.rem(me - offset + size, size) if arriving else me
        return pltpu.make_async_remote_copy(
            src_ref=small_cross.at[me],
            dst_ref=small_cross.at[origin],
            send_sem=mix_s.at[offset],
            recv_sem=mix_r.at[offset],
            device_id={"mp": lax.rem(me + offset, size)},
            device_id_type=pl.DeviceIdType.MESH,
        )

    def small_within(level):
        step = 1 << level
        return pltpu.make_async_remote_copy(
            src_ref=small_held.at[level],
            dst_ref=small_in.at[level],
            send_sem=small_s.at[level],
            recv_sem=small_r.at[level],
            device_id={"dp": pieces.mine + step - 2 * step * ((pieces.mine // step) % 2)},
            device_id_type=pl.DeviceIdType.MESH,
        )

    def small_step(tick):
        @pl.when(tick == 0)
        def _():
            small_cross[me] = small_ref[...]
            for offset in range(1, size):
                small_across(offset, False).start()

        @pl.when(tick == 2)
        def _():
            value = small_ref[...]
            shared = lax.broadcasted_iota(jnp.int32, value.shape, 0) < 2
            for offset in range(1, size):
                small_across(offset, True).wait_recv()
                origin = lax.rem(me - offset + size, size)
                value = value + jnp.where(shared, small_cross[origin], 0.0)
            small_held[0] = value
            small_within(0).start()

        for level in range(bits):

            @pl.when(tick == 4 + 2 * level)
            def _():
                small_within(level).wait_recv()
                value = small_held[level] + small_in[level]
                if level + 1 < bits:
                    small_held[level + 1] = value
                    small_within(level + 1).start()
                else:
                    small_sum[...] = value

    def settle_seg(chunk):
        slot = chunk * size + me
        line.scatter_sum(chunk, gunit_ref, seg_scatter, total)
        rows = seg_ref[slot].astype(f32)
        scale = row_scale(rows)
        normed = rows * scale
        weighted = total[...] * gain_ref[...]
        grad = gres_ref[chunk] + scale * (
            weighted - normed * jnp.mean(weighted * normed, axis=-1, keepdims=True)
        )
        low = grad.astype(bf16)
        gseg_ref[slot] = low
        whole_seg[slot] = low.astype(f32)
        line.gather_start(chunk, whole_seg, seg_gather)

    def settle_out(chunk):
        slot = chunk * size + me

        @pl.when(chunk < early)
        def _():
            total[...] = early_ref[jnp.minimum(chunk, early - 1)]

        @pl.when(chunk >= early)
        def _():
            line.scatter_sum(chunk, branch_ref, out_scatter, total)
            total[...] = res_ref[chunk] + total[...]

        low = total[...].astype(bf16)
        result_ref[slot] = low
        whole_out[slot] = low.astype(f32)
        line.gather_start(chunk, whole_out, out_gather)

    def seg_landed(slot):
        gseg_ref[slot] = whole_seg[slot].astype(bf16)

    def out_landed(slot):
        result_ref[slot] = whole_out[slot].astype(bf16)

    settle_at = hop * line.reach
    seg_lag, out_lag = 0, -line.reach * early

    def step(tick, _):
        flows = (
            (seg_lag, gunit_hbm, seg_load, gunit_ref, seg_scatter, settle_seg, whole_seg, seg_gather, seg_landed),
            (out_lag, branch_hbm, out_load, branch_ref, out_scatter, settle_out, whole_out, out_gather, out_landed),
        )
        @pl.when(tick == 0)
        def _():
            for load in loads:
                load.wait()

        for late, source, load, part, scatter, settle, whole, gather, landed in flows:
            fresh, new = line.chunk_at(tick - late)

            first = early if late < 0 else 0

            @pl.when(new & (fresh >= first))
            def _():
                part_load(source, part, load, fresh).wait()

            line.scatter_step(tick - late, part, scatter, first)
            chunk, due = line.chunk_at(tick - late - settle_at)

            @pl.when(due)
            def _():
                settle(chunk)

        for late, source, load, part, scatter, settle, whole, gather, landed in flows:
            line.gather_step(tick - late - settle_at, whole, gather, landed)
        small_step(tick)

        def piece_step(beat, _):
            pieces.step(beat, cross)
            tail_step(beat)
            return 0

        lax.fori_loop(beats(tick), beats(tick + 1), piece_step, 0)
        return 0

    line_ticks = line.reach * (chunks - 1) + 2 * settle_at + 1

    def beats(tick):
        return jnp.minimum((tick * pieces.beats) // (line_ticks - 5), pieces.beats)

    lax.fori_loop(0, line_ticks, step, 0)

    line.scatter_drain(gunit_ref, seg_scatter)
    line.scatter_drain(branch_ref, out_scatter, early)
    line.gather_drain(whole_seg, seg_gather)
    line.gather_drain(whole_out, out_gather)
    for column in range(across):
        for level in range(bits):
            tail_spread(column, level, False).wait_send()
        tail_copy(column).wait()
    for offset in range(1, size):
        small_across(offset, False).wait_send()
    for level in range(bits):
        small_within(level).wait_send()


def close(
    grad_unit, branch, seg_rows, grad_residual, residual, gain, early, grads, small, size, group, chunks
):
    rows, width = seg_rows.shape
    piece = rows // (chunks * size)
    vmem = pl.BlockSpec(memory_space=pltpu.VMEM)
    whole = (chunks * size, piece, width)
    piece_rows, columns, gap = max(256, 8 * group), width // 4, 3 if group <= 8 else 2
    bits = group.bit_length() - 1
    slots = 2 * bits * gap + 2
    views = [grad.reshape(-1, piece_rows, grad.shape[1]) for grad in grads]
    counts = tuple(view.shape[0] * (view.shape[2] // columns) for view in views)
    anywhere = pl.BlockSpec(memory_space=pl.ANY)
    dma = pltpu.SemaphoreType.DMA
    sums = [jax.ShapeDtypeStruct(view.shape, f32) for view in views]
    sums[0] = jax.ShapeDtypeStruct((1, piece_rows, width), f32)
    return pl.pallas_call(
        functools.partial(close_kernel, size, group, chunks, 2, counts, gap, early.shape[0]),
        in_specs=[anywhere] * 5 + [vmem] * 2 + [anywhere] * len(views) + [vmem],
        out_specs=[vmem] * 2 + [anywhere] * len(views) + [vmem],
        out_shape=[jax.ShapeDtypeStruct(whole, bf16)] * 2 + sums + [jax.ShapeDtypeStruct(small.shape, f32)],
        scratch_shapes=[pltpu.VMEM(whole, f32)] * 2
        + [
            pltpu.VMEM(whole, bf16),
            pltpu.VMEM(grad_residual.shape, f32),
            pltpu.VMEM(grad_residual.shape, f32),
        ]
        + [pltpu.VMEM(whole, f32)] * 6
        + [
            pltpu.VMEM((piece, width), f32),
            pltpu.VMEM((slots, piece_rows, columns), f32),
            pltpu.VMEM((slots, piece_rows, columns), f32),
            pltpu.VMEM((slots, piece_rows, columns), f32),
            pltpu.VMEM((width // columns * size, piece_rows // group, columns), f32),
            pltpu.VMEM((width // columns, piece_rows, columns), f32),
            pltpu.VMEM((size, *small.shape), f32),
            pltpu.VMEM((bits, *small.shape), f32),
            pltpu.VMEM((bits, *small.shape), f32),
        ]
        + [dma((8,))]
        + [dma((chunks * size,))] * 8
        + [dma((slots * bits,))] * 4
        + [dma((slots,))] * 2
        + [dma((width // columns * size,))] * 2
        + [dma((width // columns * bits,))] * 2
        + [dma((width // columns,))]
        + [dma((size,))] * 2
        + [dma((bits,))] * 2
        + [dma((chunks,))] * 2
        + [dma((3,))],
        compiler_params=pltpu.CompilerParams(
            collective_id=1, has_side_effects=True, vmem_limit_bytes=63 << 20
        ),
        cost_estimate=pl.CostEstimate(flops=10**11, bytes_accessed=10**9, transcendentals=0),
        name="close",
    )(
        grad_unit.reshape(whole),
        branch,
        seg_rows.reshape(whole),
        grad_residual,
        residual,
        gain[None, :],
        early,
        *views,
        small,
    )


def body(
    inputs,
    memory,
    compressed_memory,
    memory_fill,
    compressed_fill,
    first_gain,
    query_weight,
    key_weight,
    value_weight,
    relative_bias,
    output_weight,
    second_gain,
    up_weight,
    down_weight,
    compress_weight,
    grad_output,
    grad_compressed,
    *,
    mp_size,
    dp_size,
):
    streams, seg_len, width = inputs.shape
    mem_len = memory.shape[1]
    packed_len = compressed_memory.shape[1]
    local = query_weight.shape[1]
    rows = streams * seg_len
    unit, q, k, v, mixed, log_total, packed_new, grad_pack, begun = attend(
        inputs,
        memory,
        compressed_memory,
        memory_fill,
        compressed_fill,
        first_gain,
        query_weight,
        key_weight,
        value_weight,
        relative_bias,
        compress_weight,
        grad_compressed,
        output_weight,
        mp_size,
        dp_size,
    )
    seg_rows = inputs.reshape(rows, width)
    grad_mixed, grad_residual, residual, branch, grad_down, grad_up, grad_out_full, grad_second = feed(
        mixed.reshape(rows, local),
        seg_rows,
        grad_output.reshape(rows, width),
        up_weight,
        down_weight,
        begun,
        second_gain,
        mp_size,
        dp_size,
        chunk_count,
    )
    grad_mixed = grad_mixed.reshape(streams, seg_len, local)
    grad_unit, gq, gk, gv, small, early = attend_back(
        unit,
        q,
        k,
        v,
        log_total,
        grad_mixed,
        memory_fill,
        compressed_fill,
        query_weight,
        key_weight,
        value_weight,
        relative_bias,
        first_gain,
        grad_second,
        mem_len,
        packed_len,
        branch,
        residual,
        mp_size,
        early_chunks,
    )
    result, grad_seg, grad_out_w, grad_up, grad_down, gq, gk, gv, grad_pack, small = close(
        grad_unit,
        branch,
        seg_rows,
        grad_residual,
        residual,
        first_gain,
        early,
        (grad_out_full, grad_up, grad_down, gq, gk, gv, grad_pack),
        small,
        mp_size,
        dp_size,
        chunk_count,
    )
    grad_first, grad_second = small[0], small[1]
    grad_relative = small[2, : relative_bias.size].reshape(relative_bias.shape)
    result = result.reshape(inputs.shape)
    grad_seg = grad_seg.reshape(inputs.shape)
    grad_query_w = gq.reshape(local, width).T
    grad_key_w = gk.reshape(local, width).T
    grad_value_w = gv.reshape(local, width).T
    grad_out_w = grad_out_w.reshape(local, width)
    grad_compress_w = grad_pack.reshape(-1, 2 * width).T
    grad_up = grad_up.reshape(up_weight.shape)
    grad_down = grad_down.reshape(down_weight.shape)
    return (
        result,
        packed_new,
        grad_seg,
        grad_first,
        grad_query_w,
        grad_key_w,
        grad_value_w,
        grad_relative,
        grad_out_w,
        grad_second,
        grad_up,
        grad_down,
        grad_compress_w,
    )


def solution(mesh):
    in_specs = (
        P("dp", None, None),
        P("dp", None, None),
        P("dp", None, None),
        P("dp"),
        P("dp"),
        P(),
        P(None, "mp"),
        P(None, "mp"),
        P(None, "mp"),
        P("mp", None),
        P("mp", None),
        P(),
        P(None, "mp"),
        P("mp", None),
        P(None, "mp"),
        P("dp", None, None),
        P("dp", None, "mp"),
    )
    out_specs = (
        P("dp", None, None),
        P("dp", None, "mp"),
        P("dp", None, None),
        P(),
        P(None, "mp"),
        P(None, "mp"),
        P(None, "mp"),
        P("mp", None),
        P("mp", None),
        P(),
        P(None, "mp"),
        P("mp", None),
        P(None, "mp"),
    )
    return jax.shard_map(
        functools.partial(body, mp_size=mesh.shape["mp"], dp_size=mesh.shape["dp"]),
        mesh=mesh,
        in_specs=in_specs,
        out_specs=out_specs,
        check_vma=False,
    )
```

```python
import functools
import math

import jax
import jax.numpy as jnp
from jax import lax
from jax.experimental import pallas as pl
from jax.experimental.pallas import tpu as pltpu
from jax.sharding import PartitionSpec as P

reach_marks = (1, 2, 3, 4, 5, 6, 7, 8, 12, 16, 24, 32, 48, 64, 96, 128, 192, 256, 384, 512, 768, 1024)
epsilon = 1e-06
masked_score = -1e30
block = 128
query_block = 256
chunk_count = 8
early_chunks = 2
f32 = jnp.float32
bf16 = jnp.bfloat16


def mm(left, right):
    return jnp.dot(left, right, preferred_element_type=f32)


def mm_t0(left, right):
    return lax.dot_general(left, right, (((0,), (0,)), ((), ())), preferred_element_type=f32)


def mm_t1(left, right):
    return lax.dot_general(left, right, (((1,), (1,)), ((), ())), preferred_element_type=f32)


def row_scale(source):
    return lax.rsqrt(jnp.mean(source * source, axis=-1, keepdims=True) + epsilon)


def diagonal_count(seg_len, kept_count):
    return (seg_len + kept_count) // block + 1


def diagonal_of(seg_len, kept_count, column):
    return (seg_len + kept_count) // block - 1 - column


def strip_start(seg_len, sub_block):
    return (seg_len // block - 1 - sub_block) * block


def bias_block(bias_ref, head, diagonal, transposed):
    rows = lax.broadcasted_iota(jnp.int32, (block, block), 0)
    cols = lax.broadcasted_iota(jnp.int32, (block, block), 1)
    distance = diagonal * block + ((cols - rows) if transposed else (rows - cols))
    lowest, highest = diagonal * block - block + 1, diagonal * block + block - 1
    base = jnp.float32(0.0)
    for position, mark_value in enumerate(reach_marks):
        if mark_value <= lowest:
            base = base + bias_ref[head, position]
    value = jnp.full((block, block), base, f32)
    for position, mark_value in enumerate(reach_marks):
        if lowest < mark_value <= highest:
            value = value + jnp.where(distance >= mark_value, bias_ref[head, position], 0.0)
    if lowest < 0:
        value = jnp.where(distance >= 0, value, masked_score)
    return value


def live_mask(shape, axis, packed_len, mem_len, packed_count, memory_count):
    slot = lax.broadcasted_iota(jnp.int32, shape, axis)
    dead_packed = (slot < packed_len) & (slot < packed_len - packed_count)
    dead_memory = (slot >= packed_len) & (slot < packed_len + mem_len - memory_count)
    return jnp.where(dead_packed | dead_memory, masked_score, 0.0).astype(f32)


def greet(peers):
    barrier = pltpu.get_barrier_semaphore()
    for peer in peers:
        pl.semaphore_signal(barrier, inc=1, device_id=peer, device_id_type=pl.DeviceIdType.MESH)
    pl.semaphore_wait(barrier, len(peers))


class Spread:
    def __init__(self, size, group, buffer, sems):
        self.me, self.mine = lax.axis_index("mp"), lax.axis_index("dp")
        self.size, self.group, self.buffer = size, group, buffer
        self.bits = group.bit_length() - 1
        self.across_s, self.across_r, self.within_s, self.within_r = sems
        order = list(reversed(range(self.bits)))
        self.orders = (order, order[1::-1] + order[2:])
        self.spots = []
        for order in self.orders:
            spot = jnp.int32(0)
            for level, bit in enumerate(order):
                spot = spot + ((self.mine // (1 << bit)) % 2) * (1 << level)
            self.spots.append(spot)

    def place_of(self, half, member):
        return sum(((member >> bit) & 1) << level for level, bit in enumerate(self.orders[half]))

    def others(self, offset):
        return {"mp": lax.rem(self.me + offset, self.size)}

    def partner(self, half, level):
        step = 1 << self.orders[half][level]
        return {"dp": self.mine + step - 2 * step * ((self.mine // step) % 2)}

    def across(self, half, offset, arriving):
        origin = lax.rem(self.me - offset + self.size, self.size) if arriving else self.me
        return pltpu.make_async_remote_copy(
            src_ref=self.buffer.at[half, self.spots[half], origin],
            dst_ref=self.buffer.at[half, self.spots[half], origin],
            send_sem=self.across_s.at[half * self.size + offset],
            recv_sem=self.across_r.at[half * self.size + offset],
            device_id=self.others(offset),
            device_id_type=pl.DeviceIdType.MESH,
        )

    def block(self, half, level, other):
        count = 1 << level
        start = (self.spots[half] // count) * count
        if other:
            start = start + count - 2 * count * ((self.spots[half] // count) % 2)
        return pl.ds(start, count)

    def within(self, half, level, arriving):
        span = self.block(half, level, arriving)
        return pltpu.make_async_remote_copy(
            src_ref=self.buffer.at[half, span],
            dst_ref=self.buffer.at[half, span],
            send_sem=self.within_s.at[half * self.bits + level],
            recv_sem=self.within_r.at[half * self.bits + level],
            device_id=self.partner(half, level),
            device_id_type=pl.DeviceIdType.MESH,
        )

    def start_level(self, level):
        for half in range(2):
            if level:
                self.within(half, level - 1, True).wait_recv()
            self.within(half, level, False).start()


def attend_kernel(
    sizes,
    size,
    group,
    memory_fill,
    packed_fill,
    bias_ref,
    seg_ref,
    memory_ref,
    packed_ref,
    gain_ref,
    wq_ref,
    wk_ref,
    wv_ref,
    wc_ref,
    gcomp_ref,
    wo_ref,
    unit_ref,
    q_ref,
    k_ref,
    v_ref,
    mixed_ref,
    log_ref,
    packed_new_ref,
    gpack_ref,
    begun_ref,
    strip,
    live,
    mem_rows,
    spread_in,
    *sems,
):
    seg_len, mem_len, packed_len, heads, head_dim = sizes
    kept = mem_len + packed_len
    keys = kept + seg_len
    stream = pl.program_id(0)
    scale = 1.0 / math.sqrt(head_dim)
    gain = gain_ref[...]
    spread = Spread(size, group, spread_in, sems[:4])
    piece, columns = spread_in.shape[3:]
    width = gain.shape[1]

    @pl.when(stream == 0)
    def _():
        greet(
            [spread.others(offset) for offset in range(1, size)]
            + [spread.partner(half, 0) for half in range(2)]
        )
        rows = pl.ds(pl.multiple_of(spread.mine * piece, piece), piece)
        for half in range(2):
            lanes = slice(half * columns, (half + 1) * columns)
            spread_in[half, spread.spots[half], spread.me] = wo_ref[rows, lanes].astype(f32)
            for offset in range(1, size):
                spread.across(half, offset, False).start()
        gpack_ref[...] = jnp.zeros_like(gpack_ref)

    slot = lax.broadcasted_iota(jnp.int32, mem_rows.shape[1:], 0)
    keep = slot >= mem_len - memory_fill[stream]
    count = packed_new_ref.shape[1]
    for column in range(mem_rows.shape[0]):
        lanes = slice(column * block, (column + 1) * block)
        mem_rows[column] = jnp.where(keep, memory_ref[0, :, lanes].astype(f32), 0.0)
    packed_new = jnp.zeros(packed_new_ref.shape[1:], f32)
    for parity in range(2):
        rows = jnp.concatenate(
            [mem_rows[column, pl.ds(parity, count, stride=2), :] for column in range(mem_rows.shape[0])], axis=1
        ).astype(bf16)
        lanes = slice(parity * width, (parity + 1) * width)
        packed_new = packed_new + mm(rows, wc_ref[lanes, :])
        gpack_ref[:, lanes] += mm_t0(gcomp_ref[0], rows)
    packed_new_ref[0] = packed_new.astype(bf16)
    start = 0
    for part_ref, length in ((packed_ref, packed_len), (memory_ref, mem_len), (seg_ref, seg_len)):
        rows = part_ref[0].astype(f32)
        unit = (rows * row_scale(rows) * gain).astype(bf16)
        unit_ref[0, start : start + length, :] = unit
        k_ref[0, start : start + length, :] = mm(unit, wk_ref[...]).astype(bf16)
        v_ref[0, start : start + length, :] = mm(unit, wv_ref[...]).astype(bf16)
        if start == kept:
            q_ref[0] = mm(unit, wq_ref[...]).astype(bf16)
        start += length
    live[...] = live_mask((8, kept), 1, packed_len, mem_len, packed_fill[stream], memory_fill[stream])
    for head in range(heads):
        lanes = slice(head * head_dim, (head + 1) * head_dim)
        for column in range(diagonal_count(seg_len, kept)):
            strip[:, column * block : (column + 1) * block] = bias_block(
                bias_ref, head, diagonal_of(seg_len, kept, column), False
            )
        for index in range(seg_len // query_block):
            reach = kept + (index + 1) * query_block
            rows = slice(index * query_block, (index + 1) * query_block)
            score = mm_t1(q_ref[0, rows, lanes], k_ref[0, :reach, lanes]) * scale
            parts = []
            for sub in range(query_block // block):
                first = strip_start(seg_len, index * (query_block // block) + sub)
                parts.append(strip[:, first : first + reach])
            score = score + jnp.concatenate(parts, axis=0)
            score = jnp.concatenate([score[:, :kept] + live[0:1, :], score[:, kept:]], axis=1)
            top = jnp.max(score, axis=-1, keepdims=True)
            weight = jnp.exp(score - top)
            total = jnp.sum(weight, axis=-1, keepdims=True)
            log_total = jnp.broadcast_to(top + jnp.log(total), (query_block, block))
            log_ref[0, head, :, rows] = log_total.T[0:1, :]
            mixed = mm(weight.astype(bf16), v_ref[0, :reach, lanes]) * (1.0 / total)
            mixed_ref[0, rows, lanes] = mixed.astype(bf16)

    @pl.when(stream == 0)
    def _():
        for half in range(2):
            for offset in range(1, size):
                spread.across(half, offset, True).wait_recv()
        spread.start_level(0)

    @pl.when(stream == pl.num_programs(0) - 1)
    def _():
        copies = []
        for half in range(2):
            spread.within(half, 0, True).wait_recv()
            pair = spread_in.at[half, pl.ds((spread.spots[half] // 2) * 2, 2)]
            copies.append(pltpu.make_async_copy(pair, begun_ref.at[half], sems[4].at[half]))
            copies[-1].start()
        for half in range(2):
            for offset in range(1, size):
                spread.across(half, offset, False).wait_send()
            spread.within(half, 0, False).wait_send()
            copies[half].wait()


def attend(
    inputs, memory, packed, memory_fill, packed_fill, gain, wq, wk, wv, bias, wc, gcomp, wo, size, group
):
    streams, seg_len, width = inputs.shape
    mem_len, packed_len = memory.shape[1], packed.shape[1]
    heads = bias.shape[0]
    local = wq.shape[1]
    keys = seg_len + mem_len + packed_len
    sizes = (seg_len, mem_len, packed_len, heads, local // heads)
    smem = pl.BlockSpec(memory_space=pltpu.SMEM)
    compress_count = gcomp.shape[1]
    piece = wo.shape[0] // group
    bits = group.bit_length() - 1

    def rows_of(count, columns):
        return pl.BlockSpec((1, count, columns), lambda s: (s, 0, 0))

    def whole(shape):
        return pl.BlockSpec(shape, lambda s: (0,) * len(shape))

    return pl.pallas_call(
        functools.partial(attend_kernel, sizes, size, group),
        grid=(streams,),
        in_specs=[
            smem,
            smem,
            smem,
            rows_of(seg_len, width),
            rows_of(mem_len, width),
            rows_of(packed_len, width),
            whole((1, width)),
            whole(wq.shape),
            whole(wk.shape),
            whole(wv.shape),
            whole(wc.shape),
            rows_of(compress_count, local),
            whole(wo.shape),
        ],
        out_specs=[
            rows_of(keys, width),
            rows_of(seg_len, local),
            rows_of(keys, local),
            rows_of(keys, local),
            rows_of(seg_len, local),
            pl.BlockSpec((1, heads, 1, seg_len), lambda s: (s, 0, 0, 0)),
            rows_of(compress_count, local),
            whole((local, 2 * width)),
            pl.BlockSpec(memory_space=pl.ANY),
        ],
        out_shape=[
            jax.ShapeDtypeStruct((streams, keys, width), bf16),
            jax.ShapeDtypeStruct((streams, seg_len, local), bf16),
            jax.ShapeDtypeStruct((streams, keys, local), bf16),
            jax.ShapeDtypeStruct((streams, keys, local), bf16),
            jax.ShapeDtypeStruct((streams, seg_len, local), bf16),
            jax.ShapeDtypeStruct((streams, heads, 1, seg_len), f32),
            jax.ShapeDtypeStruct((streams, compress_count, local), bf16),
            jax.ShapeDtypeStruct((local, 2 * width), f32),
            jax.ShapeDtypeStruct((2, 2, size, piece, width // 2), f32),
        ],
        scratch_shapes=[
            pltpu.VMEM((block, diagonal_count(seg_len, mem_len + packed_len) * block), f32),
            pltpu.VMEM((8, mem_len + packed_len), f32),
            pltpu.VMEM((width // block, mem_len, block), f32),
            pltpu.VMEM((2, group, size, piece, width // 2), f32),
            pltpu.SemaphoreType.DMA((2 * size,)),
            pltpu.SemaphoreType.DMA((2 * size,)),
            pltpu.SemaphoreType.DMA((2 * bits,)),
            pltpu.SemaphoreType.DMA((2 * bits,)),
            pltpu.SemaphoreType.DMA((2,)),
        ],
        compiler_params=pltpu.CompilerParams(
            collective_id=2, has_side_effects=True, vmem_limit_bytes=60 << 20
        ),
        cost_estimate=pl.CostEstimate(
            flops=streams * (2 * keys * width * local * 3 + 4 * seg_len * keys * local),
            bytes_accessed=streams * keys * (width * 4 + local * 6),
            transcendentals=streams * heads * seg_len * keys,
        ),
        name="attend",
    )(memory_fill, packed_fill, bias, inputs, memory, packed, gain[None, :], wq, wk, wv, wc, gcomp, wo)


class Line:
    def __init__(self, size, chunks, hop):
        self.me = lax.axis_index("mp")
        self.size, self.chunks, self.hop = size, chunks, hop
        self.reach = size - 1

    def place(self, right):
        return self.me if right else self.reach - self.me

    def peer(self, right):
        return {"mp": self.me + 1 if right else self.me - 1}

    def copy(self, source, target, sems, slot, right):
        return pltpu.make_async_remote_copy(
            src_ref=source.at[slot],
            dst_ref=target.at[slot],
            send_sem=sems[0],
            recv_sem=sems[1].at[slot],
            device_id=self.peer(right),
            device_id_type=pl.DeviceIdType.MESH,
        )

    def chunk_at(self, tick):
        positive = jnp.maximum(tick, 0)
        chunk = positive // self.reach
        return chunk, (tick >= 0) & (positive == chunk * self.reach) & (chunk < self.chunks)

    def scatter_step(self, tick, part, lanes, first=0):
        for right, held, sems in lanes:
            place = self.place(right)
            late = tick - self.hop * place
            positive = jnp.maximum(late, 0)
            chunk = positive // self.reach
            goal = self.reach - (positive - self.reach * chunk)
            active = (late >= 0) & (chunk >= first) & (chunk < self.chunks) & (goal > place)
            slot = chunk * self.size + (goal if right else self.reach - goal)

            @pl.when(active & (place == 0))
            def _():
                self.copy(part, held, sems, slot, right).start()

            @pl.when(active & (place > 0))
            def _():
                self.copy(held, held, sems, slot, right).wait_recv()
                held[slot] = held[slot] + part[slot]
                self.copy(held, held, sems, slot, right).start()

    def scatter_sum(self, chunk, part, lanes, total):
        slot = chunk * self.size + self.me
        total[...] = part[slot]
        for right, held, sems in lanes:

            @pl.when(self.place(right) > 0)
            def _():
                self.copy(held, held, sems, slot, right).wait_recv()
                total[...] = total[...] + held[slot]

    def gather_start(self, chunk, whole, lanes):
        slot = chunk * self.size + self.me
        for right, sems in lanes:

            @pl.when(self.place(right) < self.reach)
            def _():
                self.copy(whole, whole, sems, slot, right).start()

    def gather_step(self, tick, whole, lanes, landed=None):
        for right, sems in lanes:
            place = self.place(right)
            for distance in range(1, self.size):
                chunk, due = self.chunk_at(tick - self.hop * distance)

                @pl.when(due & (distance <= place))
                def _():
                    slot = chunk * self.size + (self.me - distance if right else self.me + distance)
                    self.copy(whole, whole, sems, slot, right).wait_recv()

                    @pl.when(place < self.reach)
                    def _():
                        self.copy(whole, whole, sems, slot, right).start()

                    if landed is not None:
                        landed(slot)

    def sent(self, buffer, send_sem, count, right):
        some = buffer.at[pl.ds(0, count)]
        return pltpu.make_async_remote_copy(
            src_ref=some,
            dst_ref=some,
            send_sem=send_sem,
            recv_sem=send_sem,
            device_id=self.peer(right),
            device_id_type=pl.DeviceIdType.MESH,
        )

    def scatter_drain(self, part, lanes, first=0):
        for right, held, sems in lanes:
            for place in range(self.reach):

                @pl.when(self.place(right) == place)
                def _():
                    self.sent(part, sems[0], (self.reach - place) * (self.chunks - first), right).wait_send()

    def gather_drain(self, whole, lanes):
        for right, sems in lanes:
            for place in range(self.reach):

                @pl.when(self.place(right) == place)
                def _():
                    self.sent(whole, sems[0], (place + 1) * self.chunks, right).wait_send()


def meet(line):
    barrier = pltpu.get_barrier_semaphore()
    for right in (True, False):

        @pl.when(line.place(right) < line.reach)
        def _():
            pl.semaphore_signal(
                barrier, inc=1, device_id=line.peer(right), device_id_type=pl.DeviceIdType.MESH
            )

    inner = (line.me > 0) & (line.me < line.reach)

    @pl.when(inner)
    def _():
        pl.semaphore_wait(barrier, 2)

    @pl.when(jnp.logical_not(inner))
    def _():
        pl.semaphore_wait(barrier, 1)


def attend_back_kernel(
    sizes,
    size,
    early,
    hop,
    memory_fill,
    packed_fill,
    bias_ref,
    unit_ref,
    q_ref,
    k_ref,
    v_ref,
    log_ref,
    gm_ref,
    wq_ref,
    wk_ref,
    wv_ref,
    gain_ref,
    gsecond_ref,
    branch_hbm,
    res_hbm,
    gunit_ref,
    gq_ref,
    gk_ref,
    gv_ref,
    small_ref,
    early_ref,
    strip,
    live,
    dk_sum,
    dv_sum,
    dq_low,
    dk_low,
    dv_low,
    strip_sum,
    branch_ref,
    res_ref,
    held_right,
    held_left,
    total_ref,
    load_sem,
    line_s,
    right_r,
    left_r,
):
    seg_len, mem_len, packed_len, heads, head_dim = sizes
    kept = mem_len + packed_len
    keys = kept + seg_len
    stream = pl.program_id(0)
    scale = 1.0 / math.sqrt(head_dim)

    line = Line(size, early, hop)
    lanes_out = ((True, held_right, (line_s.at[0], right_r)), (False, held_left, (line_s.at[1], left_r)))
    loads = (
        pltpu.make_async_copy(branch_hbm.at[pl.ds(0, early * size)], branch_ref, load_sem.at[0]),
        pltpu.make_async_copy(res_hbm.at[pl.ds(0, early)], res_ref, load_sem.at[1]),
    )
    ticks = line.reach * (early - 1) + hop * line.reach + 1
    spans = heads * (seg_len // query_block)
    starts = [22 * index for index in range(spans + 1)]
    starts += [starts[-1] + 6, starts[-1] + 17, starts[-1] + 28, starts[-1] + 36]

    def line_step(tick, _):
        line.scatter_step(tick, branch_ref, lanes_out)
        chunk, due = line.chunk_at(tick - hop * line.reach)

        @pl.when(due)
        def _():
            line.scatter_sum(chunk, branch_ref, lanes_out, total_ref)
            early_ref[chunk] = (res_ref[chunk] + total_ref[...]).astype(bf16).astype(f32)

        return 0

    def line_span(index):
        every = starts[-1] * pl.num_programs(0)
        here, after = stream * starts[-1] + starts[index], stream * starts[-1] + starts[index + 1]
        lax.fori_loop((here * ticks) // every, (after * ticks) // every, line_step, 0)

    @pl.when(stream == 0)
    def _():
        for load in loads:
            load.start()
        meet(line)
        for load in loads:
            load.wait()
        strip_sum[...] = jnp.zeros_like(strip_sum)
        gq_ref[...] = jnp.zeros_like(gq_ref)
        gk_ref[...] = jnp.zeros_like(gk_ref)
        gv_ref[...] = jnp.zeros_like(gv_ref)

    live[...] = live_mask((kept, block), 0, packed_len, mem_len, packed_fill[stream], memory_fill[stream])
    subs = query_block // block
    for head in range(heads):
        lanes = slice(head * head_dim, (head + 1) * head_dim)
        for column in range(diagonal_count(seg_len, kept)):
            strip[column * block : (column + 1) * block, :] = bias_block(
                bias_ref, head, diagonal_of(seg_len, kept, column), True
            )
        for index in range(seg_len // query_block):
            line_span(head * (seg_len // query_block) + index)
            reach = kept + (index + 1) * query_block
            rows = slice(index * query_block, (index + 1) * query_block)
            queries = q_ref[0, rows, lanes]
            grads = gm_ref[0, rows, lanes]
            key_rows = k_ref[0, :reach, lanes]
            score = mm_t1(key_rows, queries) * scale
            firsts = [strip_start(seg_len, index * subs + sub) for sub in range(subs)]
            score = score + jnp.concatenate([strip[first : first + reach, :] for first in firsts], axis=1)
            live_wide = jnp.concatenate([live[...]] * subs, axis=1)
            score = jnp.concatenate([score[:kept] + live_wide, score[kept:]], axis=0)
            prob = jnp.exp(score - log_ref[0, head, :, rows])
            grad_prob = mm_t1(v_ref[0, :reach, lanes], grads)
            delta = jnp.sum(prob * grad_prob, axis=0, keepdims=True)
            grad_score = (prob * (grad_prob - delta)).astype(bf16)
            dk_part = mm(grad_score, queries)
            dv_part = mm(prob.astype(bf16), grads)
            if index == seg_len // query_block - 1:
                earlier = kept + index * query_block
                if index:
                    dk_sum[:earlier] += dk_part[:earlier]
                    dv_sum[:earlier] += dv_part[:earlier]
                    dk_sum[earlier:] = dk_part[earlier:]
                    dv_sum[earlier:] = dv_part[earlier:]
                else:
                    dk_sum[...] = dk_part
                    dv_sum[...] = dv_part
            elif index:
                earlier = kept + index * query_block
                dk_sum[:earlier] += dk_part[:earlier]
                dv_sum[:earlier] += dv_part[:earlier]
                dk_sum[earlier:reach] = dk_part[earlier:]
                dv_sum[earlier:reach] = dv_part[earlier:]
            else:
                dk_sum[:reach] = dk_part
                dv_sum[:reach] = dv_part
            dq_low[rows, lanes] = (mm_t0(grad_score, key_rows) * scale).astype(bf16)
            for sub in range(subs):
                strip_sum[head, firsts[sub] : firsts[sub] + reach, :] += grad_score[
                    :, sub * block : (sub + 1) * block
                ].astype(f32)
        dk_low[:, lanes] = (dk_sum[...] * scale).astype(bf16)
        dv_low[:, lanes] = dv_sum[...].astype(bf16)
    line_span(spans)
    gq_ref[...] += mm_t0(dq_low[...], unit_ref[0, kept:, :])
    line_span(spans + 1)
    gk_ref[...] += mm_t0(dk_low[...], unit_ref[0])
    line_span(spans + 2)
    gv_ref[...] += mm_t0(dv_low[...], unit_ref[0])
    line_span(spans + 3)
    gunit_ref[0] = (
        mm_t1(dq_low[...], wq_ref[...])
        + mm_t1(dk_low[kept:, :], wk_ref[...])
        + mm_t1(dv_low[kept:, :], wv_ref[...])
    )

    @pl.when(stream == pl.num_programs(0) - 1)
    def _():
        line.scatter_drain(branch_ref, lanes_out)
        rows = lax.broadcasted_iota(jnp.int32, (block, block), 0)
        cols = lax.broadcasted_iota(jnp.int32, (block, block), 1)
        width = gain_ref.shape[1]
        lane = lax.broadcasted_iota(jnp.int32, (1, width), 1)
        relative = [jnp.zeros((1, width), f32) for _ in range(heads)]
        for head in range(heads):
            blocks = []
            for column in range(diagonal_count(seg_len, kept)):
                blocks.append(strip_sum[head, column * block : (column + 1) * block, :])
            for position, mark_value in enumerate(reach_marks):
                total = jnp.zeros((1, block), f32)
                for column, value in enumerate(blocks):
                    diagonal = diagonal_of(seg_len, kept, column)
                    lowest, highest = diagonal * block - block + 1, diagonal * block + block - 1
                    if mark_value <= lowest:
                        total = total + jnp.sum(value, axis=0, keepdims=True)
                    elif mark_value <= highest:
                        distance = diagonal * block + cols - rows
                        total = total + jnp.sum(
                            jnp.where(distance >= mark_value, value, 0.0), axis=0, keepdims=True
                        )
                total = jnp.sum(total, axis=1, keepdims=True)
                relative[head] = jnp.where(lane == position, total, relative[head])
        first = jnp.zeros((1, width), f32)
        for grad_ref, weight_ref in ((gq_ref, wq_ref), (gk_ref, wk_ref), (gv_ref, wv_ref)):
            turned = weight_ref[...].astype(f32).T
            first = first + jnp.sum(grad_ref[...] * turned, axis=0, keepdims=True)
        small_ref[...] = jnp.concatenate(
            [first / gain_ref[...], gsecond_ref[...], *relative, jnp.zeros((6 - heads, width), f32)], axis=0
        )


def attend_back(
    unit, q, k, v, log_total, grad_mixed, memory_fill, packed_fill, wq, wk, wv, bias, gain, grad_second, mem_len, packed_len,
    branch, residual, size, early,
):
    streams, keys, width = unit.shape
    seg_len, local = q.shape[1:]
    heads = bias.shape[0]
    kept = mem_len + packed_len
    sizes = (seg_len, mem_len, packed_len, heads, local // heads)
    smem = pl.BlockSpec(memory_space=pltpu.SMEM)
    strip_len = diagonal_count(seg_len, kept) * block
    part = (early * size, *branch.shape[1:])

    def rows_of(count, columns):
        return pl.BlockSpec((1, count, columns), lambda s: (s, 0, 0))

    def whole(shape):
        return pl.BlockSpec(shape, lambda s: (0,) * len(shape))

    return pl.pallas_call(
        functools.partial(attend_back_kernel, sizes, size, early, 3),
        grid=(streams,),
        in_specs=[
            smem,
            smem,
            smem,
            rows_of(keys, width),
            rows_of(seg_len, local),
            rows_of(keys, local),
            rows_of(keys, local),
            pl.BlockSpec((1, heads, 1, seg_len), lambda s: (s, 0, 0, 0)),
            rows_of(seg_len, local),
            whole(wq.shape),
            whole(wk.shape),
            whole(wv.shape),
            whole((1, width)),
            whole((1, width)),
            pl.BlockSpec(memory_space=pl.ANY),
            pl.BlockSpec(memory_space=pl.ANY),
        ],
        out_specs=[
            rows_of(seg_len, width),
            whole((local, width)),
            whole((local, width)),
            whole((local, width)),
            whole((8, width)),
            whole((early, *residual.shape[1:])),
        ],
        out_shape=[
            jax.ShapeDtypeStruct((streams, seg_len, width), f32),
            jax.ShapeDtypeStruct((local, width), f32),
            jax.ShapeDtypeStruct((local, width), f32),
            jax.ShapeDtypeStruct((local, width), f32),
            jax.ShapeDtypeStruct((8, width), f32),
            jax.ShapeDtypeStruct((early, *residual.shape[1:]), f32),
        ],
        scratch_shapes=[
            pltpu.VMEM((strip_len, block), f32),
            pltpu.VMEM((kept, block), f32),
            pltpu.VMEM((keys, local // heads), f32),
            pltpu.VMEM((keys, local // heads), f32),
            pltpu.VMEM((seg_len, local), bf16),
            pltpu.VMEM((keys, local), bf16),
            pltpu.VMEM((keys, local), bf16),
            pltpu.VMEM((heads, strip_len, block), f32),
            pltpu.VMEM(part, f32),
            pltpu.VMEM((early, *part[1:]), f32),
            pltpu.VMEM(part, f32),
            pltpu.VMEM(part, f32),
            pltpu.VMEM(part[1:], f32),
            pltpu.SemaphoreType.DMA((2,)),
            pltpu.SemaphoreType.DMA((2,)),
            pltpu.SemaphoreType.DMA((early * size,)),
            pltpu.SemaphoreType.DMA((early * size,)),
        ],
        compiler_params=pltpu.CompilerParams(
            collective_id=3, has_side_effects=True, vmem_limit_bytes=60 << 20
        ),
        cost_estimate=pl.CostEstimate(
            flops=streams * (8 * keys * width * local + 10 * seg_len * keys * local),
            bytes_accessed=streams * keys * (width * 2 + local * 6),
            transcendentals=streams * heads * seg_len * keys,
        ),
        name="attend_back",
    )(
        memory_fill,
        packed_fill,
        bias,
        unit,
        q,
        k,
        v,
        log_total,
        grad_mixed,
        wq,
        wk,
        wv,
        gain[None, :],
        grad_second,
        branch,
        residual,
    )


def feed_kernel(
    size,
    group,
    chunks,
    hop,
    delay,
    beat,
    mixed_ref,
    seg_hbm,
    grad_hbm,
    up_hbm,
    down_hbm,
    begun_ref,
    gain_ref,
    gm_ref,
    gres_ref,
    res_ref,
    branch_hbm,
    gdown_hbm,
    gup_hbm,
    gout_hbm,
    gsecond_ref,
    seg_ref,
    grad_ref,
    up_ref,
    down_ref,
    branch_ref,
    gdown_ref,
    gup_ref,
    gout_ref,
    acted,
    graded,
    normed_low,
    heads_in,
    part,
    held_right,
    held_left,
    swap_out,
    swap_in,
    weights_in,
    weights,
    chunk_rows,
    total,
    own_mixed,
    own_grad,
    *sems,
):
    line = Line(size, chunks, hop)
    me = line.me
    (line_s, hr_r, hl_r, sr_r, sl_r, swap_sem, wd_s, wd_r, load_sem, save_sem, branch_sem) = sems
    gather_lanes = ((True, (line_s.at[0], hr_r)), (False, (line_s.at[1], hl_r)))
    scatter_lanes = ((True, held_right, (line_s.at[2], sr_r)), (False, held_left, (line_s.at[3], sl_r)))
    loads = [
        pltpu.make_async_copy(source, target, load_sem.at[index])
        for index, (source, target) in enumerate(
            ((seg_hbm, seg_ref), (grad_hbm, grad_ref), (up_hbm, up_ref), (down_hbm, down_ref))
        )
    ]
    for load in loads:
        load.start()
    spread = Spread(size, group, weights_in, (None, None, wd_s, wd_r))
    bits = spread.bits
    piece, columns = weights_in.shape[3:]
    width = weights.shape[1]
    rows = total.shape[0]
    local = mixed_ref.shape[-1]
    greet(
        [spread.others(offset) for offset in range(1, size)]
        + [spread.partner(half, level) for half in range(2) for level in range(1, bits)]
    )
    for half in range(2):
        weights_in[half, pl.ds((spread.spots[half] // 2) * 2, 2)] = begun_ref[half]
        spread.within(half, 1, False).start()

    def stage_heads(chunk, _):
        heads_in[chunk * size + me] = mixed_ref[chunk].astype(f32)
        return 0

    lax.fori_loop(0, chunks, stage_heads, 0)
    gsecond_ref[...] = jnp.zeros_like(gsecond_ref)
    gdown_ref[...] = jnp.zeros_like(gdown_ref)
    gup_ref[...] = jnp.zeros_like(gup_ref)

    def weight_step(tick):
        for level in range(2, bits):

            @pl.when(tick == beat + level - 2)
            def _():
                spread.start_level(level)

    def weight_finish():
        for half in range(2):
            spread.within(half, bits - 1, True).wait_recv()
            for index in range(size):
                pieces = [weights_in[half, spread.place_of(half, member), index] for member in range(group)]
                weights[index * group * piece : (index + 1) * group * piece, half * columns : (half + 1) * columns] = (
                    jnp.concatenate(pieces, axis=0).astype(bf16)
                )

    own = pl.ds(pl.multiple_of(me * rows, rows), rows)

    def feed_chunk(chunk):
        heads = [heads_in[chunk * size + index].astype(bf16) for index in range(size)]
        for index in range(size):
            own_mixed[chunk, :, index * local : (index + 1) * local] = heads_in[
                chunk * size + index, own, :
            ].astype(bf16)
        residual = seg_ref[chunk].astype(f32) + mm(jnp.concatenate(heads, axis=1), weights[...])
        chunk_rows[...] = residual
        res_ref[chunk] = chunk_rows[own, :]
        ffn_input = (residual * row_scale(residual) * gain_ref[...]).astype(bf16)
        pre_act = mm(ffn_input, up_ref[...])
        inner = math.sqrt(2.0 / math.pi)
        squared = pre_act * pre_act
        tanh = jnp.tanh(inner * (pre_act + 0.044715 * pre_act * squared))
        activated = (0.5 * pre_act * (1.0 + tanh)).astype(bf16)
        slope = 0.5 * (1.0 + tanh) + 0.5 * pre_act * (1.0 - tanh * tanh) * (
            inner * (1.0 + 3.0 * 0.044715 * squared)
        )
        grads = grad_ref[chunk]
        grad_pre = (slope * mm_t1(grads, down_ref[...])).astype(bf16)
        first = pl.ds(chunk * size, size)
        part[first] = mm_t1(grad_pre, up_ref[...]).reshape(size, rows, width)
        acted[...] = activated
        graded[...] = grad_pre
        normed_low[...] = ffn_input

    def save_branch(chunk):
        here = pl.ds(chunk * size, size)
        return pltpu.make_async_copy(branch_ref.at[here], branch_hbm.at[here], branch_sem.at[chunk])

    def feed_branch(chunk):
        branch_ref[pl.ds(chunk * size, size)] = mm(acted[...], down_ref[...]).reshape(size, rows, width)
        save_branch(chunk).start()
        gdown_ref[...] += mm_t0(acted[...], grad_ref[chunk])

    def feed_grads(chunk):
        gup_ref[...] += mm_t0(normed_low[...], graded[...])

    saves = [
        pltpu.make_async_copy(source, target, save_sem.at[index])
        for index, (source, target) in enumerate(
            ((gdown_ref, gdown_hbm), (gup_ref, gup_hbm), (gout_ref, gout_hbm))
        )
    ]

    def swap(chunk, offset):
        target = lax.rem(me + offset, size)
        return pltpu.make_async_remote_copy(
            src_ref=swap_out.at[chunk * size + target],
            dst_ref=swap_in.at[chunk * size + me],
            send_sem=swap_sem.at[0],
            recv_sem=swap_sem.at[1],
            device_id={"mp": target},
            device_id_type=pl.DeviceIdType.MESH,
        )

    def all_swaps():
        some = pl.ds(0, chunks * (size - 1))
        return pltpu.make_async_remote_copy(
            src_ref=swap_out.at[some],
            dst_ref=swap_in.at[some],
            send_sem=swap_sem.at[0],
            recv_sem=swap_sem.at[1],
            device_id=spread.others(1),
            device_id_type=pl.DeviceIdType.MESH,
        )

    def settle(chunk):
        line.scatter_sum(chunk, part, scatter_lanes, total)
        grad_ffn = total[...]
        residual = res_ref[chunk]
        scale = row_scale(residual)
        normed = residual * scale
        gsecond_ref[...] += jnp.sum(grad_ffn * normed, axis=0, keepdims=True)
        weighted = grad_ffn * gain_ref[...]
        own_rows = grad_ref[chunk, own, :].astype(f32)
        grad_residual = own_rows + scale * (
            weighted - normed * jnp.mean(weighted * normed, axis=-1, keepdims=True)
        )
        gres_ref[chunk] = grad_residual
        low = grad_residual.astype(bf16)
        own_grad[chunk] = low
        grad_mixed = mm_t1(low, weights[...]).astype(bf16).astype(f32)
        for index in range(size):
            swap_out[chunk * size + index] = grad_mixed[:, index * local : (index + 1) * local]
        for offset in range(1, size):
            swap(chunk, offset).start()

    feed_at = hop * line.reach + delay

    def step(tick, _):
        weight_step(tick)

        @pl.when(tick == feed_at)
        def _():
            weight_finish()
            for load in loads:
                load.wait()

        chunk, due = line.chunk_at(tick)

        @pl.when(due)
        def _():
            line.gather_start(chunk, heads_in, gather_lanes)

        line.gather_step(tick, heads_in, gather_lanes)
        chunk_f, due_f = line.chunk_at(tick - feed_at)

        @pl.when(due_f)
        def _():
            feed_chunk(chunk_f)

        line.scatter_step(tick - feed_at, part, scatter_lanes)
        for late, work in ((1, feed_branch), (2, feed_grads)):
            chunk_w, due_w = line.chunk_at(tick - feed_at - late)

            @pl.when(due_w)
            def _():
                work(chunk_w)

        @pl.when(tick == feed_at + line.reach * (chunks - 1) + 3)
        def _():
            for save in saves[:2]:
                save.start()

        chunk_s, due_s = line.chunk_at(tick - feed_at - hop * line.reach)

        @pl.when(due_s)
        def _():
            settle(chunk_s)

        return 0

    lax.fori_loop(0, feed_at + line.reach * (chunks - 1) + hop * line.reach + 1, step, 0)
    gout_ref[...] = mm_t0(
        own_mixed[...].reshape(chunks * rows, width), own_grad[...].reshape(chunks * rows, width)
    )

    saves[2].start()
    all_swaps().wait_recv()

    def finish(chunk, _):
        save_branch(chunk).wait()
        for index in range(size):

            @pl.when(index == me)
            def _():
                gm_ref[chunk * size + index] = swap_out[chunk * size + index].astype(bf16)

            @pl.when(index != me)
            def _():
                gm_ref[chunk * size + index] = swap_in[chunk * size + index].astype(bf16)

        return 0

    lax.fori_loop(0, chunks, finish, 0)
    line.gather_drain(heads_in, gather_lanes)
    line.scatter_drain(part, scatter_lanes)
    all_swaps().wait_send()
    for save in saves:
        save.wait()
    for half in range(2):
        for level in range(1, bits):
            spread.within(half, level, False).wait_send()


def feed(mixed, seg_rows, grad_rows, up, down, begun, gain, size, group, chunks):
    rows, width = seg_rows.shape
    local = mixed.shape[1]
    chunk = rows // chunks
    piece = chunk // size
    hidden = up.shape[1]
    vmem = pl.BlockSpec(memory_space=pltpu.VMEM)
    anywhere = pl.BlockSpec(memory_space=pl.ANY)
    dma = pltpu.SemaphoreType.DMA
    slots = dma((chunks * size,))
    bits = group.bit_length() - 1
    return pl.pallas_call(
        functools.partial(feed_kernel, size, group, chunks, 2, 0, 4),
        in_specs=[vmem] + [anywhere] * 4 + [vmem] * 2,
        out_specs=[vmem] * 3 + [anywhere] * 4 + [vmem],
        out_shape=[
            jax.ShapeDtypeStruct((chunks * size, piece, local), bf16),
            jax.ShapeDtypeStruct((chunks, piece, width), f32),
            jax.ShapeDtypeStruct((chunks, piece, width), f32),
            jax.ShapeDtypeStruct((chunks * size, piece, width), f32),
            jax.ShapeDtypeStruct((hidden, width), f32),
            jax.ShapeDtypeStruct((width, hidden), f32),
            jax.ShapeDtypeStruct((width, width), f32),
            jax.ShapeDtypeStruct((1, width), f32),
        ],
        scratch_shapes=[
            pltpu.VMEM((chunks, chunk, width), bf16),
            pltpu.VMEM((chunks, chunk, width), bf16),
            pltpu.VMEM(up.shape, bf16),
            pltpu.VMEM(down.shape, bf16),
            pltpu.VMEM((chunks * size, piece, width), f32),
            pltpu.VMEM((hidden, width), f32),
            pltpu.VMEM((width, hidden), f32),
            pltpu.VMEM((width, width), f32),
            pltpu.VMEM((chunk, hidden), bf16),
            pltpu.VMEM((chunk, hidden), bf16),
            pltpu.VMEM((chunk, width), bf16),
            pltpu.VMEM((chunks * size, chunk, local), f32),
            pltpu.VMEM((chunks * size, piece, width), f32),
            pltpu.VMEM((chunks * size, piece, width), f32),
            pltpu.VMEM((chunks * size, piece, width), f32),
            pltpu.VMEM((chunks * size, piece, local), f32),
            pltpu.VMEM((chunks * size, piece, local), f32),
            pltpu.VMEM((2, group, *begun.shape[2:]), f32),
            pltpu.VMEM((width, width), bf16),
            pltpu.VMEM((chunk, width), f32),
            pltpu.VMEM((piece, width), f32),
            pltpu.VMEM((chunks, piece, width), bf16),
            pltpu.VMEM((chunks, piece, width), bf16),
        ]
        + [dma((4,))]
        + [slots] * 4
        + [dma((2,)), dma((2 * bits,)), dma((2 * bits,)), dma((4,)), dma((3,)), dma((chunks,))],
        compiler_params=pltpu.CompilerParams(
            collective_id=0, has_side_effects=True, vmem_limit_bytes=63 << 20
        ),
        name="feed",
    )(
        mixed.reshape(chunks, chunk, local),
        seg_rows.reshape(chunks, chunk, width),
        grad_rows.reshape(chunks, chunk, width),
        up,
        down,
        begun,
        gain[None, :],
    )


class Pieces:
    def __init__(self, group, rows, gap, crossing, jobs, work, landing, summed, sems):
        self.mine = lax.axis_index("dp")
        self.bits = group.bit_length() - 1
        self.rows, self.gap, self.crossing, self.jobs = rows, gap, crossing, jobs
        self.work, self.landing, self.summed = work, landing, summed
        self.slots = work.shape[0]
        (self.rs_s, self.rs_r, self.ag_s, self.ag_r, self.load_sem, self.store_sem) = sems
        self.count = crossing[0] + sum(job[2] for job in jobs)
        self.turned = self.count - sum(job[2] for job in jobs if job[1].shape != job[0].shape)
        self.beats = self.count + 2 * self.bits * gap + 2

    def step_of(self, odd, level):
        even_step = 1 << level
        odd_step = 1 << ((self.bits - level) % self.bits)
        return jnp.where(odd == 1, odd_step, even_step)

    def bit_of(self, odd, level):
        return (self.mine // self.step_of(odd, level)) % 2

    def partner(self, odd, level):
        step = self.step_of(odd, level)
        return {"dp": self.mine + step - 2 * step * self.bit_of(odd, level)}

    def start_of(self, odd, level):
        start = jnp.int32(0)
        for earlier in range(level):
            start = start + self.bit_of(odd, earlier) * (self.rows >> (earlier + 1))
        return start

    def span(self, start, level):
        length = self.rows >> level
        return pl.ds(pl.multiple_of(start, self.rows >> self.bits), length)

    def halves(self, odd, level):
        start, bit, half = self.start_of(odd, level), self.bit_of(odd, level), self.rows >> (level + 1)
        return self.span(start + bit * half, level + 1), self.span(start + (1 - bit) * half, level + 1)

    def reduce_copy(self, slot, odd, level):
        _, give = self.halves(odd, level)
        region = pl.ds(self.rows - (self.rows >> level), self.rows >> (level + 1))
        return pltpu.make_async_remote_copy(
            src_ref=self.work.at[slot, give],
            dst_ref=self.landing.at[slot, region],
            send_sem=self.rs_s.at[slot * self.bits + level],
            recv_sem=self.rs_r.at[slot * self.bits + level],
            device_id=self.partner(odd, level),
            device_id_type=pl.DeviceIdType.MESH,
        )

    def absorb(self, slot, odd, level):
        self.reduce_copy(slot, odd, level).wait_recv()
        keep, _ = self.halves(odd, level)
        region = pl.ds(self.rows - (self.rows >> level), self.rows >> (level + 1))
        self.work[slot, keep, :] = self.work[slot, keep, :] + self.landing[slot, region, :]

    def spread_copy(self, buffer, sems, slot, odd, level, arriving):
        keep, give = self.halves(odd, level)
        span = give if arriving else keep
        return pltpu.make_async_remote_copy(
            src_ref=buffer.at[slot, span],
            dst_ref=buffer.at[slot, span],
            send_sem=sems[0].at[slot * self.bits + level],
            recv_sem=sems[1].at[slot * self.bits + level],
            device_id=self.partner(odd, level),
            device_id_type=pl.DeviceIdType.MESH,
        )

    def spread(self, slot, odd, level, arriving):
        return self.spread_copy(self.summed, (self.ag_s, self.ag_r), slot, odd, level, arriving)

    def move(self, piece, slot, store, start):
        columns = self.work.shape[2]
        first = self.crossing[0]
        sources = [(self.crossing[1], None, 0, first)]
        for source, target, count in self.jobs:
            sources.append((source, target, first, first + count))
            first += count
        for source, target, low, high in sources:
            if store and target is None:
                continue

            @pl.when((piece >= low) & (piece < high))
            def _():
                across = source.shape[2] // columns
                index = (piece - low) // across
                lanes = pl.ds(pl.multiple_of((piece - low - index * across) * columns, columns), columns)
                inside = self.summed.at[slot] if store else self.work.at[slot]
                if store and target.shape != source.shape:
                    copy = pltpu.make_async_copy(inside, target.at[piece - low], self.store_sem.at[slot])
                elif store:
                    copy = pltpu.make_async_copy(inside, target.at[index, :, lanes], self.store_sem.at[slot])
                else:
                    copy = pltpu.make_async_copy(source.at[index, :, lanes], inside, self.load_sem.at[slot])
                copy.start() if start else copy.wait()

    def load_first(self):
        self.move(jnp.int32(0), 0, False, True)

    def step(self, tick, cross):
        bits = self.bits
        for age in reversed(range(-1, 2 * bits + 2)):
            piece = tick - (age if age < 0 else min(age * self.gap, 2 * bits * self.gap + 1))
            safe = jnp.maximum(piece, 0)
            slot, odd = safe % self.slots, safe % 2
            plain = piece >= self.crossing[0]
            inside = (piece >= 0) & (piece < self.count)
            if age == 2 * bits + 1:

                @pl.when(inside)
                def _():
                    for level in range(bits):
                        self.reduce_copy(slot, odd, level).wait_send()

                @pl.when(inside & plain)
                def _():
                    self.move(piece, slot, True, False)

                @pl.when(inside & jnp.logical_not(plain))
                def _():
                    cross(piece, slot, odd, False)

            elif age == 2 * bits:

                @pl.when(inside & plain)
                def _():
                    self.spread(slot, odd, 0, True).wait_recv()
                    for level in range(bits):
                        self.spread(slot, odd, level, False).wait_send()

                    @pl.when(piece >= self.turned)
                    def _():
                        self.summed[slot] = self.summed[slot].T

                    self.move(piece, slot, True, True)

            elif age > bits:

                @pl.when(inside & plain)
                def _():
                    self.spread(slot, odd, 2 * bits - age, True).wait_recv()
                    self.spread(slot, odd, 2 * bits - 1 - age, False).start()

            elif age == bits:

                @pl.when(inside)
                def _():
                    self.absorb(slot, odd, bits - 1)

                @pl.when(inside & plain)
                def _():
                    own = self.span(self.start_of(odd, bits), bits)
                    self.summed[slot, own, :] = self.work[slot, own, :]
                    self.spread(slot, odd, bits - 1, False).start()

                @pl.when(inside & jnp.logical_not(plain))
                def _():
                    cross(piece, slot, odd, True)

            elif age > 0:

                @pl.when(inside)
                def _():
                    self.absorb(slot, odd, age - 1)
                    self.reduce_copy(slot, odd, age).start()

            elif age == 0:

                @pl.when(inside)
                def _():
                    self.move(piece, slot, False, False)
                    self.reduce_copy(slot, odd, 0).start()

            else:

                @pl.when(inside)
                def _():
                    self.move(piece, slot, False, True)


def close_kernel(
    size,
    group,
    chunks,
    hop,
    counts,
    gap,
    early,
    gunit_hbm,
    branch_hbm,
    seg_hbm,
    gres_hbm,
    res_hbm,
    gain_ref,
    early_ref,
    gout_ref,
    gup_ref,
    gdown_ref,
    gq_ref,
    gk_ref,
    gv_ref,
    gpack_ref,
    small_ref,
    result_ref,
    gseg_ref,
    gout_sum,
    gup_sum,
    gdown_sum,
    gq_sum,
    gk_sum,
    gv_sum,
    gpack_sum,
    small_sum,
    gunit_ref,
    branch_ref,
    seg_ref,
    gres_ref,
    res_ref,
    whole_seg,
    whole_out,
    seg_right,
    seg_left,
    out_right,
    out_left,
    total,
    work,
    landing,
    summed,
    cross_in,
    cross_work,
    small_cross,
    small_held,
    small_in,
    *sems,
):
    line = Line(size, chunks, hop)
    me = line.me
    line_s, recvs, sems = sems[0], sems[1:9], sems[9:]
    seg_scatter = ((True, seg_right, (line_s.at[0], recvs[0])), (False, seg_left, (line_s.at[1], recvs[1])))
    out_scatter = ((True, out_right, (line_s.at[2], recvs[2])), (False, out_left, (line_s.at[3], recvs[3])))
    seg_gather = ((True, (line_s.at[4], recvs[4])), (False, (line_s.at[5], recvs[5])))
    out_gather = ((True, (line_s.at[6], recvs[6])), (False, (line_s.at[7], recvs[7])))
    piece_sems = sems[:6]
    cross_s, cross_r, tail_s, tail_r, tail_store = sems[6:11]
    mix_s, mix_r, small_s, small_r = sems[11:15]
    seg_load, out_load, load_sem = sems[15:18]
    loads = [
        pltpu.make_async_copy(source, target, load_sem.at[index])
        for index, (source, target) in enumerate(((seg_hbm, seg_ref), (gres_hbm, gres_ref), (res_hbm, res_ref)))
    ]

    def part_load(source, target, load, chunk):
        here = pl.ds(chunk * size, size)
        return pltpu.make_async_copy(source.at[here], target.at[here], load.at[chunk])

    for chunk in range(chunks):
        part_load(gunit_hbm, gunit_ref, seg_load, chunk).start()
        if chunk >= early:
            part_load(branch_hbm, branch_ref, out_load, chunk).start()
    for load in loads:
        load.start()
    jobs = [
        (gup_ref, gup_sum, counts[1]),
        (gdown_ref, gdown_sum, counts[2]),
        (gq_ref, gq_sum, counts[3]),
        (gk_ref, gk_sum, counts[4]),
        (gv_ref, gv_sum, counts[5]),
        (gpack_ref, gpack_sum, counts[6]),
    ]
    pieces = Pieces(group, work.shape[1], gap, (counts[0], gout_ref), jobs, work, landing, summed, piece_sems)
    bits = pieces.bits
    pieces.load_first()
    greet(
        [{"mp": lax.rem(me + offset, size)} for offset in range(1, size)]
        + [{"dp": pieces.mine + (1 << bit) - 2 * (1 << bit) * ((pieces.mine // (1 << bit)) % 2)} for bit in range(bits)]
    )

    across, columns = cross_work.shape[0], work.shape[2]

    def cross_copy(slot, column, target, origin):
        own = pieces.span(pieces.start_of(column % 2, bits), bits)
        return pltpu.make_async_remote_copy(
            src_ref=work.at[slot, own],
            dst_ref=cross_in.at[column * size + origin],
            send_sem=cross_s.at[column * size + target],
            recv_sem=cross_r.at[column * size + origin],
            device_id={"mp": target},
            device_id_type=pl.DeviceIdType.MESH,
        )

    def cross(piece, slot, odd, start):
        target, column = piece // across, piece % across

        @pl.when(target != me)
        def _():
            copy = cross_copy(slot, column, target, me)
            copy.start() if start else copy.wait_send()

        if start:

            @pl.when(target == me)
            def _():
                own = pieces.span(pieces.start_of(odd, bits), bits)
                cross_in[column * size + me] = work[slot, own, :]

    def tail_copy(column):
        return pltpu.make_async_copy(
            cross_work.at[column],
            gout_sum.at[0, :, column * columns : (column + 1) * columns],
            tail_store.at[column],
        )

    def tail_spread(column, level, arriving):
        return pieces.spread_copy(cross_work, (tail_s, tail_r), column, column % 2, level, arriving)

    def tail_step(tick):
        base = counts[0] + bits * gap + gap
        for column in range(across):

            @pl.when(tick == base + column)
            def _():
                for offset in range(1, size):
                    cross_copy(0, column, me, lax.rem(me + offset, size)).wait_recv()
                own = pieces.span(pieces.start_of(column % 2, bits), bits)
                cross_work[column, own, :] = (
                    sum(cross_in[column * size + index] for index in range(1, size)) + cross_in[column * size]
                )
                tail_spread(column, bits - 1, False).start()

            for level in reversed(range(bits)):

                @pl.when(tick == base + column + (bits - level) * gap)
                def _():
                    tail_spread(column, level, True).wait_recv()
                    if level:
                        tail_spread(column, level - 1, False).start()
                    else:
                        tail_copy(column).start()

    def small_across(offset, arriving):
        origin = lax.rem(me - offset + size, size) if arriving else me
        return pltpu.make_async_remote_copy(
            src_ref=small_cross.at[me],
            dst_ref=small_cross.at[origin],
            send_sem=mix_s.at[offset],
            recv_sem=mix_r.at[offset],
            device_id={"mp": lax.rem(me + offset, size)},
            device_id_type=pl.DeviceIdType.MESH,
        )

    def small_within(level):
        step = 1 << level
        return pltpu.make_async_remote_copy(
            src_ref=small_held.at[level],
            dst_ref=small_in.at[level],
            send_sem=small_s.at[level],
            recv_sem=small_r.at[level],
            device_id={"dp": pieces.mine + step - 2 * step * ((pieces.mine // step) % 2)},
            device_id_type=pl.DeviceIdType.MESH,
        )

    def small_step(tick):
        @pl.when(tick == 0)
        def _():
            small_cross[me] = small_ref[...]
            for offset in range(1, size):
                small_across(offset, False).start()

        @pl.when(tick == 2)
        def _():
            value = small_ref[...]
            shared = lax.broadcasted_iota(jnp.int32, value.shape, 0) < 2
            for offset in range(1, size):
                small_across(offset, True).wait_recv()
                origin = lax.rem(me - offset + size, size)
                value = value + jnp.where(shared, small_cross[origin], 0.0)
            small_held[0] = value
            small_within(0).start()

        for level in range(bits):

            @pl.when(tick == 4 + 2 * level)
            def _():
                small_within(level).wait_recv()
                value = small_held[level] + small_in[level]
                if level + 1 < bits:
                    small_held[level + 1] = value
                    small_within(level + 1).start()
                else:
                    small_sum[...] = value

    def settle_seg(chunk):
        slot = chunk * size + me
        line.scatter_sum(chunk, gunit_ref, seg_scatter, total)
        rows = seg_ref[slot].astype(f32)
        scale = row_scale(rows)
        normed = rows * scale
        weighted = total[...] * gain_ref[...]
        grad = gres_ref[chunk] + scale * (
            weighted - normed * jnp.mean(weighted * normed, axis=-1, keepdims=True)
        )
        low = grad.astype(bf16)
        gseg_ref[slot] = low
        whole_seg[slot] = low.astype(f32)
        line.gather_start(chunk, whole_seg, seg_gather)

    def settle_out(chunk):
        slot = chunk * size + me

        @pl.when(chunk < early)
        def _():
            total[...] = early_ref[jnp.minimum(chunk, early - 1)]

        @pl.when(chunk >= early)
        def _():
            line.scatter_sum(chunk, branch_ref, out_scatter, total)
            total[...] = res_ref[chunk] + total[...]

        low = total[...].astype(bf16)
        result_ref[slot] = low
        whole_out[slot] = low.astype(f32)
        line.gather_start(chunk, whole_out, out_gather)

    def seg_landed(slot):
        gseg_ref[slot] = whole_seg[slot].astype(bf16)

    def out_landed(slot):
        result_ref[slot] = whole_out[slot].astype(bf16)

    settle_at = hop * line.reach
    seg_lag, out_lag = 0, -line.reach * early

    def step(tick, _):
        flows = (
            (seg_lag, gunit_hbm, seg_load, gunit_ref, seg_scatter, settle_seg, whole_seg, seg_gather, seg_landed),
            (out_lag, branch_hbm, out_load, branch_ref, out_scatter, settle_out, whole_out, out_gather, out_landed),
        )
        @pl.when(tick == 0)
        def _():
            for load in loads:
                load.wait()

        for late, source, load, part, scatter, settle, whole, gather, landed in flows:
            fresh, new = line.chunk_at(tick - late)

            first = early if late < 0 else 0

            @pl.when(new & (fresh >= first))
            def _():
                part_load(source, part, load, fresh).wait()

            line.scatter_step(tick - late, part, scatter, first)
            chunk, due = line.chunk_at(tick - late - settle_at)

            @pl.when(due)
            def _():
                settle(chunk)

        for late, source, load, part, scatter, settle, whole, gather, landed in flows:
            line.gather_step(tick - late - settle_at, whole, gather, landed)
        small_step(tick)

        def piece_step(beat, _):
            pieces.step(beat, cross)
            tail_step(beat)
            return 0

        lax.fori_loop(beats(tick), beats(tick + 1), piece_step, 0)
        return 0

    line_ticks = line.reach * (chunks - 1) + 2 * settle_at + 1

    def beats(tick):
        return jnp.minimum((tick * pieces.beats) // (line_ticks - 5), pieces.beats)

    lax.fori_loop(0, line_ticks, step, 0)

    line.scatter_drain(gunit_ref, seg_scatter)
    line.scatter_drain(branch_ref, out_scatter, early)
    line.gather_drain(whole_seg, seg_gather)
    line.gather_drain(whole_out, out_gather)
    for column in range(across):
        for level in range(bits):
            tail_spread(column, level, False).wait_send()
        tail_copy(column).wait()
    for offset in range(1, size):
        small_across(offset, False).wait_send()
    for level in range(bits):
        small_within(level).wait_send()


def close(
    grad_unit, branch, seg_rows, grad_residual, residual, gain, early, grads, small, size, group, chunks
):
    rows, width = seg_rows.shape
    piece = rows // (chunks * size)
    vmem = pl.BlockSpec(memory_space=pltpu.VMEM)
    whole = (chunks * size, piece, width)
    piece_rows, columns, gap = max(256, 8 * group), width // 4, 3 if group <= 8 else 2
    bits = group.bit_length() - 1
    slots = 2 * bits * gap + 2
    views = [grad.reshape(-1, piece_rows, grad.shape[1]) for grad in grads]
    counts = tuple(view.shape[0] * (view.shape[2] // columns) for view in views)
    anywhere = pl.BlockSpec(memory_space=pl.ANY)
    dma = pltpu.SemaphoreType.DMA
    sums = [jax.ShapeDtypeStruct(view.shape, f32) for view in views]
    sums[0] = jax.ShapeDtypeStruct((1, piece_rows, width), f32)
    for index in range(3, len(views)):
        turned_shape = (views[index].shape[2] // columns, columns, piece_rows)
        sums[index] = jax.ShapeDtypeStruct(turned_shape, f32)
    return pl.pallas_call(
        functools.partial(close_kernel, size, group, chunks, 2, counts, gap, early.shape[0]),
        in_specs=[anywhere] * 5 + [vmem] * 2 + [anywhere] * len(views) + [vmem],
        out_specs=[vmem] * 2 + [anywhere] * len(views) + [vmem],
        out_shape=[jax.ShapeDtypeStruct(whole, bf16)] * 2 + sums + [jax.ShapeDtypeStruct(small.shape, f32)],
        scratch_shapes=[pltpu.VMEM(whole, f32)] * 2
        + [
            pltpu.VMEM(whole, bf16),
            pltpu.VMEM(grad_residual.shape, f32),
            pltpu.VMEM(grad_residual.shape, f32),
        ]
        + [pltpu.VMEM(whole, f32)] * 6
        + [
            pltpu.VMEM((piece, width), f32),
            pltpu.VMEM((slots, piece_rows, columns), f32),
            pltpu.VMEM((slots, piece_rows, columns), f32),
            pltpu.VMEM((slots, piece_rows, columns), f32),
            pltpu.VMEM((width // columns * size, piece_rows // group, columns), f32),
            pltpu.VMEM((width // columns, piece_rows, columns), f32),
            pltpu.VMEM((size, *small.shape), f32),
            pltpu.VMEM((bits, *small.shape), f32),
            pltpu.VMEM((bits, *small.shape), f32),
        ]
        + [dma((8,))]
        + [dma((chunks * size,))] * 8
        + [dma((slots * bits,))] * 4
        + [dma((slots,))] * 2
        + [dma((width // columns * size,))] * 2
        + [dma((width // columns * bits,))] * 2
        + [dma((width // columns,))]
        + [dma((size,))] * 2
        + [dma((bits,))] * 2
        + [dma((chunks,))] * 2
        + [dma((3,))],
        compiler_params=pltpu.CompilerParams(
            collective_id=1, has_side_effects=True, vmem_limit_bytes=63 << 20
        ),
        cost_estimate=pl.CostEstimate(flops=10**11, bytes_accessed=10**9, transcendentals=0),
        name="close",
    )(
        grad_unit.reshape(whole),
        branch,
        seg_rows.reshape(whole),
        grad_residual,
        residual,
        gain[None, :],
        early,
        *views,
        small,
    )


def body(
    inputs,
    memory,
    compressed_memory,
    memory_fill,
    compressed_fill,
    first_gain,
    query_weight,
    key_weight,
    value_weight,
    relative_bias,
    output_weight,
    second_gain,
    up_weight,
    down_weight,
    compress_weight,
    grad_output,
    grad_compressed,
    *,
    mp_size,
    dp_size,
):
    streams, seg_len, width = inputs.shape
    mem_len = memory.shape[1]
    packed_len = compressed_memory.shape[1]
    local = query_weight.shape[1]
    rows = streams * seg_len
    unit, q, k, v, mixed, log_total, packed_new, grad_pack, begun = attend(
        inputs,
        memory,
        compressed_memory,
        memory_fill,
        compressed_fill,
        first_gain,
        query_weight,
        key_weight,
        value_weight,
        relative_bias,
        compress_weight,
        grad_compressed,
        output_weight,
        mp_size,
        dp_size,
    )
    seg_rows = inputs.reshape(rows, width)
    grad_mixed, grad_residual, residual, branch, grad_down, grad_up, grad_out_full, grad_second = feed(
        mixed.reshape(rows, local),
        seg_rows,
        grad_output.reshape(rows, width),
        up_weight,
        down_weight,
        begun,
        second_gain,
        mp_size,
        dp_size,
        chunk_count,
    )
    grad_mixed = grad_mixed.reshape(streams, seg_len, local)
    grad_unit, gq, gk, gv, small, early = attend_back(
        unit,
        q,
        k,
        v,
        log_total,
        grad_mixed,
        memory_fill,
        compressed_fill,
        query_weight,
        key_weight,
        value_weight,
        relative_bias,
        first_gain,
        grad_second,
        mem_len,
        packed_len,
        branch,
        residual,
        mp_size,
        early_chunks,
    )
    result, grad_seg, grad_out_w, grad_up, grad_down, gq, gk, gv, grad_pack, small = close(
        grad_unit,
        branch,
        seg_rows,
        grad_residual,
        residual,
        first_gain,
        early,
        (grad_out_full, grad_up, grad_down, gq, gk, gv, grad_pack),
        small,
        mp_size,
        dp_size,
        chunk_count,
    )
    grad_first, grad_second = small[0], small[1]
    grad_relative = small[2 : 2 + relative_bias.shape[0], : relative_bias.shape[1]]
    result = result.reshape(inputs.shape)
    grad_seg = grad_seg.reshape(inputs.shape)
    grad_query_w, grad_key_w, grad_value_w = (grad.reshape(width, local) for grad in (gq, gk, gv))
    grad_out_w = grad_out_w.reshape(local, width)
    grad_compress_w = grad_pack.reshape(2 * width, local)
    grad_up = grad_up.reshape(up_weight.shape)
    grad_down = grad_down.reshape(down_weight.shape)
    return (
        result,
        packed_new,
        grad_seg,
        grad_first,
        grad_query_w,
        grad_key_w,
        grad_value_w,
        grad_relative,
        grad_out_w,
        grad_second,
        grad_up,
        grad_down,
        grad_compress_w,
    )


def solution(mesh):
    in_specs = (
        P("dp", None, None),
        P("dp", None, None),
        P("dp", None, None),
        P("dp"),
        P("dp"),
        P(),
        P(None, "mp"),
        P(None, "mp"),
        P(None, "mp"),
        P("mp", None),
        P("mp", None),
        P(),
        P(None, "mp"),
        P("mp", None),
        P(None, "mp"),
        P("dp", None, None),
        P("dp", None, "mp"),
    )
    out_specs = (
        P("dp", None, None),
        P("dp", None, "mp"),
        P("dp", None, None),
        P(),
        P(None, "mp"),
        P(None, "mp"),
        P(None, "mp"),
        P("mp", None),
        P("mp", None),
        P(),
        P(None, "mp"),
        P("mp", None),
        P(None, "mp"),
    )
    return jax.shard_map(
        functools.partial(body, mp_size=mesh.shape["mp"], dp_size=mesh.shape["dp"]),
        mesh=mesh,
        in_specs=in_specs,
        out_specs=out_specs,
        check_vma=False,
    )
```

```python
import functools
import math

import jax
import jax.numpy as jnp
from jax import lax
from jax.experimental import pallas as pl
from jax.experimental.pallas import tpu as pltpu
from jax.sharding import PartitionSpec as P

reach_marks = (1, 2, 3, 4, 5, 6, 7, 8, 12, 16, 24, 32, 48, 64, 96, 128, 192, 256, 384, 512, 768, 1024)
epsilon = 1e-06
masked_score = -1e30
block = 128
query_block = 256
chunk_count = 8
early_chunks = 2
f32 = jnp.float32
bf16 = jnp.bfloat16


def mm(left, right):
    return jnp.dot(left, right, preferred_element_type=f32)


def mm_t0(left, right):
    return lax.dot_general(left, right, (((0,), (0,)), ((), ())), preferred_element_type=f32)


def mm_t1(left, right):
    return lax.dot_general(left, right, (((1,), (1,)), ((), ())), preferred_element_type=f32)


def row_scale(source):
    return lax.rsqrt(jnp.mean(source * source, axis=-1, keepdims=True) + epsilon)


def diagonal_count(seg_len, kept_count):
    return (seg_len + kept_count) // block + 1


def diagonal_of(seg_len, kept_count, column):
    return (seg_len + kept_count) // block - 1 - column


def strip_start(seg_len, sub_block):
    return (seg_len // block - 1 - sub_block) * block


def bias_block(bias_ref, head, diagonal, transposed):
    rows = lax.broadcasted_iota(jnp.int32, (block, block), 0)
    cols = lax.broadcasted_iota(jnp.int32, (block, block), 1)
    distance = diagonal * block + ((cols - rows) if transposed else (rows - cols))
    lowest, highest = diagonal * block - block + 1, diagonal * block + block - 1
    base = jnp.float32(0.0)
    for position, mark_value in enumerate(reach_marks):
        if mark_value <= lowest:
            base = base + bias_ref[head, position]
    value = jnp.full((block, block), base, f32)
    for position, mark_value in enumerate(reach_marks):
        if lowest < mark_value <= highest:
            value = value + jnp.where(distance >= mark_value, bias_ref[head, position], 0.0)
    if lowest < 0:
        value = jnp.where(distance >= 0, value, masked_score)
    return value


def live_mask(shape, axis, packed_len, mem_len, packed_count, memory_count):
    slot = lax.broadcasted_iota(jnp.int32, shape, axis)
    dead_packed = (slot < packed_len) & (slot < packed_len - packed_count)
    dead_memory = (slot >= packed_len) & (slot < packed_len + mem_len - memory_count)
    return jnp.where(dead_packed | dead_memory, masked_score, 0.0).astype(f32)


def call(peers):
    barrier = pltpu.get_barrier_semaphore()
    for peer in peers:
        pl.semaphore_signal(barrier, inc=1, device_id=peer, device_id_type=pl.DeviceIdType.MESH)


def hear(peers):
    pl.semaphore_wait(pltpu.get_barrier_semaphore(), len(peers))


def greet(peers):
    call(peers)
    hear(peers)


class Spread:
    def __init__(self, size, group, buffer, sems):
        self.me, self.mine = lax.axis_index("mp"), lax.axis_index("dp")
        self.size, self.group, self.buffer = size, group, buffer
        self.bits = group.bit_length() - 1
        self.across_s, self.across_r, self.within_s, self.within_r = sems
        order = list(reversed(range(self.bits)))
        self.orders = (order, order[1::-1] + order[2:])
        self.spots = []
        for order in self.orders:
            spot = jnp.int32(0)
            for level, bit in enumerate(order):
                spot = spot + ((self.mine // (1 << bit)) % 2) * (1 << level)
            self.spots.append(spot)

    def place_of(self, half, member):
        return sum(((member >> bit) & 1) << level for level, bit in enumerate(self.orders[half]))

    def others(self, offset):
        return {"mp": lax.rem(self.me + offset, self.size)}

    def partner(self, half, level):
        step = 1 << self.orders[half][level]
        return {"dp": self.mine + step - 2 * step * ((self.mine // step) % 2)}

    def across(self, half, offset, arriving):
        origin = lax.rem(self.me - offset + self.size, self.size) if arriving else self.me
        return pltpu.make_async_remote_copy(
            src_ref=self.buffer.at[half, self.spots[half], origin],
            dst_ref=self.buffer.at[half, self.spots[half], origin],
            send_sem=self.across_s.at[half * self.size + offset],
            recv_sem=self.across_r.at[half * self.size + offset],
            device_id=self.others(offset),
            device_id_type=pl.DeviceIdType.MESH,
        )

    def block(self, half, level, other):
        count = 1 << level
        start = (self.spots[half] // count) * count
        if other:
            start = start + count - 2 * count * ((self.spots[half] // count) % 2)
        return pl.ds(start, count)

    def within(self, half, level, arriving):
        span = self.block(half, level, arriving)
        return pltpu.make_async_remote_copy(
            src_ref=self.buffer.at[half, span],
            dst_ref=self.buffer.at[half, span],
            send_sem=self.within_s.at[half * self.bits + level],
            recv_sem=self.within_r.at[half * self.bits + level],
            device_id=self.partner(half, level),
            device_id_type=pl.DeviceIdType.MESH,
        )

    def start_level(self, level):
        for half in range(2):
            if level:
                self.within(half, level - 1, True).wait_recv()
            self.within(half, level, False).start()


def attend_kernel(
    sizes,
    size,
    group,
    memory_fill,
    packed_fill,
    bias_ref,
    seg_ref,
    memory_ref,
    packed_ref,
    gain_ref,
    wq_ref,
    wk_ref,
    wv_ref,
    wc_ref,
    gcomp_ref,
    wo_ref,
    unit_ref,
    q_ref,
    k_ref,
    v_ref,
    mixed_ref,
    log_ref,
    packed_new_ref,
    gpack_ref,
    begun_ref,
    strip,
    live,
    mem_rows,
    spread_in,
    *sems,
):
    seg_len, mem_len, packed_len, heads, head_dim = sizes
    kept = mem_len + packed_len
    keys = kept + seg_len
    stream = pl.program_id(0)
    scale = 1.0 / math.sqrt(head_dim)
    gain = gain_ref[...]
    spread = Spread(size, group, spread_in, sems[:4])
    piece, columns = spread_in.shape[3:]
    width = gain.shape[1]

    first_peers = [spread.others(offset) for offset in range(1, size)] + [
        spread.partner(half, 0) for half in range(2)
    ]

    @pl.when(stream == 0)
    def _():
        call(first_peers)
        gpack_ref[...] = jnp.zeros_like(gpack_ref)

    slot = lax.broadcasted_iota(jnp.int32, mem_rows.shape[1:], 0)
    keep = slot >= mem_len - memory_fill[stream]
    count = packed_new_ref.shape[1]
    for column in range(mem_rows.shape[0]):
        lanes = slice(column * block, (column + 1) * block)
        mem_rows[column] = jnp.where(keep, memory_ref[0, :, lanes].astype(f32), 0.0)
    packed_new = jnp.zeros(packed_new_ref.shape[1:], f32)
    for parity in range(2):
        rows = jnp.concatenate(
            [mem_rows[column, pl.ds(parity, count, stride=2), :] for column in range(mem_rows.shape[0])], axis=1
        ).astype(bf16)
        lanes = slice(parity * width, (parity + 1) * width)
        packed_new = packed_new + mm(rows, wc_ref[lanes, :])
        gpack_ref[:, lanes] += mm_t0(gcomp_ref[0], rows)
    packed_new_ref[0] = packed_new.astype(bf16)

    @pl.when(stream == 0)
    def _():
        hear(first_peers)
        rows = pl.ds(pl.multiple_of(spread.mine * piece, piece), piece)
        for half in range(2):
            lanes = slice(half * columns, (half + 1) * columns)
            spread_in[half, spread.spots[half], spread.me] = wo_ref[rows, lanes].astype(f32)
            for offset in range(1, size):
                spread.across(half, offset, False).start()

    start = 0
    for part_ref, length in ((packed_ref, packed_len), (memory_ref, mem_len), (seg_ref, seg_len)):
        rows = part_ref[0].astype(f32)
        unit = (rows * row_scale(rows) * gain).astype(bf16)
        unit_ref[0, start : start + length, :] = unit
        k_ref[0, start : start + length, :] = mm(unit, wk_ref[...]).astype(bf16)
        v_ref[0, start : start + length, :] = mm(unit, wv_ref[...]).astype(bf16)
        if start == kept:
            q_ref[0] = mm(unit, wq_ref[...]).astype(bf16)
        start += length
    live[...] = live_mask((8, kept), 1, packed_len, mem_len, packed_fill[stream], memory_fill[stream])
    for head in range(heads):
        lanes = slice(head * head_dim, (head + 1) * head_dim)
        for column in range(diagonal_count(seg_len, kept)):
            strip[:, column * block : (column + 1) * block] = bias_block(
                bias_ref, head, diagonal_of(seg_len, kept, column), False
            )
        for index in range(seg_len // query_block):
            reach = kept + (index + 1) * query_block
            rows = slice(index * query_block, (index + 1) * query_block)
            score = mm_t1(q_ref[0, rows, lanes], k_ref[0, :reach, lanes]) * scale
            parts = []
            for sub in range(query_block // block):
                first = strip_start(seg_len, index * (query_block // block) + sub)
                parts.append(strip[:, first : first + reach])
            score = score + jnp.concatenate(parts, axis=0)
            score = jnp.concatenate([score[:, :kept] + live[0:1, :], score[:, kept:]], axis=1)
            top = jnp.max(score, axis=-1, keepdims=True)
            weight = jnp.exp(score - top)
            total = jnp.sum(weight, axis=-1, keepdims=True)
            log_total = jnp.broadcast_to(top + jnp.log(total), (query_block, block))
            log_ref[0, head, :, rows] = log_total.T[0:1, :]
            mixed = mm(weight.astype(bf16), v_ref[0, :reach, lanes]) * (1.0 / total)
            mixed_ref[0, rows, lanes] = mixed.astype(bf16)

    @pl.when(stream == 0)
    def _():
        for half in range(2):
            for offset in range(1, size):
                spread.across(half, offset, True).wait_recv()
        spread.start_level(0)

    @pl.when(stream == pl.num_programs(0) - 1)
    def _():
        copies = []
        for half in range(2):
            spread.within(half, 0, True).wait_recv()
            pair = spread_in.at[half, pl.ds((spread.spots[half] // 2) * 2, 2)]
            copies.append(pltpu.make_async_copy(pair, begun_ref.at[half], sems[4].at[half]))
            copies[-1].start()
        for half in range(2):
            for offset in range(1, size):
                spread.across(half, offset, False).wait_send()
            spread.within(half, 0, False).wait_send()
            copies[half].wait()


def attend(
    inputs, memory, packed, memory_fill, packed_fill, gain, wq, wk, wv, bias, wc, gcomp, wo, size, group
):
    streams, seg_len, width = inputs.shape
    mem_len, packed_len = memory.shape[1], packed.shape[1]
    heads = bias.shape[0]
    local = wq.shape[1]
    keys = seg_len + mem_len + packed_len
    sizes = (seg_len, mem_len, packed_len, heads, local // heads)
    smem = pl.BlockSpec(memory_space=pltpu.SMEM)
    compress_count = gcomp.shape[1]
    piece = wo.shape[0] // group
    bits = group.bit_length() - 1

    def rows_of(count, columns):
        return pl.BlockSpec((1, count, columns), lambda s: (s, 0, 0))

    def whole(shape):
        return pl.BlockSpec(shape, lambda s: (0,) * len(shape))

    return pl.pallas_call(
        functools.partial(attend_kernel, sizes, size, group),
        grid=(streams,),
        in_specs=[
            smem,
            smem,
            smem,
            rows_of(seg_len, width),
            rows_of(mem_len, width),
            rows_of(packed_len, width),
            whole((1, width)),
            whole(wq.shape),
            whole(wk.shape),
            whole(wv.shape),
            whole(wc.shape),
            rows_of(compress_count, local),
            whole(wo.shape),
        ],
        out_specs=[
            rows_of(keys, width),
            rows_of(seg_len, local),
            rows_of(keys, local),
            rows_of(keys, local),
            rows_of(seg_len, local),
            pl.BlockSpec((1, heads, 1, seg_len), lambda s: (s, 0, 0, 0)),
            rows_of(compress_count, local),
            whole((local, 2 * width)),
            pl.BlockSpec(memory_space=pl.ANY),
        ],
        out_shape=[
            jax.ShapeDtypeStruct((streams, keys, width), bf16),
            jax.ShapeDtypeStruct((streams, seg_len, local), bf16),
            jax.ShapeDtypeStruct((streams, keys, local), bf16),
            jax.ShapeDtypeStruct((streams, keys, local), bf16),
            jax.ShapeDtypeStruct((streams, seg_len, local), bf16),
            jax.ShapeDtypeStruct((streams, heads, 1, seg_len), f32),
            jax.ShapeDtypeStruct((streams, compress_count, local), bf16),
            jax.ShapeDtypeStruct((local, 2 * width), f32),
            jax.ShapeDtypeStruct((2, 2, size, piece, width // 2), f32),
        ],
        scratch_shapes=[
            pltpu.VMEM((block, diagonal_count(seg_len, mem_len + packed_len) * block), f32),
            pltpu.VMEM((8, mem_len + packed_len), f32),
            pltpu.VMEM((width // block, mem_len, block), f32),
            pltpu.VMEM((2, group, size, piece, width // 2), f32),
            pltpu.SemaphoreType.DMA((2 * size,)),
            pltpu.SemaphoreType.DMA((2 * size,)),
            pltpu.SemaphoreType.DMA((2 * bits,)),
            pltpu.SemaphoreType.DMA((2 * bits,)),
            pltpu.SemaphoreType.DMA((2,)),
        ],
        compiler_params=pltpu.CompilerParams(
            collective_id=2, has_side_effects=True, vmem_limit_bytes=60 << 20
        ),
        cost_estimate=pl.CostEstimate(
            flops=streams * (2 * keys * width * local * 3 + 4 * seg_len * keys * local),
            bytes_accessed=streams * keys * (width * 4 + local * 6),
            transcendentals=streams * heads * seg_len * keys,
        ),
        name="attend",
    )(memory_fill, packed_fill, bias, inputs, memory, packed, gain[None, :], wq, wk, wv, wc, gcomp, wo)


class Line:
    def __init__(self, size, chunks, hop):
        self.me = lax.axis_index("mp")
        self.size, self.chunks, self.hop = size, chunks, hop
        self.reach = size - 1

    def place(self, right):
        return self.me if right else self.reach - self.me

    def peer(self, right):
        return {"mp": self.me + 1 if right else self.me - 1}

    def copy(self, source, target, sems, slot, right):
        return pltpu.make_async_remote_copy(
            src_ref=source.at[slot],
            dst_ref=target.at[slot],
            send_sem=sems[0],
            recv_sem=sems[1].at[slot],
            device_id=self.peer(right),
            device_id_type=pl.DeviceIdType.MESH,
        )

    def chunk_at(self, tick):
        positive = jnp.maximum(tick, 0)
        chunk = positive // self.reach
        return chunk, (tick >= 0) & (positive == chunk * self.reach) & (chunk < self.chunks)

    def scatter_step(self, tick, part, lanes, first=0):
        for right, held, sems in lanes:
            place = self.place(right)
            late = tick - self.hop * place
            positive = jnp.maximum(late, 0)
            chunk = positive // self.reach
            goal = self.reach - (positive - self.reach * chunk)
            active = (late >= 0) & (chunk >= first) & (chunk < self.chunks) & (goal > place)
            slot = chunk * self.size + (goal if right else self.reach - goal)

            @pl.when(active & (place == 0))
            def _():
                self.copy(part, held, sems, slot, right).start()

            @pl.when(active & (place > 0))
            def _():
                self.copy(held, held, sems, slot, right).wait_recv()
                held[slot] = held[slot] + part[slot]
                self.copy(held, held, sems, slot, right).start()

    def scatter_sum(self, chunk, part, lanes, total):
        slot = chunk * self.size + self.me
        total[...] = part[slot]
        for right, held, sems in lanes:

            @pl.when(self.place(right) > 0)
            def _():
                self.copy(held, held, sems, slot, right).wait_recv()
                total[...] = total[...] + held[slot]

    def gather_start(self, chunk, whole, lanes):
        slot = chunk * self.size + self.me
        for right, sems in lanes:

            @pl.when(self.place(right) < self.reach)
            def _():
                self.copy(whole, whole, sems, slot, right).start()

    def gather_step(self, tick, whole, lanes, landed=None):
        for right, sems in lanes:
            place = self.place(right)
            for distance in range(1, self.size):
                chunk, due = self.chunk_at(tick - self.hop * distance)

                @pl.when(due & (distance <= place))
                def _():
                    slot = chunk * self.size + (self.me - distance if right else self.me + distance)
                    self.copy(whole, whole, sems, slot, right).wait_recv()

                    @pl.when(place < self.reach)
                    def _():
                        self.copy(whole, whole, sems, slot, right).start()

                    if landed is not None:
                        landed(slot)

    def sent(self, buffer, send_sem, count, right):
        some = buffer.at[pl.ds(0, count)]
        return pltpu.make_async_remote_copy(
            src_ref=some,
            dst_ref=some,
            send_sem=send_sem,
            recv_sem=send_sem,
            device_id=self.peer(right),
            device_id_type=pl.DeviceIdType.MESH,
        )

    def scatter_drain(self, part, lanes, first=0):
        for right, held, sems in lanes:
            for place in range(self.reach):

                @pl.when(self.place(right) == place)
                def _():
                    self.sent(part, sems[0], (self.reach - place) * (self.chunks - first), right).wait_send()

    def gather_drain(self, whole, lanes):
        for right, sems in lanes:
            for place in range(self.reach):

                @pl.when(self.place(right) == place)
                def _():
                    self.sent(whole, sems[0], (place + 1) * self.chunks, right).wait_send()


def call_neighbours(line):
    barrier = pltpu.get_barrier_semaphore()
    for right in (True, False):

        @pl.when(line.place(right) < line.reach)
        def _():
            pl.semaphore_signal(
                barrier, inc=1, device_id=line.peer(right), device_id_type=pl.DeviceIdType.MESH
            )


def hear_neighbours(line):
    barrier = pltpu.get_barrier_semaphore()
    inner = (line.me > 0) & (line.me < line.reach)

    @pl.when(inner)
    def _():
        pl.semaphore_wait(barrier, 2)

    @pl.when(jnp.logical_not(inner))
    def _():
        pl.semaphore_wait(barrier, 1)


def attend_back_kernel(
    sizes,
    size,
    early,
    hop,
    memory_fill,
    packed_fill,
    bias_ref,
    unit_ref,
    q_ref,
    k_ref,
    v_ref,
    log_ref,
    gm_ref,
    wq_ref,
    wk_ref,
    wv_ref,
    gain_ref,
    gsecond_ref,
    branch_hbm,
    res_hbm,
    gunit_ref,
    gq_ref,
    gk_ref,
    gv_ref,
    small_ref,
    early_ref,
    strip,
    live,
    dk_sum,
    dv_sum,
    dq_low,
    dk_low,
    dv_low,
    strip_sum,
    branch_ref,
    res_ref,
    held_right,
    held_left,
    total_ref,
    load_sem,
    line_s,
    right_r,
    left_r,
):
    seg_len, mem_len, packed_len, heads, head_dim = sizes
    kept = mem_len + packed_len
    keys = kept + seg_len
    stream = pl.program_id(0)
    scale = 1.0 / math.sqrt(head_dim)

    line = Line(size, early, hop)
    lanes_out = ((True, held_right, (line_s.at[0], right_r)), (False, held_left, (line_s.at[1], left_r)))
    loads = (
        pltpu.make_async_copy(branch_hbm.at[pl.ds(0, early * size)], branch_ref, load_sem.at[0]),
        pltpu.make_async_copy(res_hbm.at[pl.ds(0, early)], res_ref, load_sem.at[1]),
    )
    ticks = line.reach * (early - 1) + hop * line.reach + 1
    spans = heads * (seg_len // query_block)
    starts = [22 * index for index in range(spans + 1)]
    starts += [starts[-1] + 6, starts[-1] + 17, starts[-1] + 28, starts[-1] + 36]

    def line_step(tick, _):
        line.scatter_step(tick, branch_ref, lanes_out)
        chunk, due = line.chunk_at(tick - hop * line.reach)

        @pl.when(due)
        def _():
            line.scatter_sum(chunk, branch_ref, lanes_out, total_ref)
            early_ref[chunk] = (res_ref[chunk] + total_ref[...]).astype(bf16).astype(f32)

        return 0

    def line_span(index):
        if index == 0:
            return
        late = starts[1]
        begin = starts[index] if index > 1 else 0
        every = starts[-1] * pl.num_programs(0) - late
        here = jnp.maximum(stream * starts[-1] + begin - late, 0)
        after = jnp.maximum(stream * starts[-1] + starts[index + 1] - late, 0)
        if index == 1:

            @pl.when(stream == 0)
            def _():
                hear_neighbours(line)
                for load in loads:
                    load.wait()

        lax.fori_loop((here * ticks) // every, (after * ticks) // every, line_step, 0)

    @pl.when(stream == 0)
    def _():
        for load in loads:
            load.start()
        call_neighbours(line)
        strip_sum[...] = jnp.zeros_like(strip_sum)
        gq_ref[...] = jnp.zeros_like(gq_ref)
        gk_ref[...] = jnp.zeros_like(gk_ref)
        gv_ref[...] = jnp.zeros_like(gv_ref)

    live[...] = live_mask((kept, block), 0, packed_len, mem_len, packed_fill[stream], memory_fill[stream])
    subs = query_block // block
    for head in range(heads):
        lanes = slice(head * head_dim, (head + 1) * head_dim)
        for column in range(diagonal_count(seg_len, kept)):
            strip[column * block : (column + 1) * block, :] = bias_block(
                bias_ref, head, diagonal_of(seg_len, kept, column), True
            )
        for index in range(seg_len // query_block):
            line_span(head * (seg_len // query_block) + index)
            reach = kept + (index + 1) * query_block
            rows = slice(index * query_block, (index + 1) * query_block)
            queries = q_ref[0, rows, lanes]
            grads = gm_ref[0, rows, lanes]
            key_rows = k_ref[0, :reach, lanes]
            score = mm_t1(key_rows, queries) * scale
            firsts = [strip_start(seg_len, index * subs + sub) for sub in range(subs)]
            score = score + jnp.concatenate([strip[first : first + reach, :] for first in firsts], axis=1)
            live_wide = jnp.concatenate([live[...]] * subs, axis=1)
            score = jnp.concatenate([score[:kept] + live_wide, score[kept:]], axis=0)
            prob = jnp.exp(score - log_ref[0, head, :, rows])
            grad_prob = mm_t1(v_ref[0, :reach, lanes], grads)
            delta = jnp.sum(prob * grad_prob, axis=0, keepdims=True)
            grad_score = (prob * (grad_prob - delta)).astype(bf16)
            dk_part = mm(grad_score, queries)
            dv_part = mm(prob.astype(bf16), grads)
            if index == seg_len // query_block - 1:
                earlier = kept + index * query_block
                if index:
                    dk_sum[:earlier] += dk_part[:earlier]
                    dv_sum[:earlier] += dv_part[:earlier]
                    dk_sum[earlier:] = dk_part[earlier:]
                    dv_sum[earlier:] = dv_part[earlier:]
                else:
                    dk_sum[...] = dk_part
                    dv_sum[...] = dv_part
            elif index:
                earlier = kept + index * query_block
                dk_sum[:earlier] += dk_part[:earlier]
                dv_sum[:earlier] += dv_part[:earlier]
                dk_sum[earlier:reach] = dk_part[earlier:]
                dv_sum[earlier:reach] = dv_part[earlier:]
            else:
                dk_sum[:reach] = dk_part
                dv_sum[:reach] = dv_part
            dq_low[rows, lanes] = (mm_t0(grad_score, key_rows) * scale).astype(bf16)
            for sub in range(subs):
                strip_sum[head, firsts[sub] : firsts[sub] + reach, :] += grad_score[
                    :, sub * block : (sub + 1) * block
                ].astype(f32)
        dk_low[:, lanes] = (dk_sum[...] * scale).astype(bf16)
        dv_low[:, lanes] = dv_sum[...].astype(bf16)
    line_span(spans)
    gq_ref[...] += mm_t0(dq_low[...], unit_ref[0, kept:, :])
    line_span(spans + 1)
    gk_ref[...] += mm_t0(dk_low[...], unit_ref[0])
    line_span(spans + 2)
    gv_ref[...] += mm_t0(dv_low[...], unit_ref[0])
    line_span(spans + 3)
    gunit_ref[0] = (
        mm_t1(dq_low[...], wq_ref[...])
        + mm_t1(dk_low[kept:, :], wk_ref[...])
        + mm_t1(dv_low[kept:, :], wv_ref[...])
    )

    @pl.when(stream == pl.num_programs(0) - 1)
    def _():
        line.scatter_drain(branch_ref, lanes_out)
        rows = lax.broadcasted_iota(jnp.int32, (block, block), 0)
        cols = lax.broadcasted_iota(jnp.int32, (block, block), 1)
        width = gain_ref.shape[1]
        lane = lax.broadcasted_iota(jnp.int32, (1, width), 1)
        relative = [jnp.zeros((1, width), f32) for _ in range(heads)]
        for head in range(heads):
            blocks = []
            for column in range(diagonal_count(seg_len, kept)):
                blocks.append(strip_sum[head, column * block : (column + 1) * block, :])
            for position, mark_value in enumerate(reach_marks):
                total = jnp.zeros((1, block), f32)
                for column, value in enumerate(blocks):
                    diagonal = diagonal_of(seg_len, kept, column)
                    lowest, highest = diagonal * block - block + 1, diagonal * block + block - 1
                    if mark_value <= lowest:
                        total = total + jnp.sum(value, axis=0, keepdims=True)
                    elif mark_value <= highest:
                        distance = diagonal * block + cols - rows
                        total = total + jnp.sum(
                            jnp.where(distance >= mark_value, value, 0.0), axis=0, keepdims=True
                        )
                total = jnp.sum(total, axis=1, keepdims=True)
                relative[head] = jnp.where(lane == position, total, relative[head])
        first = jnp.zeros((1, width), f32)
        for grad_ref, weight_ref in ((gq_ref, wq_ref), (gk_ref, wk_ref), (gv_ref, wv_ref)):
            turned = weight_ref[...].astype(f32).T
            first = first + jnp.sum(grad_ref[...] * turned, axis=0, keepdims=True)
        small_ref[...] = jnp.concatenate(
            [first / gain_ref[...], gsecond_ref[...], *relative, jnp.zeros((6 - heads, width), f32)], axis=0
        )


def attend_back(
    unit, q, k, v, log_total, grad_mixed, memory_fill, packed_fill, wq, wk, wv, bias, gain, grad_second, mem_len, packed_len,
    branch, residual, size, early,
):
    streams, keys, width = unit.shape
    seg_len, local = q.shape[1:]
    heads = bias.shape[0]
    kept = mem_len + packed_len
    sizes = (seg_len, mem_len, packed_len, heads, local // heads)
    smem = pl.BlockSpec(memory_space=pltpu.SMEM)
    strip_len = diagonal_count(seg_len, kept) * block
    part = (early * size, *branch.shape[1:])

    def rows_of(count, columns):
        return pl.BlockSpec((1, count, columns), lambda s: (s, 0, 0))

    def whole(shape):
        return pl.BlockSpec(shape, lambda s: (0,) * len(shape))

    return pl.pallas_call(
        functools.partial(attend_back_kernel, sizes, size, early, 3),
        grid=(streams,),
        in_specs=[
            smem,
            smem,
            smem,
            rows_of(keys, width),
            rows_of(seg_len, local),
            rows_of(keys, local),
            rows_of(keys, local),
            pl.BlockSpec((1, heads, 1, seg_len), lambda s: (s, 0, 0, 0)),
            rows_of(seg_len, local),
            whole(wq.shape),
            whole(wk.shape),
            whole(wv.shape),
            whole((1, width)),
            whole((1, width)),
            pl.BlockSpec(memory_space=pl.ANY),
            pl.BlockSpec(memory_space=pl.ANY),
        ],
        out_specs=[
            rows_of(seg_len, width),
            whole((local, width)),
            whole((local, width)),
            whole((local, width)),
            whole((8, width)),
            whole((early, *residual.shape[1:])),
        ],
        out_shape=[
            jax.ShapeDtypeStruct((streams, seg_len, width), f32),
            jax.ShapeDtypeStruct((local, width), f32),
            jax.ShapeDtypeStruct((local, width), f32),
            jax.ShapeDtypeStruct((local, width), f32),
            jax.ShapeDtypeStruct((8, width), f32),
            jax.ShapeDtypeStruct((early, *residual.shape[1:]), f32),
        ],
        scratch_shapes=[
            pltpu.VMEM((strip_len, block), f32),
            pltpu.VMEM((kept, block), f32),
            pltpu.VMEM((keys, local // heads), f32),
            pltpu.VMEM((keys, local // heads), f32),
            pltpu.VMEM((seg_len, local), bf16),
            pltpu.VMEM((keys, local), bf16),
            pltpu.VMEM((keys, local), bf16),
            pltpu.VMEM((heads, strip_len, block), f32),
            pltpu.VMEM(part, f32),
            pltpu.VMEM((early, *part[1:]), f32),
            pltpu.VMEM(part, f32),
            pltpu.VMEM(part, f32),
            pltpu.VMEM(part[1:], f32),
            pltpu.SemaphoreType.DMA((2,)),
            pltpu.SemaphoreType.DMA((2,)),
            pltpu.SemaphoreType.DMA((early * size,)),
            pltpu.SemaphoreType.DMA((early * size,)),
        ],
        compiler_params=pltpu.CompilerParams(
            collective_id=3, has_side_effects=True, vmem_limit_bytes=60 << 20
        ),
        cost_estimate=pl.CostEstimate(
            flops=streams * (8 * keys * width * local + 10 * seg_len * keys * local),
            bytes_accessed=streams * keys * (width * 2 + local * 6),
            transcendentals=streams * heads * seg_len * keys,
        ),
        name="attend_back",
    )(
        memory_fill,
        packed_fill,
        bias,
        unit,
        q,
        k,
        v,
        log_total,
        grad_mixed,
        wq,
        wk,
        wv,
        gain[None, :],
        grad_second,
        branch,
        residual,
    )


def feed_kernel(
    size,
    group,
    chunks,
    hop,
    delay,
    beat,
    mixed_ref,
    seg_hbm,
    grad_hbm,
    up_hbm,
    down_hbm,
    begun_ref,
    gain_ref,
    gm_ref,
    gres_ref,
    res_ref,
    branch_hbm,
    gdown_hbm,
    gup_hbm,
    gout_hbm,
    gsecond_ref,
    seg_ref,
    grad_ref,
    up_ref,
    down_ref,
    branch_ref,
    gdown_ref,
    gup_ref,
    gout_ref,
    acted,
    graded,
    normed_low,
    heads_in,
    part,
    held_right,
    held_left,
    swap_out,
    swap_in,
    weights_in,
    weights,
    chunk_rows,
    total,
    own_mixed,
    own_grad,
    *sems,
):
    line = Line(size, chunks, hop)
    me = line.me
    (line_s, hr_r, hl_r, sr_r, sl_r, swap_sem, wd_s, wd_r, load_sem, save_sem, branch_sem) = sems
    gather_lanes = ((True, (line_s.at[0], hr_r)), (False, (line_s.at[1], hl_r)))
    scatter_lanes = ((True, held_right, (line_s.at[2], sr_r)), (False, held_left, (line_s.at[3], sl_r)))
    loads = [
        pltpu.make_async_copy(source, target, load_sem.at[index])
        for index, (source, target) in enumerate(
            ((seg_hbm, seg_ref), (grad_hbm, grad_ref), (up_hbm, up_ref), (down_hbm, down_ref))
        )
    ]
    for load in loads:
        load.start()
    spread = Spread(size, group, weights_in, (None, None, wd_s, wd_r))
    bits = spread.bits
    piece, columns = weights_in.shape[3:]
    width = weights.shape[1]
    rows = total.shape[0]
    local = mixed_ref.shape[-1]
    greet(
        [spread.others(offset) for offset in range(1, size)]
        + [spread.partner(half, level) for half in range(2) for level in range(1, bits)]
    )
    for half in range(2):
        weights_in[half, pl.ds((spread.spots[half] // 2) * 2, 2)] = begun_ref[half]
        spread.within(half, 1, False).start()

    def stage_heads(chunk, _):
        heads_in[chunk * size + me] = mixed_ref[chunk].astype(f32)
        return 0

    lax.fori_loop(0, chunks, stage_heads, 0)
    gsecond_ref[...] = jnp.zeros_like(gsecond_ref)
    gdown_ref[...] = jnp.zeros_like(gdown_ref)
    gup_ref[...] = jnp.zeros_like(gup_ref)

    def weight_step(tick):
        for level in range(2, bits):

            @pl.when(tick == beat + level - 2)
            def _():
                spread.start_level(level)

    def weight_finish():
        for half in range(2):
            spread.within(half, bits - 1, True).wait_recv()
            for index in range(size):
                pieces = [weights_in[half, spread.place_of(half, member), index] for member in range(group)]
                weights[index * group * piece : (index + 1) * group * piece, half * columns : (half + 1) * columns] = (
                    jnp.concatenate(pieces, axis=0).astype(bf16)
                )

    own = pl.ds(pl.multiple_of(me * rows, rows), rows)

    def feed_chunk(chunk):
        heads = [heads_in[chunk * size + index].astype(bf16) for index in range(size)]
        for index in range(size):
            own_mixed[chunk, :, index * local : (index + 1) * local] = heads_in[
                chunk * size + index, own, :
            ].astype(bf16)
        residual = seg_ref[chunk].astype(f32) + mm(jnp.concatenate(heads, axis=1), weights[...])
        chunk_rows[...] = residual
        res_ref[chunk] = chunk_rows[own, :]
        ffn_input = (residual * row_scale(residual) * gain_ref[...]).astype(bf16)
        pre_act = mm(ffn_input, up_ref[...])
        inner = math.sqrt(2.0 / math.pi)
        squared = pre_act * pre_act
        tanh = jnp.tanh(inner * (pre_act + 0.044715 * pre_act * squared))
        activated = (0.5 * pre_act * (1.0 + tanh)).astype(bf16)
        slope = 0.5 * (1.0 + tanh) + 0.5 * pre_act * (1.0 - tanh * tanh) * (
            inner * (1.0 + 3.0 * 0.044715 * squared)
        )
        grads = grad_ref[chunk]
        grad_pre = (slope * mm_t1(grads, down_ref[...])).astype(bf16)
        first = pl.ds(chunk * size, size)
        part[first] = mm_t1(grad_pre, up_ref[...]).reshape(size, rows, width)
        acted[...] = activated
        graded[...] = grad_pre
        normed_low[...] = ffn_input

    def save_branch(chunk):
        here = pl.ds(chunk * size, size)
        return pltpu.make_async_copy(branch_ref.at[here], branch_hbm.at[here], branch_sem.at[chunk])

    def feed_branch(chunk):
        branch_ref[pl.ds(chunk * size, size)] = mm(acted[...], down_ref[...]).reshape(size, rows, width)
        save_branch(chunk).start()
        gdown_ref[...] += mm_t0(acted[...], grad_ref[chunk])

    def feed_grads(chunk):
        gup_ref[...] += mm_t0(normed_low[...], graded[...])

    saves = [
        pltpu.make_async_copy(source, target, save_sem.at[index])
        for index, (source, target) in enumerate(
            ((gdown_ref, gdown_hbm), (gup_ref, gup_hbm), (gout_ref, gout_hbm))
        )
    ]

    def swap(chunk, offset):
        target = lax.rem(me + offset, size)
        return pltpu.make_async_remote_copy(
            src_ref=swap_out.at[chunk * size + target],
            dst_ref=swap_in.at[chunk * size + me],
            send_sem=swap_sem.at[0],
            recv_sem=swap_sem.at[1],
            device_id={"mp": target},
            device_id_type=pl.DeviceIdType.MESH,
        )

    def all_swaps():
        some = pl.ds(0, chunks * (size - 1))
        return pltpu.make_async_remote_copy(
            src_ref=swap_out.at[some],
            dst_ref=swap_in.at[some],
            send_sem=swap_sem.at[0],
            recv_sem=swap_sem.at[1],
            device_id=spread.others(1),
            device_id_type=pl.DeviceIdType.MESH,
        )

    def settle(chunk):
        line.scatter_sum(chunk, part, scatter_lanes, total)
        grad_ffn = total[...]
        residual = res_ref[chunk]
        scale = row_scale(residual)
        normed = residual * scale
        gsecond_ref[...] += jnp.sum(grad_ffn * normed, axis=0, keepdims=True)
        weighted = grad_ffn * gain_ref[...]
        own_rows = grad_ref[chunk, own, :].astype(f32)
        grad_residual = own_rows + scale * (
            weighted - normed * jnp.mean(weighted * normed, axis=-1, keepdims=True)
        )
        gres_ref[chunk] = grad_residual
        low = grad_residual.astype(bf16)
        own_grad[chunk] = low
        grad_mixed = mm_t1(low, weights[...]).astype(bf16).astype(f32)
        for index in range(size):
            swap_out[chunk * size + index] = grad_mixed[:, index * local : (index + 1) * local]
        for offset in range(1, size):
            swap(chunk, offset).start()

    feed_at = hop * line.reach + delay

    def step(tick, _):
        weight_step(tick)

        @pl.when(tick == feed_at)
        def _():
            weight_finish()
            for load in loads:
                load.wait()

        chunk, due = line.chunk_at(tick)

        @pl.when(due)
        def _():
            line.gather_start(chunk, heads_in, gather_lanes)

        line.gather_step(tick, heads_in, gather_lanes)
        chunk_f, due_f = line.chunk_at(tick - feed_at)

        @pl.when(due_f)
        def _():
            feed_chunk(chunk_f)

        line.scatter_step(tick - feed_at, part, scatter_lanes)
        for late, work in ((1, feed_branch), (2, feed_grads)):
            chunk_w, due_w = line.chunk_at(tick - feed_at - late)

            @pl.when(due_w)
            def _():
                work(chunk_w)

        @pl.when(tick == feed_at + line.reach * (chunks - 1) + 3)
        def _():
            for save in saves[:2]:
                save.start()

        chunk_s, due_s = line.chunk_at(tick - feed_at - hop * line.reach)

        @pl.when(due_s)
        def _():
            settle(chunk_s)

        return 0

    lax.fori_loop(0, feed_at + line.reach * (chunks - 1) + hop * line.reach + 1, step, 0)
    gout_ref[...] = mm_t0(
        own_mixed[...].reshape(chunks * rows, width), own_grad[...].reshape(chunks * rows, width)
    )

    saves[2].start()
    all_swaps().wait_recv()

    def finish(chunk, _):
        save_branch(chunk).wait()
        for index in range(size):

            @pl.when(index == me)
            def _():
                gm_ref[chunk * size + index] = swap_out[chunk * size + index].astype(bf16)

            @pl.when(index != me)
            def _():
                gm_ref[chunk * size + index] = swap_in[chunk * size + index].astype(bf16)

        return 0

    lax.fori_loop(0, chunks, finish, 0)
    line.gather_drain(heads_in, gather_lanes)
    line.scatter_drain(part, scatter_lanes)
    all_swaps().wait_send()
    for save in saves:
        save.wait()
    for half in range(2):
        for level in range(1, bits):
            spread.within(half, level, False).wait_send()


def feed(mixed, seg_rows, grad_rows, up, down, begun, gain, size, group, chunks):
    rows, width = seg_rows.shape
    local = mixed.shape[1]
    chunk = rows // chunks
    piece = chunk // size
    hidden = up.shape[1]
    vmem = pl.BlockSpec(memory_space=pltpu.VMEM)
    anywhere = pl.BlockSpec(memory_space=pl.ANY)
    dma = pltpu.SemaphoreType.DMA
    slots = dma((chunks * size,))
    bits = group.bit_length() - 1
    return pl.pallas_call(
        functools.partial(feed_kernel, size, group, chunks, 2, 0, 4),
        in_specs=[vmem] + [anywhere] * 4 + [vmem] * 2,
        out_specs=[vmem] * 3 + [anywhere] * 4 + [vmem],
        out_shape=[
            jax.ShapeDtypeStruct((chunks * size, piece, local), bf16),
            jax.ShapeDtypeStruct((chunks, piece, width), f32),
            jax.ShapeDtypeStruct((chunks, piece, width), f32),
            jax.ShapeDtypeStruct((chunks * size, piece, width), f32),
            jax.ShapeDtypeStruct((hidden, width), f32),
            jax.ShapeDtypeStruct((width, hidden), f32),
            jax.ShapeDtypeStruct((width, width), f32),
            jax.ShapeDtypeStruct((1, width), f32),
        ],
        scratch_shapes=[
            pltpu.VMEM((chunks, chunk, width), bf16),
            pltpu.VMEM((chunks, chunk, width), bf16),
            pltpu.VMEM(up.shape, bf16),
            pltpu.VMEM(down.shape, bf16),
            pltpu.VMEM((chunks * size, piece, width), f32),
            pltpu.VMEM((hidden, width), f32),
            pltpu.VMEM((width, hidden), f32),
            pltpu.VMEM((width, width), f32),
            pltpu.VMEM((chunk, hidden), bf16),
            pltpu.VMEM((chunk, hidden), bf16),
            pltpu.VMEM((chunk, width), bf16),
            pltpu.VMEM((chunks * size, chunk, local), f32),
            pltpu.VMEM((chunks * size, piece, width), f32),
            pltpu.VMEM((chunks * size, piece, width), f32),
            pltpu.VMEM((chunks * size, piece, width), f32),
            pltpu.VMEM((chunks * size, piece, local), f32),
            pltpu.VMEM((chunks * size, piece, local), f32),
            pltpu.VMEM((2, group, *begun.shape[2:]), f32),
            pltpu.VMEM((width, width), bf16),
            pltpu.VMEM((chunk, width), f32),
            pltpu.VMEM((piece, width), f32),
            pltpu.VMEM((chunks, piece, width), bf16),
            pltpu.VMEM((chunks, piece, width), bf16),
        ]
        + [dma((4,))]
        + [slots] * 4
        + [dma((2,)), dma((2 * bits,)), dma((2 * bits,)), dma((4,)), dma((3,)), dma((chunks,))],
        compiler_params=pltpu.CompilerParams(
            collective_id=0, has_side_effects=True, vmem_limit_bytes=63 << 20
        ),
        name="feed",
    )(
        mixed.reshape(chunks, chunk, local),
        seg_rows.reshape(chunks, chunk, width),
        grad_rows.reshape(chunks, chunk, width),
        up,
        down,
        begun,
        gain[None, :],
    )


class Pieces:
    def __init__(self, group, rows, gap, crossing, jobs, work, landing, summed, sems):
        self.mine = lax.axis_index("dp")
        self.bits = group.bit_length() - 1
        self.rows, self.gap, self.crossing, self.jobs = rows, gap, crossing, jobs
        self.work, self.landing, self.summed = work, landing, summed
        self.slots = work.shape[0]
        (self.rs_s, self.rs_r, self.ag_s, self.ag_r, self.load_sem, self.store_sem) = sems
        self.count = crossing[0] + sum(job[2] for job in jobs)
        self.turned = self.count - sum(job[2] for job in jobs if job[1].shape != job[0].shape)
        self.beats = self.count + 2 * self.bits * gap + 2

    def step_of(self, odd, level):
        even_step = 1 << level
        odd_step = 1 << ((self.bits - level) % self.bits)
        return jnp.where(odd == 1, odd_step, even_step)

    def bit_of(self, odd, level):
        return (self.mine // self.step_of(odd, level)) % 2

    def partner(self, odd, level):
        step = self.step_of(odd, level)
        return {"dp": self.mine + step - 2 * step * self.bit_of(odd, level)}

    def start_of(self, odd, level):
        start = jnp.int32(0)
        for earlier in range(level):
            start = start + self.bit_of(odd, earlier) * (self.rows >> (earlier + 1))
        return start

    def span(self, start, level):
        length = self.rows >> level
        return pl.ds(pl.multiple_of(start, self.rows >> self.bits), length)

    def halves(self, odd, level):
        start, bit, half = self.start_of(odd, level), self.bit_of(odd, level), self.rows >> (level + 1)
        return self.span(start + bit * half, level + 1), self.span(start + (1 - bit) * half, level + 1)

    def reduce_copy(self, slot, odd, level):
        _, give = self.halves(odd, level)
        region = pl.ds(self.rows - (self.rows >> level), self.rows >> (level + 1))
        return pltpu.make_async_remote_copy(
            src_ref=self.work.at[slot, give],
            dst_ref=self.landing.at[slot, region],
            send_sem=self.rs_s.at[slot * self.bits + level],
            recv_sem=self.rs_r.at[slot * self.bits + level],
            device_id=self.partner(odd, level),
            device_id_type=pl.DeviceIdType.MESH,
        )

    def absorb(self, slot, odd, level):
        self.reduce_copy(slot, odd, level).wait_recv()
        keep, _ = self.halves(odd, level)
        region = pl.ds(self.rows - (self.rows >> level), self.rows >> (level + 1))
        self.work[slot, keep, :] = self.work[slot, keep, :] + self.landing[slot, region, :]

    def spread_copy(self, buffer, sems, slot, odd, level, arriving):
        keep, give = self.halves(odd, level)
        span = give if arriving else keep
        return pltpu.make_async_remote_copy(
            src_ref=buffer.at[slot, span],
            dst_ref=buffer.at[slot, span],
            send_sem=sems[0].at[slot * self.bits + level],
            recv_sem=sems[1].at[slot * self.bits + level],
            device_id=self.partner(odd, level),
            device_id_type=pl.DeviceIdType.MESH,
        )

    def spread(self, slot, odd, level, arriving):
        return self.spread_copy(self.summed, (self.ag_s, self.ag_r), slot, odd, level, arriving)

    def move(self, piece, slot, store, start):
        columns = self.work.shape[2]
        first = self.crossing[0]
        sources = [(self.crossing[1], None, 0, first)]
        for source, target, count in self.jobs:
            sources.append((source, target, first, first + count))
            first += count
        for source, target, low, high in sources:
            if store and target is None:
                continue

            @pl.when((piece >= low) & (piece < high))
            def _():
                across = source.shape[2] // columns
                index = (piece - low) // across
                lanes = pl.ds(pl.multiple_of((piece - low - index * across) * columns, columns), columns)
                inside = self.summed.at[slot] if store else self.work.at[slot]
                if store and target.shape != source.shape:
                    copy = pltpu.make_async_copy(inside, target.at[piece - low], self.store_sem.at[slot])
                elif store:
                    copy = pltpu.make_async_copy(inside, target.at[index, :, lanes], self.store_sem.at[slot])
                else:
                    copy = pltpu.make_async_copy(source.at[index, :, lanes], inside, self.load_sem.at[slot])
                copy.start() if start else copy.wait()

    def load_first(self):
        self.move(jnp.int32(0), 0, False, True)

    def step(self, tick, cross):
        bits = self.bits
        for age in reversed(range(-1, 2 * bits + 2)):
            piece = tick - (age if age < 0 else min(age * self.gap, 2 * bits * self.gap + 1))
            safe = jnp.maximum(piece, 0)
            slot, odd = safe % self.slots, safe % 2
            plain = piece >= self.crossing[0]
            inside = (piece >= 0) & (piece < self.count)
            if age == 2 * bits + 1:

                @pl.when(inside)
                def _():
                    for level in range(bits):
                        self.reduce_copy(slot, odd, level).wait_send()

                @pl.when(inside & plain)
                def _():
                    self.move(piece, slot, True, False)

                @pl.when(inside & jnp.logical_not(plain))
                def _():
                    cross(piece, slot, odd, False)

            elif age == 2 * bits:

                @pl.when(inside & plain)
                def _():
                    self.spread(slot, odd, 0, True).wait_recv()
                    for level in range(bits):
                        self.spread(slot, odd, level, False).wait_send()

                    @pl.when(piece >= self.turned)
                    def _():
                        self.summed[slot] = self.summed[slot].T

                    self.move(piece, slot, True, True)

            elif age > bits:

                @pl.when(inside & plain)
                def _():
                    self.spread(slot, odd, 2 * bits - age, True).wait_recv()
                    self.spread(slot, odd, 2 * bits - 1 - age, False).start()

            elif age == bits:

                @pl.when(inside)
                def _():
                    self.absorb(slot, odd, bits - 1)

                @pl.when(inside & plain)
                def _():
                    own = self.span(self.start_of(odd, bits), bits)
                    self.summed[slot, own, :] = self.work[slot, own, :]
                    self.spread(slot, odd, bits - 1, False).start()

                @pl.when(inside & jnp.logical_not(plain))
                def _():
                    cross(piece, slot, odd, True)

            elif age > 0:

                @pl.when(inside)
                def _():
                    self.absorb(slot, odd, age - 1)
                    self.reduce_copy(slot, odd, age).start()

            elif age == 0:

                @pl.when(inside)
                def _():
                    self.move(piece, slot, False, False)
                    self.reduce_copy(slot, odd, 0).start()

            else:

                @pl.when(inside)
                def _():
                    self.move(piece, slot, False, True)


def close_kernel(
    size,
    group,
    chunks,
    hop,
    counts,
    gap,
    early,
    gunit_hbm,
    branch_hbm,
    seg_hbm,
    gres_hbm,
    res_hbm,
    gain_ref,
    early_ref,
    gout_ref,
    gup_ref,
    gdown_ref,
    gq_ref,
    gk_ref,
    gv_ref,
    gpack_ref,
    small_ref,
    result_ref,
    gseg_ref,
    gout_sum,
    gup_sum,
    gdown_sum,
    gq_sum,
    gk_sum,
    gv_sum,
    gpack_sum,
    small_sum,
    gunit_ref,
    branch_ref,
    seg_ref,
    gres_ref,
    res_ref,
    whole_seg,
    whole_out,
    seg_right,
    seg_left,
    out_right,
    out_left,
    total,
    work,
    landing,
    summed,
    cross_in,
    cross_work,
    small_cross,
    small_held,
    small_in,
    *sems,
):
    line = Line(size, chunks, hop)
    me = line.me
    line_s, recvs, sems = sems[0], sems[1:9], sems[9:]
    seg_scatter = ((True, seg_right, (line_s.at[0], recvs[0])), (False, seg_left, (line_s.at[1], recvs[1])))
    out_scatter = ((True, out_right, (line_s.at[2], recvs[2])), (False, out_left, (line_s.at[3], recvs[3])))
    seg_gather = ((True, (line_s.at[4], recvs[4])), (False, (line_s.at[5], recvs[5])))
    out_gather = ((True, (line_s.at[6], recvs[6])), (False, (line_s.at[7], recvs[7])))
    piece_sems = sems[:6]
    cross_s, cross_r, tail_s, tail_r, tail_store = sems[6:11]
    mix_s, mix_r, small_s, small_r = sems[11:15]
    seg_load, out_load, load_sem = sems[15:18]
    loads = [
        pltpu.make_async_copy(source, target, load_sem.at[index])
        for index, (source, target) in enumerate(((seg_hbm, seg_ref), (gres_hbm, gres_ref), (res_hbm, res_ref)))
    ]

    def part_load(source, target, load, chunk):
        here = pl.ds(chunk * size, size)
        return pltpu.make_async_copy(source.at[here], target.at[here], load.at[chunk])

    for chunk in range(chunks):
        part_load(gunit_hbm, gunit_ref, seg_load, chunk).start()
        if chunk >= early:
            part_load(branch_hbm, branch_ref, out_load, chunk).start()
    for load in loads:
        load.start()
    jobs = [
        (gup_ref, gup_sum, counts[1]),
        (gdown_ref, gdown_sum, counts[2]),
        (gq_ref, gq_sum, counts[3]),
        (gk_ref, gk_sum, counts[4]),
        (gv_ref, gv_sum, counts[5]),
        (gpack_ref, gpack_sum, counts[6]),
    ]
    pieces = Pieces(group, work.shape[1], gap, (counts[0], gout_ref), jobs, work, landing, summed, piece_sems)
    bits = pieces.bits
    pieces.load_first()
    greet(
        [{"mp": lax.rem(me + offset, size)} for offset in range(1, size)]
        + [{"dp": pieces.mine + (1 << bit) - 2 * (1 << bit) * ((pieces.mine // (1 << bit)) % 2)} for bit in range(bits)]
    )

    across, columns = cross_work.shape[0], work.shape[2]

    def cross_copy(slot, column, target, origin):
        own = pieces.span(pieces.start_of(column % 2, bits), bits)
        return pltpu.make_async_remote_copy(
            src_ref=work.at[slot, own],
            dst_ref=cross_in.at[column * size + origin],
            send_sem=cross_s.at[column * size + target],
            recv_sem=cross_r.at[column * size + origin],
            device_id={"mp": target},
            device_id_type=pl.DeviceIdType.MESH,
        )

    def cross(piece, slot, odd, start):
        target, column = piece // across, piece % across

        @pl.when(target != me)
        def _():
            copy = cross_copy(slot, column, target, me)
            copy.start() if start else copy.wait_send()

        if start:

            @pl.when(target == me)
            def _():
                own = pieces.span(pieces.start_of(odd, bits), bits)
                cross_in[column * size + me] = work[slot, own, :]

    def tail_copy(column):
        return pltpu.make_async_copy(
            cross_work.at[column],
            gout_sum.at[0, :, column * columns : (column + 1) * columns],
            tail_store.at[column],
        )

    def tail_spread(column, level, arriving):
        return pieces.spread_copy(cross_work, (tail_s, tail_r), column, column % 2, level, arriving)

    def tail_step(tick):
        base = counts[0] + bits * gap + gap
        for column in range(across):

            @pl.when(tick == base + column)
            def _():
                for offset in range(1, size):
                    cross_copy(0, column, me, lax.rem(me + offset, size)).wait_recv()
                own = pieces.span(pieces.start_of(column % 2, bits), bits)
                cross_work[column, own, :] = (
                    sum(cross_in[column * size + index] for index in range(1, size)) + cross_in[column * size]
                )
                tail_spread(column, bits - 1, False).start()

            for level in reversed(range(bits)):

                @pl.when(tick == base + column + (bits - level) * gap)
                def _():
                    tail_spread(column, level, True).wait_recv()
                    if level:
                        tail_spread(column, level - 1, False).start()
                    else:
                        tail_copy(column).start()

    def small_across(offset, arriving):
        origin = lax.rem(me - offset + size, size) if arriving else me
        return pltpu.make_async_remote_copy(
            src_ref=small_cross.at[me],
            dst_ref=small_cross.at[origin],
            send_sem=mix_s.at[offset],
            recv_sem=mix_r.at[offset],
            device_id={"mp": lax.rem(me + offset, size)},
            device_id_type=pl.DeviceIdType.MESH,
        )

    def small_within(level):
        step = 1 << level
        return pltpu.make_async_remote_copy(
            src_ref=small_held.at[level],
            dst_ref=small_in.at[level],
            send_sem=small_s.at[level],
            recv_sem=small_r.at[level],
            device_id={"dp": pieces.mine + step - 2 * step * ((pieces.mine // step) % 2)},
            device_id_type=pl.DeviceIdType.MESH,
        )

    def small_step(tick):
        @pl.when(tick == 0)
        def _():
            small_cross[me] = small_ref[...]
            for offset in range(1, size):
                small_across(offset, False).start()

        @pl.when(tick == 2)
        def _():
            value = small_ref[...]
            shared = lax.broadcasted_iota(jnp.int32, value.shape, 0) < 2
            for offset in range(1, size):
                small_across(offset, True).wait_recv()
                origin = lax.rem(me - offset + size, size)
                value = value + jnp.where(shared, small_cross[origin], 0.0)
            small_held[0] = value
            small_within(0).start()

        for level in range(bits):

            @pl.when(tick == 4 + 2 * level)
            def _():
                small_within(level).wait_recv()
                value = small_held[level] + small_in[level]
                if level + 1 < bits:
                    small_held[level + 1] = value
                    small_within(level + 1).start()
                else:
                    small_sum[...] = value

    def settle_seg(chunk):
        slot = chunk * size + me
        line.scatter_sum(chunk, gunit_ref, seg_scatter, total)
        rows = seg_ref[slot].astype(f32)
        scale = row_scale(rows)
        normed = rows * scale
        weighted = total[...] * gain_ref[...]
        grad = gres_ref[chunk] + scale * (
            weighted - normed * jnp.mean(weighted * normed, axis=-1, keepdims=True)
        )
        low = grad.astype(bf16)
        gseg_ref[slot] = low
        whole_seg[slot] = low.astype(f32)
        line.gather_start(chunk, whole_seg, seg_gather)

    def settle_out(chunk):
        slot = chunk * size + me

        @pl.when(chunk < early)
        def _():
            total[...] = early_ref[jnp.minimum(chunk, early - 1)]

        @pl.when(chunk >= early)
        def _():
            line.scatter_sum(chunk, branch_ref, out_scatter, total)
            total[...] = res_ref[chunk] + total[...]

        low = total[...].astype(bf16)
        result_ref[slot] = low
        whole_out[slot] = low.astype(f32)
        line.gather_start(chunk, whole_out, out_gather)

    def seg_landed(slot):
        gseg_ref[slot] = whole_seg[slot].astype(bf16)

    def out_landed(slot):
        result_ref[slot] = whole_out[slot].astype(bf16)

    settle_at = hop * line.reach
    seg_lag, out_lag = 0, -line.reach * early

    def step(tick, _):
        flows = (
            (seg_lag, gunit_hbm, seg_load, gunit_ref, seg_scatter, settle_seg, whole_seg, seg_gather, seg_landed),
            (out_lag, branch_hbm, out_load, branch_ref, out_scatter, settle_out, whole_out, out_gather, out_landed),
        )
        @pl.when(tick == 0)
        def _():
            for load in loads:
                load.wait()

        for late, source, load, part, scatter, settle, whole, gather, landed in flows:
            fresh, new = line.chunk_at(tick - late)

            first = early if late < 0 else 0

            @pl.when(new & (fresh >= first))
            def _():
                part_load(source, part, load, fresh).wait()

            line.scatter_step(tick - late, part, scatter, first)
            chunk, due = line.chunk_at(tick - late - settle_at)

            @pl.when(due)
            def _():
                settle(chunk)

        for late, source, load, part, scatter, settle, whole, gather, landed in flows:
            line.gather_step(tick - late - settle_at, whole, gather, landed)
        small_step(tick)

        def piece_step(beat, _):
            pieces.step(beat, cross)
            tail_step(beat)
            return 0

        lax.fori_loop(beats(tick), beats(tick + 1), piece_step, 0)
        return 0

    line_ticks = line.reach * (chunks - 1) + 2 * settle_at + 1

    def beats(tick):
        return jnp.minimum((tick * pieces.beats) // (line_ticks - 5), pieces.beats)

    lax.fori_loop(0, line_ticks, step, 0)

    line.scatter_drain(gunit_ref, seg_scatter)
    line.scatter_drain(branch_ref, out_scatter, early)
    line.gather_drain(whole_seg, seg_gather)
    line.gather_drain(whole_out, out_gather)
    for column in range(across):
        for level in range(bits):
            tail_spread(column, level, False).wait_send()
        tail_copy(column).wait()
    for offset in range(1, size):
        small_across(offset, False).wait_send()
    for level in range(bits):
        small_within(level).wait_send()


def close(
    grad_unit, branch, seg_rows, grad_residual, residual, gain, early, grads, small, size, group, chunks
):
    rows, width = seg_rows.shape
    piece = rows // (chunks * size)
    vmem = pl.BlockSpec(memory_space=pltpu.VMEM)
    whole = (chunks * size, piece, width)
    piece_rows, columns, gap = max(256, 8 * group), width // 4, 3 if group <= 8 else 2
    bits = group.bit_length() - 1
    slots = 2 * bits * gap + 2
    views = [grad.reshape(-1, piece_rows, grad.shape[1]) for grad in grads]
    counts = tuple(view.shape[0] * (view.shape[2] // columns) for view in views)
    anywhere = pl.BlockSpec(memory_space=pl.ANY)
    dma = pltpu.SemaphoreType.DMA
    sums = [jax.ShapeDtypeStruct(view.shape, f32) for view in views]
    sums[0] = jax.ShapeDtypeStruct((1, piece_rows, width), f32)
    for index in range(3, len(views)):
        turned_shape = (views[index].shape[2] // columns, columns, piece_rows)
        sums[index] = jax.ShapeDtypeStruct(turned_shape, f32)
    return pl.pallas_call(
        functools.partial(close_kernel, size, group, chunks, 2, counts, gap, early.shape[0]),
        in_specs=[anywhere] * 5 + [vmem] * 2 + [anywhere] * len(views) + [vmem],
        out_specs=[vmem] * 2 + [anywhere] * len(views) + [vmem],
        out_shape=[jax.ShapeDtypeStruct(whole, bf16)] * 2 + sums + [jax.ShapeDtypeStruct(small.shape, f32)],
        scratch_shapes=[pltpu.VMEM(whole, f32)] * 2
        + [
            pltpu.VMEM(whole, bf16),
            pltpu.VMEM(grad_residual.shape, f32),
            pltpu.VMEM(grad_residual.shape, f32),
        ]
        + [pltpu.VMEM(whole, f32)] * 6
        + [
            pltpu.VMEM((piece, width), f32),
            pltpu.VMEM((slots, piece_rows, columns), f32),
            pltpu.VMEM((slots, piece_rows, columns), f32),
            pltpu.VMEM((slots, piece_rows, columns), f32),
            pltpu.VMEM((width // columns * size, piece_rows // group, columns), f32),
            pltpu.VMEM((width // columns, piece_rows, columns), f32),
            pltpu.VMEM((size, *small.shape), f32),
            pltpu.VMEM((bits, *small.shape), f32),
            pltpu.VMEM((bits, *small.shape), f32),
        ]
        + [dma((8,))]
        + [dma((chunks * size,))] * 8
        + [dma((slots * bits,))] * 4
        + [dma((slots,))] * 2
        + [dma((width // columns * size,))] * 2
        + [dma((width // columns * bits,))] * 2
        + [dma((width // columns,))]
        + [dma((size,))] * 2
        + [dma((bits,))] * 2
        + [dma((chunks,))] * 2
        + [dma((3,))],
        compiler_params=pltpu.CompilerParams(
            collective_id=1, has_side_effects=True, vmem_limit_bytes=63 << 20
        ),
        cost_estimate=pl.CostEstimate(flops=10**11, bytes_accessed=10**9, transcendentals=0),
        name="close",
    )(
        grad_unit.reshape(whole),
        branch,
        seg_rows.reshape(whole),
        grad_residual,
        residual,
        gain[None, :],
        early,
        *views,
        small,
    )


def body(
    inputs,
    memory,
    compressed_memory,
    memory_fill,
    compressed_fill,
    first_gain,
    query_weight,
    key_weight,
    value_weight,
    relative_bias,
    output_weight,
    second_gain,
    up_weight,
    down_weight,
    compress_weight,
    grad_output,
    grad_compressed,
    *,
    mp_size,
    dp_size,
):
    streams, seg_len, width = inputs.shape
    mem_len = memory.shape[1]
    packed_len = compressed_memory.shape[1]
    local = query_weight.shape[1]
    rows = streams * seg_len
    unit, q, k, v, mixed, log_total, packed_new, grad_pack, begun = attend(
        inputs,
        memory,
        compressed_memory,
        memory_fill,
        compressed_fill,
        first_gain,
        query_weight,
        key_weight,
        value_weight,
        relative_bias,
        compress_weight,
        grad_compressed,
        output_weight,
        mp_size,
        dp_size,
    )
    seg_rows = inputs.reshape(rows, width)
    grad_mixed, grad_residual, residual, branch, grad_down, grad_up, grad_out_full, grad_second = feed(
        mixed.reshape(rows, local),
        seg_rows,
        grad_output.reshape(rows, width),
        up_weight,
        down_weight,
        begun,
        second_gain,
        mp_size,
        dp_size,
        chunk_count,
    )
    grad_mixed = grad_mixed.reshape(streams, seg_len, local)
    grad_unit, gq, gk, gv, small, early = attend_back(
        unit,
        q,
        k,
        v,
        log_total,
        grad_mixed,
        memory_fill,
        compressed_fill,
        query_weight,
        key_weight,
        value_weight,
        relative_bias,
        first_gain,
        grad_second,
        mem_len,
        packed_len,
        branch,
        residual,
        mp_size,
        early_chunks,
    )
    result, grad_seg, grad_out_w, grad_up, grad_down, gq, gk, gv, grad_pack, small = close(
        grad_unit,
        branch,
        seg_rows,
        grad_residual,
        residual,
        first_gain,
        early,
        (grad_out_full, grad_up, grad_down, gq, gk, gv, grad_pack),
        small,
        mp_size,
        dp_size,
        chunk_count,
    )
    grad_first, grad_second = small[0], small[1]
    grad_relative = small[2 : 2 + relative_bias.shape[0], : relative_bias.shape[1]]
    result = result.reshape(inputs.shape)
    grad_seg = grad_seg.reshape(inputs.shape)
    grad_query_w, grad_key_w, grad_value_w = (grad.reshape(width, local) for grad in (gq, gk, gv))
    grad_out_w = grad_out_w.reshape(local, width)
    grad_compress_w = grad_pack.reshape(2 * width, local)
    grad_up = grad_up.reshape(up_weight.shape)
    grad_down = grad_down.reshape(down_weight.shape)
    return (
        result,
        packed_new,
        grad_seg,
        grad_first,
        grad_query_w,
        grad_key_w,
        grad_value_w,
        grad_relative,
        grad_out_w,
        grad_second,
        grad_up,
        grad_down,
        grad_compress_w,
    )


def solution(mesh):
    in_specs = (
        P("dp", None, None),
        P("dp", None, None),
        P("dp", None, None),
        P("dp"),
        P("dp"),
        P(),
        P(None, "mp"),
        P(None, "mp"),
        P(None, "mp"),
        P("mp", None),
        P("mp", None),
        P(),
        P(None, "mp"),
        P("mp", None),
        P(None, "mp"),
        P("dp", None, None),
        P("dp", None, "mp"),
    )
    out_specs = (
        P("dp", None, None),
        P("dp", None, "mp"),
        P("dp", None, None),
        P(),
        P(None, "mp"),
        P(None, "mp"),
        P(None, "mp"),
        P("mp", None),
        P("mp", None),
        P(),
        P(None, "mp"),
        P("mp", None),
        P(None, "mp"),
    )
    return jax.shard_map(
        functools.partial(body, mp_size=mesh.shape["mp"], dp_size=mesh.shape["dp"]),
        mesh=mesh,
        in_specs=in_specs,
        out_specs=out_specs,
        check_vma=False,
    )
```

```python
import functools
import math

import jax
import jax.numpy as jnp
from jax import lax
from jax.experimental import pallas as pl
from jax.experimental.pallas import tpu as pltpu
from jax.sharding import PartitionSpec as P

reach_marks = (1, 2, 3, 4, 5, 6, 7, 8, 12, 16, 24, 32, 48, 64, 96, 128, 192, 256, 384, 512, 768, 1024)
epsilon = 1e-06
masked_score = -1e30
block = 128
query_block = 256
chunk_count = 8
early_chunks = 2
f32 = jnp.float32
bf16 = jnp.bfloat16


def mm(left, right):
    return jnp.dot(left, right, preferred_element_type=f32)


def mm_t0(left, right):
    return lax.dot_general(left, right, (((0,), (0,)), ((), ())), preferred_element_type=f32)


def mm_t1(left, right):
    return lax.dot_general(left, right, (((1,), (1,)), ((), ())), preferred_element_type=f32)


def row_scale(source):
    return lax.rsqrt(jnp.mean(source * source, axis=-1, keepdims=True) + epsilon)


def diagonal_count(seg_len, kept_count):
    return (seg_len + kept_count) // block + 1


def diagonal_of(seg_len, kept_count, column):
    return (seg_len + kept_count) // block - 1 - column


def strip_start(seg_len, sub_block):
    return (seg_len // block - 1 - sub_block) * block


def bias_block(bias_ref, head, diagonal, transposed):
    rows = lax.broadcasted_iota(jnp.int32, (block, block), 0)
    cols = lax.broadcasted_iota(jnp.int32, (block, block), 1)
    distance = diagonal * block + ((cols - rows) if transposed else (rows - cols))
    lowest, highest = diagonal * block - block + 1, diagonal * block + block - 1
    base = jnp.float32(0.0)
    for position, mark_value in enumerate(reach_marks):
        if mark_value <= lowest:
            base = base + bias_ref[head, position]
    value = jnp.full((block, block), base, f32)
    for position, mark_value in enumerate(reach_marks):
        if lowest < mark_value <= highest:
            value = value + jnp.where(distance >= mark_value, bias_ref[head, position], 0.0)
    if lowest < 0:
        value = jnp.where(distance >= 0, value, masked_score)
    return value


def live_mask(shape, axis, packed_len, mem_len, packed_count, memory_count):
    slot = lax.broadcasted_iota(jnp.int32, shape, axis)
    dead_packed = (slot < packed_len) & (slot < packed_len - packed_count)
    dead_memory = (slot >= packed_len) & (slot < packed_len + mem_len - memory_count)
    return jnp.where(dead_packed | dead_memory, masked_score, 0.0).astype(f32)


def call(peers):
    barrier = pltpu.get_barrier_semaphore()
    for peer in peers:
        pl.semaphore_signal(barrier, inc=1, device_id=peer, device_id_type=pl.DeviceIdType.MESH)


def hear(peers):
    pl.semaphore_wait(pltpu.get_barrier_semaphore(), len(peers))


def greet(peers):
    call(peers)
    hear(peers)


class Spread:
    def __init__(self, size, group, buffer, sems):
        self.me, self.mine = lax.axis_index("mp"), lax.axis_index("dp")
        self.size, self.group, self.buffer = size, group, buffer
        self.bits = group.bit_length() - 1
        self.across_s, self.across_r, self.within_s, self.within_r = sems
        order = list(reversed(range(self.bits)))
        self.orders = (order, order[1::-1] + order[2:])
        self.spots = []
        for order in self.orders:
            spot = jnp.int32(0)
            for level, bit in enumerate(order):
                spot = spot + ((self.mine // (1 << bit)) % 2) * (1 << level)
            self.spots.append(spot)

    def place_of(self, half, member):
        return sum(((member >> bit) & 1) << level for level, bit in enumerate(self.orders[half]))

    def others(self, offset):
        return {"mp": lax.rem(self.me + offset, self.size)}

    def partner(self, half, level):
        step = 1 << self.orders[half][level]
        return {"dp": self.mine + step - 2 * step * ((self.mine // step) % 2)}

    def across(self, half, offset, arriving):
        origin = lax.rem(self.me - offset + self.size, self.size) if arriving else self.me
        return pltpu.make_async_remote_copy(
            src_ref=self.buffer.at[half, self.spots[half], origin],
            dst_ref=self.buffer.at[half, self.spots[half], origin],
            send_sem=self.across_s.at[half * self.size + offset],
            recv_sem=self.across_r.at[half * self.size + offset],
            device_id=self.others(offset),
            device_id_type=pl.DeviceIdType.MESH,
        )

    def block(self, half, level, other):
        count = 1 << level
        start = (self.spots[half] // count) * count
        if other:
            start = start + count - 2 * count * ((self.spots[half] // count) % 2)
        return pl.ds(start, count)

    def within(self, half, level, arriving):
        span = self.block(half, level, arriving)
        return pltpu.make_async_remote_copy(
            src_ref=self.buffer.at[half, span],
            dst_ref=self.buffer.at[half, span],
            send_sem=self.within_s.at[half * self.bits + level],
            recv_sem=self.within_r.at[half * self.bits + level],
            device_id=self.partner(half, level),
            device_id_type=pl.DeviceIdType.MESH,
        )

    def start_level(self, level):
        for half in range(2):
            if level:
                self.within(half, level - 1, True).wait_recv()
            self.within(half, level, False).start()


def attend_kernel(
    sizes,
    size,
    group,
    memory_fill,
    packed_fill,
    bias_ref,
    seg_ref,
    memory_ref,
    packed_ref,
    gain_ref,
    wq_ref,
    wk_ref,
    wv_ref,
    wc_ref,
    gcomp_ref,
    wo_ref,
    unit_ref,
    q_ref,
    k_ref,
    v_ref,
    mixed_ref,
    log_ref,
    packed_new_ref,
    gpack_ref,
    begun_ref,
    strip,
    live,
    mem_rows,
    spread_in,
    *sems,
):
    seg_len, mem_len, packed_len, heads, head_dim = sizes
    kept = mem_len + packed_len
    keys = kept + seg_len
    stream = pl.program_id(0)
    scale = 1.0 / math.sqrt(head_dim)
    gain = gain_ref[...]
    spread = Spread(size, group, spread_in, sems[:4])
    piece, columns = spread_in.shape[3:]
    width = gain.shape[1]

    first_peers = [spread.others(offset) for offset in range(1, size)] + [
        spread.partner(half, 0) for half in range(2)
    ]

    @pl.when(stream == 0)
    def _():
        call(first_peers)
        gpack_ref[...] = jnp.zeros_like(gpack_ref)

    slot = lax.broadcasted_iota(jnp.int32, mem_rows.shape[1:], 0)
    keep = slot >= mem_len - memory_fill[stream]
    count = packed_new_ref.shape[1]
    for column in range(mem_rows.shape[0]):
        lanes = slice(column * block, (column + 1) * block)
        mem_rows[column] = jnp.where(keep, memory_ref[0, :, lanes].astype(f32), 0.0)
    packed_new = jnp.zeros(packed_new_ref.shape[1:], f32)
    for parity in range(2):
        rows = jnp.concatenate(
            [mem_rows[column, pl.ds(parity, count, stride=2), :] for column in range(mem_rows.shape[0])], axis=1
        ).astype(bf16)
        lanes = slice(parity * width, (parity + 1) * width)
        packed_new = packed_new + mm(rows, wc_ref[lanes, :])
        gpack_ref[:, lanes] += mm_t0(gcomp_ref[0], rows)
    packed_new_ref[0] = packed_new.astype(bf16)

    @pl.when(stream == 0)
    def _():
        hear(first_peers)
        rows = pl.ds(pl.multiple_of(spread.mine * piece, piece), piece)
        for half in range(2):
            lanes = slice(half * columns, (half + 1) * columns)
            spread_in[half, spread.spots[half], spread.me] = wo_ref[rows, lanes].astype(f32)
            for offset in range(1, size):
                spread.across(half, offset, False).start()

    start = 0
    for part_ref, length in ((packed_ref, packed_len), (memory_ref, mem_len), (seg_ref, seg_len)):
        rows = part_ref[0].astype(f32)
        unit = (rows * row_scale(rows) * gain).astype(bf16)
        unit_ref[0, start : start + length, :] = unit
        k_ref[0, start : start + length, :] = mm(unit, wk_ref[...]).astype(bf16)
        v_ref[0, start : start + length, :] = mm(unit, wv_ref[...]).astype(bf16)
        if start == kept:
            q_ref[0] = mm(unit, wq_ref[...]).astype(bf16)
        start += length
    live[...] = live_mask((8, kept), 1, packed_len, mem_len, packed_fill[stream], memory_fill[stream])
    for head in range(heads):
        lanes = slice(head * head_dim, (head + 1) * head_dim)
        for column in range(diagonal_count(seg_len, kept)):
            strip[:, column * block : (column + 1) * block] = bias_block(
                bias_ref, head, diagonal_of(seg_len, kept, column), False
            )
        for index in range(seg_len // query_block):
            reach = kept + (index + 1) * query_block
            rows = slice(index * query_block, (index + 1) * query_block)
            score = mm_t1(q_ref[0, rows, lanes], k_ref[0, :reach, lanes]) * scale
            parts = []
            for sub in range(query_block // block):
                first = strip_start(seg_len, index * (query_block // block) + sub)
                parts.append(strip[:, first : first + reach])
            score = score + jnp.concatenate(parts, axis=0)
            score = jnp.concatenate([score[:, :kept] + live[0:1, :], score[:, kept:]], axis=1)
            top = jnp.max(score, axis=-1, keepdims=True)
            weight = jnp.exp(score - top)
            total = jnp.sum(weight, axis=-1, keepdims=True)
            log_total = jnp.broadcast_to(top + jnp.log(total), (query_block, block))
            log_ref[0, head, :, rows] = log_total.T[0:1, :]
            mixed = mm(weight.astype(bf16), v_ref[0, :reach, lanes]) * (1.0 / total)
            mixed_ref[0, rows, lanes] = mixed.astype(bf16)

    @pl.when(stream == 0)
    def _():
        for half in range(2):
            for offset in range(1, size):
                spread.across(half, offset, True).wait_recv()
        spread.start_level(0)

    @pl.when(stream == pl.num_programs(0) - 1)
    def _():
        copies = []
        for half in range(2):
            spread.within(half, 0, True).wait_recv()
            pair = spread_in.at[half, pl.ds((spread.spots[half] // 2) * 2, 2)]
            copies.append(pltpu.make_async_copy(pair, begun_ref.at[half], sems[4].at[half]))
            copies[-1].start()
        for half in range(2):
            for offset in range(1, size):
                spread.across(half, offset, False).wait_send()
            spread.within(half, 0, False).wait_send()
            copies[half].wait()


def attend(
    inputs, memory, packed, memory_fill, packed_fill, gain, wq, wk, wv, bias, wc, gcomp, wo, size, group
):
    streams, seg_len, width = inputs.shape
    mem_len, packed_len = memory.shape[1], packed.shape[1]
    heads = bias.shape[0]
    local = wq.shape[1]
    keys = seg_len + mem_len + packed_len
    sizes = (seg_len, mem_len, packed_len, heads, local // heads)
    smem = pl.BlockSpec(memory_space=pltpu.SMEM)
    compress_count = gcomp.shape[1]
    piece = wo.shape[0] // group
    bits = group.bit_length() - 1

    def rows_of(count, columns):
        return pl.BlockSpec((1, count, columns), lambda s: (s, 0, 0))

    def whole(shape):
        return pl.BlockSpec(shape, lambda s: (0,) * len(shape))

    return pl.pallas_call(
        functools.partial(attend_kernel, sizes, size, group),
        grid=(streams,),
        in_specs=[
            smem,
            smem,
            smem,
            rows_of(seg_len, width),
            rows_of(mem_len, width),
            rows_of(packed_len, width),
            whole((1, width)),
            whole(wq.shape),
            whole(wk.shape),
            whole(wv.shape),
            whole(wc.shape),
            rows_of(compress_count, local),
            whole(wo.shape),
        ],
        out_specs=[
            rows_of(keys, width),
            rows_of(seg_len, local),
            rows_of(keys, local),
            rows_of(keys, local),
            rows_of(seg_len, local),
            pl.BlockSpec((1, heads, 1, seg_len), lambda s: (s, 0, 0, 0)),
            rows_of(compress_count, local),
            whole((local, 2 * width)),
            pl.BlockSpec(memory_space=pl.ANY),
        ],
        out_shape=[
            jax.ShapeDtypeStruct((streams, keys, width), bf16),
            jax.ShapeDtypeStruct((streams, seg_len, local), bf16),
            jax.ShapeDtypeStruct((streams, keys, local), bf16),
            jax.ShapeDtypeStruct((streams, keys, local), bf16),
            jax.ShapeDtypeStruct((streams, seg_len, local), bf16),
            jax.ShapeDtypeStruct((streams, heads, 1, seg_len), f32),
            jax.ShapeDtypeStruct((streams, compress_count, local), bf16),
            jax.ShapeDtypeStruct((local, 2 * width), f32),
            jax.ShapeDtypeStruct((2, 2, size, piece, width // 2), f32),
        ],
        scratch_shapes=[
            pltpu.VMEM((block, diagonal_count(seg_len, mem_len + packed_len) * block), f32),
            pltpu.VMEM((8, mem_len + packed_len), f32),
            pltpu.VMEM((width // block, mem_len, block), f32),
            pltpu.VMEM((2, group, size, piece, width // 2), f32),
            pltpu.SemaphoreType.DMA((2 * size,)),
            pltpu.SemaphoreType.DMA((2 * size,)),
            pltpu.SemaphoreType.DMA((2 * bits,)),
            pltpu.SemaphoreType.DMA((2 * bits,)),
            pltpu.SemaphoreType.DMA((2,)),
        ],
        compiler_params=pltpu.CompilerParams(
            collective_id=2, has_side_effects=True, vmem_limit_bytes=60 << 20
        ),
        cost_estimate=pl.CostEstimate(
            flops=streams * (2 * keys * width * local * 3 + 4 * seg_len * keys * local),
            bytes_accessed=streams * keys * (width * 4 + local * 6),
            transcendentals=streams * heads * seg_len * keys,
        ),
        name="attend",
    )(memory_fill, packed_fill, bias, inputs, memory, packed, gain[None, :], wq, wk, wv, wc, gcomp, wo)


class Line:
    def __init__(self, size, chunks, hop):
        self.me = lax.axis_index("mp")
        self.size, self.chunks, self.hop = size, chunks, hop
        self.reach = size - 1

    def place(self, right):
        return self.me if right else self.reach - self.me

    def peer(self, right):
        return {"mp": self.me + 1 if right else self.me - 1}

    def copy(self, source, target, sems, slot, right):
        return pltpu.make_async_remote_copy(
            src_ref=source.at[slot],
            dst_ref=target.at[slot],
            send_sem=sems[0],
            recv_sem=sems[1].at[slot],
            device_id=self.peer(right),
            device_id_type=pl.DeviceIdType.MESH,
        )

    def chunk_at(self, tick):
        positive = jnp.maximum(tick, 0)
        chunk = positive // self.reach
        return chunk, (tick >= 0) & (positive == chunk * self.reach) & (chunk < self.chunks)

    def scatter_step(self, tick, part, lanes, first=0):
        for right, held, sems in lanes:
            place = self.place(right)
            late = tick - self.hop * place
            positive = jnp.maximum(late, 0)
            chunk = positive // self.reach
            goal = self.reach - (positive - self.reach * chunk)
            active = (late >= 0) & (chunk >= first) & (chunk < self.chunks) & (goal > place)
            slot = chunk * self.size + (goal if right else self.reach - goal)

            @pl.when(active & (place == 0))
            def _():
                self.copy(part, held, sems, slot, right).start()

            @pl.when(active & (place > 0))
            def _():
                self.copy(held, held, sems, slot, right).wait_recv()
                held[slot] = held[slot] + part[slot]
                self.copy(held, held, sems, slot, right).start()

    def scatter_sum(self, chunk, part, lanes, total):
        slot = chunk * self.size + self.me
        total[...] = part[slot]
        for right, held, sems in lanes:

            @pl.when(self.place(right) > 0)
            def _():
                self.copy(held, held, sems, slot, right).wait_recv()
                total[...] = total[...] + held[slot]

    def gather_start(self, chunk, whole, lanes):
        slot = chunk * self.size + self.me
        for right, sems in lanes:

            @pl.when(self.place(right) < self.reach)
            def _():
                self.copy(whole, whole, sems, slot, right).start()

    def gather_step(self, tick, whole, lanes, landed=None):
        for right, sems in lanes:
            place = self.place(right)
            for distance in range(1, self.size):
                chunk, due = self.chunk_at(tick - self.hop * distance)

                @pl.when(due & (distance <= place))
                def _():
                    slot = chunk * self.size + (self.me - distance if right else self.me + distance)
                    self.copy(whole, whole, sems, slot, right).wait_recv()

                    @pl.when(place < self.reach)
                    def _():
                        self.copy(whole, whole, sems, slot, right).start()

                    if landed is not None:
                        landed(slot)

    def sent(self, buffer, send_sem, count, right):
        some = buffer.at[pl.ds(0, count)]
        return pltpu.make_async_remote_copy(
            src_ref=some,
            dst_ref=some,
            send_sem=send_sem,
            recv_sem=send_sem,
            device_id=self.peer(right),
            device_id_type=pl.DeviceIdType.MESH,
        )

    def scatter_drain(self, part, lanes, first=0):
        for right, held, sems in lanes:
            for place in range(self.reach):

                @pl.when(self.place(right) == place)
                def _():
                    self.sent(part, sems[0], (self.reach - place) * (self.chunks - first), right).wait_send()

    def gather_drain(self, whole, lanes):
        for right, sems in lanes:
            for place in range(self.reach):

                @pl.when(self.place(right) == place)
                def _():
                    self.sent(whole, sems[0], (place + 1) * self.chunks, right).wait_send()


def call_neighbours(line):
    barrier = pltpu.get_barrier_semaphore()
    for right in (True, False):

        @pl.when(line.place(right) < line.reach)
        def _():
            pl.semaphore_signal(
                barrier, inc=1, device_id=line.peer(right), device_id_type=pl.DeviceIdType.MESH
            )


def hear_neighbours(line):
    barrier = pltpu.get_barrier_semaphore()
    inner = (line.me > 0) & (line.me < line.reach)

    @pl.when(inner)
    def _():
        pl.semaphore_wait(barrier, 2)

    @pl.when(jnp.logical_not(inner))
    def _():
        pl.semaphore_wait(barrier, 1)


def attend_back_kernel(
    sizes,
    size,
    early,
    hop,
    memory_fill,
    packed_fill,
    bias_ref,
    unit_ref,
    q_ref,
    k_ref,
    v_ref,
    log_ref,
    gm_ref,
    wq_ref,
    wk_ref,
    wv_ref,
    gain_ref,
    gsecond_ref,
    branch_hbm,
    res_hbm,
    gunit_ref,
    gq_ref,
    gk_ref,
    gv_ref,
    small_ref,
    early_ref,
    strip,
    live,
    dk_sum,
    dv_sum,
    dq_low,
    dk_low,
    dv_low,
    strip_sum,
    branch_ref,
    res_ref,
    held_right,
    held_left,
    total_ref,
    load_sem,
    line_s,
    right_r,
    left_r,
):
    seg_len, mem_len, packed_len, heads, head_dim = sizes
    kept = mem_len + packed_len
    keys = kept + seg_len
    stream = pl.program_id(0)
    scale = 1.0 / math.sqrt(head_dim)

    line = Line(size, early, hop)
    lanes_out = ((True, held_right, (line_s.at[0], right_r)), (False, held_left, (line_s.at[1], left_r)))
    loads = (
        pltpu.make_async_copy(branch_hbm.at[pl.ds(0, early * size)], branch_ref, load_sem.at[0]),
        pltpu.make_async_copy(res_hbm.at[pl.ds(0, early)], res_ref, load_sem.at[1]),
    )
    ticks = line.reach * (early - 1) + hop * line.reach + 1
    spans = heads * (seg_len // query_block)
    starts = [22 * index for index in range(spans + 1)]
    starts += [starts[-1] + 6, starts[-1] + 17, starts[-1] + 28, starts[-1] + 36]

    def line_step(tick, _):
        line.scatter_step(tick, branch_ref, lanes_out)
        chunk, due = line.chunk_at(tick - hop * line.reach)

        @pl.when(due)
        def _():
            line.scatter_sum(chunk, branch_ref, lanes_out, total_ref)
            early_ref[chunk] = (res_ref[chunk] + total_ref[...]).astype(bf16).astype(f32)

        return 0

    def line_span(index):
        if index == 0:
            return
        late = starts[1]
        begin = starts[index] if index > 1 else 0
        every = starts[-1] * pl.num_programs(0) - late
        here = jnp.maximum(stream * starts[-1] + begin - late, 0)
        after = jnp.maximum(stream * starts[-1] + starts[index + 1] - late, 0)
        if index == 1:

            @pl.when(stream == 0)
            def _():
                hear_neighbours(line)
                for load in loads:
                    load.wait()

        lax.fori_loop((here * ticks) // every, (after * ticks) // every, line_step, 0)

    @pl.when(stream == 0)
    def _():
        for load in loads:
            load.start()
        call_neighbours(line)
        strip_sum[...] = jnp.zeros_like(strip_sum)
        gq_ref[...] = jnp.zeros_like(gq_ref)
        gk_ref[...] = jnp.zeros_like(gk_ref)
        gv_ref[...] = jnp.zeros_like(gv_ref)

    live[...] = live_mask((kept, block), 0, packed_len, mem_len, packed_fill[stream], memory_fill[stream])
    subs = query_block // block
    for head in range(heads):
        lanes = slice(head * head_dim, (head + 1) * head_dim)
        for column in range(diagonal_count(seg_len, kept)):
            strip[column * block : (column + 1) * block, :] = bias_block(
                bias_ref, head, diagonal_of(seg_len, kept, column), True
            )
        for index in range(seg_len // query_block):
            line_span(head * (seg_len // query_block) + index)
            reach = kept + (index + 1) * query_block
            rows = slice(index * query_block, (index + 1) * query_block)
            queries = q_ref[0, rows, lanes]
            grads = gm_ref[0, rows, lanes]
            key_rows = k_ref[0, :reach, lanes]
            score = mm_t1(key_rows, queries) * scale
            firsts = [strip_start(seg_len, index * subs + sub) for sub in range(subs)]
            score = score + jnp.concatenate([strip[first : first + reach, :] for first in firsts], axis=1)
            live_wide = jnp.concatenate([live[...]] * subs, axis=1)
            score = jnp.concatenate([score[:kept] + live_wide, score[kept:]], axis=0)
            prob = jnp.exp(score - log_ref[0, head, :, rows])
            grad_prob = mm_t1(v_ref[0, :reach, lanes], grads)
            delta = jnp.sum(prob * grad_prob, axis=0, keepdims=True)
            grad_score = (prob * (grad_prob - delta)).astype(bf16)
            dk_part = mm(grad_score, queries)
            dv_part = mm(prob.astype(bf16), grads)
            if index == seg_len // query_block - 1:
                earlier = kept + index * query_block
                if index:
                    dk_sum[:earlier] += dk_part[:earlier]
                    dv_sum[:earlier] += dv_part[:earlier]
                    dk_sum[earlier:] = dk_part[earlier:]
                    dv_sum[earlier:] = dv_part[earlier:]
                else:
                    dk_sum[...] = dk_part
                    dv_sum[...] = dv_part
            elif index:
                earlier = kept + index * query_block
                dk_sum[:earlier] += dk_part[:earlier]
                dv_sum[:earlier] += dv_part[:earlier]
                dk_sum[earlier:reach] = dk_part[earlier:]
                dv_sum[earlier:reach] = dv_part[earlier:]
            else:
                dk_sum[:reach] = dk_part
                dv_sum[:reach] = dv_part
            dq_low[rows, lanes] = (mm_t0(grad_score, key_rows) * scale).astype(bf16)
            for sub in range(subs):
                strip_sum[head, firsts[sub] : firsts[sub] + reach, :] += grad_score[
                    :, sub * block : (sub + 1) * block
                ].astype(f32)
        dk_low[:, lanes] = (dk_sum[...] * scale).astype(bf16)
        dv_low[:, lanes] = dv_sum[...].astype(bf16)
    line_span(spans)
    gq_ref[...] += mm_t0(dq_low[...], unit_ref[0, kept:, :])
    line_span(spans + 1)
    gk_ref[...] += mm_t0(dk_low[...], unit_ref[0])
    line_span(spans + 2)
    gv_ref[...] += mm_t0(dv_low[...], unit_ref[0])
    line_span(spans + 3)
    gunit_ref[0] = (
        mm_t1(dq_low[...], wq_ref[...])
        + mm_t1(dk_low[kept:, :], wk_ref[...])
        + mm_t1(dv_low[kept:, :], wv_ref[...])
    )

    @pl.when(stream == pl.num_programs(0) - 1)
    def _():
        line.scatter_drain(branch_ref, lanes_out)
        rows = lax.broadcasted_iota(jnp.int32, (block, block), 0)
        cols = lax.broadcasted_iota(jnp.int32, (block, block), 1)
        width = gain_ref.shape[1]
        lane = lax.broadcasted_iota(jnp.int32, (1, width), 1)
        relative = [jnp.zeros((1, width), f32) for _ in range(heads)]
        for head in range(heads):
            blocks = []
            for column in range(diagonal_count(seg_len, kept)):
                blocks.append(strip_sum[head, column * block : (column + 1) * block, :])
            for position, mark_value in enumerate(reach_marks):
                total = jnp.zeros((1, block), f32)
                for column, value in enumerate(blocks):
                    diagonal = diagonal_of(seg_len, kept, column)
                    lowest, highest = diagonal * block - block + 1, diagonal * block + block - 1
                    if mark_value <= lowest:
                        total = total + jnp.sum(value, axis=0, keepdims=True)
                    elif mark_value <= highest:
                        distance = diagonal * block + cols - rows
                        total = total + jnp.sum(
                            jnp.where(distance >= mark_value, value, 0.0), axis=0, keepdims=True
                        )
                total = jnp.sum(total, axis=1, keepdims=True)
                relative[head] = jnp.where(lane == position, total, relative[head])
        first = jnp.zeros((1, width), f32)
        for grad_ref, weight_ref in ((gq_ref, wq_ref), (gk_ref, wk_ref), (gv_ref, wv_ref)):
            turned = weight_ref[...].astype(f32).T
            first = first + jnp.sum(grad_ref[...] * turned, axis=0, keepdims=True)
        small_ref[...] = jnp.concatenate(
            [first / gain_ref[...], gsecond_ref[...], *relative, jnp.zeros((6 - heads, width), f32)], axis=0
        )


def attend_back(
    unit, q, k, v, log_total, grad_mixed, memory_fill, packed_fill, wq, wk, wv, bias, gain, grad_second, mem_len, packed_len,
    branch, residual, size, early,
):
    streams, keys, width = unit.shape
    seg_len, local = q.shape[1:]
    heads = bias.shape[0]
    kept = mem_len + packed_len
    sizes = (seg_len, mem_len, packed_len, heads, local // heads)
    smem = pl.BlockSpec(memory_space=pltpu.SMEM)
    strip_len = diagonal_count(seg_len, kept) * block
    part = (early * size, *branch.shape[1:])

    def rows_of(count, columns):
        return pl.BlockSpec((1, count, columns), lambda s: (s, 0, 0))

    def whole(shape):
        return pl.BlockSpec(shape, lambda s: (0,) * len(shape))

    return pl.pallas_call(
        functools.partial(attend_back_kernel, sizes, size, early, 3),
        grid=(streams,),
        in_specs=[
            smem,
            smem,
            smem,
            rows_of(keys, width),
            rows_of(seg_len, local),
            rows_of(keys, local),
            rows_of(keys, local),
            pl.BlockSpec((1, heads, 1, seg_len), lambda s: (s, 0, 0, 0)),
            rows_of(seg_len, local),
            whole(wq.shape),
            whole(wk.shape),
            whole(wv.shape),
            whole((1, width)),
            whole((1, width)),
            pl.BlockSpec(memory_space=pl.ANY),
            pl.BlockSpec(memory_space=pl.ANY),
        ],
        out_specs=[
            rows_of(seg_len, width),
            whole((local, width)),
            whole((local, width)),
            whole((local, width)),
            whole((8, width)),
            whole((early, *residual.shape[1:])),
        ],
        out_shape=[
            jax.ShapeDtypeStruct((streams, seg_len, width), f32),
            jax.ShapeDtypeStruct((local, width), f32),
            jax.ShapeDtypeStruct((local, width), f32),
            jax.ShapeDtypeStruct((local, width), f32),
            jax.ShapeDtypeStruct((8, width), f32),
            jax.ShapeDtypeStruct((early, *residual.shape[1:]), f32),
        ],
        scratch_shapes=[
            pltpu.VMEM((strip_len, block), f32),
            pltpu.VMEM((kept, block), f32),
            pltpu.VMEM((keys, local // heads), f32),
            pltpu.VMEM((keys, local // heads), f32),
            pltpu.VMEM((seg_len, local), bf16),
            pltpu.VMEM((keys, local), bf16),
            pltpu.VMEM((keys, local), bf16),
            pltpu.VMEM((heads, strip_len, block), f32),
            pltpu.VMEM(part, f32),
            pltpu.VMEM((early, *part[1:]), f32),
            pltpu.VMEM(part, f32),
            pltpu.VMEM(part, f32),
            pltpu.VMEM(part[1:], f32),
            pltpu.SemaphoreType.DMA((2,)),
            pltpu.SemaphoreType.DMA((2,)),
            pltpu.SemaphoreType.DMA((early * size,)),
            pltpu.SemaphoreType.DMA((early * size,)),
        ],
        compiler_params=pltpu.CompilerParams(
            collective_id=3, has_side_effects=True, vmem_limit_bytes=60 << 20
        ),
        cost_estimate=pl.CostEstimate(
            flops=streams * (8 * keys * width * local + 10 * seg_len * keys * local),
            bytes_accessed=streams * keys * (width * 2 + local * 6),
            transcendentals=streams * heads * seg_len * keys,
        ),
        name="attend_back",
    )(
        memory_fill,
        packed_fill,
        bias,
        unit,
        q,
        k,
        v,
        log_total,
        grad_mixed,
        wq,
        wk,
        wv,
        gain[None, :],
        grad_second,
        branch,
        residual,
    )


def feed_kernel(
    size,
    group,
    chunks,
    hop,
    delay,
    beat,
    mixed_ref,
    seg_hbm,
    grad_hbm,
    up_hbm,
    down_hbm,
    begun_ref,
    gain_ref,
    gm_ref,
    gres_ref,
    res_ref,
    branch_hbm,
    gdown_hbm,
    gup_hbm,
    gout_hbm,
    gsecond_ref,
    seg_ref,
    grad_ref,
    up_ref,
    down_ref,
    branch_ref,
    gdown_ref,
    gup_ref,
    gout_ref,
    acted,
    graded,
    normed_low,
    heads_in,
    part,
    held_right,
    held_left,
    swap_out,
    swap_in,
    weights_in,
    weights,
    chunk_rows,
    total,
    own_mixed,
    own_grad,
    *sems,
):
    line = Line(size, chunks, hop)
    me = line.me
    (line_s, hr_r, hl_r, sr_r, sl_r, swap_sem, wd_s, wd_r, load_sem, save_sem, branch_sem) = sems
    gather_lanes = ((True, (line_s.at[0], hr_r)), (False, (line_s.at[1], hl_r)))
    scatter_lanes = ((True, held_right, (line_s.at[2], sr_r)), (False, held_left, (line_s.at[3], sl_r)))
    loads = [
        pltpu.make_async_copy(source, target, load_sem.at[index])
        for index, (source, target) in enumerate(
            ((seg_hbm, seg_ref), (grad_hbm, grad_ref), (up_hbm, up_ref), (down_hbm, down_ref))
        )
    ]
    for load in loads:
        load.start()
    spread = Spread(size, group, weights_in, (None, None, wd_s, wd_r))
    bits = spread.bits
    piece, columns = weights_in.shape[3:]
    width = weights.shape[1]
    rows = total.shape[0]
    local = mixed_ref.shape[-1]
    greet(
        [spread.others(offset) for offset in range(1, size)]
        + [spread.partner(half, level) for half in range(2) for level in range(1, bits)]
    )
    for half in range(2):
        weights_in[half, pl.ds((spread.spots[half] // 2) * 2, 2)] = begun_ref[half]
        spread.within(half, 1, False).start()

    def stage_heads(chunk, _):
        heads_in[chunk * size + me] = mixed_ref[chunk].astype(f32)
        return 0

    lax.fori_loop(0, chunks, stage_heads, 0)
    gsecond_ref[...] = jnp.zeros_like(gsecond_ref)
    gdown_ref[...] = jnp.zeros_like(gdown_ref)
    gup_ref[...] = jnp.zeros_like(gup_ref)

    def weight_step(tick):
        for level in range(2, bits):

            @pl.when(tick == beat + level - 2)
            def _():
                spread.start_level(level)

    def weight_finish():
        for half in range(2):
            spread.within(half, bits - 1, True).wait_recv()
            for index in range(size):
                pieces = [weights_in[half, spread.place_of(half, member), index] for member in range(group)]
                weights[index * group * piece : (index + 1) * group * piece, half * columns : (half + 1) * columns] = (
                    jnp.concatenate(pieces, axis=0).astype(bf16)
                )

    own = pl.ds(pl.multiple_of(me * rows, rows), rows)

    def feed_chunk(chunk):
        heads = [heads_in[chunk * size + index].astype(bf16) for index in range(size)]
        for index in range(size):
            own_mixed[chunk, :, index * local : (index + 1) * local] = heads_in[
                chunk * size + index, own, :
            ].astype(bf16)
        residual = seg_ref[chunk].astype(f32) + mm(jnp.concatenate(heads, axis=1), weights[...])
        chunk_rows[...] = residual
        res_ref[chunk] = chunk_rows[own, :]
        ffn_input = (residual * row_scale(residual) * gain_ref[...]).astype(bf16)
        pre_act = mm(ffn_input, up_ref[...])
        inner = math.sqrt(2.0 / math.pi)
        squared = pre_act * pre_act
        tanh = jnp.tanh(inner * (pre_act + 0.044715 * pre_act * squared))
        activated = (0.5 * pre_act * (1.0 + tanh)).astype(bf16)
        slope = 0.5 * (1.0 + tanh) + 0.5 * pre_act * (1.0 - tanh * tanh) * (
            inner * (1.0 + 3.0 * 0.044715 * squared)
        )
        grads = grad_ref[chunk]
        grad_pre = (slope * mm_t1(grads, down_ref[...])).astype(bf16)
        first = pl.ds(chunk * size, size)
        part[first] = mm_t1(grad_pre, up_ref[...]).reshape(size, rows, width)
        acted[...] = activated
        graded[...] = grad_pre
        normed_low[...] = ffn_input

    def save_branch(chunk):
        here = pl.ds(chunk * size, size)
        return pltpu.make_async_copy(branch_ref.at[here], branch_hbm.at[here], branch_sem.at[chunk])

    def feed_branch(chunk):
        branch_ref[pl.ds(chunk * size, size)] = mm(acted[...], down_ref[...]).reshape(size, rows, width)
        save_branch(chunk).start()
        gdown_ref[...] += mm_t0(acted[...], grad_ref[chunk])

    def feed_grads(chunk):
        gup_ref[...] += mm_t0(normed_low[...], graded[...])

    saves = [
        pltpu.make_async_copy(source, target, save_sem.at[index])
        for index, (source, target) in enumerate(
            ((gdown_ref, gdown_hbm), (gup_ref, gup_hbm), (gout_ref, gout_hbm))
        )
    ]

    def swap(chunk, offset):
        target = lax.rem(me + offset, size)
        return pltpu.make_async_remote_copy(
            src_ref=swap_out.at[chunk * size + target],
            dst_ref=swap_in.at[chunk * size + me],
            send_sem=swap_sem.at[0],
            recv_sem=swap_sem.at[1],
            device_id={"mp": target},
            device_id_type=pl.DeviceIdType.MESH,
        )

    def all_swaps():
        some = pl.ds(0, chunks * (size - 1))
        return pltpu.make_async_remote_copy(
            src_ref=swap_out.at[some],
            dst_ref=swap_in.at[some],
            send_sem=swap_sem.at[0],
            recv_sem=swap_sem.at[1],
            device_id=spread.others(1),
            device_id_type=pl.DeviceIdType.MESH,
        )

    def settle(chunk):
        line.scatter_sum(chunk, part, scatter_lanes, total)
        grad_ffn = total[...]
        residual = res_ref[chunk]
        scale = row_scale(residual)
        normed = residual * scale
        gsecond_ref[...] += jnp.sum(grad_ffn * normed, axis=0, keepdims=True)
        weighted = grad_ffn * gain_ref[...]
        own_rows = grad_ref[chunk, own, :].astype(f32)
        grad_residual = own_rows + scale * (
            weighted - normed * jnp.mean(weighted * normed, axis=-1, keepdims=True)
        )
        gres_ref[chunk] = grad_residual
        low = grad_residual.astype(bf16)
        own_grad[chunk] = low
        grad_mixed = mm_t1(low, weights[...]).astype(bf16).astype(f32)
        for index in range(size):
            swap_out[chunk * size + index] = grad_mixed[:, index * local : (index + 1) * local]
        for offset in range(1, size):
            swap(chunk, offset).start()

    feed_at = hop * line.reach + delay

    def step(tick, _):
        weight_step(tick)

        @pl.when(tick == feed_at)
        def _():
            weight_finish()
            for load in loads:
                load.wait()

        chunk, due = line.chunk_at(tick)

        @pl.when(due)
        def _():
            line.gather_start(chunk, heads_in, gather_lanes)

        line.gather_step(tick, heads_in, gather_lanes)
        chunk_f, due_f = line.chunk_at(tick - feed_at)

        @pl.when(due_f)
        def _():
            feed_chunk(chunk_f)

        line.scatter_step(tick - feed_at, part, scatter_lanes)
        for late, work in ((1, feed_branch), (2, feed_grads)):
            chunk_w, due_w = line.chunk_at(tick - feed_at - late)

            @pl.when(due_w)
            def _():
                work(chunk_w)

        @pl.when(tick == feed_at + line.reach * (chunks - 1) + 3)
        def _():
            for save in saves[:2]:
                save.start()

        chunk_s, due_s = line.chunk_at(tick - feed_at - hop * line.reach)

        @pl.when(due_s)
        def _():
            settle(chunk_s)

        return 0

    lax.fori_loop(0, feed_at + line.reach * (chunks - 1) + hop * line.reach + 1, step, 0)
    gout_ref[...] = mm_t0(
        own_mixed[...].reshape(chunks * rows, width), own_grad[...].reshape(chunks * rows, width)
    )

    saves[2].start()
    all_swaps().wait_recv()

    def finish(chunk, _):
        save_branch(chunk).wait()
        for index in range(size):

            @pl.when(index == me)
            def _():
                gm_ref[chunk * size + index] = swap_out[chunk * size + index].astype(bf16)

            @pl.when(index != me)
            def _():
                gm_ref[chunk * size + index] = swap_in[chunk * size + index].astype(bf16)

        return 0

    lax.fori_loop(0, chunks, finish, 0)
    line.gather_drain(heads_in, gather_lanes)
    line.scatter_drain(part, scatter_lanes)
    all_swaps().wait_send()
    for save in saves:
        save.wait()
    for half in range(2):
        for level in range(1, bits):
            spread.within(half, level, False).wait_send()


def feed(mixed, seg_rows, grad_rows, up, down, begun, gain, size, group, chunks):
    rows, width = seg_rows.shape
    local = mixed.shape[1]
    chunk = rows // chunks
    piece = chunk // size
    hidden = up.shape[1]
    vmem = pl.BlockSpec(memory_space=pltpu.VMEM)
    anywhere = pl.BlockSpec(memory_space=pl.ANY)
    dma = pltpu.SemaphoreType.DMA
    slots = dma((chunks * size,))
    bits = group.bit_length() - 1
    return pl.pallas_call(
        functools.partial(feed_kernel, size, group, chunks, 2, 0, 4),
        in_specs=[vmem] + [anywhere] * 4 + [vmem] * 2,
        out_specs=[vmem] * 3 + [anywhere] * 4 + [vmem],
        out_shape=[
            jax.ShapeDtypeStruct((chunks * size, piece, local), bf16),
            jax.ShapeDtypeStruct((chunks, piece, width), f32),
            jax.ShapeDtypeStruct((chunks, piece, width), f32),
            jax.ShapeDtypeStruct((chunks * size, piece, width), f32),
            jax.ShapeDtypeStruct((hidden, width), f32),
            jax.ShapeDtypeStruct((width, hidden), f32),
            jax.ShapeDtypeStruct((width, width), f32),
            jax.ShapeDtypeStruct((1, width), f32),
        ],
        scratch_shapes=[
            pltpu.VMEM((chunks, chunk, width), bf16),
            pltpu.VMEM((chunks, chunk, width), bf16),
            pltpu.VMEM(up.shape, bf16),
            pltpu.VMEM(down.shape, bf16),
            pltpu.VMEM((chunks * size, piece, width), f32),
            pltpu.VMEM((hidden, width), f32),
            pltpu.VMEM((width, hidden), f32),
            pltpu.VMEM((width, width), f32),
            pltpu.VMEM((chunk, hidden), bf16),
            pltpu.VMEM((chunk, hidden), bf16),
            pltpu.VMEM((chunk, width), bf16),
            pltpu.VMEM((chunks * size, chunk, local), f32),
            pltpu.VMEM((chunks * size, piece, width), f32),
            pltpu.VMEM((chunks * size, piece, width), f32),
            pltpu.VMEM((chunks * size, piece, width), f32),
            pltpu.VMEM((chunks * size, piece, local), f32),
            pltpu.VMEM((chunks * size, piece, local), f32),
            pltpu.VMEM((2, group, *begun.shape[2:]), f32),
            pltpu.VMEM((width, width), bf16),
            pltpu.VMEM((chunk, width), f32),
            pltpu.VMEM((piece, width), f32),
            pltpu.VMEM((chunks, piece, width), bf16),
            pltpu.VMEM((chunks, piece, width), bf16),
        ]
        + [dma((4,))]
        + [slots] * 4
        + [dma((2,)), dma((2 * bits,)), dma((2 * bits,)), dma((4,)), dma((3,)), dma((chunks,))],
        compiler_params=pltpu.CompilerParams(
            collective_id=0, has_side_effects=True, vmem_limit_bytes=63 << 20
        ),
        name="feed",
    )(
        mixed.reshape(chunks, chunk, local),
        seg_rows.reshape(chunks, chunk, width),
        grad_rows.reshape(chunks, chunk, width),
        up,
        down,
        begun,
        gain[None, :],
    )


class Pieces:
    def __init__(self, group, rows, gap, crossing, jobs, work, landing, summed, sems):
        self.mine = lax.axis_index("dp")
        self.bits = group.bit_length() - 1
        self.rows, self.gap, self.crossing, self.jobs = rows, gap, crossing, jobs
        self.work, self.landing, self.summed = work, landing, summed
        self.slots = work.shape[0]
        (self.rs_s, self.rs_r, self.ag_s, self.ag_r, self.load_sem, self.store_sem) = sems
        self.count = crossing[0] + sum(job[2] for job in jobs)
        self.turned = self.count - sum(job[2] for job in jobs if job[1].shape != job[0].shape)
        self.beats = self.count + 2 * self.bits * gap + 2

    def step_of(self, odd, level):
        even_step = 1 << level
        odd_step = 1 << ((self.bits - level) % self.bits)
        return jnp.where(odd == 1, odd_step, even_step)

    def bit_of(self, odd, level):
        return (self.mine // self.step_of(odd, level)) % 2

    def partner(self, odd, level):
        step = self.step_of(odd, level)
        return {"dp": self.mine + step - 2 * step * self.bit_of(odd, level)}

    def start_of(self, odd, level):
        start = jnp.int32(0)
        for earlier in range(level):
            start = start + self.bit_of(odd, earlier) * (self.rows >> (earlier + 1))
        return start

    def span(self, start, level):
        length = self.rows >> level
        return pl.ds(pl.multiple_of(start, self.rows >> self.bits), length)

    def halves(self, odd, level):
        start, bit, half = self.start_of(odd, level), self.bit_of(odd, level), self.rows >> (level + 1)
        return self.span(start + bit * half, level + 1), self.span(start + (1 - bit) * half, level + 1)

    def reduce_copy(self, slot, odd, level):
        _, give = self.halves(odd, level)
        region = pl.ds(self.rows - (self.rows >> level), self.rows >> (level + 1))
        return pltpu.make_async_remote_copy(
            src_ref=self.work.at[slot, give],
            dst_ref=self.landing.at[slot, region],
            send_sem=self.rs_s.at[slot * self.bits + level],
            recv_sem=self.rs_r.at[slot * self.bits + level],
            device_id=self.partner(odd, level),
            device_id_type=pl.DeviceIdType.MESH,
        )

    def absorb(self, slot, odd, level):
        self.reduce_copy(slot, odd, level).wait_recv()
        keep, _ = self.halves(odd, level)
        region = pl.ds(self.rows - (self.rows >> level), self.rows >> (level + 1))
        self.work[slot, keep, :] = self.work[slot, keep, :] + self.landing[slot, region, :]

    def spread_copy(self, buffer, sems, slot, odd, level, arriving):
        keep, give = self.halves(odd, level)
        span = give if arriving else keep
        return pltpu.make_async_remote_copy(
            src_ref=buffer.at[slot, span],
            dst_ref=buffer.at[slot, span],
            send_sem=sems[0].at[slot * self.bits + level],
            recv_sem=sems[1].at[slot * self.bits + level],
            device_id=self.partner(odd, level),
            device_id_type=pl.DeviceIdType.MESH,
        )

    def spread(self, slot, odd, level, arriving):
        return self.spread_copy(self.summed, (self.ag_s, self.ag_r), slot, odd, level, arriving)

    def move(self, piece, slot, store, start):
        columns = self.work.shape[2]
        first = self.crossing[0]
        sources = [(self.crossing[1], None, 0, first)]
        for source, target, count in self.jobs:
            sources.append((source, target, first, first + count))
            first += count
        for source, target, low, high in sources:
            if store and target is None:
                continue

            @pl.when((piece >= low) & (piece < high))
            def _():
                across = source.shape[2] // columns
                index = (piece - low) // across
                lanes = pl.ds(pl.multiple_of((piece - low - index * across) * columns, columns), columns)
                inside = self.summed.at[slot] if store else self.work.at[slot]
                if store and target.shape != source.shape:
                    copy = pltpu.make_async_copy(inside, target.at[piece - low], self.store_sem.at[slot])
                elif store:
                    copy = pltpu.make_async_copy(inside, target.at[index, :, lanes], self.store_sem.at[slot])
                else:
                    copy = pltpu.make_async_copy(source.at[index, :, lanes], inside, self.load_sem.at[slot])
                copy.start() if start else copy.wait()

    def load_first(self):
        self.move(jnp.int32(0), 0, False, True)

    def step(self, tick, cross):
        bits = self.bits
        for age in reversed(range(-1, 2 * bits + 2)):
            piece = tick - (age if age < 0 else min(age * self.gap, 2 * bits * self.gap + 1))
            safe = jnp.maximum(piece, 0)
            slot, odd = safe % self.slots, safe % 2
            plain = piece >= self.crossing[0]
            inside = (piece >= 0) & (piece < self.count)
            if age == 2 * bits + 1:

                @pl.when(inside)
                def _():
                    for level in range(bits):
                        self.reduce_copy(slot, odd, level).wait_send()

                @pl.when(inside & plain)
                def _():
                    self.move(piece, slot, True, False)

                @pl.when(inside & jnp.logical_not(plain))
                def _():
                    cross(piece, slot, odd, False)

            elif age == 2 * bits:

                @pl.when(inside & plain)
                def _():
                    self.spread(slot, odd, 0, True).wait_recv()
                    for level in range(bits):
                        self.spread(slot, odd, level, False).wait_send()

                    @pl.when(piece >= self.turned)
                    def _():
                        self.summed[slot] = self.summed[slot].T

                    self.move(piece, slot, True, True)

            elif age > bits:

                @pl.when(inside & plain)
                def _():
                    self.spread(slot, odd, 2 * bits - age, True).wait_recv()
                    self.spread(slot, odd, 2 * bits - 1 - age, False).start()

            elif age == bits:

                @pl.when(inside)
                def _():
                    self.absorb(slot, odd, bits - 1)

                @pl.when(inside & plain)
                def _():
                    own = self.span(self.start_of(odd, bits), bits)
                    self.summed[slot, own, :] = self.work[slot, own, :]
                    self.spread(slot, odd, bits - 1, False).start()

                @pl.when(inside & jnp.logical_not(plain))
                def _():
                    cross(piece, slot, odd, True)

            elif age > 0:

                @pl.when(inside)
                def _():
                    self.absorb(slot, odd, age - 1)
                    self.reduce_copy(slot, odd, age).start()

            elif age == 0:

                @pl.when(inside)
                def _():
                    self.move(piece, slot, False, False)
                    self.reduce_copy(slot, odd, 0).start()

            else:

                @pl.when(inside)
                def _():
                    self.move(piece, slot, False, True)


def close_kernel(
    size,
    group,
    chunks,
    hop,
    counts,
    gap,
    early,
    gunit_hbm,
    branch_hbm,
    seg_hbm,
    gres_hbm,
    res_hbm,
    gain_ref,
    early_ref,
    gout_ref,
    gup_ref,
    gdown_ref,
    gq_ref,
    gk_ref,
    gv_ref,
    gpack_ref,
    small_ref,
    result_ref,
    gseg_ref,
    gout_sum,
    gup_sum,
    gdown_sum,
    gq_sum,
    gk_sum,
    gv_sum,
    gpack_sum,
    first_out,
    second_out,
    relative_out,
    gunit_ref,
    branch_ref,
    seg_ref,
    gres_ref,
    res_ref,
    whole_seg,
    whole_out,
    seg_right,
    seg_left,
    out_right,
    out_left,
    total,
    work,
    landing,
    summed,
    cross_in,
    cross_work,
    small_cross,
    small_held,
    small_in,
    *sems,
):
    line = Line(size, chunks, hop)
    me = line.me
    line_s, recvs, sems = sems[0], sems[1:9], sems[9:]
    seg_scatter = ((True, seg_right, (line_s.at[0], recvs[0])), (False, seg_left, (line_s.at[1], recvs[1])))
    out_scatter = ((True, out_right, (line_s.at[2], recvs[2])), (False, out_left, (line_s.at[3], recvs[3])))
    seg_gather = ((True, (line_s.at[4], recvs[4])), (False, (line_s.at[5], recvs[5])))
    out_gather = ((True, (line_s.at[6], recvs[6])), (False, (line_s.at[7], recvs[7])))
    piece_sems = sems[:6]
    cross_s, cross_r, tail_s, tail_r, tail_store = sems[6:11]
    mix_s, mix_r, small_s, small_r = sems[11:15]
    seg_load, out_load, load_sem = sems[15:18]
    loads = [
        pltpu.make_async_copy(source, target, load_sem.at[index])
        for index, (source, target) in enumerate(((seg_hbm, seg_ref), (gres_hbm, gres_ref), (res_hbm, res_ref)))
    ]

    def part_load(source, target, load, chunk):
        here = pl.ds(chunk * size, size)
        return pltpu.make_async_copy(source.at[here], target.at[here], load.at[chunk])

    for chunk in range(chunks):
        part_load(gunit_hbm, gunit_ref, seg_load, chunk).start()
        if chunk >= early:
            part_load(branch_hbm, branch_ref, out_load, chunk).start()
    for load in loads:
        load.start()
    jobs = [
        (gup_ref, gup_sum, counts[1]),
        (gdown_ref, gdown_sum, counts[2]),
        (gq_ref, gq_sum, counts[3]),
        (gk_ref, gk_sum, counts[4]),
        (gv_ref, gv_sum, counts[5]),
        (gpack_ref, gpack_sum, counts[6]),
    ]
    pieces = Pieces(group, work.shape[1], gap, (counts[0], gout_ref), jobs, work, landing, summed, piece_sems)
    bits = pieces.bits
    pieces.load_first()
    greet(
        [{"mp": lax.rem(me + offset, size)} for offset in range(1, size)]
        + [{"dp": pieces.mine + (1 << bit) - 2 * (1 << bit) * ((pieces.mine // (1 << bit)) % 2)} for bit in range(bits)]
    )

    across, columns = cross_work.shape[0], work.shape[2]

    def cross_copy(slot, column, target, origin):
        own = pieces.span(pieces.start_of(column % 2, bits), bits)
        return pltpu.make_async_remote_copy(
            src_ref=work.at[slot, own],
            dst_ref=cross_in.at[column * size + origin],
            send_sem=cross_s.at[column * size + target],
            recv_sem=cross_r.at[column * size + origin],
            device_id={"mp": target},
            device_id_type=pl.DeviceIdType.MESH,
        )

    def cross(piece, slot, odd, start):
        target, column = piece // across, piece % across

        @pl.when(target != me)
        def _():
            copy = cross_copy(slot, column, target, me)
            copy.start() if start else copy.wait_send()

        if start:

            @pl.when(target == me)
            def _():
                own = pieces.span(pieces.start_of(odd, bits), bits)
                cross_in[column * size + me] = work[slot, own, :]

    def tail_copy(column):
        return pltpu.make_async_copy(
            cross_work.at[column],
            gout_sum.at[0, :, column * columns : (column + 1) * columns],
            tail_store.at[column],
        )

    def tail_spread(column, level, arriving):
        return pieces.spread_copy(cross_work, (tail_s, tail_r), column, column % 2, level, arriving)

    def tail_step(tick):
        base = counts[0] + bits * gap + gap
        for column in range(across):

            @pl.when(tick == base + column)
            def _():
                for offset in range(1, size):
                    cross_copy(0, column, me, lax.rem(me + offset, size)).wait_recv()
                own = pieces.span(pieces.start_of(column % 2, bits), bits)
                cross_work[column, own, :] = (
                    sum(cross_in[column * size + index] for index in range(1, size)) + cross_in[column * size]
                )
                tail_spread(column, bits - 1, False).start()

            for level in reversed(range(bits)):

                @pl.when(tick == base + column + (bits - level) * gap)
                def _():
                    tail_spread(column, level, True).wait_recv()
                    if level:
                        tail_spread(column, level - 1, False).start()
                    else:
                        tail_copy(column).start()

    def small_across(offset, arriving):
        origin = lax.rem(me - offset + size, size) if arriving else me
        return pltpu.make_async_remote_copy(
            src_ref=small_cross.at[me],
            dst_ref=small_cross.at[origin],
            send_sem=mix_s.at[offset],
            recv_sem=mix_r.at[offset],
            device_id={"mp": lax.rem(me + offset, size)},
            device_id_type=pl.DeviceIdType.MESH,
        )

    def small_within(level):
        step = 1 << level
        return pltpu.make_async_remote_copy(
            src_ref=small_held.at[level],
            dst_ref=small_in.at[level],
            send_sem=small_s.at[level],
            recv_sem=small_r.at[level],
            device_id={"dp": pieces.mine + step - 2 * step * ((pieces.mine // step) % 2)},
            device_id_type=pl.DeviceIdType.MESH,
        )

    def small_step(tick):
        @pl.when(tick == 0)
        def _():
            small_cross[me] = small_ref[...]
            for offset in range(1, size):
                small_across(offset, False).start()

        @pl.when(tick == 2)
        def _():
            value = small_ref[...]
            shared = lax.broadcasted_iota(jnp.int32, value.shape, 0) < 2
            for offset in range(1, size):
                small_across(offset, True).wait_recv()
                origin = lax.rem(me - offset + size, size)
                value = value + jnp.where(shared, small_cross[origin], 0.0)
            small_held[0] = value
            small_within(0).start()

        for level in range(bits):

            @pl.when(tick == 4 + 2 * level)
            def _():
                small_within(level).wait_recv()
                value = small_held[level] + small_in[level]
                if level + 1 < bits:
                    small_held[level + 1] = value
                    small_within(level + 1).start()
                else:
                    first_out[...] = value[0:1]
                    second_out[...] = value[1:2]
                    relative_out[...] = value[2 : 2 + relative_out.shape[0], : relative_out.shape[1]]

    def settle_seg(chunk):
        slot = chunk * size + me
        line.scatter_sum(chunk, gunit_ref, seg_scatter, total)
        rows = seg_ref[slot].astype(f32)
        scale = row_scale(rows)
        normed = rows * scale
        weighted = total[...] * gain_ref[...]
        grad = gres_ref[chunk] + scale * (
            weighted - normed * jnp.mean(weighted * normed, axis=-1, keepdims=True)
        )
        low = grad.astype(bf16)
        gseg_ref[slot] = low
        whole_seg[slot] = low.astype(f32)
        line.gather_start(chunk, whole_seg, seg_gather)

    def settle_out(chunk):
        slot = chunk * size + me

        @pl.when(chunk < early)
        def _():
            total[...] = early_ref[jnp.minimum(chunk, early - 1)]

        @pl.when(chunk >= early)
        def _():
            line.scatter_sum(chunk, branch_ref, out_scatter, total)
            total[...] = res_ref[chunk] + total[...]

        low = total[...].astype(bf16)
        result_ref[slot] = low
        whole_out[slot] = low.astype(f32)
        line.gather_start(chunk, whole_out, out_gather)

    def seg_landed(slot):
        gseg_ref[slot] = whole_seg[slot].astype(bf16)

    def out_landed(slot):
        result_ref[slot] = whole_out[slot].astype(bf16)

    settle_at = hop * line.reach
    seg_lag, out_lag = 0, -line.reach * early

    def step(tick, _):
        flows = (
            (seg_lag, gunit_hbm, seg_load, gunit_ref, seg_scatter, settle_seg, whole_seg, seg_gather, seg_landed),
            (out_lag, branch_hbm, out_load, branch_ref, out_scatter, settle_out, whole_out, out_gather, out_landed),
        )
        @pl.when(tick == 0)
        def _():
            for load in loads:
                load.wait()

        for late, source, load, part, scatter, settle, whole, gather, landed in flows:
            fresh, new = line.chunk_at(tick - late)

            first = early if late < 0 else 0

            @pl.when(new & (fresh >= first))
            def _():
                part_load(source, part, load, fresh).wait()

            line.scatter_step(tick - late, part, scatter, first)
            chunk, due = line.chunk_at(tick - late - settle_at)

            @pl.when(due)
            def _():
                settle(chunk)

        for late, source, load, part, scatter, settle, whole, gather, landed in flows:
            line.gather_step(tick - late - settle_at, whole, gather, landed)
        small_step(tick)

        def piece_step(beat, _):
            pieces.step(beat, cross)
            tail_step(beat)
            return 0

        lax.fori_loop(beats(tick), beats(tick + 1), piece_step, 0)
        return 0

    line_ticks = line.reach * (chunks - 1) + 2 * settle_at + 1

    def beats(tick):
        return jnp.minimum((tick * pieces.beats) // (line_ticks - 5), pieces.beats)

    lax.fori_loop(0, line_ticks, step, 0)

    line.scatter_drain(gunit_ref, seg_scatter)
    line.scatter_drain(branch_ref, out_scatter, early)
    line.gather_drain(whole_seg, seg_gather)
    line.gather_drain(whole_out, out_gather)
    for column in range(across):
        for level in range(bits):
            tail_spread(column, level, False).wait_send()
        tail_copy(column).wait()
    for offset in range(1, size):
        small_across(offset, False).wait_send()
    for level in range(bits):
        small_within(level).wait_send()


def close(
    grad_unit, branch, seg_rows, grad_residual, residual, gain, early, grads, small, relative_shape, size, group, chunks
):
    rows, width = seg_rows.shape
    piece = rows // (chunks * size)
    vmem = pl.BlockSpec(memory_space=pltpu.VMEM)
    whole = (chunks * size, piece, width)
    piece_rows, columns, gap = max(256, 8 * group), width // 4, 3 if group <= 8 else 2
    bits = group.bit_length() - 1
    slots = 2 * bits * gap + 2
    views = [grad.reshape(-1, piece_rows, grad.shape[1]) for grad in grads]
    counts = tuple(view.shape[0] * (view.shape[2] // columns) for view in views)
    anywhere = pl.BlockSpec(memory_space=pl.ANY)
    dma = pltpu.SemaphoreType.DMA
    sums = [jax.ShapeDtypeStruct(view.shape, f32) for view in views]
    sums[0] = jax.ShapeDtypeStruct((1, piece_rows, width), f32)
    for index in range(3, len(views)):
        turned_shape = (views[index].shape[2] // columns, columns, piece_rows)
        sums[index] = jax.ShapeDtypeStruct(turned_shape, f32)
    return pl.pallas_call(
        functools.partial(close_kernel, size, group, chunks, 2, counts, gap, early.shape[0]),
        in_specs=[anywhere] * 5 + [vmem] * 2 + [anywhere] * len(views) + [vmem],
        out_specs=[vmem] * 2 + [anywhere] * len(views) + [vmem] * 3,
        out_shape=[jax.ShapeDtypeStruct(whole, bf16)] * 2 + sums
        + [jax.ShapeDtypeStruct(shape, f32) for shape in ((1, width), (1, width), relative_shape)],
        scratch_shapes=[pltpu.VMEM(whole, f32)] * 2
        + [
            pltpu.VMEM(whole, bf16),
            pltpu.VMEM(grad_residual.shape, f32),
            pltpu.VMEM(grad_residual.shape, f32),
        ]
        + [pltpu.VMEM(whole, f32)] * 6
        + [
            pltpu.VMEM((piece, width), f32),
            pltpu.VMEM((slots, piece_rows, columns), f32),
            pltpu.VMEM((slots, piece_rows, columns), f32),
            pltpu.VMEM((slots, piece_rows, columns), f32),
            pltpu.VMEM((width // columns * size, piece_rows // group, columns), f32),
            pltpu.VMEM((width // columns, piece_rows, columns), f32),
            pltpu.VMEM((size, *small.shape), f32),
            pltpu.VMEM((bits, *small.shape), f32),
            pltpu.VMEM((bits, *small.shape), f32),
        ]
        + [dma((8,))]
        + [dma((chunks * size,))] * 8
        + [dma((slots * bits,))] * 4
        + [dma((slots,))] * 2
        + [dma((width // columns * size,))] * 2
        + [dma((width // columns * bits,))] * 2
        + [dma((width // columns,))]
        + [dma((size,))] * 2
        + [dma((bits,))] * 2
        + [dma((chunks,))] * 2
        + [dma((3,))],
        compiler_params=pltpu.CompilerParams(
            collective_id=1, has_side_effects=True, vmem_limit_bytes=63 << 20
        ),
        cost_estimate=pl.CostEstimate(flops=10**11, bytes_accessed=10**9, transcendentals=0),
        name="close",
    )(
        grad_unit.reshape(whole),
        branch,
        seg_rows.reshape(whole),
        grad_residual,
        residual,
        gain[None, :],
        early,
        *views,
        small,
    )


def body(
    inputs,
    memory,
    compressed_memory,
    memory_fill,
    compressed_fill,
    first_gain,
    query_weight,
    key_weight,
    value_weight,
    relative_bias,
    output_weight,
    second_gain,
    up_weight,
    down_weight,
    compress_weight,
    grad_output,
    grad_compressed,
    *,
    mp_size,
    dp_size,
):
    streams, seg_len, width = inputs.shape
    mem_len = memory.shape[1]
    packed_len = compressed_memory.shape[1]
    local = query_weight.shape[1]
    rows = streams * seg_len
    unit, q, k, v, mixed, log_total, packed_new, grad_pack, begun = attend(
        inputs,
        memory,
        compressed_memory,
        memory_fill,
        compressed_fill,
        first_gain,
        query_weight,
        key_weight,
        value_weight,
        relative_bias,
        compress_weight,
        grad_compressed,
        output_weight,
        mp_size,
        dp_size,
    )
    seg_rows = inputs.reshape(rows, width)
    grad_mixed, grad_residual, residual, branch, grad_down, grad_up, grad_out_full, grad_second = feed(
        mixed.reshape(rows, local),
        seg_rows,
        grad_output.reshape(rows, width),
        up_weight,
        down_weight,
        begun,
        second_gain,
        mp_size,
        dp_size,
        chunk_count,
    )
    grad_mixed = grad_mixed.reshape(streams, seg_len, local)
    grad_unit, gq, gk, gv, small, early = attend_back(
        unit,
        q,
        k,
        v,
        log_total,
        grad_mixed,
        memory_fill,
        compressed_fill,
        query_weight,
        key_weight,
        value_weight,
        relative_bias,
        first_gain,
        grad_second,
        mem_len,
        packed_len,
        branch,
        residual,
        mp_size,
        early_chunks,
    )
    result, grad_seg, grad_out_w, grad_up, grad_down, gq, gk, gv, grad_pack, grad_first, grad_second, grad_relative = close(
        grad_unit,
        branch,
        seg_rows,
        grad_residual,
        residual,
        first_gain,
        early,
        (grad_out_full, grad_up, grad_down, gq, gk, gv, grad_pack),
        small,
        relative_bias.shape,
        mp_size,
        dp_size,
        chunk_count,
    )
    grad_first, grad_second = grad_first[0], grad_second[0]
    result = result.reshape(inputs.shape)
    grad_seg = grad_seg.reshape(inputs.shape)
    grad_query_w, grad_key_w, grad_value_w = (grad.reshape(width, local) for grad in (gq, gk, gv))
    grad_out_w = grad_out_w.reshape(local, width)
    grad_compress_w = grad_pack.reshape(2 * width, local)
    grad_up = grad_up.reshape(up_weight.shape)
    grad_down = grad_down.reshape(down_weight.shape)
    return (
        result,
        packed_new,
        grad_seg,
        grad_first,
        grad_query_w,
        grad_key_w,
        grad_value_w,
        grad_relative,
        grad_out_w,
        grad_second,
        grad_up,
        grad_down,
        grad_compress_w,
    )


def solution(mesh):
    in_specs = (
        P("dp", None, None),
        P("dp", None, None),
        P("dp", None, None),
        P("dp"),
        P("dp"),
        P(),
        P(None, "mp"),
        P(None, "mp"),
        P(None, "mp"),
        P("mp", None),
        P("mp", None),
        P(),
        P(None, "mp"),
        P("mp", None),
        P(None, "mp"),
        P("dp", None, None),
        P("dp", None, "mp"),
    )
    out_specs = (
        P("dp", None, None),
        P("dp", None, "mp"),
        P("dp", None, None),
        P(),
        P(None, "mp"),
        P(None, "mp"),
        P(None, "mp"),
        P("mp", None),
        P("mp", None),
        P(),
        P(None, "mp"),
        P("mp", None),
        P(None, "mp"),
    )
    return jax.shard_map(
        functools.partial(body, mp_size=mesh.shape["mp"], dp_size=mesh.shape["dp"]),
        mesh=mesh,
        in_specs=in_specs,
        out_specs=out_specs,
        check_vma=False,
    )
```
